32 devices in a mesh: dp: 32 (over z, y, x, core).
Axes of the slice: x: 2, y: 2, z: 4, core: 2. Of those that a mesh axis runs over, the one named last changes fastest.
Arguments:
- tokens: bfloat16 [32768, 1024], P('dp'), may hold values from -6 to 6
- cotangent: bfloat16 [32768, 1024], P('dp'), may hold values from -6 to 6
- seq_lengths: int32 [64], replicated, may hold values from 256 to 512, as said below
- seq_place: int32 [64], replicated, may hold values from 0 to 63, each once
- ln1_gain: bfloat16 [1024], P('dp'), may hold values from 0.5 to 1.5
- ln1_bias: bfloat16 [1024], P('dp'), may hold values from -1.5 to 1.5
- w_qkv: bfloat16 [1024, 3072], P('dp'), may hold values from -6 to 6
- q_bias: bfloat16 [1024], P('dp'), may hold values from -2.5 to 2.5
- v_bias: bfloat16 [1024], P('dp'), may hold values from -2.5 to 2.5
- w_out: bfloat16 [1024, 1024], P('dp'), may hold values from -1.5 to 1.5
- out_bias: bfloat16 [1024], P('dp'), may hold values from -1.5 to 1.5
- ln2_gain: bfloat16 [1024], P('dp'), may hold values from 0.5 to 1.5
- ln2_bias: bfloat16 [1024], P('dp'), may hold values from -1.5 to 1.5
- w_fc: bfloat16 [1024, 4096], P('dp'), may hold values from -0.1875 to 0.1875
- fc_bias: bfloat16 [4096], P('dp'), may hold values from -2.5 to 2.5
- w_proj: bfloat16 [4096, 1024], P('dp'), may hold values from -0.09375 to 0.09375
- proj_bias: bfloat16 [1024], P('dp'), may hold values from -1.5 to 1.5
Outputs:
- block_output: bfloat16 [32768, 1024], P('dp')
- tokens_grad: bfloat16 [32768, 1024], P('dp')
- ln1_gain_grad: float32 [1024], P('dp')
- ln1_bias_grad: float32 [1024], P('dp')
- w_qkv_grad: float32 [1024, 3072], P('dp')
- q_bias_grad: float32 [1024], P('dp')
- v_bias_grad: float32 [1024], P('dp')
- w_out_grad: float32 [1024, 1024], P('dp')
- out_bias_grad: float32 [1024], P('dp')
- ln2_gain_grad: float32 [1024], P('dp')
- ln2_bias_grad: float32 [1024], P('dp')
- w_fc_grad: float32 [1024, 4096], P('dp')
- fc_bias_grad: float32 [4096], P('dp')
- w_proj_grad: float32 [4096, 1024], P('dp')
- proj_bias_grad: float32 [1024], P('dp')
The draws below stay inside these ranges and needn't reach their ends.
Inputs may be any that keep to these rules, and one draw needn't show every extreme that they name: `seq_lengths`: some sequence has exactly 512 tokens and some exactly 256. `seq_place`: every slot receives exactly one sequence.
All inputs are finite; a program needn't handle non-finite values.
Results may differ from the reference program's by a relative error of at most 0.012.
Values may be sent and summed in bfloat16 or wider, within the bound.
A program may use at most 256 MiB of HBM per device.

```python
import jax
import jax.numpy as jnp
from jax import lax

D = 1024
HEADS = 16
HEAD_DIM = 64
FF = 4096
LEN_MAX = 512
MB = 2
LEN_MIN = 256
NSEQ = 64
TOKENS = 32768
N_DP = 32


def draw_seq_lengths(key, part):
    key_one, key_two, key_three = jax.random.split(key, 3)
    lengths = jax.random.randint(key_one, (NSEQ,), LEN_MIN, LEN_MAX + 1)
    longest_at = jax.random.randint(key_two, (), 0, NSEQ)
    shortest_at = (longest_at + 1 + jax.random.randint(key_three, (), 0, NSEQ - 1)) % NSEQ
    lengths = lengths.at[longest_at].set(LEN_MAX)
    lengths = lengths.at[shortest_at].set(LEN_MIN)
    return lengths.astype(jnp.int32)


def draw_w_qkv(key, part):
    key_one = jax.random.fold_in(key, 0)
    weights = jax.random.truncated_normal(key_one, -4.0, 4.0, (D, 3 * D), jnp.float32) * D ** (-0.5)
    return weights.astype(jnp.bfloat16)


def spiked(entries, rng, source, target, blocks, factor):
    def block_of(dim):
        return (jnp.arange(entries.shape[dim]) // (entries.shape[dim] // blocks)).reshape((-1,) + (1,) * (entries.ndim - 1 - dim))

    near = jax.random.permutation(rng, blocks)[block_of(target)]
    other_side = (block_of(target) + blocks // 2) % blocks
    return jnp.where((block_of(source) == near) | (block_of(source) == other_side), factor * entries, entries)


def shard_levels(key, extent, cuts, low, high):
    def one(axis_at, shards_of):
        steps = jax.random.uniform(jax.random.fold_in(jax.random.fold_in(key, 6), axis_at), (shards_of,), jnp.float32, low / len(cuts), high / len(cuts))
        return jnp.repeat(jnp.exp(steps), extent[axis_at] // shards_of).reshape((-1,) + (1,) * (len(extent) - axis_at - 1))

    gain = one(*cuts[0])
    for cut in cuts[1:]:
        gain = gain * one(*cut)
    return gain


def scatter_about(stream_key, extent, deviation, bound, shards=(), kind=jnp.bfloat16):
    level = shard_levels(stream_key, extent, shards, -0.22, 0.18) if shards else 1.0
    array = jax.random.normal(stream_key, extent, jnp.float32) * deviation * level
    return jnp.minimum(jnp.maximum(array, -bound), bound).astype(kind)


def bell_draw_with(key, dims, scale, bound, cuts, heavy, kind=jnp.bfloat16):
    array = scale * jax.random.normal(key, dims, jnp.float32)
    if cuts:
        array = array * shard_levels(key, dims, cuts, -0.22, 0.18)
    return jnp.clip(spiked(array, jax.random.fold_in(key, 3), *heavy), -bound, bound).astype(kind)


def setup_inputs(seed: int = 0) -> dict:
    splits = jax.random.split(jax.random.key(seed), 18)
    tokens = scatter_about(splits[0], (TOKENS, D), 1.0, 6.0, ((0, 32),))
    cotangent = bell_draw_with(splits[1], (TOKENS, D), 1.0, 6.0, ((0, 32),), (0, 1, 32, 2.75))
    seq_lengths = draw_seq_lengths(jax.random.fold_in(splits[17], 71), 0)
    seq_place = jax.random.permutation(splits[3], NSEQ).astype(jnp.int32)
    ln1_gain = jnp.clip(1.0 + 0.1 * jax.random.normal(splits[4], (D,), jnp.float32), 0.5, 1.5).astype(jnp.bfloat16)
    ln1_bias = scatter_about(splits[5], (D,), 0.3, 1.5, ((0, 32),))
    w_qkv = draw_w_qkv(jax.random.fold_in(splits[17], 71), 0)
    q_bias = scatter_about(splits[7], (D,), 0.5, 2.5, ((0, 32),))
    v_bias = scatter_about(splits[8], (D,), 0.5, 2.5, ((0, 32),))
    w_out = scatter_about(splits[9], (D, D), (D // 64) ** -0.5, 1.5, ((0, 32),))
    out_bias = scatter_about(splits[10], (D,), 0.3, 1.5, ((0, 32),))
    ln2_gain = jnp.clip(1.0 + 0.1 * jax.random.normal(splits[11], (D,), jnp.float32), 0.5, 1.5).astype(jnp.bfloat16)
    ln2_bias = scatter_about(splits[12], (D,), 0.3, 1.5, ((0, 32),))
    w_fc = scatter_about(splits[13], (D, FF), D ** -0.5, 0.1875, ((0, 32),))
    fc_bias = scatter_about(splits[14], (FF,), 0.5, 2.5, ((0, 32),))
    w_proj = scatter_about(splits[15], (FF, D), FF ** -0.5, 0.09375, ((0, 32),))
    proj_bias = scatter_about(splits[16], (D,), 0.3, 1.5, ((0, 32),))
    return {"tokens": tokens, "cotangent": cotangent, "seq_lengths": seq_lengths, "seq_place": seq_place, "ln1_gain": ln1_gain, "ln1_bias": ln1_bias, "w_qkv": w_qkv, "q_bias": q_bias, "v_bias": v_bias, "w_out": w_out, "out_bias": out_bias, "ln2_gain": ln2_gain, "ln2_bias": ln2_bias, "w_fc": w_fc, "fc_bias": fc_bias, "w_proj": w_proj, "proj_bias": proj_bias}


@jax.custom_vjp
def low(v):
    return lax.optimization_barrier(v.astype(jnp.bfloat16)).astype(jnp.float32)

@jax.custom_vjp
def low_back(v):
    return v

def low_keep(v):
    return (low(v), None)

def low_pass(kept, grad):
    return (grad,)

def back_keep(v):
    return (v, None)

def back_low(kept, grad):
    return (low(grad),)
low.defvjp(low_keep, low_pass)
low_back.defvjp(back_keep, back_low)
epsilon = 1e-05

def layer_norm(inputs, scaling, offset):
    center = inputs - lax.optimization_barrier(jnp.mean(inputs, axis=-1, keepdims=True))
    spread = lax.optimization_barrier(jnp.mean(center * center, axis=-1, keepdims=True))
    return center * lax.rsqrt(spread + epsilon) * scaling + offset

def matmul_high(left_side, right_side):
    return jnp.einsum('...i,ij->...j', left_side, right_side, precision=lax.Precision.HIGHEST)

def forward(params, slot_tokens, slot_lengths):
    ln1_gain, ln1_bias, w_qkv, q_bias, v_bias, w_out, out_bias, ln2_gain, ln2_bias, w_fc, fc_bias, w_proj, proj_bias = params
    slot_count = slot_tokens.shape[0]
    row_count = slot_tokens.shape[1]
    model_width = slot_tokens.shape[2]
    normed = low(layer_norm(slot_tokens, ln1_gain, ln1_bias))
    zeros_mid = jnp.zeros_like(q_bias)
    projected = matmul_high(normed, w_qkv) + jnp.concatenate([q_bias, zeros_mid, v_bias])
    projected = low_back(low(projected))
    split_heads = projected.reshape(slot_count, row_count, 3, HEADS, HEAD_DIM)
    queries = split_heads[:, :, 0]
    key_vectors = split_heads[:, :, 1]
    values = split_heads[:, :, 2]
    scores = jnp.einsum('sqhd,skhd->shqk', queries, key_vectors, precision=lax.Precision.HIGHEST) * HEAD_DIM ** (-0.5)
    scores = low_back(scores)
    position = jnp.arange(row_count, dtype=jnp.int32)
    allowed = (position[None, :] <= position[:, None])[None] & (position[None, None, :] < slot_lengths[:, None, None])
    scores = jnp.where(allowed[:, None], scores, -1e+30)
    attend = low(jax.nn.softmax(scores, axis=-1))
    context = jnp.einsum('shqk,skhd->sqhd', attend, values, precision=lax.Precision.HIGHEST)
    context = low_back(low(context.reshape(slot_count, row_count, model_width)))
    residual = slot_tokens + low_back(matmul_high(context, w_out) + out_bias)
    normed_two = low(layer_norm(residual, ln2_gain, ln2_bias))
    hidden = low_back(matmul_high(normed_two, w_fc) + fc_bias)
    activated = low(jax.nn.gelu(hidden, approximate=True))
    branch = low_back(matmul_high(activated, w_proj) + proj_bias)
    valid_rows = (position[None, :] < slot_lengths[:, None])[:, :, None]
    return jnp.where(valid_rows, residual + branch, 0.0)

def reference(tokens, cotangent, seq_lengths, seq_place, ln1_gain, ln1_bias, w_qkv, q_bias, v_bias, w_out, out_bias, ln2_gain, ln2_bias, w_fc, fc_bias, w_proj, proj_bias):
    params = tuple((argument.astype(jnp.float32) for argument in (ln1_gain, ln1_bias, w_qkv, q_bias, v_bias, w_out, out_bias, ln2_gain, ln2_bias, w_fc, fc_bias, w_proj, proj_bias)))
    slot_lengths = jnp.zeros((NSEQ,), jnp.int32).at[seq_place.astype(jnp.int32)].set(seq_lengths.astype(jnp.int32))
    grouped = tokens.astype(jnp.float32).reshape(N_DP, MB, LEN_MAX, D)
    group_lengths = slot_lengths.reshape(N_DP, MB)

    def whole_block(weights, inputs):

        def one_group(group_pair):
            return forward(weights, group_pair[0], group_pair[1])
        return lax.map(jax.checkpoint(one_group), (inputs, group_lengths))
    result, pullback = jax.vjp(whole_block, params, grouped)
    grad_params, grad_inputs = pullback(cotangent.astype(jnp.float32).reshape(N_DP, MB, LEN_MAX, D))
    return (result.reshape(TOKENS, D).astype(jnp.bfloat16), grad_inputs.reshape(TOKENS, D).astype(jnp.bfloat16), grad_params[0], grad_params[1], grad_params[2], grad_params[3], grad_params[4], grad_params[5], grad_params[6], grad_params[7], grad_params[8], grad_params[9], grad_params[10], grad_params[11], grad_params[12])
```

```python
import jax
import jax.numpy as jnp
from jax import lax
from jax.experimental import pallas as pl
from jax.experimental.pallas import tpu as pltpu
from jax.sharding import PartitionSpec as P

MESH = pl.DeviceIdType.MESH
ANY = pl.BlockSpec(memory_space=pl.ANY)
VMEM = pl.BlockSpec(memory_space=pltpu.VMEM)
DMA = pltpu.SemaphoreType.DMA


def grid_dims(n):
    half = n // 2
    first = 4 if half % 4 == 0 else half
    rest = half // first
    second = 1
    while second * second < rest:
        second *= 2
    return first, second, rest // second


class Place:
    def __init__(self, dims):
        self.dims = dims
        d1, d2, d3 = dims
        me = lax.axis_index("dp")
        self.z = me // (d2 * d3 * 2)
        self.y = (me // (d3 * 2)) % d2
        self.x = (me // 2) % d3
        self.c = me % 2
        self.zs = [(self.z + k) % d1 for k in range(1, d1)]
        self.ys = [(self.y + k) % d2 for k in range(1, d2)]
        self.xs = [(self.x + k) % d3 for k in range(1, d3)]
        self.to_z = [self.dev(z=v) for v in self.zs]
        self.to_y = [self.dev(y=v) for v in self.ys]
        self.to_x = [self.dev(x=v) for v in self.xs]
        self.to_p = self.dev(c=1 - self.c)

    def dev(self, **at):
        z, y, x, c = (at.get(name, getattr(self, name)) for name in "zyxc")
        _, d2, d3 = self.dims
        return (((z * d2 + y) * d3 + x) * 2 + c,)

    def barrier(self):
        semaphore = pltpu.get_barrier_semaphore()
        peers = self.to_z + self.to_y + self.to_x + [self.to_p]
        for peer in peers:
            pl.semaphore_signal(semaphore, inc=1, device_id=peer, device_id_type=MESH)
        pl.semaphore_wait(semaphore, len(peers))


def send(source, target, send_sem, recv_sem, device):
    return pltpu.make_async_remote_copy(
        src_ref=source,
        dst_ref=target,
        send_sem=send_sem,
        recv_sem=recv_sem,
        device_id=device,
        device_id_type=MESH,
    )


class Gather:
    def __init__(self, place, shards, wholes, chunks, kinds, sems, small=None):
        self.at, self.shards, self.wholes = place, shards, wholes
        self.chunks, self.kinds, self.small = chunks, kinds, small
        self.sems = sems
        self.flying = {}
        self.ahead = 3

    @staticmethod
    def semaphores(dims, count):
        d1, d2, d3 = dims
        sizes = [max(d1, d2 + d3), 2 * d1 + d2 + d3, d2 + d3, 1, 4 * (d1 + d2 + d3)]
        shapes = []
        for size in sizes[:4]:
            shapes += [DMA((count, size)), DMA((count, size))]
        return shapes + [DMA((sizes[4],)), DMA((sizes[4],))]

    def copies(self, stage, t):
        p = self.at
        z, y, x, c = p.z, p.y, p.x, p.c
        i, first, width = self.chunks[t]
        whole, shard, half = self.wholes[i], self.shards[i], width // 2
        full = pl.ds(first, width)
        a, b = pl.ds(first, half), pl.ds(first + half, half)
        pieces = []
        if stage == 0 and self.kinds[t] == 0:
            pieces = [(shard.at[:, full], whole.at[z, y, x, c, :, full], d) for d in p.to_z]
        elif stage == 0:
            pieces = [(shard.at[:, a], whole.at[z, y, x, c, :, a], d) for d in p.to_x]
            pieces += [(shard.at[:, b], whole.at[z, y, x, c, :, b], d) for d in p.to_y]
        elif stage == 1 and self.kinds[t] == 0:
            part = whole.at[:, y, x, c, :, a]
            pieces = [(part, part, d) for d in p.to_x]
            part = whole.at[:, y, x, c, :, b]
            pieces += [(part, part, d) for d in p.to_y]
        elif stage == 1:
            left, right = whole.at[z, y, :, c, :, a], whole.at[z, :, x, c, :, b]
            pieces = [(part, part, d) for d in p.to_z for part in (left, right)]
        elif stage == 2:
            part = whole.at[:, y, :, c, :, a]
            pieces = [(part, part, d) for d in p.to_y]
            part = whole.at[:, :, x, c, :, b]
            pieces += [(part, part, d) for d in p.to_x]
        else:
            part = whole.at[:, :, :, c, :, full]
            pieces = [(part, part, p.to_p)]
        out, back = self.sems[2 * stage], self.sems[2 * stage + 1]
        made = [send(s, d, out.at[t, k], back.at[t, k], to) for k, (s, d, to) in enumerate(pieces)]
        if t == 0 and self.small is not None:
            source, target = self.small
            if stage == 0:
                pieces = [(source, target.at[z, y, x, c], d) for d in p.to_z]
            elif stage == 1:
                part = target.at[:, y, x, c]
                pieces = [(part, part, d) for d in p.to_x]
            elif stage == 2:
                part = target.at[:, y, :, c]
                pieces = [(part, part, d) for d in p.to_y]
            else:
                part = target.at[:, :, :, c]
                pieces = [(part, part, p.to_p)]
            base = stage * sum(p.dims)
            out, back = self.sems[8], self.sems[9]
            made += [
                send(s, d, out.at[base + k], back.at[base + k], to)
                for k, (s, d, to) in enumerate(pieces)
            ]
        return made

    def go(self, stage, t):
        if 0 <= t < len(self.chunks):
            self.flying[stage, t] = self.copies(stage, t)
            for copy in self.flying[stage, t]:
                copy.start()

    def arrived(self, stage, t):
        for copy in self.flying[stage, t]:
            copy.wait_recv()

    def begin(self):
        for t in range(self.ahead):
            self.go(0, t)

    def advance(self, t):
        count = len(self.chunks)
        if t < count:
            self.arrived(0, t)
            self.go(1, t)
            self.go(0, t + self.ahead)
        if 0 <= t - 1 < count:
            self.arrived(1, t - 1)
            self.go(2, t - 1)
        if 0 <= t - 2 < count:
            self.arrived(2, t - 2)
            self.go(3, t - 2)

    def finish(self):
        for copies in self.flying.values():
            for copy in copies:
                copy.wait_send()


def gather_kernel(dims, chunks, kinds, count, *refs):
    shards, small = refs[:count], refs[count]
    wholes, small_whole = refs[count + 1 : 2 * count + 1], refs[2 * count + 1]
    local = refs[2 * count + 2]
    sems = refs[2 * count + 3 :]
    place = Place(dims)
    z, y, x, c = place.z, place.y, place.x, place.c
    moves = [
        pltpu.make_async_copy(s, w.at[z, y, x, c], local.at[i])
        for i, (s, w) in enumerate(zip((*shards, small), (*wholes, small_whole)))
    ]
    for move in moves:
        move.start()
    place.barrier()
    gather = Gather(place, shards, wholes, chunks, kinds, sems, (small, small_whole))
    gather.begin()
    for move in moves:
        move.wait()
    for t in range(len(chunks) + 2):
        gather.advance(t)
    for t in range(len(chunks)):
        gather.arrived(3, t)
    gather.finish()


def gather_all(dims, shards, small, chunks, kinds):
    count = len(shards)
    shapes = [jax.ShapeDtypeStruct((*dims, 2, *s.shape), s.dtype) for s in (*shards, small)]
    return pl.pallas_call(
        lambda *refs: gather_kernel(dims, chunks, kinds, count, *refs),
        out_shape=shapes,
        in_specs=[VMEM] * (count + 1),
        out_specs=[ANY] * (count + 1),
        scratch_shapes=[DMA((count + 1,)), *Gather.semaphores(dims, len(chunks))],
        compiler_params=pltpu.CompilerParams(collective_id=0, has_side_effects=True),
        name="gather",
    )(*shards, small)


class Reduce:
    @staticmethod
    def scratch(dims, rows, width, dtype, halves=True):
        d1, d2, d3 = dims
        half = width // 2 if halves else width
        shapes = [pltpu.VMEM((d1, d2, d3, rows, width), dtype)]
        shapes.append(pltpu.VMEM((d2 - 1, d1, d3, rows, half), dtype))
        shapes.append(pltpu.VMEM((d3 - 1, d1, rows, half), dtype))
        if halves:
            shapes.append(pltpu.VMEM((d3 - 1, d1, d2, rows, half), dtype))
            shapes.append(pltpu.VMEM((d2 - 1, d1, rows, half), dtype))
        shapes.append(pltpu.VMEM((d1 - 1, rows, width), dtype))
        sizes = (1, d2 + d3, d2 + d3, d1)
        for size in sizes:
            shapes += [DMA((size,)), DMA((size,))]
        return shapes

    def __init__(self, place, refs, source, own, result, halves=True):
        self.at, self.halves = place, halves
        self.source, self.own, self.result = source, own, result
        if halves:
            self.total, self.ya, self.xa, self.xb, self.yb, self.zz = refs[:6]
            self.sems = refs[6:]
        else:
            self.total, self.ya, self.xa, self.zz = refs[:4]
            self.sems = refs[4:]
        self.flying = {}
        width = self.total.shape[-1]
        half = width // 2 if halves else width
        self.a, self.b = pl.ds(0, half), pl.ds(half, half)

    def pieces(self, stage):
        p, h = self.at, self.total
        y, x = p.y, p.x
        if stage == 0:
            return [(self.source.at[:, :, :, 1 - p.c], h, p.to_p)]
        if stage == 1:
            made = [
                (h.at[:, v, :, :, self.a], self.ya.at[k], d)
                for k, (v, d) in enumerate(zip(p.ys, p.to_y))
            ]
            if self.halves:
                made += [
                    (h.at[:, :, v, :, self.b], self.xb.at[k], d)
                    for k, (v, d) in enumerate(zip(p.xs, p.to_x))
                ]
            return made
        if stage == 2:
            made = [
                (h.at[:, y, v, :, self.a], self.xa.at[k], d)
                for k, (v, d) in enumerate(zip(p.xs, p.to_x))
            ]
            if self.halves:
                made += [
                    (h.at[:, v, x, :, self.b], self.yb.at[k], d)
                    for k, (v, d) in enumerate(zip(p.ys, p.to_y))
                ]
            return made
        return [(h.at[v, y, x], self.zz.at[k], d) for k, (v, d) in enumerate(zip(p.zs, p.to_z))]

    def go(self, stage):
        out, back = self.sems[2 * stage], self.sems[2 * stage + 1]
        self.flying[stage] = [
            send(s, d, out.at[k], back.at[k], to) for k, (s, d, to) in enumerate(self.pieces(stage))
        ]
        for copy in self.flying[stage]:
            copy.start()

    def arrived(self, stage):
        for copy in self.flying[stage]:
            copy.wait_recv()

    def add(self, stage):
        p, h = self.at, self.total
        d1, d2, d3 = p.dims
        f32 = jnp.float32

        def into(at, terms):
            value = h[at].astype(f32)
            for term in terms:
                value = value + term.astype(f32)
            h[at] = value.astype(h.dtype)

        if stage == 0:

            @pl.loop(0, d1)
            def _(i):
                for j in range(d2):
                    for k in range(d3):
                        into((i, j, k), [self.own[i, j, k]])

        elif stage == 1:

            @pl.loop(0, d1)
            def _(i):
                for k in range(d3):
                    into(
                        (i, p.y, k, slice(None), self.a),
                        [self.ya[m, i, k] for m in range(d2 - 1)],
                    )
                if self.halves:
                    for j in range(d2):
                        into(
                            (i, j, p.x, slice(None), self.b),
                            [self.xb[m, i, j] for m in range(d3 - 1)],
                        )

        elif stage == 2:

            @pl.loop(0, d1)
            def _(i):
                into((i, p.y, p.x, slice(None), self.a), [self.xa[m, i] for m in range(d3 - 1)])
                if self.halves:
                    into(
                        (i, p.y, p.x, slice(None), self.b),
                        [self.yb[m, i] for m in range(d2 - 1)],
                    )

        else:
            value = h[p.z, p.y, p.x].astype(f32)
            for m in range(d1 - 1):
                value = value + self.zz[m].astype(f32)
            self.result[...] = value

    def step(self, stage):
        self.arrived(stage)
        self.add(stage)
        if stage < 3:
            self.go(stage + 1)

    def finish(self):
        for copies in self.flying.values():
            for copy in copies:
                copy.wait_send()


def reduce_kernel(dims, chunks, count, per, per_small, *refs):
    terms, small = refs[:count], refs[count]
    results, small_result = refs[count + 1 : 2 * count + 1], refs[2 * count + 1]
    refs = refs[2 * count + 2 :]
    load_sems, refs = refs[0], refs[1:]
    owns, refs = refs[: len(chunks)], refs[len(chunks) :]
    place = Place(dims)
    c = place.c
    parts, loads = [], []
    for t, (i, first, width) in enumerate(chunks):
        cut = pl.ds(first, width)
        parts.append(
            Reduce(
                place,
                refs[t * per : (t + 1) * per],
                terms[i].at[:, :, :, :, :, cut],
                owns[t],
                results[i].at[:, cut],
            )
        )
        loads.append(
            pltpu.make_async_copy(terms[i].at[:, :, :, c, :, cut], owns[t], load_sems.at[t])
        )
    last = Reduce(place, refs[len(chunks) * per :], small, small.at[:, :, :, c], small_result, halves=False)
    place.barrier()
    count_t = len(chunks)
    for s in range(count_t + 4):
        for stage in (3, 2, 1, 0):
            t = s - 1 - stage
            if 0 <= t < count_t:
                if stage == 0:
                    loads[t].wait()
                parts[t].step(stage)
                if t == 0:
                    last.step(stage)
        if s < count_t:
            parts[s].go(0)
            loads[s].start()
            if s == 0:
                last.go(0)
    for part in (*parts, last):
        part.finish()


def reduce_all(dims, terms, small, chunks):
    n = dims[0] * dims[1] * dims[2] * 2
    views = [t.reshape(*dims, 2, t.shape[0] // n, t.shape[1]) for t in terms]
    small = small.reshape(*dims, 2, small.shape[0] // n, small.shape[1])
    scratch = [DMA((len(chunks),))]
    for i, _, width in chunks:
        scratch.append(pltpu.VMEM((*dims, views[i].shape[4], width), views[i].dtype))
    per = 0
    for i, _, width in chunks:
        made = Reduce.scratch(dims, views[i].shape[4], width, views[i].dtype)
        per = len(made)
        scratch += made
    made = Reduce.scratch(dims, small.shape[4], small.shape[5], small.dtype, halves=False)
    scratch += made
    count = len(terms)
    return pl.pallas_call(
        lambda *refs: reduce_kernel(dims, chunks, count, per, len(made), *refs),
        out_shape=[jax.ShapeDtypeStruct(v.shape[4:], jnp.float32) for v in (*views, small)],
        in_specs=[ANY] * count + [VMEM],
        out_specs=[VMEM] * (count + 1),
        scratch_shapes=scratch,
        compiler_params=pltpu.CompilerParams(
            collective_id=1, has_side_effects=True, vmem_limit_bytes=60 * 1024 * 1024
        ),
        name="reduce",
    )(*views, small)


HEAD_DIM = 64
MB = 2
EPS = 1e-05
BF = jnp.bfloat16
F32 = jnp.float32


def layer_norm(inputs, scaling, offset):
    center = inputs - jnp.mean(inputs, axis=-1, keepdims=True)
    spread = jnp.mean(center * center, axis=-1, keepdims=True)
    return center * lax.rsqrt(spread + EPS) * scaling + offset


def gelu_tanh(inputs):
    return jax.nn.gelu(inputs, approximate=True)


def dot(left, right, dims):
    return lax.dot_general(left, right, (dims, ((), ())), preferred_element_type=F32)


def attention(qkv, lengths, seq, width):
    heads = width // HEAD_DIM
    split = qkv.reshape(MB, seq, 3, heads, HEAD_DIM)
    q, k, v = split[:, :, 0], split[:, :, 1], split[:, :, 2]
    at = jnp.arange(seq, dtype=jnp.int32)
    allowed = (at[None, None, :] <= at[None, :, None]) & (at[None, None, :] < lengths[:, None, None])
    scores = jnp.einsum("sqhd,skhd->shqk", q, k, preferred_element_type=F32) * HEAD_DIM**-0.5
    scores = jnp.where(allowed[:, None], scores, -1e30)
    p = jax.nn.softmax(scores, axis=-1)
    ctx = jnp.einsum("shqk,skhd->sqhd", p.astype(BF), v, preferred_element_type=F32)
    return ctx.reshape(MB * seq, width).astype(BF), (q, k, v, p.astype(BF))


def attention_back(saved, dctx, seq, width):
    q, k, v, p = saved
    d = dctx.reshape(MB, seq, width // HEAD_DIM, HEAD_DIM)
    dv = jnp.einsum("shqk,sqhd->skhd", p, d, preferred_element_type=F32)
    dp = jnp.einsum("sqhd,skhd->shqk", d, v, preferred_element_type=F32)
    p32 = p.astype(F32)
    ds = (p32 * (dp - jnp.sum(p32 * dp, axis=-1, keepdims=True))).astype(BF)
    dq = jnp.einsum("shqk,skhd->sqhd", ds, k, preferred_element_type=F32) * HEAD_DIM**-0.5
    dk = jnp.einsum("shqk,sqhd->skhd", ds, q, preferred_element_type=F32) * HEAD_DIM**-0.5
    return jnp.stack([dq, dk, dv], axis=2).reshape(MB * seq, 3 * width).astype(BF)


def body(dims, tokens, cotangent, seq_lengths, seq_place, ln1_gain, ln1_bias, w_qkv, q_bias, v_bias, w_out, out_bias, ln2_gain, ln2_bias, w_fc, fc_bias, w_proj, proj_bias):
    rows, width = tokens.shape
    hidden = fc_bias.shape[0] * dims[0] * dims[1] * dims[2] * 2
    seq = rows // MB
    n = dims[0] * dims[1] * dims[2] * 2
    per, per_fc = width // n, hidden // n
    slots = lax.axis_index("dp") * MB + jnp.arange(MB, dtype=jnp.int32)
    lengths = jnp.sum(jnp.where(seq_place[None, :] == slots[:, None], seq_lengths[None, :], 0), axis=1)
    live = (jnp.arange(seq, dtype=jnp.int32)[None] < lengths[:, None]).reshape(rows, 1)

    vectors = (ln1_gain, ln1_bias, q_bias, v_bias, out_bias, ln2_gain, ln2_bias, proj_bias)
    small = jnp.concatenate([*vectors, fc_bias])
    small = jnp.pad(small, (0, 2048 - small.shape[0])).reshape(16, 128)
    chunks = [(0, i, width) for i in range(0, 3 * width, width)] + [(1, 0, width)]
    chunks += [(2, i, width) for i in range(0, hidden, width)]
    chunks += [(3, i, width // 4) for i in range(0, width, width // 4)]
    kinds = [0, 0, 0, 0, 0, 1, 0, 1, 0, 1, 0, 1]
    w_qkv, w_out, w_fc, w_proj, small = (
        whole.reshape(n * whole.shape[-2], whole.shape[-1])
        for whole in gather_all(dims, (w_qkv, w_out, w_fc, w_proj), small, chunks, kinds)
    )
    small = small.reshape(n, 2048)
    full = [small[:, i * per : (i + 1) * per].reshape(width).astype(F32) for i in range(8)]
    ln1_gain, ln1_bias, q_bias, v_bias, out_bias, ln2_gain, ln2_bias, proj_bias = full
    fc_bias = small[:, 8 * per : 8 * per + per_fc].reshape(hidden).astype(F32)

    x = tokens.astype(F32)
    h1 = layer_norm(x, ln1_gain, ln1_bias).astype(BF)
    bias = jnp.concatenate([q_bias, jnp.zeros_like(q_bias), v_bias])
    qkv = (dot(h1, w_qkv, ((1,), (0,))) + bias).astype(BF)
    ctx, saved = attention(qkv, lengths, seq, width)
    r1 = x + (dot(ctx, w_out, ((1,), (0,))) + out_bias)
    h2 = layer_norm(r1, ln2_gain, ln2_bias).astype(BF)
    u = dot(h2, w_fc, ((1,), (0,))) + fc_bias
    act = gelu_tanh(u).astype(BF)
    out = r1 + (dot(act, w_proj, ((1,), (0,))) + proj_bias)
    out = jnp.where(live, out, 0.0).astype(BF)

    dyb = jnp.where(live, cotangent, 0)
    dy = dyb.astype(F32)
    g_proj_bias = jnp.sum(dy, axis=0)
    g_proj = dot(act, dyb, ((0,), (0,))).astype(BF)
    da = dot(dyb, w_proj, ((1,), (1,)))
    du = jax.vjp(gelu_tanh, u)[1](da)[0].astype(BF)
    g_fc_bias = jnp.sum(du, axis=0, dtype=F32)
    g_fc = dot(h2, du, ((0,), (0,))).astype(BF)
    dh2 = dot(du, w_fc, ((1,), (1,)))
    dr1, g_ln2_gain, g_ln2_bias = jax.vjp(layer_norm, r1, ln2_gain, ln2_bias)[1](dh2)
    dr1 = dy + dr1
    dr1b = dr1.astype(BF)
    g_out_bias = jnp.sum(dr1b, axis=0, dtype=F32)
    g_out = dot(ctx, dr1b, ((0,), (0,))).astype(BF)
    dctx = dot(dr1b, w_out, ((1,), (1,))).astype(BF)
    dqkv = attention_back(saved, dctx, seq, width)
    g_q_bias = jnp.sum(dqkv[:, :width], axis=0, dtype=F32)
    g_v_bias = jnp.sum(dqkv[:, 2 * width :], axis=0, dtype=F32)
    g_qkv = dot(h1, dqkv, ((0,), (0,))).astype(BF)
    dh1 = dot(dqkv, w_qkv, ((1,), (1,)))
    dx, g_ln1_gain, g_ln1_bias = jax.vjp(layer_norm, x, ln1_gain, ln1_bias)[1](dh1)
    dx = (dr1 + dx).astype(BF)

    vectors = (g_ln1_gain, g_ln1_bias, g_q_bias, g_v_bias, g_out_bias, g_ln2_gain, g_ln2_bias, g_proj_bias)
    small = jnp.concatenate([v.reshape(n, per) for v in vectors] + [g_fc_bias.reshape(n, per_fc)], axis=1)
    small = jnp.pad(small, ((0, 0), (0, 1024 - small.shape[1]))).reshape(n * 8, 128)
    g_qkv, g_out, g_fc, g_proj, small = reduce_all(dims, (g_qkv, g_out, g_fc, g_proj), small, chunks)
    small = small.reshape(1024)
    own = [small[i * per : (i + 1) * per] for i in range(8)]
    g_ln1_gain, g_ln1_bias, g_q_bias, g_v_bias, g_out_bias, g_ln2_gain, g_ln2_bias, g_proj_bias = own
    g_fc_bias = small[8 * per : 8 * per + per_fc]
    return (out, dx, g_ln1_gain, g_ln1_bias, g_qkv, g_q_bias, g_v_bias, g_out, g_out_bias, g_ln2_gain, g_ln2_bias, g_fc, g_fc_bias, g_proj, g_proj_bias)


def solution(mesh):
    dims = grid_dims(mesh.shape["dp"])
    row, vec = P("dp", None), P("dp")
    return jax.shard_map(
        lambda *args: body(dims, *args),
        mesh=mesh,
        in_specs=(row, row, P(), P(), vec, vec, row, vec, vec, row, vec, vec, vec, row, vec, row, vec),
        out_specs=(row, row, vec, vec, row, vec, vec, row, vec, vec, vec, row, vec, row, vec),
        check_vma=False,
    )
```

```python
import jax
import jax.numpy as jnp
from jax import lax
from jax.experimental import pallas as pl
from jax.experimental.pallas import tpu as pltpu
from jax.sharding import PartitionSpec as P

MESH = pl.DeviceIdType.MESH
ANY = pl.BlockSpec(memory_space=pl.ANY)
VMEM = pl.BlockSpec(memory_space=pltpu.VMEM)
DMA = pltpu.SemaphoreType.DMA


def grid_dims(n):
    half = n // 2
    first = 4 if half % 4 == 0 else half
    rest = half // first
    second = 1
    while second * second < rest:
        second *= 2
    return first, second, rest // second


class Place:
    def __init__(self, dims):
        self.dims = dims
        d1, d2, d3 = dims
        me = lax.axis_index("dp")
        self.z = me // (d2 * d3 * 2)
        self.y = (me // (d3 * 2)) % d2
        self.x = (me // 2) % d3
        self.c = me % 2
        self.zs = [(self.z + k) % d1 for k in range(1, d1)]
        self.ys = [(self.y + k) % d2 for k in range(1, d2)]
        self.xs = [(self.x + k) % d3 for k in range(1, d3)]
        self.to_z = [self.dev(z=v) for v in self.zs]
        self.to_y = [self.dev(y=v) for v in self.ys]
        self.to_x = [self.dev(x=v) for v in self.xs]
        self.to_p = self.dev(c=1 - self.c)

    def dev(self, **at):
        z, y, x, c = (at.get(name, getattr(self, name)) for name in "zyxc")
        _, d2, d3 = self.dims
        return (((z * d2 + y) * d3 + x) * 2 + c,)

    def barrier(self):
        semaphore = pltpu.get_barrier_semaphore()
        peers = self.to_z + self.to_y + self.to_x + [self.to_p]
        for peer in peers:
            pl.semaphore_signal(semaphore, inc=1, device_id=peer, device_id_type=MESH)
        pl.semaphore_wait(semaphore, len(peers))


def send(source, target, send_sem, recv_sem, device):
    return pltpu.make_async_remote_copy(
        src_ref=source,
        dst_ref=target,
        send_sem=send_sem,
        recv_sem=recv_sem,
        device_id=device,
        device_id_type=MESH,
    )


class Gather:
    def __init__(self, place, shards, wholes, chunks, kinds, sems, small=None):
        self.at, self.shards, self.wholes = place, shards, wholes
        self.chunks, self.kinds, self.small = chunks, kinds, small
        self.sems = sems
        self.ahead = 3

    @staticmethod
    def semaphores(dims, count):
        d1, d2, d3 = dims
        sizes = [max(d1, d2 + d3), 2 * d1 + d2 + d3, d2 + d3, 1, 4 * (d1 + d2 + d3)]
        shapes = []
        for size in sizes[:4]:
            shapes += [DMA((count, size)), DMA((count, size))]
        return shapes + [DMA((sizes[4],)), DMA((sizes[4],))]

    def copies(self, stage, t):
        p = self.at
        z, y, x, c = p.z, p.y, p.x, p.c
        i, first, width = self.chunks[t]
        whole, shard, half = self.wholes[i], self.shards[i], width // 2
        full = pl.ds(first, width)
        a, b = pl.ds(first, half), pl.ds(first + half, half)
        pieces = []
        if stage == 0 and self.kinds[t] == 0:
            pieces = [(shard.at[:, full], whole.at[z, y, x, c, :, full], d) for d in p.to_z]
        elif stage == 0:
            pieces = [(shard.at[:, a], whole.at[z, y, x, c, :, a], d) for d in p.to_x]
            pieces += [(shard.at[:, b], whole.at[z, y, x, c, :, b], d) for d in p.to_y]
        elif stage == 1 and self.kinds[t] == 0:
            part = whole.at[:, y, x, c, :, a]
            pieces = [(part, part, d) for d in p.to_x]
            part = whole.at[:, y, x, c, :, b]
            pieces += [(part, part, d) for d in p.to_y]
        elif stage == 1:
            left, right = whole.at[z, y, :, c, :, a], whole.at[z, :, x, c, :, b]
            pieces = [(part, part, d) for d in p.to_z for part in (left, right)]
        elif stage == 2:
            part = whole.at[:, y, :, c, :, a]
            pieces = [(part, part, d) for d in p.to_y]
            part = whole.at[:, :, x, c, :, b]
            pieces += [(part, part, d) for d in p.to_x]
        else:
            part = whole.at[:, :, :, c, :, full]
            pieces = [(part, part, p.to_p)]
        out, back = self.sems[2 * stage], self.sems[2 * stage + 1]
        made = [send(s, d, out.at[t, k], back.at[t, k], to) for k, (s, d, to) in enumerate(pieces)]
        if t == 0 and self.small is not None:
            source, target = self.small
            if stage == 0:
                pieces = [(source, target.at[z, y, x, c], d) for d in p.to_z]
            elif stage == 1:
                part = target.at[:, y, x, c]
                pieces = [(part, part, d) for d in p.to_x]
            elif stage == 2:
                part = target.at[:, y, :, c]
                pieces = [(part, part, d) for d in p.to_y]
            else:
                part = target.at[:, :, :, c]
                pieces = [(part, part, p.to_p)]
            base = stage * sum(p.dims)
            out, back = self.sems[8], self.sems[9]
            made += [
                send(s, d, out.at[base + k], back.at[base + k], to)
                for k, (s, d, to) in enumerate(pieces)
            ]
        return made

    def go(self, stage, t):
        if 0 <= t < len(self.chunks):
            for copy in self.copies(stage, t):
                copy.start()

    def arrived(self, stage, t):
        for copy in self.copies(stage, t):
            copy.wait_recv()

    def begin(self):
        for t in range(self.ahead):
            self.go(0, t)

    def advance(self, t):
        count = len(self.chunks)
        if t < count:
            self.arrived(0, t)
            self.go(1, t)
            self.go(0, t + self.ahead)
        if 0 <= t - 1 < count:
            self.arrived(1, t - 1)
            self.go(2, t - 1)
        if 0 <= t - 2 < count:
            self.arrived(2, t - 2)
            self.go(3, t - 2)

    def finish(self):
        for stage in range(4):
            for t in range(len(self.chunks)):
                for copy in self.copies(stage, t):
                    copy.wait_send()


class Reduce:
    @staticmethod
    def scratch(dims, rows, width, dtype, halves=True):
        d1, d2, d3 = dims
        half = width // 2 if halves else width
        shapes = [pltpu.VMEM((d1, d2, d3, rows, width), dtype)]
        shapes.append(pltpu.VMEM((d2 - 1, d1, d3, rows, half), dtype))
        shapes.append(pltpu.VMEM((d3 - 1, d1, rows, half), dtype))
        if halves:
            shapes.append(pltpu.VMEM((d3 - 1, d1, d2, rows, half), dtype))
            shapes.append(pltpu.VMEM((d2 - 1, d1, rows, half), dtype))
        shapes.append(pltpu.VMEM((d1 - 1, rows, width), dtype))
        sizes = (1, d2 + d3, d2 + d3, d1)
        for size in sizes:
            shapes += [DMA((size,)), DMA((size,))]
        return shapes

    def __init__(self, place, refs, source, own, result, halves=True):
        self.at, self.halves = place, halves
        self.source, self.own, self.result = source, own, result
        if halves:
            self.total, self.ya, self.xa, self.xb, self.yb, self.zz = refs[:6]
            self.sems = refs[6:]
        else:
            self.total, self.ya, self.xa, self.zz = refs[:4]
            self.sems = refs[4:]
        width = self.total.shape[-1]
        half = width // 2 if halves else width
        self.a, self.b = pl.ds(0, half), pl.ds(half, half)

    def pieces(self, stage):
        p, h = self.at, self.total
        y, x = p.y, p.x
        if stage == 0:
            return [(self.source.at[:, :, :, 1 - p.c], h, p.to_p)]
        if stage == 1:
            made = [
                (h.at[:, v, :, :, self.a], self.ya.at[k], d)
                for k, (v, d) in enumerate(zip(p.ys, p.to_y))
            ]
            if self.halves:
                made += [
                    (h.at[:, :, v, :, self.b], self.xb.at[k], d)
                    for k, (v, d) in enumerate(zip(p.xs, p.to_x))
                ]
            return made
        if stage == 2:
            made = [
                (h.at[:, y, v, :, self.a], self.xa.at[k], d)
                for k, (v, d) in enumerate(zip(p.xs, p.to_x))
            ]
            if self.halves:
                made += [
                    (h.at[:, v, x, :, self.b], self.yb.at[k], d)
                    for k, (v, d) in enumerate(zip(p.ys, p.to_y))
                ]
            return made
        return [(h.at[v, y, x], self.zz.at[k], d) for k, (v, d) in enumerate(zip(p.zs, p.to_z))]

    def go(self, stage):
        for copy in self.copies(stage):
            copy.start()

    def copies(self, stage):
        out, back = self.sems[2 * stage], self.sems[2 * stage + 1]
        return [
            send(s, d, out.at[k], back.at[k], to) for k, (s, d, to) in enumerate(self.pieces(stage))
        ]

    def arrived(self, stage):
        for copy in self.copies(stage):
            copy.wait()

    def add(self, stage):
        p, h = self.at, self.total
        d1, d2, d3 = p.dims
        f32 = jnp.float32

        def into(at, terms):
            value = h[at].astype(f32)
            for term in terms:
                value = value + term.astype(f32)
            h[at] = value.astype(h.dtype)

        if stage == 0:

            @pl.loop(0, d1)
            def _(i):
                for j in range(d2):
                    for k in range(d3):
                        into((i, j, k), [self.own[i, j, k]])

        elif stage == 1:

            @pl.loop(0, d1)
            def _(i):
                for k in range(d3):
                    into(
                        (i, p.y, k, slice(None), self.a),
                        [self.ya[m, i, k] for m in range(d2 - 1)],
                    )
                if self.halves:
                    for j in range(d2):
                        into(
                            (i, j, p.x, slice(None), self.b),
                            [self.xb[m, i, j] for m in range(d3 - 1)],
                        )

        elif stage == 2:

            @pl.loop(0, d1)
            def _(i):
                into((i, p.y, p.x, slice(None), self.a), [self.xa[m, i] for m in range(d3 - 1)])
                if self.halves:
                    into(
                        (i, p.y, p.x, slice(None), self.b),
                        [self.yb[m, i] for m in range(d2 - 1)],
                    )

        else:
            value = h[p.z, p.y, p.x].astype(f32)
            for m in range(d1 - 1):
                value = value + self.zz[m].astype(f32)
            self.result[...] = value

    def step(self, stage):
        self.arrived(stage)
        self.add(stage)
        if stage < 3:
            self.go(stage + 1)


HEAD_DIM = 64
MB = 2
EPS = 1e-05
BF = jnp.bfloat16
F32 = jnp.float32
NEG = -1e30
GELU_A = 0.044715
GELU_C = 0.7978845608028654


def mm(left, right):
    return lax.dot_general(left, right, (((1,), (0,)), ((), ())), preferred_element_type=F32)


def mm_nt(left, right):
    return lax.dot_general(left, right, (((1,), (1,)), ((), ())), preferred_element_type=F32)


def mm_tn(left, right):
    return lax.dot_general(left, right, (((0,), (0,)), ((), ())), preferred_element_type=F32)


def iota(shape, axis):
    return lax.broadcasted_iota(jnp.int32, shape, axis)


def unpack_vector(block, start, per, width, first):
    row0, lane0 = start // 128, start % 128
    rows = block.shape[0]
    column = iota((128, width), 1) + first
    pick = (iota((128, width), 0) - lane0 == column % per).astype(BF)
    spread = mm(block, pick)
    column = iota((rows, width), 1) + first
    mine = iota((rows, width), 0) == column // per * 8 + row0
    return jnp.sum(jnp.where(mine, spread, 0.0), axis=0, keepdims=True)


def moments(value):
    mean = jnp.mean(value, axis=-1, keepdims=True)
    center = value - mean
    return center, lax.rsqrt(jnp.mean(center * center, axis=-1, keepdims=True) + EPS)


def attend_pair(q2, k2, v2, kbias, diag, seq):
    half = seq // 2
    lane = iota((1, 128), 1) // HEAD_DIM
    vt = v2.T
    tops, sums, rows = [], [], []
    for head in range(2):
        qh = jnp.where(lane == head, q2 * jnp.asarray(HEAD_DIM**-0.5, BF), 0)
        vh = vt[head * HEAD_DIM : (head + 1) * HEAD_DIM]
        parts, logs = [], []
        for block in range(2):
            keys = half * (block + 1)
            s = mm_nt(k2[:keys], qh[block * half : (block + 1) * half])
            if block == 0:
                s = s + (diag + kbias[:half])
            else:
                s = jnp.concatenate([s[:half] + kbias[:half], s[half:] + (diag + kbias[half:])], axis=0)
            top = jnp.max(s, axis=0, keepdims=True)
            e = jnp.exp(s - top)
            total = jnp.sum(e, axis=0, keepdims=True)
            parts.append(mm(vh[:, :keys], e.astype(BF)) * (1.0 / total))
            logs.append(top + jnp.log(total))
        rows.append(jnp.concatenate(parts, axis=1))
        sums.append(jnp.concatenate(logs, axis=1))
    return jnp.concatenate(rows, axis=0).T, sums


def forward_kernel(dims, chunks, kinds, comm, *refs):
    (tokens, live, s_qkv, s_out, s_fc, s_proj, small) = refs[:7]
    (w_qkv, w_out, w_fc, w_proj, smalls, vecs_o, h1_o, qkv_o, lse_o, ctx_o, r1_o, h2_o, act_o, gp_o, out_o) = refs[7:22]
    (vecs, fcb, h1, qkv, ctx, lse, r1, h2, act, gp, out, sm, wbuf, pbuf, diag) = refs[22:37]
    local, wsem, psem, osem, gpsem = refs[37:42]
    sems = refs[42:]
    rows, width = tokens.shape
    seq = rows // MB
    hidden = act.shape[1]
    n = dims[0] * dims[1] * dims[2] * 2
    per, per_fc = width // n, hidden // n
    tile = 256
    tiles = rows // tile
    thirds, fcs = 3, hidden // width
    place = Place(dims)
    z, y, x, c = place.z, place.y, place.x, place.c
    shards = (s_qkv, s_out, s_fc, s_proj)
    wholes = (w_qkv, w_out, w_fc, w_proj)
    gather = Gather(place, shards, wholes, chunks, kinds, sems, (small, smalls))
    moves = [
        pltpu.make_async_copy(s, w.at[z, y, x, c], local.at[i])
        for i, (s, w) in enumerate(zip((*shards, small), (*wholes, smalls)))
    ]
    count = len(chunks)

    def advance(t):
        if comm and t < count + 2:
            gather.advance(t)

    def ready(t):
        if comm:
            gather.arrived(3, t)

    def fetch(t):
        i, first, w = chunks[t]
        if i == 3:
            return pltpu.make_async_copy(wholes[i].at[:, :, :, :, :, pl.ds(first, w)], pbuf.at[t % 2], psem.at[t % 2])
        return pltpu.make_async_copy(wholes[i].at[:, :, :, :, :, pl.ds(first, w)], wbuf.at[t % 2], wsem.at[t % 2])

    def keep(k, source, target):
        return pltpu.make_async_copy(source, target, osem.at[k])

    for move in moves:
        move.start()
    place.barrier()
    if comm:
        gather.begin()
    half = seq // 2
    diag[...] = jnp.where(iota((half, half), 0) <= iota((half, half), 1), 0.0, NEG)
    for move in moves:
        move.wait()
    for t in range(3):
        advance(t)
    ready(0)
    fetch(0).start()
    load_small = pltpu.make_async_copy(smalls, sm, gpsem.at[0])
    load_small.start()
    load_small.wait()
    block = sm[...].reshape(n * 8, 128).astype(BF)
    for v in range(8):
        vecs[v : v + 1, :] = unpack_vector(block, v * per, per, width, 0)
    for piece in range(fcs):
        fcb[:, piece * width : (piece + 1) * width] = unpack_vector(block, 8 * per, per_fc, width, piece * width)

    @pl.loop(0, rows // 128)
    def _(i):
        at = pl.ds(pl.multiple_of(i * 128, 128), 128)
        center, scale = moments(tokens[at, :].astype(F32))
        h1[at, :] = (center * scale * vecs[0:1, :] + vecs[1:2, :]).astype(BF)

    saves = [keep(0, h1, h1_o), keep(1, vecs, vecs_o)]
    for save in saves:
        save.start()
    for t in range(thirds):
        if t > 0:
            advance(t + 2)
            ready(t)
            fetch(t).start()
        fetch(t).wait()
        bias = vecs[2:3, :] if t == 0 else vecs[3:4, :] if t == 2 else None

        @pl.loop(0, tiles)
        def _(i):
            at = pl.ds(pl.multiple_of(i * tile, tile), tile)
            value = mm(h1[at, :], wbuf[t % 2].reshape(width, width))
            if bias is not None:
                value = value + bias
            qkv[at, t * width : (t + 1) * width] = value.astype(BF)

    keep(2, qkv, qkv_o).start()
    saves.append(keep(2, qkv, qkv_o))
    pairs = width // 128
    steps = MB * pairs
    events = {1: thirds + 2, 5: thirds + 3, 9: thirds + 4, 13: thirds + 5}

    @pl.loop(0, steps)
    def _(i):
        for at_step, t in events.items():

            @pl.when(i == at_step)
            def _():
                advance(t)

        slot, pair = i // pairs, i % pairs
        at = pl.ds(pl.multiple_of(slot * seq, seq), seq)
        col = pl.multiple_of(pair * 128, 128)
        kbias = (live[at, :] - 1.0) * -NEG
        value, sums = attend_pair(
            qkv[at, pl.ds(col, 128)],
            qkv[at, pl.ds(width + col, 128)],
            qkv[at, pl.ds(2 * width + col, 128)],
            kbias,
            diag[...],
            seq,
        )
        ctx[at, pl.ds(col, 128)] = value.astype(BF)
        for head in range(2):
            lse[i * 2 + head] = sums[head]

    keep(3, ctx, ctx_o).start()
    keep(4, lse, lse_o).start()
    saves += [keep(3, ctx, ctx_o), keep(4, lse, lse_o)]
    t = thirds
    ready(t)
    fetch(t).start()
    fetch(t).wait()

    @pl.loop(0, tiles)
    def _(i):
        at = pl.ds(pl.multiple_of(i * tile, tile), tile)
        value = mm(ctx[at, :], wbuf[t % 2].reshape(width, width)) + vecs[4:5, :]
        value = value + tokens[at, :].astype(F32)
        r1[at, :] = value
        center, scale = moments(value)
        h2[at, :] = (center * scale * vecs[5:6, :] + vecs[6:7, :]).astype(BF)

    keep(5, r1, r1_o).start()
    keep(6, h2, h2_o).start()
    saves += [keep(5, r1, r1_o), keep(6, h2, h2_o)]
    ready(thirds + 1)
    fetch(thirds + 1).start()

    def keep_gp(k):
        return pltpu.make_async_copy(gp.at[k % 2], gp_o.at[:, pl.ds(k * width, width)], gpsem.at[k % 2])

    for k in range(fcs):
        t = thirds + 1 + k
        fetch(t).wait()
        if k >= 2:
            keep_gp(k - 2).wait()

        @pl.loop(0, tiles)
        def _(i):
            at = pl.ds(pl.multiple_of(i * tile, tile), tile)
            u = mm(h2[at, :], wbuf[t % 2].reshape(width, width)) + fcb[:, k * width : (k + 1) * width]
            square = u * u
            inner = u * (GELU_C + (GELU_C * GELU_A) * square)
            gate = 0.5 + 0.5 * jnp.tanh(inner)
            value = u * gate
            act[at, k * width : (k + 1) * width] = value.astype(BF)
            slope = gate + value * (2.0 - 2.0 * gate) * (GELU_C + (3.0 * GELU_C * GELU_A) * square)
            gp[k % 2, at, :] = slope.astype(BF)

        keep_gp(k).start()
        advance(t + 4 + 1)
        if k + 1 < fcs:
            ready(t + 1)
        else:
            ready(t + 1)
        fetch(t + 1).start()
    keep(7, act, act_o).start()
    saves.append(keep(7, act, act_o))
    pw = chunks[-1][2]
    first = thirds + 1 + fcs
    for k in range(width // pw):
        t = first + k
        fetch(t).wait()
        if t + 1 < count:
            advance(t + 5)
            ready(t + 1)
            fetch(t + 1).start()
        cols = slice(k * pw, (k + 1) * pw)

        @pl.loop(0, tiles)
        def _(i):
            at = pl.ds(pl.multiple_of(i * tile, tile), tile)
            value = mm(act[at, :], pbuf[t % 2].reshape(hidden, pw)) + (r1[at, cols] + vecs[7:8, cols])
            out[at, cols] = jnp.where(live[at, :] > 0.5, value, 0.0).astype(BF)

    keep(8, out, out_o).start()
    saves.append(keep(8, out, out_o))
    for k in range(max(fcs - 2, 0), fcs):
        keep_gp(k).wait()
    for save in saves:
        save.wait()
    if comm:
        gather.finish()


def forward(dims, tokens, live, shards, small, chunks, kinds, comm=True):
    rows, width = tokens.shape
    n = dims[0] * dims[1] * dims[2] * 2
    hidden = shards[2].shape[1]
    heads = width // HEAD_DIM
    seq = rows // MB
    pw = chunks[-1][2]
    sds = jax.ShapeDtypeStruct
    shapes = [sds((*dims, 2, *s.shape), s.dtype) for s in (*shards, small)]
    shapes += [
        sds((8, width), F32),
        sds((rows, width), BF),
        sds((rows, 3 * width), BF),
        sds((MB * heads, 1, seq), F32),
        sds((rows, width), BF),
        sds((rows, width), F32),
        sds((rows, width), BF),
        sds((rows, hidden), BF),
        sds((rows, hidden), BF),
        sds((rows, width), BF),
    ]
    scratch = [
        pltpu.VMEM((8, width), F32),
        pltpu.VMEM((1, hidden), F32),
        pltpu.VMEM((rows, width), BF),
        pltpu.VMEM((rows, 3 * width), BF),
        pltpu.VMEM((rows, width), BF),
        pltpu.VMEM((MB * heads, 1, seq), F32),
        pltpu.VMEM((rows, width), F32),
        pltpu.VMEM((rows, width), BF),
        pltpu.VMEM((rows, hidden), BF),
        pltpu.VMEM((2, rows, width), BF),
        pltpu.VMEM((rows, width), BF),
        pltpu.VMEM((*dims, 2, *small.shape), small.dtype),
        pltpu.VMEM((2, *dims, 2, width // n, width), BF),
        pltpu.VMEM((2, *dims, 2, hidden // n, pw), BF),
        pltpu.VMEM((seq // 2, seq // 2), F32),
        DMA((5,)),
        DMA((2,)),
        DMA((2,)),
        DMA((9,)),
        DMA((2,)),
        *Gather.semaphores(dims, len(chunks)),
    ]
    return pl.pallas_call(
        lambda *refs: forward_kernel(dims, chunks, kinds, comm, *refs),
        out_shape=shapes,
        in_specs=[VMEM] * 7,
        out_specs=[ANY] * 15,
        scratch_shapes=scratch,
        compiler_params=pltpu.CompilerParams(
            collective_id=0, has_side_effects=True, vmem_limit_bytes=60 * 1024 * 1024
        ),
        name="forward",
    )(tokens, live, *shards, small)


class Flow:
    def __init__(self):
        self.active = []

    def start(self, part):
        part.go(0)
        self.active.append([part, 0])

    def poll(self):
        for entry in self.active:
            entry[0].step(entry[1])
            entry[1] += 1
        self.active = [entry for entry in self.active if entry[1] < 4]


def pack_vector(row, start, per, rows):
    row0, lane0 = start // 128, start % 128
    width = row.shape[1]
    pick = (iota((128, width), 0) - lane0 == iota((128, width), 1) % per).astype(BF)
    mine = iota((rows, width), 0) == iota((rows, width), 1) // per * 8 + row0
    total = None
    for _ in range(3):
        part = row.astype(BF)
        row = row - part.astype(F32)
        value = mm_nt(jnp.where(mine, part.astype(F32), 0.0).astype(BF), pick)
        total = value if total is None else total + value
    return total


def norm_back(value, gain, grad):
    center, scale = moments(value)
    normed = center * scale
    scaled = grad * gain
    mean = jnp.mean(scaled, axis=-1, keepdims=True)
    cross = jnp.mean(scaled * normed, axis=-1, keepdims=True)
    return (scaled - mean - normed * cross) * scale, grad * normed


def attend_back(q2, k2, v2, o2, c2, lse, kbias, diag, seq):
    half = seq // 2
    lane = iota((1, 128), 1) // HEAD_DIM
    prod = o2.astype(F32) * c2.astype(F32)
    heads = (iota((8, 128), 1) // HEAD_DIM == iota((8, 128), 0)).astype(BF)
    high = prod.astype(BF)
    delta = mm_nt(heads, high) + mm_nt(heads, (prod - high.astype(F32)).astype(BF))
    kt = k2.T
    dk, dv = [None, None], [None, None]
    dq = []
    for head in range(2):
        qh = jnp.where(lane == head, q2 * jnp.asarray(HEAD_DIM**-0.5, BF), 0)
        oh = jnp.where(lane == head, o2, 0)
        kh = kt[head * HEAD_DIM : (head + 1) * HEAD_DIM]
        parts = []
        for block in range(2):
            keys = half * (block + 1)
            cut = slice(block * half, (block + 1) * half)
            s = mm_nt(k2[:keys], qh[cut]) - lse[head][:, cut]
            if block == 0:
                s = s + (diag + kbias[:half])
            else:
                s = jnp.concatenate([s[:half] + kbias[:half], s[half:] + (diag + kbias[half:])], axis=0)
            p = jnp.exp(s)
            dp = mm_nt(v2[:keys], oh[cut])
            ds = (p * (dp - delta[head : head + 1, cut])).astype(BF)
            gv = mm(p.astype(BF), oh[cut])
            gk = mm(ds, qh[cut])
            parts.append(mm(kh[:, :keys], ds))
            for at in range(block + 1):
                rows = slice(at * half, (at + 1) * half)
                dv[at] = gv[rows] if dv[at] is None else dv[at] + gv[rows]
                dk[at] = gk[rows] if dk[at] is None else dk[at] + gk[rows]
        dq.append(jnp.concatenate(parts, axis=1))
    dq = jnp.concatenate(dq, axis=0).T * HEAD_DIM**-0.5
    return dq, jnp.concatenate(dk, axis=0), jnp.concatenate(dv, axis=0)


def sets_of(wide):
    return len(wide) - 2


def backward_kernel(dims, wide, tall, per_part, per_small, comm, *refs):
    (tokens, cot, live, vecs, h1_i, qkv_i, lse_i, ctx_i, r1_i, h2_i, act_i, gp_i, w_qkv, w_out, w_fc, w_proj) = refs[:16]
    (dx_o, g_qkv, g_out, g_fc, g_proj, g_small) = refs[16:22]
    slots, wp, f_dh, f_r1, gvec, gfc, lse, diag, stage, tstage, sstage = refs[22:33]
    lsem, wsem = refs[33:35]
    refs = refs[35:]
    d1, d2, d3 = dims
    n = d1 * d2 * d3 * 2
    rows, width = f_dh.shape
    hidden = gfc.shape[1]
    seq = rows // MB
    per, per_fc = width // n, hidden // n
    fcs = hidden // width
    tile = rows // d1
    place = Place(dims)
    c = place.c
    flow = Flow()
    counts = sets_of(wide) + len(tall)
    sets = [refs[t * per_part : (t + 1) * per_part] for t in range(counts)]
    small_refs = refs[counts * per_part :]

    def poll():
        if comm:
            flow.poll()

    def reduce_wide(t, buffer, result):
        part = Reduce(place, sets[len(tall) + t % sets_of(wide)], stage.at[buffer], stage.at[buffer, :, :, :, c], result)
        if comm:
            flow.start(part)

    def reduce_tall(t, buffer, result):
        part = Reduce(place, sets[t], tstage.at[buffer], tstage.at[buffer, :, :, :, c], result)
        if comm:
            flow.start(part)

    def load(source, slot, k):
        return pltpu.make_async_copy(source, slots.at[slot], lsem.at[k])

    def cols(source, k):
        return source.at[:, :, :, :, :, pl.ds(k * width, width)]

    def whole(slot):
        return slots[slot].reshape(rows, width)

    def piece(slot, i):
        return slots[slot, i].reshape(tile, width)

    def put(slot, i, value):
        slots[slot, i] = value.astype(BF).reshape(d2, d3, 2, tile // (2 * d2 * d3), width)

    place.barrier()
    load(cot, 0, 0).start()
    for k in range(fcs):
        load(cols(act_i, k), 1 + k, 1 + k).start()
    load(h2_i, 6, 6).start()
    half = seq // 2
    diag[...] = jnp.where(iota((half, half), 0) <= iota((half, half), 1), 0.0, NEG)
    gvec[...] = jnp.zeros_like(gvec)
    gfc[...] = jnp.zeros_like(gfc)
    lload = pltpu.make_async_copy(lse_i, lse, lsem.at[7])
    lload.start()
    load(cot, 0, 0).wait()

    @pl.loop(0, d1)
    def _(i):
        at = pl.ds(pl.multiple_of(i * tile, tile), tile)
        value = jnp.where(live[at, :] > 0.5, piece(0, i), 0)
        put(0, i, value)
        gvec[7:8, :] += jnp.sum(value.astype(F32), axis=0, keepdims=True)

    for k in range(fcs):
        load(cols(act_i, k), 1 + k, 1 + k).wait()

    pw = tall[0][2]
    for j in range(len(tall)):
        b = j % 2
        cut = slice(j * pw, (j + 1) * pw)

        @pl.loop(0, fcs)
        def _(f):
            value = mm_tn(slots[1 + f].reshape(rows, width), slots[0, :, :, :, :, :, cut].reshape(rows, pw))
            tstage[b, f] = value.astype(BF).reshape(d2, d3, 2, per_fc, pw)

        if j == 0:
            wpl = [pltpu.make_async_copy(w_proj.at[f], wp.at[f % 2], wsem.at[f % 2]) for f in range(fcs)]
            wpl[0].start()
        if j > 0:
            poll()
        reduce_tall(j, b, g_proj.at[:, cut])

    def fetch_ff(f):
        return [load(cols(w_fc, f), 1 + f % 2, 1 + f % 2), load(cols(gp_i, f), 3 + f % 2, 3 + f % 2), wpl[f]]

    for move in fetch_ff(0)[:2]:
        move.start()
    load(h2_i, 6, 6).wait()
    lload.wait()
    load(ctx_i, 7, 7).start()
    for f in range(fcs):
        for move in fetch_ff(f):
            move.wait()
        if f + 1 < fcs:
            for move in fetch_ff(f + 1):
                move.start()
        cut = slice(f * width, (f + 1) * width)

        @pl.loop(0, d1)
        def _(i):
            da = mm_nt(piece(0, i), wp[f % 2].reshape(rows, width))
            du = (da * piece(3 + f % 2, i).astype(F32)).astype(BF)
            put(5, i, du)
            gfc[:, cut] += jnp.sum(du.astype(F32), axis=0, keepdims=True)

        poll()

        @pl.loop(0, d1)
        def _(i):
            at = pl.ds(pl.multiple_of(i * tile, tile), tile)
            value = mm_nt(piece(5, i), whole(1 + f % 2))
            if f == 0:
                f_dh[at, :] = value
            else:
                f_dh[at, :] += value

        b = f % 2

        @pl.loop(0, d1)
        def _(i):
            col = pl.ds(pl.multiple_of(i * tile, tile), tile)
            value = mm_tn(slots[6, :, :, :, :, :, col].reshape(rows, tile), whole(5))
            stage[b, i] = value.astype(BF).reshape(d2, d3, 2, per, width)

        reduce_wide(f, b, g_fc.at[:, cut])

    load(w_out, 1, 1).start()
    for k, slot in enumerate((3, 4, 6)):
        load(cols(qkv_i, k), slot, slot).start()

    def r1_tile(i):
        return pltpu.make_async_copy(r1_i.at[pl.ds(i * tile, tile)], f_r1.at[i % 2], wsem.at[i % 2])

    r1_tile(0).start()
    for i in range(d1):
        r1_tile(i).wait()
        if i + 1 < d1:
            r1_tile(i + 1).start()
        at = pl.ds(i * tile, tile)
        grad = f_dh[at, :]
        value, terms = norm_back(f_r1[i % 2], vecs[5:6, :], grad)
        value = value + piece(0, i).astype(F32)
        f_dh[at, :] = value
        low = value.astype(BF)
        put(5, i, low)
        gvec[5:6, :] += jnp.sum(terms, axis=0, keepdims=True)
        gvec[6:7, :] += jnp.sum(grad, axis=0, keepdims=True)
        gvec[4:5, :] += jnp.sum(low.astype(F32), axis=0, keepdims=True)

    poll()
    load(ctx_i, 7, 7).wait()
    load(w_out, 1, 1).wait()

    @pl.loop(0, d1)
    def _(i):
        put(2, i, mm_nt(piece(5, i), whole(1)))

    @pl.loop(0, d1)
    def _(i):
        col = pl.ds(pl.multiple_of(i * tile, tile), tile)
        value = mm_tn(slots[7, :, :, :, :, :, col].reshape(rows, tile), whole(5))
        stage[0, i] = value.astype(BF).reshape(d2, d3, 2, per, width)

    poll()
    reduce_wide(fcs, 0, g_out)
    load(h1_i, 0, 0).start()
    for slot, k in zip((3, 4, 6), range(3)):
        load(cols(qkv_i, k), slot, slot).wait()
    load(cols(w_qkv, 0), 1, 1).start()
    pairs = width // 128
    hslab = d1 // MB
    events = {2: 0, 5: 0, 8: 0, 11: 0, 14: 0}

    @pl.loop(0, MB * pairs)
    def _(i):
        for at_step in events:

            @pl.when(i == at_step)
            def _():
                poll()

        slot, pair = i // pairs, i % pairs
        slab = pl.ds(slot * hslab, hslab)
        at = pl.ds(pl.multiple_of(slot * seq, seq), seq)
        lanes = pl.ds(pl.multiple_of(pair * 128, 128), 128)

        def take(s):
            return slots[s, slab, :, :, :, :, lanes].reshape(seq, 128)

        kbias = (live[at, :] - 1.0) * -NEG
        grads = attend_back(
            take(3), take(4), take(6), take(2), take(7), [lse[2 * i], lse[2 * i + 1]], kbias, diag[...], seq
        )
        for s, value in zip((3, 4, 6), grads):
            slots[s, slab, :, :, :, :, lanes] = value.astype(BF).reshape(hslab, d2, d3, 2, per, 128)

    load(h1_i, 0, 0).wait()
    load(tokens, 2, 2).start()
    load(cols(w_qkv, 1), 5, 5).start()
    load(cols(w_qkv, 2), 7, 7).start()
    for k, slot in enumerate((3, 4, 6)):
        b = (k + 1) % 2

        @pl.loop(0, d1)
        def _(i):
            col = pl.ds(pl.multiple_of(i * tile, tile), tile)
            value = mm_tn(slots[0, :, :, :, :, :, col].reshape(rows, tile), whole(slot))
            stage[b, i] = value.astype(BF).reshape(d2, d3, 2, per, width)

        poll()
        reduce_wide(fcs + 1 + k, b, g_qkv.at[:, k * width : (k + 1) * width])

    load(cols(w_qkv, 0), 1, 1).wait()
    load(cols(w_qkv, 1), 5, 5).wait()
    load(cols(w_qkv, 2), 7, 7).wait()
    load(tokens, 2, 2).wait()

    @pl.loop(0, d1)
    def _(i):
        at = pl.ds(pl.multiple_of(i * tile, tile), tile)
        grad = mm_nt(piece(3, i), whole(1)) + mm_nt(piece(4, i), whole(5)) + mm_nt(piece(6, i), whole(7))
        value, terms = norm_back(piece(2, i).astype(F32), vecs[0:1, :], grad)
        put(2, i, value + f_dh[at, :])
        gvec[0:1, :] += jnp.sum(terms, axis=0, keepdims=True)
        gvec[1:2, :] += jnp.sum(grad, axis=0, keepdims=True)
        gvec[2:3, :] += jnp.sum(piece(3, i).astype(F32), axis=0, keepdims=True)
        gvec[3:4, :] += jnp.sum(piece(6, i).astype(F32), axis=0, keepdims=True)

    save = pltpu.make_async_copy(slots.at[2], dx_o, lsem.at[0])
    save.start()
    poll()
    total = jnp.zeros((n * 8, 128), F32)
    for v in range(8):
        total = total + pack_vector(gvec[v : v + 1, :], v * per, per, n * 8)
    groups = n // fcs
    for k in range(fcs):
        part = pack_vector(gfc[:, k * width : (k + 1) * width], 8 * per, per_fc, groups * 8)
        total = total + jnp.concatenate(
            [part if m == k else jnp.zeros_like(part) for m in range(fcs)], axis=0
        )
    sstage[...] = total.reshape(*dims, 2, 8, 128)
    small = Reduce(place, small_refs, sstage, sstage.at[:, :, :, c], g_small, halves=False)
    if comm:
        flow.start(small)
    for _ in range(4):
        poll()
    save.wait()


def backward(dims, tokens, cot, live, saved, weights, comm=True):
    vecs, h1, qkv, lse, ctx, r1, h2, act, gp = saved
    rows, width = tokens.shape
    n = dims[0] * dims[1] * dims[2] * 2
    hidden = act.shape[1]
    seq = rows // MB
    per, per_fc = width // n, hidden // n
    fcs = hidden // width
    pw = width // fcs
    tall = [(3, i * pw, pw) for i in range(fcs)]
    wide = [(2, i * width, width) for i in range(fcs)] + [(1, 0, width)] + [(0, i * width, width) for i in range(3)]

    def six(a):
        return a.reshape(*dims, 2, a.shape[0] // n, a.shape[1])

    sds = jax.ShapeDtypeStruct
    scratch = [
        pltpu.VMEM((8, *dims, 2, per, width), BF),
        pltpu.VMEM((2, *dims[1:], 2, per_fc, width), BF),
        pltpu.VMEM((rows, width), F32),
        pltpu.VMEM((2, rows // dims[0], width), F32),
        pltpu.VMEM((8, width), F32),
        pltpu.VMEM((1, hidden), F32),
        pltpu.VMEM(lse.shape, F32),
        pltpu.VMEM((seq // 2, seq // 2), F32),
        pltpu.VMEM((2, *dims, 2, per, width), BF),
        pltpu.VMEM((2, *dims, 2, per_fc, pw), BF),
        pltpu.VMEM((*dims, 2, 8, 128), F32),
        DMA((8,)),
        DMA((2,)),
    ]
    for _ in tall:
        made = Reduce.scratch(dims, per_fc, pw, BF)
        scratch += made
    for _ in range(sets_of(wide)):
        made = Reduce.scratch(dims, per, width, BF)
        scratch += made
    made_small = Reduce.scratch(dims, 8, 128, F32, halves=False)
    scratch += made_small
    shapes = [
        sds((*dims, 2, per, width), BF),
        sds((per, 3 * width), F32),
        sds((per, width), F32),
        sds((per, hidden), F32),
        sds((per_fc, width), F32),
        sds((8, 128), F32),
    ]
    return pl.pallas_call(
        lambda *refs: backward_kernel(dims, wide, tall, len(made), len(made_small), comm, *refs),
        out_shape=shapes,
        in_specs=[ANY, ANY, VMEM, VMEM] + [ANY] * 12,
        out_specs=[ANY] + [VMEM] * 5,
        scratch_shapes=scratch,
        compiler_params=pltpu.CompilerParams(
            collective_id=1, has_side_effects=True, vmem_limit_bytes=67043328
        ),
        name="backward",
    )(six(tokens), six(cot), live, vecs, six(h1), six(qkv), lse, six(ctx), r1, six(h2), six(act), six(gp), *weights)


def body(dims, tokens, cotangent, seq_lengths, seq_place, ln1_gain, ln1_bias, w_qkv, q_bias, v_bias, w_out, out_bias, ln2_gain, ln2_bias, w_fc, fc_bias, w_proj, proj_bias):
    rows, width = tokens.shape
    n = dims[0] * dims[1] * dims[2] * 2
    hidden = fc_bias.shape[0] * n
    seq = rows // MB
    per, per_fc = width // n, hidden // n
    slots = lax.axis_index("dp") * MB + jnp.arange(MB, dtype=jnp.int32)
    lengths = jnp.sum(jnp.where(seq_place[None, :] == slots[:, None], seq_lengths[None, :], 0), axis=1)
    live = (jnp.arange(seq, dtype=jnp.int32)[None] < lengths[:, None]).astype(F32).reshape(rows, 1)

    vectors = (ln1_gain, ln1_bias, q_bias, v_bias, out_bias, ln2_gain, ln2_bias, proj_bias)
    small = jnp.concatenate([*vectors, fc_bias]).astype(F32)
    small = jnp.pad(small, (0, 1024 - small.shape[0])).reshape(8, 128)
    chunks = [(0, i, width) for i in range(0, 3 * width, width)] + [(1, 0, width)]
    chunks += [(2, i, width) for i in range(0, hidden, width)]
    chunks += [(3, i, width // 4) for i in range(0, width, width // 4)]
    kinds = [0, 0, 0, 0, 0, 1, 0, 1, 0, 1, 0, 1]
    made = forward(dims, tokens, live, (w_qkv, w_out, w_fc, w_proj), small, chunks, kinds)
    out = made[14]
    dx, g_qkv, g_out, g_fc, g_proj, small = backward(dims, tokens, cotangent, live, made[5:14], made[:4])
    small = small.reshape(1024)
    own = [small[i * per : (i + 1) * per] for i in range(8)]
    g_ln1_gain, g_ln1_bias, g_q_bias, g_v_bias, g_out_bias, g_ln2_gain, g_ln2_bias, g_proj_bias = own
    g_fc_bias = small[8 * per : 8 * per + per_fc]
    return (out, dx.reshape(rows, width), g_ln1_gain, g_ln1_bias, g_qkv, g_q_bias, g_v_bias, g_out, g_out_bias, g_ln2_gain, g_ln2_bias, g_fc, g_fc_bias, g_proj, g_proj_bias)


def solution(mesh):
    dims = grid_dims(mesh.shape["dp"])
    row, vec = P("dp", None), P("dp")
    return jax.shard_map(
        lambda *args: body(dims, *args),
        mesh=mesh,
        in_specs=(row, row, P(), P(), vec, vec, row, vec, vec, row, vec, vec, vec, row, vec, row, vec),
        out_specs=(row, row, vec, vec, row, vec, vec, row, vec, vec, vec, row, vec, row, vec),
        check_vma=False,
    )
```

```python
import jax
import jax.numpy as jnp
from jax import lax
from jax.experimental import pallas as pl
from jax.experimental.pallas import tpu as pltpu
from jax.sharding import PartitionSpec as P

MESH = pl.DeviceIdType.MESH
ANY = pl.BlockSpec(memory_space=pl.ANY)
VMEM = pl.BlockSpec(memory_space=pltpu.VMEM)
DMA = pltpu.SemaphoreType.DMA


def grid_dims(n):
    half = n // 2
    first = 4 if half % 4 == 0 else half
    rest = half // first
    second = 1
    while second * second < rest:
        second *= 2
    return first, second, rest // second


class Place:
    def __init__(self, dims):
        self.dims = dims
        d1, d2, d3 = dims
        me = lax.axis_index("dp")
        self.z = me // (d2 * d3 * 2)
        self.y = (me // (d3 * 2)) % d2
        self.x = (me // 2) % d3
        self.c = me % 2
        self.zs = [(self.z + k) % d1 for k in range(1, d1)]
        self.ys = [(self.y + k) % d2 for k in range(1, d2)]
        self.xs = [(self.x + k) % d3 for k in range(1, d3)]
        self.to_z = [self.dev(z=v) for v in self.zs]
        self.to_y = [self.dev(y=v) for v in self.ys]
        self.to_x = [self.dev(x=v) for v in self.xs]
        self.to_p = self.dev(c=1 - self.c)

    def dev(self, **at):
        z, y, x, c = (at.get(name, getattr(self, name)) for name in "zyxc")
        _, d2, d3 = self.dims
        return (((z * d2 + y) * d3 + x) * 2 + c,)

    def barrier(self):
        semaphore = pltpu.get_barrier_semaphore()
        peers = self.to_z + self.to_y + self.to_x + [self.to_p]
        for peer in peers:
            pl.semaphore_signal(semaphore, inc=1, device_id=peer, device_id_type=MESH)
        pl.semaphore_wait(semaphore, len(peers))


def send(source, target, send_sem, recv_sem, device):
    return pltpu.make_async_remote_copy(
        src_ref=source,
        dst_ref=target,
        send_sem=send_sem,
        recv_sem=recv_sem,
        device_id=device,
        device_id_type=MESH,
    )


class Plan:
    def __init__(self, costs, follow):
        self.costs, self.follow = costs, follow
        self.now, self.free, self.flying, self.taken, self.table = 0.0, {}, [], set(), {}

    def issue(self, key, events):
        lane, cost = self.costs(key)
        begin = max(self.now, self.free.get(lane, 0.0))
        self.free[lane] = begin + cost
        self.flying.append((begin + cost + 1.0, key))
        self.flying.sort()
        events.append(("go", key))

    def pump(self, point, passed=0.0, start=(), force=()):
        self.now += passed
        events = self.table.setdefault(point, [])

        def take():
            when, key = self.flying.pop(0)
            self.now = max(self.now, when)
            self.taken.add(key)
            events.append(("take", key))
            for after in self.follow(key, self.taken):
                self.issue(after, events)

        while self.flying and self.flying[0][0] <= self.now:
            take()
        while any(key not in self.taken for key in force):
            take()
        for key in start:
            self.issue(key, events)


class Gather:
    AHEAD = 3

    def __init__(self, place, shards, wholes, chunks, kinds, sems):
        self.at, self.shards, self.wholes = place, shards, wholes
        self.chunks, self.kinds, self.sems = chunks, kinds, sems

    @staticmethod
    def semaphores(dims, count):
        d1, d2, d3 = dims
        shapes = []
        for size in (max(d1, d2 + d3), 2 * d1 + d2 + d3, d2 + d3, 1):
            shapes += [DMA((count, size)), DMA((count, size))]
        return shapes

    @staticmethod
    def plan(chunks, kinds, unit):
        def costs(key):
            stage, t = key
            size = unit(t)
            if stage == 3:
                return "p", 1.4 * size
            over_z = stage == kinds[t]
            if over_z:
                return "z", (8 if kinds[t] else 4) * size
            return "xy", (0.5, 2, 4)[stage] * size

        def follow(key, taken):
            stage, t = key
            after = [] if stage == 3 else [(stage + 1, t)]
            if stage == 0 and t + Gather.AHEAD < len(chunks):
                after.append((0, t + Gather.AHEAD))
            return after

        return Plan(costs, follow)

    def copies(self, stage, t):
        p = self.at
        z, y, x, c = p.z, p.y, p.x, p.c
        i, first, width = self.chunks[t]
        whole, shard, half = self.wholes[i], self.shards[i], width // 2
        full = pl.ds(first, width)
        a, b = pl.ds(first, half), pl.ds(first + half, half)
        pieces = []
        if stage == 0 and self.kinds[t] == 0:
            pieces = [(shard.at[:, full], whole.at[z, y, x, c, :, full], d) for d in p.to_z]
        elif stage == 0:
            pieces = [(shard.at[:, a], whole.at[z, y, x, c, :, a], d) for d in p.to_x]
            pieces += [(shard.at[:, b], whole.at[z, y, x, c, :, b], d) for d in p.to_y]
        elif stage == 1 and self.kinds[t] == 0:
            part = whole.at[:, y, x, c, :, a]
            pieces = [(part, part, d) for d in p.to_x]
            part = whole.at[:, y, x, c, :, b]
            pieces += [(part, part, d) for d in p.to_y]
        elif stage == 1:
            left, right = whole.at[z, y, :, c, :, a], whole.at[z, :, x, c, :, b]
            pieces = [(part, part, d) for d in p.to_z for part in (left, right)]
        elif stage == 2:
            part = whole.at[:, y, :, c, :, a]
            pieces = [(part, part, d) for d in p.to_y]
            part = whole.at[:, :, x, c, :, b]
            pieces += [(part, part, d) for d in p.to_x]
        else:
            part = whole.at[:, :, :, c, :, full]
            pieces = [(part, part, p.to_p)]
        out, back = self.sems[2 * stage], self.sems[2 * stage + 1]
        return [send(s, d, out.at[t, k], back.at[t, k], to) for k, (s, d, to) in enumerate(pieces)]

    def run(self, events):
        for what, (stage, t) in events:
            for copy in self.copies(stage, t):
                if what == "go":
                    copy.start()
                else:
                    copy.wait_recv()

    def finish(self):
        for stage in range(4):
            for t in range(len(self.chunks)):
                for copy in self.copies(stage, t):
                    copy.wait_send()


def small_copies(place, source, target, sems, stage):
    z, y, x, c = place.z, place.y, place.x, place.c
    if stage == 0:
        pieces = [(source, target.at[z, y, x, c], d) for d in place.to_z]
    elif stage == 1:
        part = target.at[:, y, x, c]
        pieces = [(part, part, d) for d in place.to_x]
    elif stage == 2:
        part = target.at[:, y, :, c]
        pieces = [(part, part, d) for d in place.to_y]
    else:
        part = target.at[:, :, :, c]
        pieces = [(part, part, place.to_p)]
    base = stage * max(place.dims)
    return [send(s, d, sems[0].at[base + k], sems[1].at[base + k], to) for k, (s, d, to) in enumerate(pieces)]


class Reduce:
    @staticmethod
    def scratch(dims, rows, width, dtype, halves=True):
        d1, d2, d3 = dims
        half = width // 2 if halves else width
        shapes = [pltpu.VMEM((d1, d2, d3, rows, width), dtype)]
        shapes.append(pltpu.VMEM((d2 - 1, d1, d3, rows, half), dtype))
        shapes.append(pltpu.VMEM((d3 - 1, d1, rows, half), dtype))
        if halves:
            shapes.append(pltpu.VMEM((d3 - 1, d1, d2, rows, half), dtype))
            shapes.append(pltpu.VMEM((d2 - 1, d1, rows, half), dtype))
        shapes.append(pltpu.VMEM((d1 - 1, rows, width), dtype))
        sizes = (1, d2 + d3, d2 + d3, d1)
        for size in sizes:
            shapes += [DMA((size,)), DMA((size,))]
        return shapes

    @staticmethod
    def plan(unit):
        def costs(key):
            stage, t = key
            return ("p", "xy", "xy", "z")[stage], (1.4, 4, 2, 4)[stage] * unit(t)

        def follow(key, taken):
            stage, t = key
            after = []
            if stage == 0 and (t < 2 or (1, t - 2) in taken):
                after.append((1, t))
            if stage == 1:
                if (0, t + 2) in taken:
                    after.append((1, t + 2))
                after.append((2, t))
            if stage == 2:
                after.append((3, t))
            return after

        return Plan(costs, follow)

    def __init__(self, place, refs, source, own, result, halves=True, load=None):
        self.at, self.halves, self.load = place, halves, load
        self.source, self.own, self.result = source, own, result
        if halves:
            self.total, self.ya, self.xa, self.xb, self.yb, self.zz = refs[:6]
            self.sems = refs[6:]
        else:
            self.total, self.ya, self.xa, self.zz = refs[:4]
            self.sems = refs[4:]
        width = self.total.shape[-1]
        half = width // 2 if halves else width
        self.a, self.b = pl.ds(0, half), pl.ds(half, half)

    def pieces(self, stage):
        p, h = self.at, self.total
        y, x = p.y, p.x
        if stage == 0:
            return [(self.source.at[:, :, :, 1 - p.c], h, p.to_p)]
        if stage == 1:
            made = [
                (h.at[:, v, :, :, self.a], self.ya.at[k], d)
                for k, (v, d) in enumerate(zip(p.ys, p.to_y))
            ]
            if self.halves:
                made += [
                    (h.at[:, :, v, :, self.b], self.xb.at[k], d)
                    for k, (v, d) in enumerate(zip(p.xs, p.to_x))
                ]
            return made
        if stage == 2:
            made = [
                (h.at[:, y, v, :, self.a], self.xa.at[k], d)
                for k, (v, d) in enumerate(zip(p.xs, p.to_x))
            ]
            if self.halves:
                made += [
                    (h.at[:, v, x, :, self.b], self.yb.at[k], d)
                    for k, (v, d) in enumerate(zip(p.ys, p.to_y))
                ]
            return made
        return [(h.at[v, y, x], self.zz.at[k], d) for k, (v, d) in enumerate(zip(p.zs, p.to_z))]

    def go(self, stage):
        for copy in self.copies(stage):
            copy.start()

    def copies(self, stage):
        out, back = self.sems[2 * stage], self.sems[2 * stage + 1]
        return [
            send(s, d, out.at[k], back.at[k], to) for k, (s, d, to) in enumerate(self.pieces(stage))
        ]

    def arrived(self, stage):
        for copy in self.copies(stage):
            copy.wait()

    def add(self, stage):
        p, h = self.at, self.total
        d1, d2, d3 = p.dims
        f32 = jnp.float32

        def into(at, terms):
            value = h[at].astype(f32)
            for term in terms:
                value = value + term.astype(f32)
            h[at] = value.astype(h.dtype)

        if stage == 0:

            @pl.loop(0, d1)
            def _(i):
                for j in range(d2):
                    for k in range(d3):
                        into((i, j, k), [self.own[i, j, k]])

        elif stage == 1:

            @pl.loop(0, d1)
            def _(i):
                for k in range(d3):
                    into(
                        (i, p.y, k, slice(None), self.a),
                        [self.ya[m, i, k] for m in range(d2 - 1)],
                    )
                if self.halves:
                    for j in range(d2):
                        into(
                            (i, j, p.x, slice(None), self.b),
                            [self.xb[m, i, j] for m in range(d3 - 1)],
                        )

        elif stage == 2:

            @pl.loop(0, d1)
            def _(i):
                into((i, p.y, p.x, slice(None), self.a), [self.xa[m, i] for m in range(d3 - 1)])
                if self.halves:
                    into(
                        (i, p.y, p.x, slice(None), self.b),
                        [self.yb[m, i] for m in range(d2 - 1)],
                    )

        else:
            value = h[p.z, p.y, p.x].astype(f32)
            for m in range(d1 - 1):
                value = value + self.zz[m].astype(f32)
            for cut, target in self.result:
                target[...] = value[:, cut]

    def take(self, stage):
        if stage == 0 and self.load is not None:
            self.load.wait()
        self.arrived(stage)
        self.add(stage)


HEAD_DIM = 64
MB = 2
EPS = 1e-05
BF = jnp.bfloat16
F32 = jnp.float32
NEG = -1e30
GELU_A = 0.044715
GELU_C = 0.7978845608028654


def mm(left, right):
    return lax.dot_general(left, right, (((1,), (0,)), ((), ())), preferred_element_type=F32)


def mm_nt(left, right):
    return lax.dot_general(left, right, (((1,), (1,)), ((), ())), preferred_element_type=F32)


def mm_tn(left, right):
    return lax.dot_general(left, right, (((0,), (0,)), ((), ())), preferred_element_type=F32)


def iota(shape, axis):
    return lax.broadcasted_iota(jnp.int32, shape, axis)


def unpack_vector(block, start, per, width, first):
    row0, lane0 = start // 128, start % 128
    rows = block.shape[0]
    column = iota((128, width), 1) + first
    pick = (iota((128, width), 0) - lane0 == column % per).astype(BF)
    spread = mm(block, pick)
    column = iota((rows, width), 1) + first
    mine = iota((rows, width), 0) == column // per * 8 + row0
    return jnp.sum(jnp.where(mine, spread, 0.0), axis=0, keepdims=True)


def moments(value):
    mean = jnp.mean(value, axis=-1, keepdims=True)
    center = value - mean
    return center, lax.rsqrt(jnp.mean(center * center, axis=-1, keepdims=True) + EPS)


def attend_pair(q2, k2, v2, masks, seq):
    half = seq // 2
    lane = iota((1, 128), 1) // HEAD_DIM
    vt = v2.T
    q2 = q2 * jnp.asarray(HEAD_DIM**-0.5, BF)
    ka, kb = k2[:half], k2[half:]
    sums, rows = [], []
    for head in range(2):
        qh = jnp.where(lane == head, q2, 0)
        va, vb = (vt[head * HEAD_DIM : (head + 1) * HEAD_DIM, i * half : (i + 1) * half] for i in range(2))
        first, second = qh[:half], qh[half:]
        s = mm_nt(ka, first) + masks[0]
        sa, sb = mm_nt(ka, second), mm_nt(kb, second) + masks[1]
        top = jnp.max(s, axis=0, keepdims=True)
        e = jnp.exp(s - top)
        total = jnp.sum(e, axis=0, keepdims=True)
        low = mm(va, e.astype(BF)) * (1.0 / total)
        logs = top + jnp.log(total)
        top = jnp.maximum(jnp.max(sa, axis=0, keepdims=True), jnp.max(sb, axis=0, keepdims=True))
        ea, eb = jnp.exp(sa - top), jnp.exp(sb - top)
        total = jnp.sum(ea, axis=0, keepdims=True) + jnp.sum(eb, axis=0, keepdims=True)
        high = (mm(va, ea.astype(BF)) + mm(vb, eb.astype(BF))) * (1.0 / total)
        rows.append(jnp.concatenate([low, high], axis=1))
        sums.append(jnp.concatenate([logs, top + jnp.log(total)], axis=1))
    return jnp.concatenate(rows, axis=0).T, sums


def forward_plan(chunks, kinds, groups, fcs, projs, steps):
    widest = max(width for i, _, width in chunks if i != 3)
    plan = Gather.plan(chunks, kinds, lambda t: 1.2 * (1.0 if chunks[t][0] == 3 else chunks[t][2] / widest))
    fetched, used = set(), set()

    def pump(point, passed=0.0, done=None, **rest):
        if done is not None:
            used.add(done)
        plan.pump(point, passed, **rest)
        for t in range(len(chunks)):
            first = t < 2 or (chunks[t][0] == 3) != (chunks[t - 2][0] == 3)
            if (3, t) in plan.taken and t not in fetched and (first or t - 2 in used):
                fetched.add(t)
                plan.table[point].append(("fetch", (3, t)))

    pump("begin", 0.0, start=[(0, t) for t in range(Gather.AHEAD)])
    for k in range(4):
        pump(("small", k), 2.0)
    pump("norm", 4.0)
    for g in range(groups):
        pump(("qkv", g), 0.0, force=[(3, g)])
        pump(("scores", g), 2.4, done=g)
        for i in range(steps):
            pump(("attend", g, i), 0.0 if i == 0 else 1.6)
        pump(("group", g), 1.6)
    t = groups
    pump("out", 0.0, force=[(3, t)])
    for i in range(2):
        pump(("norm2", i), 2.1)
    used.add(t)
    for k in range(fcs):
        pump(("fc", k), 0.0, force=[(3, t + 1 + k)])
        for i in range(2):
            pump(("gelu", k, i), 2.4)
        used.add(t + 1 + k)
    for k in range(projs):
        pump(("terms", k), 3.1)
        pump(("proj", k), 0.0, force=[(3, t + 1 + fcs + k)])
        pump(("done", k), 2.8, done=t + 1 + fcs + k)
    pump("end", 0.0, force=[(3, k) for k in range(len(chunks))])
    return plan.table


def forward_kernel(dims, chunks, kinds, comm, *refs):
    (lens, tokens, cot, s_qkv, s_out, s_fc, s_proj, small) = refs[:8]
    (w_qkv, w_out, w_fc, w_proj, vecs_o, h1_o, qkv_o, lse_o, ctx_o, r1_o, h2_o, gp_o, dy_o, terms_o, out_o) = refs[8:23]
    (x_, dy, live, vecs, fcb, h1, qkv, ctx, lse, r1, h2, act, gp, out, sm, wbuf, pbuf, tbuf, diag, shuffled) = refs[23:43]
    local, wsem, psem, osem, gpsem, tsem, shsem, s_sem, r_sem = refs[43:52]
    sems = refs[52:]
    rows, width = x_.shape
    seq = rows // MB
    hidden = act.shape[1]
    n = dims[0] * dims[1] * dims[2] * 2
    per, per_fc = width // n, hidden // n
    tile = 256
    tiles = rows // tile
    fcs = hidden // width
    groups = sum(i == 0 for i, _, _ in chunks)
    gw = width // groups
    pw = chunks[-1][2]
    projs = width // pw
    gpairs = gw // 128
    steps = MB * gpairs
    plan = forward_plan(chunks, kinds, groups, fcs, projs, steps)
    place = Place(dims)
    z, y, x, c = place.z, place.y, place.x, place.c
    shards = (shuffled, s_out, s_fc, s_proj)
    wholes = (w_qkv, w_out, w_fc, w_proj)
    gather = Gather(place, shards, wholes, chunks, kinds, sems)

    def at_point(*key):
        for event in plan[key[0] if len(key) == 1 else key]:
            if event[0] == "fetch":
                fetch(event[1][1]).start()
            elif comm:
                gather.run([event])

    def fetch(t):
        i, first, w = chunks[t]
        source = wholes[i].at[:, :, :, :, :, pl.ds(first, w)]
        if i == 3:
            return pltpu.make_async_copy(source, pbuf.at[t % 2], psem.at[t % 2])
        return pltpu.make_async_copy(source, wbuf.at[t % 2, :, :, :, :, :, pl.ds(0, w)], wsem.at[t % 2])

    saves = []

    def keep(source, target):
        save = pltpu.make_async_copy(source, target, osem.at[len(saves)])
        save.start()
        saves.append(save)

    shuffle = [
        pltpu.make_async_copy(
            s_qkv.at[:, pl.ds(k * width + g * gw, gw)], shuffled.at[:, pl.ds((3 * g + k) * gw, gw)], shsem.at[3 * g + k]
        )
        for g in range(groups)
        for k in range(3)
    ]
    for move in shuffle:
        move.start()
    loads = [pltpu.make_async_copy(tokens, x_, gpsem.at[0]), pltpu.make_async_copy(cot, dy, gpsem.at[1])]
    for move in loads:
        move.start()
    moves = [
        pltpu.make_async_copy(s, w.at[z, y, x, c], local.at[i])
        for i, (s, w) in enumerate(zip((*shards, small), (*wholes, sm)))
    ]
    for move in moves[1:]:
        move.start()
    place.barrier()
    for move in shuffle:
        move.wait()
    moves[0].start()
    tiny = [small_copies(place, small, sm, (s_sem, r_sem), stage) for stage in range(4)]
    half = seq // 2
    for stage in range(4):
        if comm:
            for copy in tiny[stage]:
                copy.start()
        if stage == 0:
            at_point("begin")
            for slot in range(MB):
                length = lens[slot : slot + 1, 0:1]
                live[slot * seq : (slot + 1) * seq, :] = jnp.where(iota((seq, 1), 0).astype(F32) < length, 1.0, 0.0)
                causal = iota((half, half), 0) <= iota((half, half), 1)
                late = (iota((half, half), 0) + half).astype(F32) < length
                diag[0] = jnp.where(causal, 0.0, NEG)
                diag[1 + slot] = jnp.where(causal & late, 0.0, NEG)
            for move in moves:
                move.wait()
        if stage == 1:
            loads[1].wait()
            vecs[8:16, :] = jnp.zeros((8, width), F32)

            @pl.loop(0, tiles)
            def _(i):
                at = pl.ds(pl.multiple_of(i * tile, tile), tile)
                value = jnp.where(live[at, :] > 0.5, dy[at, :].astype(F32), 0.0)
                dy[at, :] = value.astype(BF)
                vecs[8:9, :] += jnp.sum(value, axis=0, keepdims=True)

            keep(dy, dy_o)
        if comm:
            for copy in tiny[stage]:
                copy.wait_recv()
        at_point("small", stage)
    block = sm[...].reshape(n * 8, 128).astype(BF)
    for v in range(8):
        vecs[v : v + 1, :] = unpack_vector(block, v * per, per, width, 0)
    for part in range(fcs):
        fcb[:, part * width : (part + 1) * width] = unpack_vector(block, 8 * per, per_fc, width, part * width)
    loads[0].wait()

    @pl.loop(0, rows // 128)
    def _(i):
        at = pl.ds(pl.multiple_of(i * 128, 128), 128)
        center, scale = moments(x_[at, :].astype(F32))
        h1[at, :] = (center * scale * vecs[0:1, :] + vecs[1:2, :]).astype(BF)

    keep(h1, h1_o)
    keep(vecs, vecs_o)
    at_point("norm")

    @pl.loop(0, groups)
    def _(g):
        for k in range(groups):

            @pl.when(g == k)
            def _():
                at_point("qkv", k)
                fetch(k).wait()

        first = pl.multiple_of(g * gw, gw)

        @pl.loop(0, tiles)
        def _(i):
            at = pl.ds(pl.multiple_of(i * tile, tile), tile)
            value = mm(h1[at, :], wbuf[g % 2, :, :, :, :, :, 0 : 3 * gw].reshape(width, 3 * gw))
            for k, bias in ((0, 2), (1, None), (2, 3)):
                part = value[:, k * gw : (k + 1) * gw]
                if bias is not None:
                    part = part + vecs[bias : bias + 1, pl.ds(first, gw)]
                qkv[at, pl.ds(k * width + first, gw)] = part.astype(BF)

        for k in range(groups):
            if plan["scores", k]:

                @pl.when(g == k)
                def _():
                    at_point("scores", k)

        @pl.loop(0, steps)
        def _(i):
            for k in range(groups):
                for m in range(steps):
                    if plan["attend", k, m]:

                        @pl.when((g == k) & (i == m))
                        def _():
                            at_point("attend", k, m)

            slot, pair = i // gpairs, g * gpairs + i % gpairs
            at = pl.ds(pl.multiple_of(slot * seq, seq), seq)
            col = pl.multiple_of(pair * 128, 128)
            value, sums = attend_pair(
                qkv[at, pl.ds(col, 128)],
                qkv[at, pl.ds(width + col, 128)],
                qkv[at, pl.ds(2 * width + col, 128)],
                [diag[0], diag[1 + slot]],
                seq,
            )
            ctx[at, pl.ds(col, 128)] = value.astype(BF)
            for head in range(2):
                lse[slot * (width // HEAD_DIM) + pair * 2 + head] = sums[head]

        for k in range(groups):
            if plan["group", k]:

                @pl.when(g == k)
                def _():
                    at_point("group", k)

    keep(qkv, qkv_o)
    keep(ctx, ctx_o)
    keep(lse, lse_o)
    t = groups
    at_point("out")
    fetch(t).wait()

    @pl.loop(0, tiles)
    def _(i):
        at = pl.ds(pl.multiple_of(i * tile, tile), tile)
        value = mm(ctx[at, :], wbuf[t % 2].reshape(width, width)) + vecs[4:5, :]
        value = value + x_[at, :].astype(F32)
        r1[at, :] = value
        center, scale = moments(value)
        h2[at, :] = (center * scale * vecs[5:6, :] + vecs[6:7, :]).astype(BF)
        for k in range(2):

            @pl.when(i == (k + 1) * tiles // 2 - 1)
            def _():
                at_point("norm2", k)

    keep(r1, r1_o)
    keep(h2, h2_o)

    def keep_gp(k):
        return pltpu.make_async_copy(gp.at[k % 2], gp_o.at[:, pl.ds(k * width, width)], gpsem.at[k % 2])

    for k in range(fcs):
        t = groups + 1 + k
        at_point("fc", k)
        if k >= 2:
            keep_gp(k - 2).wait()
        fetch(t).wait()

        @pl.loop(0, 2)
        def _(i):
            for part in range(tiles // 2):
                at = pl.ds(pl.multiple_of((i * (tiles // 2) + part) * tile, tile), tile)
                u = mm(h2[at, :], wbuf[t % 2].reshape(width, width)) + fcb[:, k * width : (k + 1) * width]
                square = u * u
                inner = u * (GELU_C + (GELU_C * GELU_A) * square)
                gate = 0.5 + 0.5 * jnp.tanh(inner)
                value = u * gate
                act[at, k * width : (k + 1) * width] = value.astype(BF)
                slope = gate + value * (2.0 - 2.0 * gate) * (GELU_C + (3.0 * GELU_C * GELU_A) * square)
                gp[k % 2, at, :] = slope.astype(BF)
            for m in range(2):
                if plan["gelu", k, m]:

                    @pl.when(i == m)
                    def _():
                        at_point("gelu", k, m)

        keep_gp(k).start()

    def keep_terms(k):
        return pltpu.make_async_copy(
            tbuf.at[k % 2], terms_o.at[:, :, :, :, :, pl.ds(k * pw, pw)], tsem.at[k % 2]
        )

    for k in range(projs):
        t = groups + 1 + fcs + k
        cols = slice(k * pw, (k + 1) * pw)
        if k >= 2:
            keep_terms(k - 2).wait()

        @pl.loop(0, dims[0])
        def _(i):
            span = hidden // dims[0]
            value = mm_tn(act[:, pl.ds(pl.multiple_of(i * span, span), span)], dy[:, cols])
            tbuf[k % 2, i] = value.astype(BF).reshape(dims[1], dims[2], 2, per_fc, pw)

        keep_terms(k).start()
        at_point("terms", k)
        at_point("proj", k)
        fetch(t).wait()

        @pl.loop(0, tiles)
        def _(i):
            at = pl.ds(pl.multiple_of(i * tile, tile), tile)
            value = mm(act[at, :], pbuf[t % 2].reshape(hidden, pw)) + (r1[at, cols] + vecs[7:8, cols])
            out[at, cols] = jnp.where(live[at, :] > 0.5, value, 0.0).astype(BF)

        keep(out.at[:, pl.ds(k * pw, pw)], out_o.at[:, pl.ds(k * pw, pw)])
        at_point("done", k)

    at_point("end")
    for k in range(max(fcs - 2, 0), fcs):
        keep_gp(k).wait()
    for k in range(max(projs - 2, 0), projs):
        keep_terms(k).wait()
    for save in saves:
        save.wait()
    if comm:
        gather.finish()
        for copies in tiny:
            for copy in copies:
                copy.wait_send()


def forward(dims, lens, tokens, cot, shards, small, chunks, kinds, comm=True):
    rows, width = tokens.shape
    n = dims[0] * dims[1] * dims[2] * 2
    hidden = shards[2].shape[1]
    heads = width // HEAD_DIM
    seq = rows // MB
    pw = chunks[-1][2]
    groups = sum(i == 0 for i, _, _ in chunks)
    sds = jax.ShapeDtypeStruct
    shapes = [sds((*dims, 2, *s.shape), s.dtype) for s in shards]
    shapes += [
        sds((16, width), F32),
        sds((rows, width), BF),
        sds((rows, 3 * width), BF),
        sds((MB * heads, 1, seq), F32),
        sds((rows, width), BF),
        sds((rows, width), F32),
        sds((rows, width), BF),
        sds((rows, hidden), BF),
        sds((rows, width), BF),
        sds((*dims, 2, hidden // n, width), BF),
        sds((rows, width), BF),
    ]
    scratch = [
        pltpu.VMEM((rows, width), BF),
        pltpu.VMEM((rows, width), BF),
        pltpu.VMEM((rows, 1), F32),
        pltpu.VMEM((16, width), F32),
        pltpu.VMEM((1, hidden), F32),
        pltpu.VMEM((rows, width), BF),
        pltpu.VMEM((rows, 3 * width), BF),
        pltpu.VMEM((rows, width), BF),
        pltpu.VMEM((MB * heads, 1, seq), F32),
        pltpu.VMEM((rows, width), F32),
        pltpu.VMEM((rows, width), BF),
        pltpu.VMEM((rows, hidden), BF),
        pltpu.VMEM((2, rows, width), BF),
        pltpu.VMEM((rows, width), BF),
        pltpu.VMEM((*dims, 2, *small.shape), small.dtype),
        pltpu.VMEM((2, *dims, 2, width // n, width), BF),
        pltpu.VMEM((2, *dims, 2, hidden // n, pw), BF),
        pltpu.VMEM((2, *dims, 2, hidden // n, pw), BF),
        pltpu.VMEM((1 + MB, seq // 2, seq // 2), F32),
        pltpu.VMEM(shards[0].shape, BF),
        DMA((5,)),
        DMA((2,)),
        DMA((2,)),
        DMA((8 + width // pw,)),
        DMA((2,)),
        DMA((2,)),
        DMA((3 * groups,)),
        DMA((4 * max(dims),)),
        DMA((4 * max(dims),)),
        *Gather.semaphores(dims, len(chunks)),
    ]
    return pl.pallas_call(
        lambda *refs: forward_kernel(dims, chunks, kinds, comm, *refs),
        out_shape=shapes,
        in_specs=[VMEM, ANY, ANY, ANY] + [VMEM] * 4,
        out_specs=[ANY] * 15,
        scratch_shapes=scratch,
        compiler_params=pltpu.CompilerParams(
            collective_id=0, has_side_effects=True, vmem_limit_bytes=60 * 1024 * 1024
        ),
        name="forward",
    )(lens, tokens, cot, *shards, small)


def pack_vector(row, start, per, rows):
    row0, lane0 = start // 128, start % 128
    width = row.shape[1]
    pick = (iota((128, width), 0) - lane0 == iota((128, width), 1) % per).astype(BF)
    mine = iota((rows, width), 0) == iota((rows, width), 1) // per * 8 + row0
    total = None
    for _ in range(3):
        part = row.astype(BF)
        row = row - part.astype(F32)
        value = mm_nt(jnp.where(mine, part.astype(F32), 0.0).astype(BF), pick)
        total = value if total is None else total + value
    return total


def norm_back(value, gain, grad):
    center, scale = moments(value)
    normed = center * scale
    scaled = grad * gain
    mean = jnp.mean(scaled, axis=-1, keepdims=True)
    cross = jnp.mean(scaled * normed, axis=-1, keepdims=True)
    return (scaled - mean - normed * cross) * scale, grad * normed


def attend_back(q2, k2, v2, o2, c2, lse, masks, seq):
    half = seq // 2
    lane = iota((1, 128), 1) // HEAD_DIM
    prod = o2.astype(F32) * c2.astype(F32)
    heads = (iota((8, 128), 1) // HEAD_DIM == iota((8, 128), 0)).astype(BF)
    high = prod.astype(BF)
    delta = mm_nt(heads, high) + mm_nt(heads, (prod - high.astype(F32)).astype(BF))
    kt = k2.T
    q2 = q2 * jnp.asarray(HEAD_DIM**-0.5, BF)
    cuts = (slice(0, half), slice(half, seq))
    dk, dv, dq = [0.0, 0.0], [0.0, 0.0], []
    for head in range(2):
        qh = jnp.where(lane == head, q2, 0)
        oh = jnp.where(lane == head, o2, 0)
        kh = kt[head * HEAD_DIM : (head + 1) * HEAD_DIM]
        parts = [0.0, 0.0]
        for key, query in ((0, 0), (0, 1), (1, 1)):
            qb, ob, cut = qh[cuts[query]], oh[cuts[query]], cuts[query]
            s = mm_nt(k2[cuts[key]], qb) - lse[head][:, cut]
            if key == query:
                s = s + masks[key]
            p = jnp.exp(s)
            dp = mm_nt(v2[cuts[key]], ob)
            ds = (p * (dp - delta[head : head + 1, cut])).astype(BF)
            dv[key] = dv[key] + mm(p.astype(BF), ob)
            dk[key] = dk[key] + mm(ds, qb)
            parts[query] = parts[query] + mm(kh[:, cuts[key]], ds)
        dq.append(jnp.concatenate(parts, axis=1))
    dq = jnp.concatenate(dq, axis=0).T * HEAD_DIM**-0.5
    return dq, jnp.concatenate(dk, axis=0), jnp.concatenate(dv, axis=0)


def backward_plan(projs, fcs, groups, steps, slabs):
    out = projs + fcs
    plan = Reduce.plan(lambda t: 1.3 if t <= out else 1.0)
    pump = plan.pump
    pump("start", 0.0, start=[(0, 0), (0, 1)])
    pump("loaded", 4.0)
    late = list(range(2, projs))
    for f in range(fcs):
        for name, passed in (("da", 3.2), ("dh", 2.9)):
            j = late.pop(0) if late else None
            force = [] if j is None else [(0, j - 2)]
            if name == "dh" and f >= 2:
                force.append((0, projs + f - 2))
            pump((name, f), passed, force=force, start=[] if j is None else [(0, j)])
        pump(("gfc", f), 2.9, start=[(0, projs + f)])
    for i in range(slabs):
        pump(("ln2", i), 2.2)
    pump("dctx", 3.0, force=[(0, out - 2)])
    pump("gout", 3.0, start=[(0, out)])
    for g in range(groups):
        for i in range(steps):
            pump(("back", g, i), 0.0 if i == 0 else 2.0)
        pump(("grads", g), 2.0, force=[(0, out - 1 + g)])
        pump(("gqkv", g), 2.2, start=[(0, out + 1 + g)])
    for i in range(slabs):
        pump(("dx", i), 3.4)
    pump("end", 4.0, force=[(3, t) for t in range(out + 1 + groups)])
    return plan.table


def backward_kernel(dims, groups, sizes, comm, *refs):
    (lens, tokens, dy, vecs, h1_i, qkv_i, lse_i, ctx_i, r1_i, h2_i, gp_i, terms, w_qkv, w_out, w_fc, w_proj) = refs[:16]
    (dx_o, g_qkv, g_out, g_fc, g_proj, g_small) = refs[16:22]
    slots, wp, f_dh, f_r1, gvec, gfc, lse, diag, stage, owns, sstage = refs[22:33]
    lsem, wsem, osem, qsem = refs[33:37]
    refs = refs[37:]
    d1, d2, d3 = dims
    n = d1 * d2 * d3 * 2
    rows, width = f_dh.shape
    hidden = gfc.shape[1]
    seq = rows // MB
    half = seq // 2
    per, per_fc = width // n, hidden // n
    fcs = hidden // width
    gw = width // groups
    pw = owns.shape[-1]
    projs = width // pw
    tile = rows // d1
    gpairs = gw // 128
    steps = MB * gpairs
    place = Place(dims)
    c = place.c
    plan = backward_plan(projs, fcs, groups, steps, d1)
    sets = []
    for size in sizes:
        sets.append(refs[:size])
        refs = refs[size:]
    parts = []
    for j in range(projs):
        cut = pl.ds(j * pw, pw)
        own = owns.at[j % 2]
        move = pltpu.make_async_copy(terms.at[:, :, :, c, :, cut], own, osem.at[j % 2])
        result = [(slice(None), g_proj.at[:, cut])]
        parts.append(Reduce(place, sets[j], terms.at[:, :, :, :, :, cut], own, result, load=move))
    for f in range(fcs):
        result = [(slice(None), g_fc.at[:, pl.ds(f * width, width)])]
        parts.append(Reduce(place, sets[projs + f], stage.at[f % 2], stage.at[f % 2, :, :, :, c], result))
    b = fcs % 2
    parts.append(Reduce(place, sets[projs + fcs], stage.at[b], stage.at[b, :, :, :, c], [(slice(None), g_out)]))
    gcut = pl.ds(0, 3 * gw)
    for g in range(groups):
        b = (fcs + 1 + g) % 2
        result = [
            (slice(k * gw, (k + 1) * gw), g_qkv.at[:, pl.ds(k * width + g * gw, gw)]) for k in range(3)
        ]
        source, own = stage.at[b, :, :, :, :, :, gcut], stage.at[b, :, :, :, c, :, gcut]
        parts.append(Reduce(place, sets[projs + fcs + 1 + g], source, own, result))

    def at_point(*key):
        if not comm:
            return
        for what, (step, t) in plan[key[0] if len(key) == 1 else key]:
            if what == "take":
                parts[t].take(step)
            else:
                parts[t].go(step)
                if step == 0 and parts[t].load is not None:
                    parts[t].load.start()

    def load(source, slot, k):
        return pltpu.make_async_copy(source, slots.at[slot], lsem.at[k])

    def cols(source, k):
        return source.at[:, :, :, :, :, pl.ds(k * width, width)]

    def whole(slot):
        return slots[slot].reshape(rows, width)

    def piece(slot, i):
        return slots[slot, i].reshape(tile, width)

    def put(slot, i, value):
        slots[slot, i] = value.astype(BF).reshape(d2, d3, 2, per, width)

    def fetch_proj(f):
        return pltpu.make_async_copy(w_proj.at[f], wp.at[f % 2], wsem.at[f % 2])

    def fetch_ff(f):
        return [fetch_proj(f), load(cols(gp_i, f), 3 + f % 2, 3 + f % 2), load(cols(w_fc, f), 1 + f % 2, 1 + f % 2)]

    def w_third(k, slot):
        return [
            pltpu.make_async_copy(
                w_qkv.at[:, :, :, :, :, pl.ds((3 * g + k) * gw, gw)],
                slots.at[slot, :, :, :, :, :, pl.ds(g * gw, gw)],
                qsem.at[k, g],
            )
            for g in range(groups)
        ]

    load(dy, 0, 0).start()
    for move in fetch_ff(0):
        move.start()
    load(h2_i, 6, 6).start()
    load(ctx_i, 7, 7).start()
    lload = pltpu.make_async_copy(lse_i, lse, lsem.at[5])
    lload.start()
    place.barrier()
    at_point("start")
    for slot in range(MB):
        causal = iota((half, half), 0) <= iota((half, half), 1)
        late = (iota((half, half), 0) + half).astype(F32) < lens[slot : slot + 1, 0:1]
        diag[0] = jnp.where(causal, 0.0, NEG)
        diag[1 + slot] = jnp.where(causal & late, 0.0, NEG)
    gvec[...] = jnp.zeros_like(gvec)
    gfc[...] = jnp.zeros_like(gfc)
    gvec[7:8, :] = vecs[8:9, :]
    load(dy, 0, 0).wait()
    at_point("loaded")
    for f in range(fcs):
        for move in fetch_ff(f):
            move.wait()
        if f + 1 < fcs:
            for move in fetch_ff(f + 1):
                move.start()
        cut = slice(f * width, (f + 1) * width)

        @pl.loop(0, d1)
        def _(i):
            da = mm_nt(piece(0, i), wp[f % 2].reshape(rows, width))
            du = (da * piece(3 + f % 2, i).astype(F32)).astype(BF)
            put(5, i, du)
            gfc[:, cut] += jnp.sum(du.astype(F32), axis=0, keepdims=True)

        at_point("da", f)

        @pl.loop(0, d1)
        def _(i):
            at = pl.ds(pl.multiple_of(i * tile, tile), tile)
            value = mm_nt(piece(5, i), whole(1 + f % 2))
            if f == 0:
                f_dh[at, :] = value
            else:
                f_dh[at, :] += value

        at_point("dh", f)
        if f == 0:
            load(h2_i, 6, 6).wait()

        @pl.loop(0, 2)
        def _(i):
            col = pl.ds(pl.multiple_of(i * (width // 2), width // 2), width // 2)
            value = mm_tn(slots[6, :, :, :, :, :, col].reshape(rows, width // 2), whole(5)).astype(BF)
            stage[f % 2, pl.ds(i * (d1 // 2), d1 // 2)] = value.reshape(d1 // 2, d2, d3, 2, per, width)

        at_point("gfc", f)

    def r1_tile(i):
        return pltpu.make_async_copy(r1_i.at[pl.ds(i * tile, tile)], f_r1.at[i % 2], wsem.at[i % 2])

    r1_tile(0).start()
    load(w_out, 1, 1).start()
    for k, slot in enumerate((3, 4, 6)):
        load(cols(qkv_i, k), slot, slot).start()

    @pl.loop(0, d1)
    def _(i):
        r1_tile(i).wait()

        @pl.when(i + 1 < d1)
        def _():
            r1_tile(i + 1).start()

        at = pl.ds(pl.multiple_of(i * tile, tile), tile)
        grad = f_dh[at, :]
        value, norms = norm_back(f_r1[i % 2], vecs[5:6, :], grad)
        value = value + piece(0, i).astype(F32)
        f_dh[at, :] = value
        low = value.astype(BF)
        put(5, i, low)
        gvec[5:6, :] += jnp.sum(norms, axis=0, keepdims=True)
        gvec[6:7, :] += jnp.sum(grad, axis=0, keepdims=True)
        gvec[4:5, :] += jnp.sum(low.astype(F32), axis=0, keepdims=True)
        for k in range(d1):
            if plan["ln2", k]:

                @pl.when(i == k)
                def _():
                    at_point("ln2", k)

    load(ctx_i, 7, 7).wait()
    load(w_out, 1, 1).wait()
    load(h1_i, 0, 0).start()

    @pl.loop(0, d1)
    def _(i):
        put(2, i, mm_nt(piece(5, i), whole(1)))

    for move in w_third(0, 1):
        move.start()
    at_point("dctx")

    @pl.loop(0, 2)
    def _(i):
        col = pl.ds(pl.multiple_of(i * (width // 2), width // 2), width // 2)
        value = mm_tn(slots[7, :, :, :, :, :, col].reshape(rows, width // 2), whole(5)).astype(BF)
        stage[fcs % 2, pl.ds(i * (d1 // 2), d1 // 2)] = value.reshape(d1 // 2, d2, d3, 2, per, width)

    for move in w_third(1, 5):
        move.start()
    at_point("gout")
    for k, slot in enumerate((3, 4, 6)):
        load(cols(qkv_i, k), slot, slot).wait()
    lload.wait()
    load(h1_i, 0, 0).wait()
    hslab = d1 // MB

    @pl.loop(0, groups)
    def _(g):
        @pl.loop(0, steps)
        def _(i):
            for k in range(groups):
                for m in range(steps):
                    if plan["back", k, m]:

                        @pl.when((g == k) & (i == m))
                        def _():
                            at_point("back", k, m)

            slot, pair = i // gpairs, g * gpairs + i % gpairs
            slab = pl.ds(slot * hslab, hslab)
            lanes = pl.ds(pl.multiple_of(pair * 128, 128), 128)

            def get(s):
                return slots[s, slab, :, :, :, :, lanes].reshape(seq, 128)

            head = slot * (width // HEAD_DIM) + 2 * pair
            grads = attend_back(
                get(3), get(4), get(6), get(2), get(7), [lse[head], lse[head + 1]], [diag[0], diag[1 + slot]], seq
            )
            for s, value in zip((3, 4, 6), grads):
                slots[s, slab, :, :, :, :, lanes] = value.astype(BF).reshape(hslab, d2, d3, 2, per, 128)

        for k in range(groups):
            if plan["grads", k]:

                @pl.when(g == k)
                def _():
                    at_point("grads", k)

        mine = pl.ds(pl.multiple_of(g * gw, gw), gw)
        buffer = (fcs + 1 + g) % 2

        @pl.loop(0, 2)
        def _(i):
            col = pl.ds(pl.multiple_of(i * (width // 2), width // 2), width // 2)
            left = slots[0, :, :, :, :, :, col].reshape(rows, width // 2)
            for k, s in enumerate((3, 4, 6)):
                value = mm_tn(left, slots[s, :, :, :, :, :, mine].reshape(rows, gw)).astype(BF)
                stage[buffer, pl.ds(i * (d1 // 2), d1 // 2), :, :, :, :, k * gw : (k + 1) * gw] = value.reshape(
                    d1 // 2, d2, d3, 2, per, gw
                )

        for k in range(groups):

            @pl.when(g == k)
            def _():
                at_point("gqkv", k)

    for move in w_third(2, 7):
        move.start()
    load(tokens, 2, 2).start()
    for k, slot in enumerate((1, 5, 7)):
        for move in w_third(k, slot):
            move.wait()
    load(tokens, 2, 2).wait()

    @pl.loop(0, d1)
    def _(i):
        at = pl.ds(pl.multiple_of(i * tile, tile), tile)
        grad = mm_nt(piece(3, i), whole(1)) + mm_nt(piece(4, i), whole(5)) + mm_nt(piece(6, i), whole(7))
        value, norms = norm_back(piece(2, i).astype(F32), vecs[0:1, :], grad)
        put(2, i, value + f_dh[at, :])
        gvec[0:1, :] += jnp.sum(norms, axis=0, keepdims=True)
        gvec[1:2, :] += jnp.sum(grad, axis=0, keepdims=True)
        gvec[2:3, :] += jnp.sum(piece(3, i).astype(F32), axis=0, keepdims=True)
        gvec[3:4, :] += jnp.sum(piece(6, i).astype(F32), axis=0, keepdims=True)
        for k in range(d1):
            if plan["dx", k]:

                @pl.when(i == k)
                def _():
                    at_point("dx", k)

    save = pltpu.make_async_copy(slots.at[2], dx_o, lsem.at[0])
    save.start()
    total = jnp.zeros((n * 8, 128), F32)
    for v in range(8):
        total = total + pack_vector(gvec[v : v + 1, :], v * per, per, n * 8)
    for k in range(fcs):
        part = pack_vector(gfc[:, k * width : (k + 1) * width], 8 * per, per_fc, n // fcs * 8)
        total = total + jnp.concatenate([part if m == k else jnp.zeros_like(part) for m in range(fcs)], axis=0)
    sstage[...] = total.reshape(*dims, 2, 8, 128)
    result = [(slice(None), g_small)]
    small = Reduce(place, refs, sstage, sstage.at[:, :, :, c], result, halves=False)
    if comm:
        small.go(0)
        small.take(0)
        small.go(1)
    at_point("end")
    if comm:
        for stage_k in range(1, 4):
            small.take(stage_k)
            if stage_k < 3:
                small.go(stage_k + 1)
    save.wait()


def backward(dims, lens, tokens, saved, weights, groups, comm=True):
    vecs, h1, qkv, lse, ctx, r1, h2, gp, dy, terms = saved
    rows, width = tokens.shape
    n = dims[0] * dims[1] * dims[2] * 2
    hidden = gp.shape[1]
    seq = rows // MB
    per, per_fc = width // n, hidden // n
    fcs = hidden // width
    projs = 4
    pw = width // projs

    def six(a):
        return a.reshape(*dims, 2, a.shape[0] // n, a.shape[1])

    sds = jax.ShapeDtypeStruct
    scratch = [
        pltpu.VMEM((8, *dims, 2, per, width), BF),
        pltpu.VMEM((2, *dims[1:], 2, per_fc, width), BF),
        pltpu.VMEM((rows, width), F32),
        pltpu.VMEM((2, rows // dims[0], width), F32),
        pltpu.VMEM((8, width), F32),
        pltpu.VMEM((1, hidden), F32),
        pltpu.VMEM(lse.shape, F32),
        pltpu.VMEM((1 + MB, seq // 2, seq // 2), F32),
        pltpu.VMEM((2, *dims, 2, per, width), BF),
        pltpu.VMEM((2, *dims, per_fc, pw), BF),
        pltpu.VMEM((*dims, 2, 8, 128), F32),
        DMA((8,)),
        DMA((2,)),
        DMA((2,)),
        DMA((3, groups)),
    ]
    sizes = []
    shapes = [(per_fc, pw)] * projs + [(per, width)] * (fcs + 1) + [(per, 3 * width // groups)] * groups
    for block_rows, block_cols in shapes:
        made = Reduce.scratch(dims, block_rows, block_cols, BF)
        sizes.append(len(made))
        scratch += made
    scratch += Reduce.scratch(dims, 8, 128, F32, halves=False)
    outs = [
        sds((*dims, 2, per, width), BF),
        sds((per, 3 * width), F32),
        sds((per, width), F32),
        sds((per, hidden), F32),
        sds((per_fc, width), F32),
        sds((8, 128), F32),
    ]
    return pl.pallas_call(
        lambda *refs: backward_kernel(dims, groups, sizes, comm, *refs),
        out_shape=outs,
        in_specs=[VMEM, ANY, ANY, VMEM] + [ANY] * 12,
        out_specs=[ANY] + [VMEM] * 5,
        scratch_shapes=scratch,
        compiler_params=pltpu.CompilerParams(
            collective_id=1, has_side_effects=True, vmem_limit_bytes=67043328
        ),
        name="backward",
    )(lens, six(tokens), six(dy), vecs, six(h1), six(qkv), lse, six(ctx), r1, six(h2), six(gp), terms, *weights)


def body(dims, tokens, cotangent, seq_lengths, seq_place, ln1_gain, ln1_bias, w_qkv, q_bias, v_bias, w_out, out_bias, ln2_gain, ln2_bias, w_fc, fc_bias, w_proj, proj_bias):
    rows, width = tokens.shape
    n = dims[0] * dims[1] * dims[2] * 2
    hidden = fc_bias.shape[0] * n
    seq = rows // MB
    per, per_fc = width // n, hidden // n
    slots = lax.axis_index("dp") * MB + jnp.arange(MB, dtype=jnp.int32)
    lengths = jnp.sum(jnp.where(seq_place[None, :] == slots[:, None], seq_lengths[None, :], 0), axis=1)
    lens = jnp.broadcast_to(jnp.pad(lengths, (0, 8 - MB))[:, None], (8, 128)).astype(F32)

    vectors = (ln1_gain, ln1_bias, q_bias, v_bias, out_bias, ln2_gain, ln2_bias, proj_bias, fc_bias)
    small, first = 0.0, 0
    for vector in vectors:
        small = small + jnp.pad(vector.astype(F32), (first, 1024 - first - vector.shape[0]))
        first += vector.shape[0]
    small = small.reshape(8, 128)
    groups = 4
    chunks = [(0, i, 3 * width // groups) for i in range(0, 3 * width, 3 * width // groups)] + [(1, 0, width)]
    chunks += [(2, i, width) for i in range(0, hidden, width)]
    chunks += [(3, i, width // 4) for i in range(0, width, width // 4)]
    kinds = [0, 0, 0, 0, 0, 0, 1, 0, 1, 0, 1, 0, 1]
    made = forward(dims, lens, tokens, cotangent, (w_qkv, w_out, w_fc, w_proj), small, chunks, kinds)
    out = made[14]
    dx, g_qkv, g_out, g_fc, g_proj, small = backward(dims, lens, tokens, made[4:14], made[:4], groups)
    small = small.reshape(1024)
    own = [small[i * per : (i + 1) * per] for i in range(8)]
    g_ln1_gain, g_ln1_bias, g_q_bias, g_v_bias, g_out_bias, g_ln2_gain, g_ln2_bias, g_proj_bias = own
    g_fc_bias = small[8 * per : 8 * per + per_fc]
    return (out, dx.reshape(rows, width), g_ln1_gain, g_ln1_bias, g_qkv, g_q_bias, g_v_bias, g_out, g_out_bias, g_ln2_gain, g_ln2_bias, g_fc, g_fc_bias, g_proj, g_proj_bias)


def solution(mesh):
    dims = grid_dims(mesh.shape["dp"])
    row, vec = P("dp", None), P("dp")
    return jax.shard_map(
        lambda *args: body(dims, *args),
        mesh=mesh,
        in_specs=(row, row, P(), P(), vec, vec, row, vec, vec, row, vec, vec, vec, row, vec, row, vec),
        out_specs=(row, row, vec, vec, row, vec, vec, row, vec, vec, vec, row, vec, row, vec),
        check_vma=False,
    )
```

```python
import jax
import jax.numpy as jnp
from jax import lax
from jax.experimental import pallas as pl
from jax.experimental.pallas import tpu as pltpu
from jax.sharding import PartitionSpec as P

MESH = pl.DeviceIdType.MESH
ANY = pl.BlockSpec(memory_space=pl.ANY)
VMEM = pl.BlockSpec(memory_space=pltpu.VMEM)
DMA = pltpu.SemaphoreType.DMA


def grid_dims(n):
    half = n // 2
    first = 4 if half % 4 == 0 else half
    rest = half // first
    second = 1
    while second * second < rest:
        second *= 2
    return first, second, rest // second


class Place:
    def __init__(self, dims):
        self.dims = dims
        d1, d2, d3 = dims
        me = lax.axis_index("dp")
        self.z = me // (d2 * d3 * 2)
        self.y = (me // (d3 * 2)) % d2
        self.x = (me // 2) % d3
        self.c = me % 2
        self.zs = [(self.z + k) % d1 for k in range(1, d1)]
        self.ys = [(self.y + k) % d2 for k in range(1, d2)]
        self.xs = [(self.x + k) % d3 for k in range(1, d3)]
        self.to_z = [self.dev(z=v) for v in self.zs]
        self.to_y = [self.dev(y=v) for v in self.ys]
        self.to_x = [self.dev(x=v) for v in self.xs]
        self.to_p = self.dev(c=1 - self.c)

    def dev(self, **at):
        z, y, x, c = (at.get(name, getattr(self, name)) for name in "zyxc")
        _, d2, d3 = self.dims
        return (((z * d2 + y) * d3 + x) * 2 + c,)

    def barrier(self):
        semaphore = pltpu.get_barrier_semaphore()
        peers = self.to_z + self.to_y + self.to_x + [self.to_p]
        for peer in peers:
            pl.semaphore_signal(semaphore, inc=1, device_id=peer, device_id_type=MESH)
        pl.semaphore_wait(semaphore, len(peers))


def send(source, target, send_sem, recv_sem, device):
    return pltpu.make_async_remote_copy(
        src_ref=source,
        dst_ref=target,
        send_sem=send_sem,
        recv_sem=recv_sem,
        device_id=device,
        device_id_type=MESH,
    )


class Plan:
    def __init__(self, costs, follow):
        self.costs, self.follow = costs, follow
        self.now, self.free, self.flying, self.taken, self.table = 0.0, {}, [], set(), {}

    def issue(self, key, events):
        lane, cost = self.costs(key)
        begin = max(self.now, self.free.get(lane, 0.0))
        self.free[lane] = begin + cost
        self.flying.append((begin + cost + 1.0, key))
        self.flying.sort()
        events.append(("go", key))

    def pump(self, point, passed=0.0, start=(), force=()):
        self.now += passed
        events = self.table.setdefault(point, [])

        def take():
            when, key = self.flying.pop(0)
            self.now = max(self.now, when)
            self.taken.add(key)
            events.append(("take", key))
            for after in self.follow(key, self.taken):
                self.issue(after, events)

        while self.flying and self.flying[0][0] <= self.now:
            take()
        while any(key not in self.taken for key in force):
            take()
        for key in start:
            self.issue(key, events)


class Gather:
    AHEAD = 3

    def __init__(self, place, shards, wholes, chunks, kinds, sems):
        self.at, self.shards, self.wholes = place, shards, wholes
        self.chunks, self.kinds, self.sems = chunks, kinds, sems
        self.first = [first for first, _ in Gather.starts(place.dims, kinds)]

    @staticmethod
    def starts(dims, kinds):
        d1, d2, d3 = dims
        near, starts = d2 + d3 - 2, []
        for stage in range(4):
            at, first = 0, []
            for kind in kinds:
                first.append(at)
                at += ((d1 - 1, near, near, 1), (near, 2 * (d1 - 1), near, 1))[kind][stage]
            starts.append((first, at))
        return starts

    @staticmethod
    def semaphores(dims, kinds):
        return [DMA((size,)) for _, size in Gather.starts(dims, kinds) for _ in range(2)]

    @staticmethod
    def plan(chunks, kinds, unit):
        def costs(key):
            stage, t = key
            size = unit(t)
            if stage == 3:
                return "p", 1.4 * size
            over_z = stage == kinds[t]
            if over_z:
                return "z", (8 if kinds[t] else 4) * size
            return "xy", (0.5, 2, 4)[stage] * size

        def follow(key, taken):
            stage, t = key
            after = [] if stage == 3 else [(stage + 1, t)]
            if stage == 0:
                more = ((1, 2), (3, 4))[t] if t < 2 else (t + Gather.AHEAD,)
                after += [(0, m) for m in more if m < len(chunks)]
            return after

        return Plan(costs, follow)

    def copies(self, stage, t):
        p = self.at
        z, y, x, c = p.z, p.y, p.x, p.c
        i, first, width = self.chunks[t]
        whole, shard, half = self.wholes[i], self.shards[i], width // 2
        full = pl.ds(first, width)
        a, b = pl.ds(first, half), pl.ds(first + half, half)
        pieces = []
        if stage == 0 and self.kinds[t] == 0:
            pieces = [(shard.at[:, full], whole.at[z, y, x, c, :, full], d) for d in p.to_z]
        elif stage == 0:
            pieces = [(shard.at[:, a], whole.at[z, y, x, c, :, a], d) for d in p.to_x]
            pieces += [(shard.at[:, b], whole.at[z, y, x, c, :, b], d) for d in p.to_y]
        elif stage == 1 and self.kinds[t] == 0:
            part = whole.at[:, y, x, c, :, a]
            pieces = [(part, part, d) for d in p.to_x]
            part = whole.at[:, y, x, c, :, b]
            pieces += [(part, part, d) for d in p.to_y]
        elif stage == 1:
            left, right = whole.at[z, y, :, c, :, a], whole.at[z, :, x, c, :, b]
            pieces = [(part, part, d) for d in p.to_z for part in (left, right)]
        elif stage == 2:
            part = whole.at[:, y, :, c, :, a]
            pieces = [(part, part, d) for d in p.to_y]
            part = whole.at[:, :, x, c, :, b]
            pieces += [(part, part, d) for d in p.to_x]
        else:
            part = whole.at[:, :, :, c, :, full]
            pieces = [(part, part, p.to_p)]
        out, back = self.sems[2 * stage], self.sems[2 * stage + 1]
        first = self.first[stage][t]
        return [send(s, d, out.at[first + k], back.at[first + k], to) for k, (s, d, to) in enumerate(pieces)]

    def run(self, events):
        for what, (stage, t) in events:
            for copy in self.copies(stage, t):
                if what == "go":
                    copy.start()
                else:
                    copy.wait_recv()

    def finish(self):
        for stage in range(4):
            for t in range(len(self.chunks)):
                for copy in self.copies(stage, t):
                    copy.wait_send()


def small_copies(place, source, target, sems, stage):
    z, y, x, c = place.z, place.y, place.x, place.c
    d1, d2, d3 = place.dims
    if stage == 0:
        pieces = [(source, target.at[z, y, x, c], d) for d in place.to_z]
    elif stage == 1:
        part = target.at[:, y, x, c]
        pieces = [(part, part, d) for d in place.to_x]
    elif stage == 2:
        part = target.at[:, y, :, c]
        pieces = [(part, part, d) for d in place.to_y]
    else:
        part = target.at[:, :, :, c]
        pieces = [(part, part, place.to_p)]
    base = (0, d1, d1 + d3, d1 + d2 + d3)[stage]
    return [send(s, d, sems[0].at[base + k], sems[1].at[base + k], to) for k, (s, d, to) in enumerate(pieces)]


class Reduce:
    @staticmethod
    def scratch(dims, rows, width, dtype, halves=True):
        d1, d2, d3 = dims
        half = width // 2 if halves else width
        shapes = [pltpu.VMEM((d1, d2, d3, rows, width), dtype)]
        shapes.append(pltpu.VMEM((d2 - 1, d1, d3, rows, half), dtype))
        shapes.append(pltpu.VMEM((d3 - 1, d1, rows, half), dtype))
        if halves:
            shapes.append(pltpu.VMEM((d3 - 1, d1, d2, rows, half), dtype))
            shapes.append(pltpu.VMEM((d2 - 1, d1, rows, half), dtype))
        shapes.append(pltpu.VMEM((d1 - 1, rows, width), dtype))
        near = d2 + d3 - 2
        sizes = (1, near, near, d1 - 1) if halves else (1, d2 - 1, d3 - 1, d1 - 1)
        for size in sizes:
            shapes += [DMA((size,)), DMA((size,))]
        return shapes

    @staticmethod
    def plan(unit):
        def costs(key):
            stage, t = key
            return ("p", "xy", "xy", "z")[stage], (1.4, 4, 2, 4)[stage] * unit(t)

        def follow(key, taken):
            stage, t = key
            after = []
            if stage == 0 and (t < 2 or (1, t - 2) in taken):
                after.append((1, t))
            if stage == 1:
                if (0, t + 2) in taken:
                    after.append((1, t + 2))
                after.append((2, t))
            if stage == 2:
                after.append((3, t))
            return after

        return Plan(costs, follow)

    def __init__(self, place, refs, source, own, result, halves=True, load=None):
        self.at, self.halves, self.load = place, halves, load
        self.source, self.own, self.result = source, own, result
        if halves:
            self.total, self.ya, self.xa, self.xb, self.yb, self.zz = refs[:6]
            self.sems = refs[6:]
        else:
            self.total, self.ya, self.xa, self.zz = refs[:4]
            self.sems = refs[4:]
        width = self.total.shape[-1]
        half = width // 2 if halves else width
        self.a, self.b = pl.ds(0, half), pl.ds(half, half)

    def pieces(self, stage):
        p, h = self.at, self.total
        y, x = p.y, p.x
        if stage == 0:
            return [(self.source.at[:, :, :, 1 - p.c], h, p.to_p)]
        if stage == 1:
            made = [
                (h.at[:, v, :, :, self.a], self.ya.at[k], d)
                for k, (v, d) in enumerate(zip(p.ys, p.to_y))
            ]
            if self.halves:
                made += [
                    (h.at[:, :, v, :, self.b], self.xb.at[k], d)
                    for k, (v, d) in enumerate(zip(p.xs, p.to_x))
                ]
            return made
        if stage == 2:
            made = [
                (h.at[:, y, v, :, self.a], self.xa.at[k], d)
                for k, (v, d) in enumerate(zip(p.xs, p.to_x))
            ]
            if self.halves:
                made += [
                    (h.at[:, v, x, :, self.b], self.yb.at[k], d)
                    for k, (v, d) in enumerate(zip(p.ys, p.to_y))
                ]
            return made
        return [(h.at[v, y, x], self.zz.at[k], d) for k, (v, d) in enumerate(zip(p.zs, p.to_z))]

    def go(self, stage):
        for copy in self.copies(stage):
            copy.start()

    def copies(self, stage):
        out, back = self.sems[2 * stage], self.sems[2 * stage + 1]
        return [
            send(s, d, out.at[k], back.at[k], to) for k, (s, d, to) in enumerate(self.pieces(stage))
        ]

    def arrived(self, stage):
        for copy in self.copies(stage):
            copy.wait()

    def add(self, stage):
        p, h = self.at, self.total
        d1, d2, d3 = p.dims
        f32 = jnp.float32

        def into(at, terms):
            value = h[at].astype(f32)
            for term in terms:
                value = value + term.astype(f32)
            h[at] = value.astype(h.dtype)

        if stage == 0:

            @pl.loop(0, d1)
            def _(i):
                for j in range(d2):
                    for k in range(d3):
                        into((i, j, k), [self.own[i, j, k]])

        elif stage == 1:

            @pl.loop(0, d1)
            def _(i):
                for k in range(d3):
                    into(
                        (i, p.y, k, slice(None), self.a),
                        [self.ya[m, i, k] for m in range(d2 - 1)],
                    )
                if self.halves:
                    for j in range(d2):
                        into(
                            (i, j, p.x, slice(None), self.b),
                            [self.xb[m, i, j] for m in range(d3 - 1)],
                        )

        elif stage == 2:

            @pl.loop(0, d1)
            def _(i):
                into((i, p.y, p.x, slice(None), self.a), [self.xa[m, i] for m in range(d3 - 1)])
                if self.halves:
                    into(
                        (i, p.y, p.x, slice(None), self.b),
                        [self.yb[m, i] for m in range(d2 - 1)],
                    )

        else:
            value = h[p.z, p.y, p.x].astype(f32)
            for m in range(d1 - 1):
                value = value + self.zz[m].astype(f32)
            for cut, target in self.result:
                target[...] = value[:, cut]

    def take(self, stage):
        if stage == 0 and self.load is not None:
            self.load.wait()
        self.arrived(stage)
        self.add(stage)


HEAD_DIM = 64
MB = 2
EPS = 1e-05
BF = jnp.bfloat16
F32 = jnp.float32
NEG = -1e30
GELU_A = 0.044715
GELU_C = 0.7978845608028654


def mm(left, right):
    return lax.dot_general(left, right, (((1,), (0,)), ((), ())), preferred_element_type=F32)


def mm_nt(left, right):
    return lax.dot_general(left, right, (((1,), (1,)), ((), ())), preferred_element_type=F32)


def mm_tn(left, right):
    return lax.dot_general(left, right, (((0,), (0,)), ((), ())), preferred_element_type=F32)


def iota(shape, axis):
    return lax.broadcasted_iota(jnp.int32, shape, axis)


def unpack_vector(block, start, per, width, first):
    row0, lane0 = start // 128, start % 128
    rows = block.shape[0]
    column = iota((128, width), 1) + first
    pick = (iota((128, width), 0) - lane0 == column % per).astype(BF)
    spread = mm(block, pick)
    column = iota((rows, width), 1) + first
    mine = iota((rows, width), 0) == column // per * 8 + row0
    return jnp.sum(jnp.where(mine, spread, 0.0), axis=0, keepdims=True)


def moments(value, keep, first):
    mean = jnp.mean(value, axis=-1, keepdims=True)
    center = value - mean
    scale = lax.rsqrt(jnp.mean(center * center, axis=-1, keepdims=True) + EPS)
    keep[:, first : first + 1] = mean
    keep[:, first + 1 : first + 2] = scale
    return center, scale


def attend_pair(q2, k2, v2, masks, seq):
    half = seq // 2
    lane = iota((1, 128), 1) // HEAD_DIM
    vt = v2.T
    q2 = q2 * jnp.asarray(HEAD_DIM**-0.5, BF)
    ka, kb = k2[:half], k2[half:]
    sums, rows = [], []
    for head in range(2):
        qh = jnp.where(lane == head, q2, 0)
        va, vb = (vt[head * HEAD_DIM : (head + 1) * HEAD_DIM, i * half : (i + 1) * half] for i in range(2))
        first, second = qh[:half], qh[half:]
        s = mm_nt(ka, first) + masks[0]
        sa, sb = mm_nt(ka, second), mm_nt(kb, second) + masks[1]
        top = jnp.max(s, axis=0, keepdims=True)
        e = jnp.exp(s - top)
        total = jnp.sum(e, axis=0, keepdims=True)
        low = mm(va, e.astype(BF)) * (1.0 / total)
        logs = top + jnp.log(total)
        top = jnp.maximum(jnp.max(sa, axis=0, keepdims=True), jnp.max(sb, axis=0, keepdims=True))
        ea, eb = jnp.exp(sa - top), jnp.exp(sb - top)
        total = jnp.sum(ea, axis=0, keepdims=True) + jnp.sum(eb, axis=0, keepdims=True)
        high = (mm(va, ea.astype(BF)) + mm(vb, eb.astype(BF))) * (1.0 / total)
        rows.append(jnp.concatenate([low, high], axis=1))
        sums.append(jnp.concatenate([logs, top + jnp.log(total)], axis=1))
    return jnp.concatenate(rows, axis=0).T, sums


def forward_plan(chunks, kinds, groups, fcs, projs, steps):
    widest = max(width for i, _, width in chunks if i != 3)
    plan = Gather.plan(chunks, kinds, lambda t: 1.2 * (1.0 if chunks[t][0] == 3 else chunks[t][2] / widest))
    fetched, used = set(), set()

    def pump(point, passed=0.0, done=None, **rest):
        if done is not None:
            used.add(done)
        plan.pump(point, passed, **rest)
        for t in range(len(chunks)):
            first = t < 2 or (chunks[t][0] == 3) != (chunks[t - 2][0] == 3)
            if (3, t) in plan.taken and t not in fetched and (first or t - 2 in used):
                fetched.add(t)
                plan.table[point].append(("fetch", (3, t)))

    pump("begin", 0.0, start=[(0, 0)])
    for k in range(4):
        pump(("small", k), 2.0, force=[(k - 1, 0)] if 0 < k < 3 else ())
    pump("spread", 2.5, force=[(2, 0)])
    pump("norm", 2.0)
    for g in range(groups):
        pump(("qkv", g), 0.0, force=[(3, g)])
        pump(("scores", g), 2.4, done=g)
        for i in range(steps):
            pump(("attend", g, i), 0.0 if i == 0 else 1.6)
        pump(("group", g), 1.6)
    t = groups
    pump("out", 0.0, force=[(3, t)])
    for i in range(2):
        pump(("norm2", i), 2.1)
    used.add(t)
    for k in range(fcs):
        pump(("fc", k), 0.0, force=[(3, t + 1 + k)])
        for i in range(2):
            pump(("gelu", k, i), 2.4, force=[(3, t + 2 + k)])
        used.add(t + 1 + k)
    for k in range(projs):
        pump(("terms", k), 3.1, force=[(3, t + 1 + fcs + k)])
        pump(("proj", k), 0.0, force=[(3, t + 1 + fcs + k)])
        pump(("done", k), 2.8, done=t + 1 + fcs + k)
    pump("end", 0.0, force=[(3, k) for k in range(len(chunks))])
    return plan.table


def forward_kernel(dims, chunks, kinds, comm, *refs):
    (lens, tokens, cot, s_qkv, s_out, s_fc, s_proj, small) = refs[:8]
    (w_qkv, w_out, w_fc, w_proj, vecs_o, h1_o, qkv_o, lse_o, ctx_o, r1_o, h2_o, gp_o, dy_o, terms_o, out_o, stats_o) = refs[8:24]
    (x_, dy, live, vecs, fcb, h1, qkv, ctx, lse, r1, h2, act, gp, out, sm, wbuf, pbuf, tbuf, diag, shuffled, stats) = refs[24:45]
    local, wsem, psem, osem, outsem, gpsem, tsem, shsem, s_sem, r_sem = refs[45:55]
    sems = refs[55:]
    rows, width = x_.shape
    seq = rows // MB
    hidden = act.shape[1]
    n = dims[0] * dims[1] * dims[2] * 2
    per, per_fc = width // n, hidden // n
    tile = 256
    tiles = rows // tile
    fcs = hidden // width
    groups = sum(i == 0 for i, _, _ in chunks)
    gw = width // groups
    pw = chunks[-1][2]
    projs = width // pw
    gpairs = gw // 128
    steps = MB * gpairs
    plan = forward_plan(chunks, kinds, groups, fcs, projs, steps)
    place = Place(dims)
    z, y, x, c = place.z, place.y, place.x, place.c
    shards = (shuffled, s_out, s_fc, s_proj)
    wholes = (w_qkv, w_out, w_fc, w_proj)
    gather = Gather(place, shards, wholes, chunks, kinds, sems)

    def at_point(*key):
        for event in plan[key[0] if len(key) == 1 else key]:
            if event[0] == "fetch":
                fetch(event[1][1]).start()
            elif comm:
                gather.run([event])

    def fetch(t):
        i, first, w = chunks[t]
        source = wholes[i].at[:, :, :, :, :, pl.ds(first, w)]
        if i == 3:
            return pltpu.make_async_copy(source, pbuf.at[t % 2], psem.at[t % 2])
        return pltpu.make_async_copy(source, wbuf.at[t % 2, :, :, :, :, :, pl.ds(0, w)], wsem.at[t % 2])

    saves = []

    def keep(source, target):
        save = pltpu.make_async_copy(source, target, osem.at[len(saves)])
        save.start()
        saves.append(save)

    shuffle = [
        pltpu.make_async_copy(
            s_qkv.at[:, pl.ds(k * width + g * gw, gw)], shuffled.at[:, pl.ds((3 * g + k) * gw, gw)], shsem.at[3 * g + k]
        )
        for g in range(groups)
        for k in range(3)
    ]
    for move in shuffle:
        move.start()
    loads = [pltpu.make_async_copy(tokens, x_, gpsem.at[0]), pltpu.make_async_copy(cot, dy, gpsem.at[1])]
    for move in loads:
        move.start()
    moves = [
        pltpu.make_async_copy(s, w.at[z, y, x, c], local.at[i])
        for i, (s, w) in enumerate(zip((*shards, small), (*wholes, sm)))
    ]
    for move in moves[1:]:
        move.start()
    place.barrier()
    for move in shuffle:
        move.wait()
    moves[0].start()
    tiny = [small_copies(place, small, sm, (s_sem, r_sem), stage) for stage in range(4)]
    half = seq // 2
    for stage in range(4):
        if comm:
            for copy in tiny[stage]:
                copy.start()
        if stage == 0:
            at_point("begin")
            for slot in range(MB):
                length = lens[slot : slot + 1, 0:1]
                live[slot * seq : (slot + 1) * seq, :] = jnp.where(iota((seq, 1), 0).astype(F32) < length, 1.0, 0.0)
                causal = iota((half, half), 0) <= iota((half, half), 1)
                late = (iota((half, half), 0) + half).astype(F32) < length
                diag[0] = jnp.where(causal, 0.0, NEG)
                diag[1 + slot] = jnp.where(causal & late, 0.0, NEG)
            for move in moves:
                move.wait()
        if stage == 1:
            loads[1].wait()
            vecs[8:16, :] = jnp.zeros((8, width), F32)

            @pl.loop(0, tiles)
            def _(i):
                at = pl.ds(pl.multiple_of(i * tile, tile), tile)
                value = jnp.where(live[at, :] > 0.5, dy[at, :].astype(F32), 0.0)
                dy[at, :] = value.astype(BF)
                vecs[8:9, :] += jnp.sum(value, axis=0, keepdims=True)

            keep(dy, dy_o)
        if comm:
            for copy in tiny[stage]:
                copy.wait_recv()
        at_point("small", stage)
    block = sm[...].reshape(n * 8, 128).astype(BF)
    for v in range(8):
        vecs[v : v + 1, :] = unpack_vector(block, v * per, per, width, 0)
    for part in range(fcs):
        fcb[:, part * width : (part + 1) * width] = unpack_vector(block, 8 * per, per_fc, width, part * width)
    at_point("spread")
    loads[0].wait()

    @pl.loop(0, rows // 128)
    def _(i):
        at = pl.ds(pl.multiple_of(i * 128, 128), 128)
        center, scale = moments(x_[at, :].astype(F32), stats.at[at, :], 0)
        h1[at, :] = (center * scale * vecs[0:1, :] + vecs[1:2, :]).astype(BF)

    keep(h1, h1_o)
    keep(vecs, vecs_o)
    at_point("norm")

    @pl.loop(0, groups)
    def _(g):
        for k in range(groups):

            @pl.when(g == k)
            def _():
                at_point("qkv", k)
                fetch(k).wait()

        first = pl.multiple_of(g * gw, gw)

        @pl.loop(0, tiles)
        def _(i):
            at = pl.ds(pl.multiple_of(i * tile, tile), tile)
            value = mm(h1[at, :], wbuf[g % 2, :, :, :, :, :, 0 : 3 * gw].reshape(width, 3 * gw))
            for k, bias in ((0, 2), (1, None), (2, 3)):
                part = value[:, k * gw : (k + 1) * gw]
                if bias is not None:
                    part = part + vecs[bias : bias + 1, pl.ds(first, gw)]
                qkv[at, pl.ds(k * width + first, gw)] = part.astype(BF)

        for k in range(groups):
            if plan["scores", k]:

                @pl.when(g == k)
                def _():
                    at_point("scores", k)

        @pl.loop(0, steps)
        def _(i):
            for k in range(groups):
                for m in range(steps):
                    if plan["attend", k, m]:

                        @pl.when((g == k) & (i == m))
                        def _():
                            at_point("attend", k, m)

            slot, pair = i // gpairs, g * gpairs + i % gpairs
            at = pl.ds(pl.multiple_of(slot * seq, seq), seq)
            col = pl.multiple_of(pair * 128, 128)
            value, sums = attend_pair(
                qkv[at, pl.ds(col, 128)],
                qkv[at, pl.ds(width + col, 128)],
                qkv[at, pl.ds(2 * width + col, 128)],
                [diag[0], diag[1 + slot]],
                seq,
            )
            ctx[at, pl.ds(col, 128)] = value.astype(BF)
            for head in range(2):
                lse[slot * (width // HEAD_DIM) + pair * 2 + head] = sums[head]

        for k in range(groups):
            if plan["group", k]:

                @pl.when(g == k)
                def _():
                    at_point("group", k)

    keep(qkv, qkv_o)
    keep(ctx, ctx_o)
    keep(lse, lse_o)
    t = groups
    at_point("out")
    fetch(t).wait()

    @pl.loop(0, tiles)
    def _(i):
        at = pl.ds(pl.multiple_of(i * tile, tile), tile)
        value = mm(ctx[at, :], wbuf[t % 2].reshape(width, width)) + vecs[4:5, :]
        value = value + x_[at, :].astype(F32)
        r1[at, :] = value
        center, scale = moments(value, stats.at[at, :], 2)
        h2[at, :] = (center * scale * vecs[5:6, :] + vecs[6:7, :]).astype(BF)
        for k in range(2):

            @pl.when(i == (k + 1) * tiles // 2 - 1)
            def _():
                at_point("norm2", k)

    keep(r1, r1_o)
    keep(h2, h2_o)
    keep(stats, stats_o)

    def keep_gp(k):
        return pltpu.make_async_copy(gp.at[k % 2], gp_o.at[:, pl.ds(pl.multiple_of(k * width, width), width)], gpsem.at[k % 2])

    def each(index, count, *name):
        for k in range(count):
            key = (*name, k)
            if plan[key]:

                @pl.when(index == k)
                def _():
                    at_point(*key)

    @pl.loop(0, fcs)
    def _(k):
        each(k, fcs, "fc")
        buffer = (groups + 1 + k) % 2
        for m in range(fcs):

            @pl.when(k == m)
            def _():
                fetch(groups + 1 + m).wait()

        @pl.when(k >= 2)
        def _():
            keep_gp(k - 2).wait()

        cut = pl.ds(pl.multiple_of(k * width, width), width)

        @pl.loop(0, 2)
        def _(i):
            for part in range(tiles // 2):
                at = pl.ds(pl.multiple_of((i * (tiles // 2) + part) * tile, tile), tile)
                u = mm(h2[at, :], wbuf[buffer].reshape(width, width)) + fcb[:, cut]
                square = u * u
                inner = u * (GELU_C + (GELU_C * GELU_A) * square)
                gate = 0.5 + 0.5 * jnp.tanh(inner)
                value = u * gate
                act[at, cut] = value.astype(BF)
                slope = gate + value * (2.0 - 2.0 * gate) * (GELU_C + (3.0 * GELU_C * GELU_A) * square)
                gp[k % 2, at, :] = slope.astype(BF)
            for n_k in range(fcs):
                for m in range(2):
                    if plan["gelu", n_k, m]:

                        @pl.when((k == n_k) & (i == m))
                        def _():
                            at_point("gelu", n_k, m)

        keep_gp(k).start()

    def keep_terms(k):
        return pltpu.make_async_copy(
            tbuf.at[k % 2], terms_o.at[:, :, :, :, :, pl.ds(pl.multiple_of(k * pw, pw), pw)], tsem.at[k % 2]
        )

    def keep_out(k):
        cut = pl.ds(pl.multiple_of(k * pw, pw), pw)
        return pltpu.make_async_copy(out.at[:, cut], out_o.at[:, cut], outsem.at[k])

    @pl.loop(0, projs)
    def _(k):
        cut = pl.ds(pl.multiple_of(k * pw, pw), pw)
        buffer = (groups + 1 + fcs + k) % 2

        @pl.when(k >= 2)
        def _():
            keep_terms(k - 2).wait()

        @pl.loop(0, dims[0])
        def _(i):
            span = hidden // dims[0]
            value = mm_tn(act[:, pl.ds(pl.multiple_of(i * span, span), span)], dy[:, cut])
            tbuf[k % 2, i] = value.astype(BF).reshape(dims[1], dims[2], 2, per_fc, pw)

        keep_terms(k).start()
        each(k, projs, "terms")
        for m in range(projs):

            @pl.when(k == m)
            def _():
                at_point("proj", m)
                fetch(groups + 1 + fcs + m).wait()

        @pl.loop(0, tiles)
        def _(i):
            at = pl.ds(pl.multiple_of(i * tile, tile), tile)
            value = mm(act[at, :], pbuf[buffer].reshape(hidden, pw)) + (r1[at, cut] + vecs[7:8, cut])
            out[at, cut] = jnp.where(live[at, :] > 0.5, value, 0.0).astype(BF)

        keep_out(k).start()
        each(k, projs, "done")

    at_point("end")
    for k in range(max(fcs - 2, 0), fcs):
        keep_gp(k).wait()
    for k in range(max(projs - 2, 0), projs):
        keep_terms(k).wait()
    for k in range(projs):
        keep_out(k).wait()
    for save in saves:
        save.wait()
    if comm:
        gather.finish()
        for copies in tiny:
            for copy in copies:
                copy.wait_send()


def forward(dims, lens, tokens, cot, shards, small, chunks, kinds, comm=True):
    rows, width = tokens.shape
    n = dims[0] * dims[1] * dims[2] * 2
    hidden = shards[2].shape[1]
    heads = width // HEAD_DIM
    seq = rows // MB
    pw = chunks[-1][2]
    groups = sum(i == 0 for i, _, _ in chunks)
    sds = jax.ShapeDtypeStruct
    shapes = [sds((*dims, 2, *s.shape), s.dtype) for s in shards]
    shapes += [
        sds((16, width), F32),
        sds((rows, width), BF),
        sds((rows, 3 * width), BF),
        sds((MB * heads, 1, seq), F32),
        sds((rows, width), BF),
        sds((rows, width), F32),
        sds((rows, width), BF),
        sds((rows, hidden), BF),
        sds((rows, width), BF),
        sds((*dims, 2, hidden // n, width), BF),
        sds((rows, width), BF),
        sds((rows, 128), F32),
    ]
    scratch = [
        pltpu.VMEM((rows, width), BF),
        pltpu.VMEM((rows, width), BF),
        pltpu.VMEM((rows, 1), F32),
        pltpu.VMEM((16, width), F32),
        pltpu.VMEM((1, hidden), F32),
        pltpu.VMEM((rows, width), BF),
        pltpu.VMEM((rows, 3 * width), BF),
        pltpu.VMEM((rows, width), BF),
        pltpu.VMEM((MB * heads, 1, seq), F32),
        pltpu.VMEM((rows, width), F32),
        pltpu.VMEM((rows, width), BF),
        pltpu.VMEM((rows, hidden), BF),
        pltpu.VMEM((2, rows, width), BF),
        pltpu.VMEM((rows, width), BF),
        pltpu.VMEM((*dims, 2, *small.shape), small.dtype),
        pltpu.VMEM((2, *dims, 2, width // n, width), BF),
        pltpu.VMEM((2, *dims, 2, hidden // n, pw), BF),
        pltpu.VMEM((2, *dims, 2, hidden // n, pw), BF),
        pltpu.VMEM((1 + MB, seq // 2, seq // 2), F32),
        pltpu.VMEM(shards[0].shape, BF),
        pltpu.VMEM((rows, 128), F32),
        DMA((5,)),
        DMA((2,)),
        DMA((2,)),
        DMA((9,)),
        DMA((width // pw,)),
        DMA((2,)),
        DMA((2,)),
        DMA((3 * groups,)),
        DMA((sum(dims) + 1,)),
        DMA((sum(dims) + 1,)),
        *Gather.semaphores(dims, kinds),
    ]
    return pl.pallas_call(
        lambda *refs: forward_kernel(dims, chunks, kinds, comm, *refs),
        out_shape=shapes,
        in_specs=[VMEM, ANY, ANY, ANY] + [VMEM] * 4,
        out_specs=[ANY] * 16,
        scratch_shapes=scratch,
        compiler_params=pltpu.CompilerParams(
            collective_id=0, has_side_effects=True, vmem_limit_bytes=60 * 1024 * 1024
        ),
        name="forward",
    )(lens, tokens, cot, *shards, small)


def pack_vector(row, start, per, n):
    width = row.shape[1]
    pick = (iota((128, width), 0) - start % 128 == iota((128, width), 1) % per).astype(BF)
    mine = iota((n, width), 0) == iota((n, width), 1) // per
    total = 0.0
    for _ in range(3):
        part = row.astype(BF)
        row = row - part.astype(F32)
        total = total + mm_nt(jnp.where(mine, part.astype(F32), 0.0).astype(BF), pick)
    return total


def norm_back(value, kept, gain, grad):
    scale = kept[:, 1:2]
    normed = (value - kept[:, 0:1]) * scale
    scaled = grad * gain
    mean = jnp.mean(scaled, axis=-1, keepdims=True)
    cross = jnp.mean(scaled * normed, axis=-1, keepdims=True)
    return (scaled - mean - normed * cross) * scale, grad * normed


def attend_back(q2, k2, v2, o2, c2, lse, masks, seq):
    half = seq // 2
    lane = iota((1, 128), 1) // HEAD_DIM
    prod = o2.astype(F32) * c2.astype(F32)
    heads = (iota((8, 128), 1) // HEAD_DIM == iota((8, 128), 0)).astype(BF)
    high = prod.astype(BF)
    delta = mm_nt(heads, high) + mm_nt(heads, (prod - high.astype(F32)).astype(BF))
    kt = k2.T
    q2 = q2 * jnp.asarray(HEAD_DIM**-0.5, BF)
    cuts = (slice(0, half), slice(half, seq))
    dk, dv, dq = [0.0, 0.0], [0.0, 0.0], []
    for head in range(2):
        qh = jnp.where(lane == head, q2, 0)
        oh = jnp.where(lane == head, o2, 0)
        kh = kt[head * HEAD_DIM : (head + 1) * HEAD_DIM]
        parts = [0.0, 0.0]
        for key, query in ((0, 0), (0, 1), (1, 1)):
            qb, ob, cut = qh[cuts[query]], oh[cuts[query]], cuts[query]
            s = mm_nt(k2[cuts[key]], qb) - lse[head][:, cut]
            if key == query:
                s = s + masks[key]
            p = jnp.exp(s)
            dp = mm_nt(v2[cuts[key]], ob)
            ds = (p * (dp - delta[head : head + 1, cut])).astype(BF)
            dv[key] = dv[key] + mm(p.astype(BF), ob)
            dk[key] = dk[key] + mm(ds, qb)
            parts[query] = parts[query] + mm(kh[:, cuts[key]], ds)
        dq.append(jnp.concatenate(parts, axis=1))
    dq = jnp.concatenate(dq, axis=0).T * HEAD_DIM**-0.5
    return dq, jnp.concatenate(dk, axis=0), jnp.concatenate(dv, axis=0)


def backward_plan(projs, fcs, groups, steps, slabs):
    out = projs + fcs
    plan = Reduce.plan(lambda t: 1.3 if t <= out else 1.0)
    pump = plan.pump
    pump("start", 0.0, start=[(0, 0), (0, 1)])
    pump("loaded", 4.0)
    late = list(range(2, projs))
    for f in range(fcs):
        for name, passed in (("da", 3.2), ("dh", 2.9)):
            j = late.pop(0) if late else None
            force = [] if j is None else [(0, j - 2)]
            if name == "dh" and f >= 2:
                force.append((0, projs + f - 2))
            pump((name, f), passed, force=force, start=[] if j is None else [(0, j)])
        pump(("gfc", f), 2.9, start=[(0, projs + f)])
    for i in range(slabs):
        pump(("ln2", i), 2.2)
    pump("dctx", 3.0, force=[(0, out - 2)])
    pump("gout", 3.0, start=[(0, out)])
    for g in range(groups):
        for i in range(steps):
            pump(("back", g, i), 0.0 if i == 0 else 2.0)
        pump(("grads", g), 2.0, force=[(0, out - 1 + g)])
        pump(("gqkv", g), 2.2, start=[(0, out + 1 + g)])
    for i in range(slabs):
        pump(("dx", i), 3.4)
    pump("end", 4.0, force=[(3, t) for t in range(out + 1 + groups)])
    return plan.table


def backward_kernel(dims, groups, sizes, comm, *refs):
    (lens, tokens, dy, vecs, stats, h1_i, qkv_i, lse_i, ctx_i, r1_i, h2_i, gp_i, terms, w_qkv, w_out, w_fc, w_proj) = refs[:17]
    (dx_o, g_qkv, g_out, g_fc, g_proj, g_small) = refs[17:23]
    slots, wp, f_dh, f_r1, gvec, gfc, lse, diag, stage, owns, sstage = refs[23:34]
    lsem, wsem, osem, qsem = refs[34:38]
    refs = refs[38:]
    d1, d2, d3 = dims
    n = d1 * d2 * d3 * 2
    rows, width = f_dh.shape
    hidden = gfc.shape[1]
    seq = rows // MB
    half = seq // 2
    per, per_fc = width // n, hidden // n
    fcs = hidden // width
    gw = width // groups
    pw = owns.shape[-1]
    projs = width // pw
    tile = rows // d1
    gpairs = gw // 128
    steps = MB * gpairs
    place = Place(dims)
    c = place.c
    plan = backward_plan(projs, fcs, groups, steps, d1)
    sets = []
    for size in sizes:
        sets.append(refs[:size])
        refs = refs[size:]
    parts = []
    for j in range(projs):
        cut = pl.ds(j * pw, pw)
        own = owns.at[j % 2]
        move = pltpu.make_async_copy(terms.at[:, :, :, c, :, cut], own, osem.at[j % 2])
        result = [(slice(None), g_proj.at[:, cut])]
        parts.append(Reduce(place, sets[j], terms.at[:, :, :, :, :, cut], own, result, load=move))
    for f in range(fcs):
        result = [(slice(None), g_fc.at[:, pl.ds(f * width, width)])]
        parts.append(Reduce(place, sets[projs + f], stage.at[f % 2], stage.at[f % 2, :, :, :, c], result))
    b = fcs % 2
    parts.append(Reduce(place, sets[projs + fcs], stage.at[b], stage.at[b, :, :, :, c], [(slice(None), g_out)]))
    gcut = pl.ds(0, 3 * gw)
    for g in range(groups):
        b = (fcs + 1 + g) % 2
        result = [
            (slice(k * gw, (k + 1) * gw), g_qkv.at[:, pl.ds(k * width + g * gw, gw)]) for k in range(3)
        ]
        source, own = stage.at[b, :, :, :, :, :, gcut], stage.at[b, :, :, :, c, :, gcut]
        parts.append(Reduce(place, sets[projs + fcs + 1 + g], source, own, result))

    def at_point(*key):
        if not comm:
            return
        for what, (step, t) in plan[key[0] if len(key) == 1 else key]:
            if what == "take":
                parts[t].take(step)
            else:
                parts[t].go(step)
                if step == 0 and parts[t].load is not None:
                    parts[t].load.start()

    def load(source, slot, k):
        return pltpu.make_async_copy(source, slots.at[slot], lsem.at[k])

    def cols(source, k):
        return source.at[:, :, :, :, :, pl.ds(pl.multiple_of(k * width, width), width)]

    def whole(slot):
        return slots[slot].reshape(rows, width)

    def piece(slot, i):
        return slots[slot, i].reshape(tile, width)

    def put(slot, i, value):
        slots[slot, i] = value.astype(BF).reshape(d2, d3, 2, per, width)

    def fetch_proj(f):
        return pltpu.make_async_copy(w_proj.at[f], wp.at[f % 2], wsem.at[f % 2])

    def fetch_ff(f):
        return [fetch_proj(f), load(cols(gp_i, f), 3 + f % 2, 3 + f % 2), load(cols(w_fc, f), 1 + f % 2, 1 + f % 2)]

    def w_third(k, slot):
        return [
            pltpu.make_async_copy(
                w_qkv.at[:, :, :, :, :, pl.ds((3 * g + k) * gw, gw)],
                slots.at[slot, :, :, :, :, :, pl.ds(g * gw, gw)],
                qsem.at[k, g],
            )
            for g in range(groups)
        ]

    load(dy, 0, 0).start()
    for move in fetch_ff(0):
        move.start()
    load(h2_i, 6, 6).start()
    load(ctx_i, 7, 7).start()
    lload = pltpu.make_async_copy(lse_i, lse, lsem.at[5])
    lload.start()
    place.barrier()
    at_point("start")
    for slot in range(MB):
        causal = iota((half, half), 0) <= iota((half, half), 1)
        late = (iota((half, half), 0) + half).astype(F32) < lens[slot : slot + 1, 0:1]
        diag[0] = jnp.where(causal, 0.0, NEG)
        diag[1 + slot] = jnp.where(causal & late, 0.0, NEG)
    gvec[...] = jnp.zeros_like(gvec)
    gfc[...] = jnp.zeros_like(gfc)
    f_dh[...] = jnp.zeros_like(f_dh)
    gvec[7:8, :] = vecs[8:9, :]
    load(dy, 0, 0).wait()
    at_point("loaded")
    load(h2_i, 6, 6).wait()

    def each(index, count, *name):
        for k in range(count):
            key = (*name, k)
            if plan[key]:

                @pl.when(index == k)
                def _():
                    at_point(*key)

    @pl.loop(0, fcs)
    def _(f):
        for move in fetch_ff(f):
            move.wait()

        @pl.when(f + 1 < fcs)
        def _():
            for move in fetch_ff(f + 1):
                move.start()

        cut = pl.ds(pl.multiple_of(f * width, width), width)

        @pl.loop(0, d1)
        def _(i):
            da = mm_nt(piece(0, i), wp[f % 2].reshape(rows, width))
            du = (da * piece(3 + f % 2, i).astype(F32)).astype(BF)
            put(5, i, du)
            gfc[:, cut] += jnp.sum(du.astype(F32), axis=0, keepdims=True)

        each(f, fcs, "da")

        @pl.loop(0, d1)
        def _(i):
            at = pl.ds(pl.multiple_of(i * tile, tile), tile)
            f_dh[at, :] += mm_nt(piece(5, i), whole(1 + f % 2))

        each(f, fcs, "dh")

        @pl.loop(0, 2)
        def _(i):
            col = pl.ds(pl.multiple_of(i * (width // 2), width // 2), width // 2)
            value = mm_tn(slots[6, :, :, :, :, :, col].reshape(rows, width // 2), whole(5)).astype(BF)
            stage[f % 2, pl.ds(i * (d1 // 2), d1 // 2)] = value.reshape(d1 // 2, d2, d3, 2, per, width)

        each(f, fcs, "gfc")

    def r1_tile(i):
        return pltpu.make_async_copy(r1_i.at[pl.ds(i * tile, tile)], f_r1.at[i % 2], wsem.at[i % 2])

    r1_tile(0).start()
    load(w_out, 1, 1).start()
    for k, slot in enumerate((3, 4, 6)):
        load(cols(qkv_i, k), slot, slot).start()

    @pl.loop(0, d1)
    def _(i):
        r1_tile(i).wait()

        @pl.when(i + 1 < d1)
        def _():
            r1_tile(i + 1).start()

        at = pl.ds(pl.multiple_of(i * tile, tile), tile)
        grad = f_dh[at, :]
        value, norms = norm_back(f_r1[i % 2], stats[at, 2:4], vecs[5:6, :], grad)
        value = value + piece(0, i).astype(F32)
        f_dh[at, :] = value
        low = value.astype(BF)
        put(5, i, low)
        gvec[5:6, :] += jnp.sum(norms, axis=0, keepdims=True)
        gvec[6:7, :] += jnp.sum(grad, axis=0, keepdims=True)
        gvec[4:5, :] += jnp.sum(low.astype(F32), axis=0, keepdims=True)
        for k in range(d1):
            if plan["ln2", k]:

                @pl.when(i == k)
                def _():
                    at_point("ln2", k)

    load(ctx_i, 7, 7).wait()
    load(w_out, 1, 1).wait()
    load(h1_i, 0, 0).start()

    @pl.loop(0, d1)
    def _(i):
        put(2, i, mm_nt(piece(5, i), whole(1)))

    for move in w_third(0, 1):
        move.start()
    at_point("dctx")

    @pl.loop(0, 2)
    def _(i):
        col = pl.ds(pl.multiple_of(i * (width // 2), width // 2), width // 2)
        value = mm_tn(slots[7, :, :, :, :, :, col].reshape(rows, width // 2), whole(5)).astype(BF)
        stage[fcs % 2, pl.ds(i * (d1 // 2), d1 // 2)] = value.reshape(d1 // 2, d2, d3, 2, per, width)

    for move in w_third(1, 5):
        move.start()
    at_point("gout")
    for k, slot in enumerate((3, 4, 6)):
        load(cols(qkv_i, k), slot, slot).wait()
    lload.wait()
    load(h1_i, 0, 0).wait()
    hslab = d1 // MB

    @pl.loop(0, groups)
    def _(g):
        @pl.loop(0, steps)
        def _(i):
            for k in range(groups):
                for m in range(steps):
                    if plan["back", k, m]:

                        @pl.when((g == k) & (i == m))
                        def _():
                            at_point("back", k, m)

            slot, pair = i // gpairs, g * gpairs + i % gpairs
            slab = pl.ds(slot * hslab, hslab)
            lanes = pl.ds(pl.multiple_of(pair * 128, 128), 128)

            def get(s):
                return slots[s, slab, :, :, :, :, lanes].reshape(seq, 128)

            head = slot * (width // HEAD_DIM) + 2 * pair
            grads = attend_back(
                get(3), get(4), get(6), get(2), get(7), [lse[head], lse[head + 1]], [diag[0], diag[1 + slot]], seq
            )
            for s, value in zip((3, 4, 6), grads):
                slots[s, slab, :, :, :, :, lanes] = value.astype(BF).reshape(hslab, d2, d3, 2, per, 128)

        for k in range(groups):
            if plan["grads", k]:

                @pl.when(g == k)
                def _():
                    at_point("grads", k)

        mine = pl.ds(pl.multiple_of(g * gw, gw), gw)
        buffer = (fcs + 1 + g) % 2

        @pl.loop(0, 2)
        def _(i):
            col = pl.ds(pl.multiple_of(i * (width // 2), width // 2), width // 2)
            left = slots[0, :, :, :, :, :, col].reshape(rows, width // 2)
            for k, s in enumerate((3, 4, 6)):
                value = mm_tn(left, slots[s, :, :, :, :, :, mine].reshape(rows, gw)).astype(BF)
                stage[buffer, pl.ds(i * (d1 // 2), d1 // 2), :, :, :, :, k * gw : (k + 1) * gw] = value.reshape(
                    d1 // 2, d2, d3, 2, per, gw
                )

        for k in range(groups):

            @pl.when(g == k)
            def _():
                at_point("gqkv", k)

    for move in w_third(2, 7):
        move.start()
    load(tokens, 2, 2).start()
    for k, slot in enumerate((1, 5, 7)):
        for move in w_third(k, slot):
            move.wait()
    load(tokens, 2, 2).wait()

    @pl.loop(0, d1)
    def _(i):
        at = pl.ds(pl.multiple_of(i * tile, tile), tile)
        grad = mm_nt(piece(3, i), whole(1)) + mm_nt(piece(4, i), whole(5)) + mm_nt(piece(6, i), whole(7))
        value, norms = norm_back(piece(2, i).astype(F32), stats[at, 0:2], vecs[0:1, :], grad)
        put(2, i, value + f_dh[at, :])
        gvec[0:1, :] += jnp.sum(norms, axis=0, keepdims=True)
        gvec[1:2, :] += jnp.sum(grad, axis=0, keepdims=True)
        gvec[2:3, :] += jnp.sum(piece(3, i).astype(F32), axis=0, keepdims=True)
        gvec[3:4, :] += jnp.sum(piece(6, i).astype(F32), axis=0, keepdims=True)
        for k in range(d1):
            if plan["dx", k]:

                @pl.when(i == k)
                def _():
                    at_point("dx", k)

    save = pltpu.make_async_copy(slots.at[2], dx_o, lsem.at[0])
    save.start()
    lines = [0.0] * (sstage.shape[-1] // 128)
    for v in range(8):
        lines[v * per // 128] += pack_vector(gvec[v : v + 1, :], v * per, per, n)
    some = n // fcs
    packed = [pack_vector(gfc[:, k * width : (k + 1) * width], 8 * per, per_fc, some) for k in range(fcs)]
    lines[8 * per // 128] += jnp.concatenate(packed, axis=0)
    for k, line in enumerate(lines):
        for d in range(n):
            at = (d // (d2 * d3 * 2), d // (d3 * 2) % d2, d // 2 % d3, d % 2)
            sstage[(*at, slice(None), slice(k * 128, (k + 1) * 128))] = line[d : d + 1, :]
    result = [(slice(None), g_small)]
    small = Reduce(place, refs, sstage, sstage.at[:, :, :, c], result, halves=False)
    if comm:
        for step in range(2):
            small.go(step)
            small.take(step)
        small.go(2)
    at_point("end")
    if comm:
        small.take(2)
        small.go(3)
        small.take(3)
    save.wait()


def backward(dims, lens, tokens, saved, weights, groups, comm=True):
    vecs, h1, qkv, lse, ctx, r1, h2, gp, dy, terms, stats = saved
    rows, width = tokens.shape
    n = dims[0] * dims[1] * dims[2] * 2
    hidden = gp.shape[1]
    seq = rows // MB
    per, per_fc = width // n, hidden // n
    fcs = hidden // width
    projs = 4
    pw = width // projs
    lanes = (8 * per + per_fc + 127) // 128 * 128

    def six(a):
        return a.reshape(*dims, 2, a.shape[0] // n, a.shape[1])

    sds = jax.ShapeDtypeStruct
    scratch = [
        pltpu.VMEM((8, *dims, 2, per, width), BF),
        pltpu.VMEM((2, *dims[1:], 2, per_fc, width), BF),
        pltpu.VMEM((rows, width), F32),
        pltpu.VMEM((2, rows // dims[0], width), F32),
        pltpu.VMEM((8, width), F32),
        pltpu.VMEM((1, hidden), F32),
        pltpu.VMEM(lse.shape, F32),
        pltpu.VMEM((1 + MB, seq // 2, seq // 2), F32),
        pltpu.VMEM((2, *dims, 2, per, width), BF),
        pltpu.VMEM((2, *dims, per_fc, pw), BF),
        pltpu.VMEM((*dims, 2, 1, lanes), F32),
        DMA((8,)),
        DMA((2,)),
        DMA((2,)),
        DMA((3, groups)),
    ]
    sizes = []
    shapes = [(per_fc, pw)] * projs + [(per, width)] * (fcs + 1) + [(per, 3 * width // groups)] * groups
    for block_rows, block_cols in shapes:
        made = Reduce.scratch(dims, block_rows, block_cols, BF)
        sizes.append(len(made))
        scratch += made
    scratch += Reduce.scratch(dims, 1, lanes, F32, halves=False)
    outs = [
        sds((*dims, 2, per, width), BF),
        sds((per, 3 * width), F32),
        sds((per, width), F32),
        sds((per, hidden), F32),
        sds((per_fc, width), F32),
        sds((1, lanes), F32),
    ]
    return pl.pallas_call(
        lambda *refs: backward_kernel(dims, groups, sizes, comm, *refs),
        out_shape=outs,
        in_specs=[VMEM, ANY, ANY, VMEM, VMEM] + [ANY] * 12,
        out_specs=[ANY] + [VMEM] * 5,
        scratch_shapes=scratch,
        compiler_params=pltpu.CompilerParams(
            collective_id=1, has_side_effects=True, vmem_limit_bytes=67043328
        ),
        name="backward",
    )(lens, six(tokens), six(dy), vecs, stats, six(h1), six(qkv), lse, six(ctx), r1, six(h2), six(gp), terms, *weights)


def finish_kernel(sizes, *refs):
    arrays, small = refs[:6], refs[6]
    results, vectors = refs[7:13], refs[13 : 13 + len(sizes)]
    rest = refs[13 + len(sizes) :]
    buffers, (sems_in, sems_out) = rest[:6], rest[6:]
    pieces = []
    for k, (array, result, buffer) in enumerate(zip(arrays, results, buffers)):
        parts = 4 if array.shape[0] >= 512 else 1
        rows = array.shape[0] // parts
        for part in range(parts):
            cut = pl.ds(part * rows, rows)
            at = len(pieces)
            pieces.append(
                (
                    pltpu.make_async_copy(array.at[cut], buffer.at[cut], sems_in.at[at]),
                    pltpu.make_async_copy(buffer.at[cut], result.at[cut], sems_out.at[at]),
                )
            )
    for load, _ in pieces:
        load.start()
    first = 0
    for size, vector in zip(sizes, vectors):
        vector[...] = small[:, first : first + size]
        first += size
    for load, store in pieces:
        load.wait()
        store.start()
    for _, store in pieces:
        store.wait()


def finish(arrays, small, sizes):
    sds = jax.ShapeDtypeStruct
    count = sum(4 if a.shape[0] >= 512 else 1 for a in arrays)
    made = pl.pallas_call(
        lambda *refs: finish_kernel(sizes, *refs),
        out_shape=[sds(a.shape, a.dtype) for a in arrays] + [sds((1, size), F32) for size in sizes],
        in_specs=[ANY] * 6 + [VMEM],
        out_specs=[ANY] * 6 + [VMEM] * len(sizes),
        scratch_shapes=[pltpu.VMEM(a.shape, a.dtype) for a in arrays] + [DMA((count,)), DMA((count,))],
        name="finish",
    )(*arrays, small)
    return made[:6], [vector.reshape(-1) for vector in made[6:]]


def body(dims, tokens, cotangent, seq_lengths, seq_place, ln1_gain, ln1_bias, w_qkv, q_bias, v_bias, w_out, out_bias, ln2_gain, ln2_bias, w_fc, fc_bias, w_proj, proj_bias):
    rows, width = tokens.shape
    n = dims[0] * dims[1] * dims[2] * 2
    hidden = fc_bias.shape[0] * n
    seq = rows // MB
    per, per_fc = width // n, hidden // n
    slots = lax.axis_index("dp") * MB + jnp.arange(MB, dtype=jnp.int32)
    lengths = jnp.sum(jnp.where(seq_place[None, :] == slots[:, None], seq_lengths[None, :], 0), axis=1)
    lens = jnp.broadcast_to(jnp.pad(lengths, (0, 8 - MB))[:, None], (8, 128)).astype(F32)

    vectors = (ln1_gain, ln1_bias, q_bias, v_bias, out_bias, ln2_gain, ln2_bias, proj_bias, fc_bias)
    small, first = 0.0, 0
    for vector in vectors:
        small = small + jnp.pad(vector.astype(F32), (first, 1024 - first - vector.shape[0]))
        first += vector.shape[0]
    small = small.reshape(8, 128)
    groups = 4
    chunks = [(0, i, 3 * width // groups) for i in range(0, 3 * width, 3 * width // groups)] + [(1, 0, width)]
    chunks += [(2, i, width) for i in range(0, hidden, width)]
    chunks += [(3, i, width // 4) for i in range(0, width, width // 4)]
    kinds = [0, 0, 0, 0, 0, 0, 1, 0, 1, 0, 1, 0, 1]
    made = forward(dims, lens, tokens, cotangent, (w_qkv, w_out, w_fc, w_proj), small, chunks, kinds)
    out = made[14]
    dx, g_qkv, g_out, g_fc, g_proj, small = backward(dims, lens, tokens, (*made[4:14], made[15]), made[:4], groups)
    sizes = [per] * 8 + [per_fc]
    arrays, own = finish((out, dx.reshape(rows, width), g_qkv, g_out, g_fc, g_proj), small, sizes)
    out, dx, g_qkv, g_out, g_fc, g_proj = arrays
    g_ln1_gain, g_ln1_bias, g_q_bias, g_v_bias, g_out_bias, g_ln2_gain, g_ln2_bias, g_proj_bias, g_fc_bias = own
    return (out, dx, g_ln1_gain, g_ln1_bias, g_qkv, g_q_bias, g_v_bias, g_out, g_out_bias, g_ln2_gain, g_ln2_bias, g_fc, g_fc_bias, g_proj, g_proj_bias)


def solution(mesh):
    dims = grid_dims(mesh.shape["dp"])
    row, vec = P("dp", None), P("dp")
    return jax.shard_map(
        lambda *args: body(dims, *args),
        mesh=mesh,
        in_specs=(row, row, P(), P(), vec, vec, row, vec, vec, row, vec, vec, vec, row, vec, row, vec),
        out_specs=(row, row, vec, vec, row, vec, vec, row, vec, vec, vec, row, vec, row, vec),
        check_vma=False,
    )
```

```python
import jax
import jax.numpy as jnp
from jax import lax
from jax.experimental import pallas as pl
from jax.experimental.pallas import tpu as pltpu
from jax.sharding import PartitionSpec as P

MESH = pl.DeviceIdType.MESH
ANY = pl.BlockSpec(memory_space=pl.ANY)
VMEM = pl.BlockSpec(memory_space=pltpu.VMEM)
DMA = pltpu.SemaphoreType.DMA


def grid_dims(n):
    half = n // 2
    first = 4 if half % 4 == 0 else half
    rest = half // first
    second = 1
    while second * second < rest:
        second *= 2
    return first, second, rest // second


class Place:
    def __init__(self, dims):
        self.dims = dims
        d1, d2, d3 = dims
        me = lax.axis_index("dp")
        self.z = me // (d2 * d3 * 2)
        self.y = (me // (d3 * 2)) % d2
        self.x = (me // 2) % d3
        self.c = me % 2
        self.zs = [(self.z + k) % d1 for k in range(1, d1)]
        self.ys = [(self.y + k) % d2 for k in range(1, d2)]
        self.xs = [(self.x + k) % d3 for k in range(1, d3)]
        self.to_z = [self.dev(z=v) for v in self.zs]
        self.to_y = [self.dev(y=v) for v in self.ys]
        self.to_x = [self.dev(x=v) for v in self.xs]
        self.to_p = self.dev(c=1 - self.c)

    def dev(self, **at):
        z, y, x, c = (at.get(name, getattr(self, name)) for name in "zyxc")
        _, d2, d3 = self.dims
        return (((z * d2 + y) * d3 + x) * 2 + c,)

    def others(self):
        d1, d2, d3 = self.dims
        found = []
        for i in range(1, d1 * d2 * d3):
            z, y, x = (self.z + i // (d2 * d3)) % d1, (self.y + i // d3 % d2) % d2, (self.x + i % d3) % d3
            found.append((z, y, x, self.dev(z=z, y=y, x=x)))
        return found

    def barrier(self, everyone=False):
        semaphore = pltpu.get_barrier_semaphore()
        peers = self.to_z + self.to_y + self.to_x
        if everyone:
            peers = [device for _, _, _, device in self.others()]
        peers = peers + [self.to_p]
        for peer in peers:
            pl.semaphore_signal(semaphore, inc=1, device_id=peer, device_id_type=MESH)
        pl.semaphore_wait(semaphore, len(peers))


def send(source, target, send_sem, recv_sem, device):
    return pltpu.make_async_remote_copy(
        src_ref=source,
        dst_ref=target,
        send_sem=send_sem,
        recv_sem=recv_sem,
        device_id=device,
        device_id_type=MESH,
    )


class Plan:
    def __init__(self, costs, follow):
        self.costs, self.follow = costs, follow
        self.now, self.free, self.flying, self.taken, self.table = 0.0, {}, [], set(), {}

    def issue(self, key, events):
        lane, cost = self.costs(key)
        begin = max(self.now, self.free.get(lane, 0.0))
        self.free[lane] = begin + cost
        self.flying.append((begin + cost + 1.0, key))
        self.flying.sort()
        events.append(("go", key))

    def pump(self, point, passed=0.0, start=(), force=()):
        self.now += passed
        events = self.table.setdefault(point, [])

        def take():
            when, key = self.flying.pop(0)
            self.now = max(self.now, when)
            self.taken.add(key)
            events.append(("take", key))
            for after in self.follow(key, self.taken):
                self.issue(after, events)

        while self.flying and self.flying[0][0] <= self.now:
            take()
        while any(key not in self.taken for key in force):
            take()
        for key in start:
            self.issue(key, events)


class Gather:
    AHEAD = 3

    def __init__(self, place, shards, wholes, chunks, kinds, sems):
        self.at, self.shards, self.wholes = place, shards, wholes
        self.chunks, self.kinds, self.sems = chunks, kinds, sems
        self.first = [first for first, _ in Gather.starts(place.dims, kinds)]

    @staticmethod
    def starts(dims, kinds):
        d1, d2, d3 = dims
        near, starts = d2 + d3 - 2, []
        for stage in range(4):
            at, first = 0, []
            for kind in kinds:
                first.append(at)
                at += ((d1 - 1, near, near, 1), (near, 2 * (d1 - 1), near, 1))[kind][stage]
            starts.append((first, at))
        return starts

    @staticmethod
    def semaphores(dims, kinds):
        return [DMA((size,)) for _, size in Gather.starts(dims, kinds) for _ in range(2)]

    @staticmethod
    def plan(chunks, kinds, unit):
        def costs(key):
            stage, t = key
            size = unit(t)
            if stage == 3:
                return "p", 1.4 * size
            over_z = stage == kinds[t]
            if over_z:
                return "z", (8 if kinds[t] else 4) * size
            return "xy", (0.5, 2, 4)[stage] * size

        def follow(key, taken):
            stage, t = key
            after = [] if stage == 3 else [(stage + 1, t)]
            if stage == 0:
                more = ((1, 2), (3, 4))[t] if t < 2 else (t + Gather.AHEAD,)
                after += [(0, m) for m in more if m < len(chunks)]
            return after

        return Plan(costs, follow)

    def copies(self, stage, t):
        p = self.at
        z, y, x, c = p.z, p.y, p.x, p.c
        i, first, width = self.chunks[t]
        whole, shard, half = self.wholes[i], self.shards[i], width // 2
        full = pl.ds(first, width)
        a, b = pl.ds(first, half), pl.ds(first + half, half)
        pieces = []
        if stage == 0 and self.kinds[t] == 0:
            pieces = [(shard.at[:, full], whole.at[z, y, x, c, :, full], d) for d in p.to_z]
        elif stage == 0:
            pieces = [(shard.at[:, a], whole.at[z, y, x, c, :, a], d) for d in p.to_x]
            pieces += [(shard.at[:, b], whole.at[z, y, x, c, :, b], d) for d in p.to_y]
        elif stage == 1 and self.kinds[t] == 0:
            part = whole.at[:, y, x, c, :, a]
            pieces = [(part, part, d) for d in p.to_x]
            part = whole.at[:, y, x, c, :, b]
            pieces += [(part, part, d) for d in p.to_y]
        elif stage == 1:
            left, right = whole.at[z, y, :, c, :, a], whole.at[z, :, x, c, :, b]
            pieces = [(part, part, d) for d in p.to_z for part in (left, right)]
        elif stage == 2:
            part = whole.at[:, y, :, c, :, a]
            pieces = [(part, part, d) for d in p.to_y]
            part = whole.at[:, :, x, c, :, b]
            pieces += [(part, part, d) for d in p.to_x]
        else:
            part = whole.at[:, :, :, c, :, full]
            pieces = [(part, part, p.to_p)]
        out, back = self.sems[2 * stage], self.sems[2 * stage + 1]
        first = self.first[stage][t]
        return [send(s, d, out.at[first + k], back.at[first + k], to) for k, (s, d, to) in enumerate(pieces)]

    def run(self, events):
        for what, (stage, t) in events:
            for copy in self.copies(stage, t):
                if what == "go":
                    copy.start()
                else:
                    copy.wait_recv()

    def finish(self):
        for stage in range(4):
            for t in range(len(self.chunks)):
                for copy in self.copies(stage, t):
                    copy.wait_send()


def small_copies(place, source, target, sems, stage):
    z, y, x, c = place.z, place.y, place.x, place.c
    d1, d2, d3 = place.dims
    if stage == 0:
        pieces = [(source, target.at[z, y, x, c], d) for d in place.to_z]
    elif stage == 1:
        part = target.at[:, y, x, c]
        pieces = [(part, part, d) for d in place.to_x]
    elif stage == 2:
        part = target.at[:, y, :, c]
        pieces = [(part, part, d) for d in place.to_y]
    else:
        part = target.at[:, :, :, c]
        pieces = [(part, part, place.to_p)]
    base = (0, d1, d1 + d3, d1 + d2 + d3)[stage]
    return [send(s, d, sems[0].at[base + k], sems[1].at[base + k], to) for k, (s, d, to) in enumerate(pieces)]


class Reduce:
    @staticmethod
    def scratch(dims, rows, width, dtype, halves=True):
        d1, d2, d3 = dims
        half = width // 2 if halves else width
        shapes = [pltpu.VMEM((d1, d2, d3, rows, width), dtype)]
        shapes.append(pltpu.VMEM((d2 - 1, d1, d3, rows, half), dtype))
        shapes.append(pltpu.VMEM((d3 - 1, d1, rows, half), dtype))
        if halves:
            shapes.append(pltpu.VMEM((d3 - 1, d1, d2, rows, half), dtype))
            shapes.append(pltpu.VMEM((d2 - 1, d1, rows, half), dtype))
        shapes.append(pltpu.VMEM((d1 - 1, rows, width), dtype))
        near = d2 + d3 - 2
        sizes = (1, near, near, d1 - 1) if halves else (1, d2 - 1, d3 - 1, d1 - 1)
        for size in sizes:
            shapes += [DMA((size,)), DMA((size,))]
        return shapes

    @staticmethod
    def plan(unit):
        def costs(key):
            stage, t = key
            return ("p", "xy", "xy", "z")[stage], (1.4, 4, 2, 4)[stage] * unit(t)

        def follow(key, taken):
            stage, t = key
            after = []
            if stage == 0 and (t < 2 or (1, t - 2) in taken):
                after.append((1, t))
            if stage == 1:
                if (0, t + 2) in taken:
                    after.append((1, t + 2))
                after.append((2, t))
            if stage == 2:
                after.append((3, t))
            return after

        return Plan(costs, follow)

    def __init__(self, place, refs, source, own, result, halves=True, load=None):
        self.at, self.halves, self.load = place, halves, load
        self.source, self.own, self.result = source, own, result
        if halves:
            self.total, self.ya, self.xa, self.xb, self.yb, self.zz = refs[:6]
            self.sems = refs[6:]
        else:
            self.total, self.ya, self.xa, self.zz = refs[:4]
            self.sems = refs[4:]
        width = self.total.shape[-1]
        half = width // 2 if halves else width
        self.a, self.b = pl.ds(0, half), pl.ds(half, half)

    def pieces(self, stage):
        p, h = self.at, self.total
        y, x = p.y, p.x
        if stage == 0:
            return [(self.source.at[:, :, :, 1 - p.c], h, p.to_p)]
        if stage == 1:
            made = [
                (h.at[:, v, :, :, self.a], self.ya.at[k], d)
                for k, (v, d) in enumerate(zip(p.ys, p.to_y))
            ]
            if self.halves:
                made += [
                    (h.at[:, :, v, :, self.b], self.xb.at[k], d)
                    for k, (v, d) in enumerate(zip(p.xs, p.to_x))
                ]
            return made
        if stage == 2:
            made = [
                (h.at[:, y, v, :, self.a], self.xa.at[k], d)
                for k, (v, d) in enumerate(zip(p.xs, p.to_x))
            ]
            if self.halves:
                made += [
                    (h.at[:, v, x, :, self.b], self.yb.at[k], d)
                    for k, (v, d) in enumerate(zip(p.ys, p.to_y))
                ]
            return made
        return [(h.at[v, y, x], self.zz.at[k], d) for k, (v, d) in enumerate(zip(p.zs, p.to_z))]

    def go(self, stage):
        for copy in self.copies(stage):
            copy.start()

    def copies(self, stage):
        out, back = self.sems[2 * stage], self.sems[2 * stage + 1]
        return [
            send(s, d, out.at[k], back.at[k], to) for k, (s, d, to) in enumerate(self.pieces(stage))
        ]

    def arrived(self, stage):
        for copy in self.copies(stage):
            copy.wait()

    def add(self, stage):
        p, h = self.at, self.total
        d1, d2, d3 = p.dims
        f32 = jnp.float32

        def into(at, terms):
            value = h[at].astype(f32)
            for term in terms:
                value = value + term.astype(f32)
            h[at] = value.astype(h.dtype)

        if stage == 0:

            @pl.loop(0, d1)
            def _(i):
                for j in range(d2):
                    for k in range(d3):
                        into((i, j, k), [self.own[i, j, k]])

        elif stage == 1:

            @pl.loop(0, d1)
            def _(i):
                for k in range(d3):
                    into(
                        (i, p.y, k, slice(None), self.a),
                        [self.ya[m, i, k] for m in range(d2 - 1)],
                    )
                if self.halves:
                    for j in range(d2):
                        into(
                            (i, j, p.x, slice(None), self.b),
                            [self.xb[m, i, j] for m in range(d3 - 1)],
                        )

        elif stage == 2:

            @pl.loop(0, d1)
            def _(i):
                into((i, p.y, p.x, slice(None), self.a), [self.xa[m, i] for m in range(d3 - 1)])
                if self.halves:
                    into(
                        (i, p.y, p.x, slice(None), self.b),
                        [self.yb[m, i] for m in range(d2 - 1)],
                    )

        else:
            value = h[p.z, p.y, p.x].astype(f32)
            for m in range(d1 - 1):
                value = value + self.zz[m].astype(f32)
            for cut, target in self.result:
                target[...] = value[:, cut]

    def take(self, stage):
        if stage == 0 and self.load is not None:
            self.load.wait()
        self.arrived(stage)
        self.add(stage)


HEAD_DIM = 64
MB = 2
EPS = 1e-05
BF = jnp.bfloat16
F32 = jnp.float32
NEG = -1e30
GELU_A = 0.044715
GELU_C = 0.7978845608028654


def mm(left, right):
    return lax.dot_general(left, right, (((1,), (0,)), ((), ())), preferred_element_type=F32)


def mm_nt(left, right):
    return lax.dot_general(left, right, (((1,), (1,)), ((), ())), preferred_element_type=F32)


def mm_tn(left, right):
    return lax.dot_general(left, right, (((0,), (0,)), ((), ())), preferred_element_type=F32)


def iota(shape, axis):
    return lax.broadcasted_iota(jnp.int32, shape, axis)


def unpack_vector(block, start, per, width, first):
    row0, lane0 = start // 128, start % 128
    rows = block.shape[0]
    column = iota((128, width), 1) + first
    pick = (iota((128, width), 0) - lane0 == column % per).astype(BF)
    spread = mm(block, pick)
    column = iota((rows, width), 1) + first
    mine = iota((rows, width), 0) == column // per * 8 + row0
    return jnp.sum(jnp.where(mine, spread, 0.0), axis=0, keepdims=True)


def moments(value, keep, first):
    mean = jnp.mean(value, axis=-1, keepdims=True)
    center = value - mean
    scale = lax.rsqrt(jnp.mean(center * center, axis=-1, keepdims=True) + EPS)
    keep[:, first : first + 1] = mean
    keep[:, first + 1 : first + 2] = scale
    return center, scale


def attend_pair(q2, k2, v2, masks, seq):
    half = seq // 2
    lane = iota((1, 128), 1) // HEAD_DIM
    vt = v2.T
    q2 = q2 * jnp.asarray(HEAD_DIM**-0.5, BF)
    ka, kb = k2[:half], k2[half:]
    sums, rows = [], []
    for head in range(2):
        qh = jnp.where(lane == head, q2, 0)
        va, vb = (vt[head * HEAD_DIM : (head + 1) * HEAD_DIM, i * half : (i + 1) * half] for i in range(2))
        first, second = qh[:half], qh[half:]
        s = mm_nt(ka, first) + masks[0]
        sa, sb = mm_nt(ka, second), mm_nt(kb, second) + masks[1]
        top = jnp.max(s, axis=0, keepdims=True)
        e = jnp.exp(s - top)
        total = jnp.sum(e, axis=0, keepdims=True)
        low = mm(va, e.astype(BF)) * (1.0 / total)
        logs = top + jnp.log(total)
        top = jnp.maximum(jnp.max(sa, axis=0, keepdims=True), jnp.max(sb, axis=0, keepdims=True))
        ea, eb = jnp.exp(sa - top), jnp.exp(sb - top)
        total = jnp.sum(ea, axis=0, keepdims=True) + jnp.sum(eb, axis=0, keepdims=True)
        high = (mm(va, ea.astype(BF)) + mm(vb, eb.astype(BF))) * (1.0 / total)
        rows.append(jnp.concatenate([low, high], axis=1))
        sums.append(jnp.concatenate([logs, top + jnp.log(total)], axis=1))
    return jnp.concatenate(rows, axis=0).T, sums


def forward_plan(chunks, kinds, groups, fcs, projs, steps):
    widest = max(width for i, _, width in chunks if i != 3)
    plan = Gather.plan(chunks, kinds, lambda t: 1.2 * (1.0 if chunks[t][0] == 3 else chunks[t][2] / widest))
    fetched, used = set(), set()

    def pump(point, passed=0.0, done=None, **rest):
        if done is not None:
            used.add(done)
        plan.pump(point, passed, **rest)
        for t in range(len(chunks)):
            first = t < 2 or (chunks[t][0] == 3) != (chunks[t - 2][0] == 3)
            if (3, t) in plan.taken and t not in fetched and (first or t - 2 in used):
                fetched.add(t)
                plan.table[point].append(("fetch", (3, t)))

    pump("begin", 0.0, start=[(0, 0)])
    for k in range(4):
        pump(("small", k), 2.0, force=[(k - 1, 0)] if 0 < k < 3 else ())
    pump("spread", 2.5, force=[(2, 0)])
    pump("norm", 2.0)
    for g in range(groups):
        pump(("qkv", g), 0.0, force=[(3, g)])
        pump(("scores", g), 2.4, done=g)
        for i in range(steps):
            pump(("attend", g, i), 0.0 if i == 0 else 1.6)
        pump(("group", g), 1.6)
    t = groups
    pump("out", 0.0, force=[(3, t)])
    for i in range(2):
        pump(("norm2", i), 2.1)
    used.add(t)
    for k in range(fcs):
        pump(("fc", k), 0.0, force=[(3, t + 1 + k)])
        for i in range(2):
            pump(("gelu", k, i), 2.4)
        used.add(t + 1 + k)
        pump(("terms", k), 2.9, force=[(3, t + 2 + k)])
    for k in range(projs):
        pump(("proj", k), 0.0, force=[(3, t + 1 + fcs + k)])
        pump(("done", k), 2.8, done=t + 1 + fcs + k)
    pump("end", 0.0, force=[(3, k) for k in range(len(chunks))])
    return plan.table


def forward_kernel(dims, chunks, kinds, comm, *refs):
    (lens, tokens, cot, s_qkv, s_out, s_fc, s_proj, small) = refs[:8]
    (w_qkv, w_out, w_fc, w_proj, vecs_o, h1_o, qkv_o, lse_o, ctx_o, r1_o, h2_o, gp_o, dy_o, terms_o, out_o, stats_o) = refs[8:24]
    (x_, dy, live, vecs, fcb, h1, qkv, ctx, lse, r1, h2, act, gp, out, sm, wbuf, pbuf, tbuf, diag, shuffled, stats) = refs[24:45]
    local, wsem, psem, osem, outsem, gpsem, tsem, shsem, s_sem, r_sem = refs[45:55]
    sems = refs[55:]
    rows, width = x_.shape
    seq = rows // MB
    hidden = act.shape[1]
    n = dims[0] * dims[1] * dims[2] * 2
    per, per_fc = width // n, hidden // n
    tile = 256
    tiles = rows // tile
    fcs = hidden // width
    groups = sum(i == 0 for i, _, _ in chunks)
    gw = width // groups
    pw = chunks[-1][2]
    projs = width // pw
    gpairs = gw // 128
    steps = MB * gpairs
    plan = forward_plan(chunks, kinds, groups, fcs, projs, steps)
    place = Place(dims)
    z, y, x, c = place.z, place.y, place.x, place.c
    shards = (shuffled, s_out, s_fc, s_proj)
    wholes = (w_qkv, w_out, w_fc, w_proj)
    gather = Gather(place, shards, wholes, chunks, kinds, sems)

    def at_point(*key):
        for event in plan[key[0] if len(key) == 1 else key]:
            if event[0] == "fetch":
                fetch(event[1][1]).start()
            elif comm:
                gather.run([event])

    def fetch(t):
        i, first, w = chunks[t]
        source = wholes[i].at[:, :, :, :, :, pl.ds(first, w)]
        if i == 3:
            return pltpu.make_async_copy(source, pbuf.at[t % 2], psem.at[t % 2])
        return pltpu.make_async_copy(source, wbuf.at[t % 2, :, :, :, :, :, pl.ds(0, w)], wsem.at[t % 2])

    saves = []

    def keep(source, target):
        save = pltpu.make_async_copy(source, target, osem.at[len(saves)])
        save.start()
        saves.append(save)

    shuffle = [
        pltpu.make_async_copy(
            s_qkv.at[:, pl.ds(k * width + g * gw, gw)], shuffled.at[:, pl.ds((3 * g + k) * gw, gw)], shsem.at[3 * g + k]
        )
        for g in range(groups)
        for k in range(3)
    ]
    for move in shuffle:
        move.start()
    loads = [pltpu.make_async_copy(tokens, x_, gpsem.at[0]), pltpu.make_async_copy(cot, dy, gpsem.at[1])]
    for move in loads:
        move.start()
    moves = [
        pltpu.make_async_copy(s, w.at[z, y, x, c], local.at[i])
        for i, (s, w) in enumerate(zip((*shards, small), (*wholes, sm)))
    ]
    for move in moves[1:]:
        move.start()
    place.barrier()
    for move in shuffle:
        move.wait()
    moves[0].start()
    tiny = [small_copies(place, small, sm, (s_sem, r_sem), stage) for stage in range(4)]
    half = seq // 2
    for stage in range(4):
        if comm:
            for copy in tiny[stage]:
                copy.start()
        if stage == 0:
            at_point("begin")
            for slot in range(MB):
                length = lens[slot : slot + 1, 0:1]
                live[slot * seq : (slot + 1) * seq, :] = jnp.where(iota((seq, 1), 0).astype(F32) < length, 1.0, 0.0)
                causal = iota((half, half), 0) <= iota((half, half), 1)
                late = (iota((half, half), 0) + half).astype(F32) < length
                diag[0] = jnp.where(causal, 0.0, NEG)
                diag[1 + slot] = jnp.where(causal & late, 0.0, NEG)
            for move in moves:
                move.wait()
        if stage == 1:
            loads[1].wait()
            vecs[8:16, :] = jnp.zeros((8, width), F32)

            @pl.loop(0, tiles)
            def _(i):
                at = pl.ds(pl.multiple_of(i * tile, tile), tile)
                value = jnp.where(live[at, :] > 0.5, dy[at, :].astype(F32), 0.0)
                dy[at, :] = value.astype(BF)
                vecs[8:9, :] += jnp.sum(value, axis=0, keepdims=True)

            keep(dy, dy_o)
        if comm:
            for copy in tiny[stage]:
                copy.wait_recv()
        at_point("small", stage)
    block = sm[...].reshape(n * 8, 128).astype(BF)
    for v in range(8):
        vecs[v : v + 1, :] = unpack_vector(block, v * per, per, width, 0)
    for part in range(fcs):
        fcb[:, part * width : (part + 1) * width] = unpack_vector(block, 8 * per, per_fc, width, part * width)
    at_point("spread")
    loads[0].wait()

    @pl.loop(0, rows // 128)
    def _(i):
        at = pl.ds(pl.multiple_of(i * 128, 128), 128)
        center, scale = moments(x_[at, :].astype(F32), stats.at[at, :], 0)
        h1[at, :] = (center * scale * vecs[0:1, :] + vecs[1:2, :]).astype(BF)

    keep(h1, h1_o)
    keep(vecs, vecs_o)
    at_point("norm")

    @pl.loop(0, groups)
    def _(g):
        for k in range(groups):

            @pl.when(g == k)
            def _():
                at_point("qkv", k)
                fetch(k).wait()

        first = pl.multiple_of(g * gw, gw)

        @pl.loop(0, tiles)
        def _(i):
            at = pl.ds(pl.multiple_of(i * tile, tile), tile)
            value = mm(h1[at, :], wbuf[g % 2, :, :, :, :, :, 0 : 3 * gw].reshape(width, 3 * gw))
            for k, bias in ((0, 2), (1, None), (2, 3)):
                part = value[:, k * gw : (k + 1) * gw]
                if bias is not None:
                    part = part + vecs[bias : bias + 1, pl.ds(first, gw)]
                qkv[at, pl.ds(k * width + first, gw)] = part.astype(BF)

        for k in range(groups):
            if plan["scores", k]:

                @pl.when(g == k)
                def _():
                    at_point("scores", k)

        @pl.loop(0, steps)
        def _(i):
            for k in range(groups):
                for m in range(steps):
                    if plan["attend", k, m]:

                        @pl.when((g == k) & (i == m))
                        def _():
                            at_point("attend", k, m)

            slot, pair = i // gpairs, g * gpairs + i % gpairs
            at = pl.ds(pl.multiple_of(slot * seq, seq), seq)
            col = pl.multiple_of(pair * 128, 128)
            value, sums = attend_pair(
                qkv[at, pl.ds(col, 128)],
                qkv[at, pl.ds(width + col, 128)],
                qkv[at, pl.ds(2 * width + col, 128)],
                [diag[0], diag[1 + slot]],
                seq,
            )
            ctx[at, pl.ds(col, 128)] = value.astype(BF)
            for head in range(2):
                lse[slot * (width // HEAD_DIM) + pair * 2 + head] = sums[head]

        for k in range(groups):
            if plan["group", k]:

                @pl.when(g == k)
                def _():
                    at_point("group", k)

    keep(qkv, qkv_o)
    keep(ctx, ctx_o)
    keep(lse, lse_o)
    t = groups
    at_point("out")
    fetch(t).wait()

    @pl.loop(0, tiles)
    def _(i):
        at = pl.ds(pl.multiple_of(i * tile, tile), tile)
        value = mm(ctx[at, :], wbuf[t % 2].reshape(width, width)) + vecs[4:5, :]
        value = value + x_[at, :].astype(F32)
        r1[at, :] = value
        center, scale = moments(value, stats.at[at, :], 2)
        h2[at, :] = (center * scale * vecs[5:6, :] + vecs[6:7, :]).astype(BF)
        for k in range(2):

            @pl.when(i == (k + 1) * tiles // 2 - 1)
            def _():
                at_point("norm2", k)

    keep(r1, r1_o)
    keep(h2, h2_o)
    keep(stats, stats_o)

    def keep_gp(k):
        return pltpu.make_async_copy(gp.at[k % 2], gp_o.at[:, pl.ds(pl.multiple_of(k * width, width), width)], gpsem.at[k % 2])

    def each(index, count, *name):
        for k in range(count):
            key = (*name, k)
            if plan[key]:

                @pl.when(index == k)
                def _():
                    at_point(*key)

    def keep_terms(k):
        return pltpu.make_async_copy(tbuf.at[k % 2], terms_o.at[k], tsem.at[k % 2])

    @pl.loop(0, fcs)
    def _(k):
        each(k, fcs, "fc")
        buffer = (groups + 1 + k) % 2
        for m in range(fcs):

            @pl.when(k == m)
            def _():
                fetch(groups + 1 + m).wait()

        @pl.when(k >= 2)
        def _():
            keep_gp(k - 2).wait()
            keep_terms(k - 2).wait()

        cut = pl.ds(pl.multiple_of(k * width, width), width)

        @pl.loop(0, 2)
        def _(i):
            for part in range(tiles // 2):
                at = pl.ds(pl.multiple_of((i * (tiles // 2) + part) * tile, tile), tile)
                u = mm(h2[at, :], wbuf[buffer].reshape(width, width)) + fcb[:, cut]
                square = u * u
                inner = u * (GELU_C + (GELU_C * GELU_A) * square)
                gate = 0.5 + 0.5 * jnp.tanh(inner)
                value = u * gate
                act[at, cut] = value.astype(BF)
                slope = gate + value * (2.0 - 2.0 * gate) * (GELU_C + (3.0 * GELU_C * GELU_A) * square)
                gp[k % 2, at, :] = slope.astype(BF)
            for n_k in range(fcs):
                for m in range(2):
                    if plan["gelu", n_k, m]:

                        @pl.when((k == n_k) & (i == m))
                        def _():
                            at_point("gelu", n_k, m)

        keep_gp(k).start()

        @pl.loop(0, 2)
        def _(i):
            some = pl.ds(pl.multiple_of(k * width + i * (width // 2), width // 2), width // 2)
            value = mm_tn(act[:, some], dy[...]).astype(BF)
            blocks = (dims[1] // 2, dims[2], 2, per_fc, width)
            tbuf[k % 2, pl.ds(i * blocks[0], blocks[0])] = value.reshape(blocks)

        keep_terms(k).start()
        each(k, fcs, "terms")

    def keep_out(k):
        cut = pl.ds(pl.multiple_of(k * pw, pw), pw)
        return pltpu.make_async_copy(out.at[:, cut], out_o.at[:, cut], outsem.at[k])

    @pl.loop(0, projs)
    def _(k):
        cut = pl.ds(pl.multiple_of(k * pw, pw), pw)
        buffer = (groups + 1 + fcs + k) % 2

        for m in range(projs):

            @pl.when(k == m)
            def _():
                at_point("proj", m)
                fetch(groups + 1 + fcs + m).wait()

        @pl.loop(0, tiles)
        def _(i):
            at = pl.ds(pl.multiple_of(i * tile, tile), tile)
            value = mm(act[at, :], pbuf[buffer].reshape(hidden, pw)) + (r1[at, cut] + vecs[7:8, cut])
            out[at, cut] = jnp.where(live[at, :] > 0.5, value, 0.0).astype(BF)

        keep_out(k).start()
        each(k, projs, "done")

    at_point("end")
    for k in range(max(fcs - 2, 0), fcs):
        keep_gp(k).wait()
    for k in range(max(fcs - 2, 0), fcs):
        keep_terms(k).wait()
    for k in range(projs):
        keep_out(k).wait()
    for save in saves:
        save.wait()
    if comm:
        gather.finish()
        for copies in tiny:
            for copy in copies:
                copy.wait_send()


def forward(dims, lens, tokens, cot, shards, small, chunks, kinds, comm=True):
    rows, width = tokens.shape
    n = dims[0] * dims[1] * dims[2] * 2
    hidden = shards[2].shape[1]
    heads = width // HEAD_DIM
    seq = rows // MB
    pw = chunks[-1][2]
    groups = sum(i == 0 for i, _, _ in chunks)
    sds = jax.ShapeDtypeStruct
    shapes = [sds((*dims, 2, *s.shape), s.dtype) for s in shards]
    shapes += [
        sds((16, width), F32),
        sds((rows, width), BF),
        sds((rows, 3 * width), BF),
        sds((MB * heads, 1, seq), F32),
        sds((rows, width), BF),
        sds((rows, width), F32),
        sds((rows, width), BF),
        sds((rows, hidden), BF),
        sds((rows, width), BF),
        sds((*dims, 2, hidden // n, width), BF),
        sds((rows, width), BF),
        sds((rows, 128), F32),
    ]
    scratch = [
        pltpu.VMEM((rows, width), BF),
        pltpu.VMEM((rows, width), BF),
        pltpu.VMEM((rows, 1), F32),
        pltpu.VMEM((16, width), F32),
        pltpu.VMEM((1, hidden), F32),
        pltpu.VMEM((rows, width), BF),
        pltpu.VMEM((rows, 3 * width), BF),
        pltpu.VMEM((rows, width), BF),
        pltpu.VMEM((MB * heads, 1, seq), F32),
        pltpu.VMEM((rows, width), F32),
        pltpu.VMEM((rows, width), BF),
        pltpu.VMEM((rows, hidden), BF),
        pltpu.VMEM((2, rows, width), BF),
        pltpu.VMEM((rows, width), BF),
        pltpu.VMEM((*dims, 2, *small.shape), small.dtype),
        pltpu.VMEM((2, *dims, 2, width // n, width), BF),
        pltpu.VMEM((2, *dims, 2, hidden // n, pw), BF),
        pltpu.VMEM((2, *dims[1:], 2, hidden // n, width), BF),
        pltpu.VMEM((1 + MB, seq // 2, seq // 2), F32),
        pltpu.VMEM(shards[0].shape, BF),
        pltpu.VMEM((rows, 128), F32),
        DMA((5,)),
        DMA((2,)),
        DMA((2,)),
        DMA((9,)),
        DMA((width // pw,)),
        DMA((2,)),
        DMA((2,)),
        DMA((3 * groups,)),
        DMA((sum(dims) + 1,)),
        DMA((sum(dims) + 1,)),
        *Gather.semaphores(dims, kinds),
    ]
    return pl.pallas_call(
        lambda *refs: forward_kernel(dims, chunks, kinds, comm, *refs),
        out_shape=shapes,
        in_specs=[VMEM, ANY, ANY, ANY] + [VMEM] * 4,
        out_specs=[ANY] * 16,
        scratch_shapes=scratch,
        compiler_params=pltpu.CompilerParams(
            collective_id=0, has_side_effects=True, vmem_limit_bytes=60 * 1024 * 1024
        ),
        name="forward",
    )(lens, tokens, cot, *shards, small)


def pack_vector(row, start, per, n):
    width = row.shape[1]
    pick = (iota((128, width), 0) - start % 128 == iota((128, width), 1) % per).astype(BF)
    mine = iota((n, width), 0) == iota((n, width), 1) // per
    total = 0.0
    for _ in range(3):
        part = row.astype(BF)
        row = row - part.astype(F32)
        total = total + mm_nt(jnp.where(mine, part.astype(F32), 0.0).astype(BF), pick)
    return total


def norm_back(value, kept, gain, grad):
    scale = kept[:, 1:2]
    normed = (value - kept[:, 0:1]) * scale
    scaled = grad * gain
    mean = jnp.mean(scaled, axis=-1, keepdims=True)
    cross = jnp.mean(scaled * normed, axis=-1, keepdims=True)
    return (scaled - mean - normed * cross) * scale, grad * normed


def attend_back(q2, k2, v2, o2, c2, lse, masks, seq):
    half = seq // 2
    lane = iota((1, 128), 1) // HEAD_DIM
    prod = o2.astype(F32) * c2.astype(F32)
    heads = (iota((8, 128), 1) // HEAD_DIM == iota((8, 128), 0)).astype(BF)
    high = prod.astype(BF)
    delta = mm_nt(heads, high) + mm_nt(heads, (prod - high.astype(F32)).astype(BF))
    kt = k2.T
    q2 = q2 * jnp.asarray(HEAD_DIM**-0.5, BF)
    cuts = (slice(0, half), slice(half, seq))
    dk, dv, dq = [0.0, 0.0], [0.0, 0.0], []
    for head in range(2):
        qh = jnp.where(lane == head, q2, 0)
        oh = jnp.where(lane == head, o2, 0)
        kh = kt[head * HEAD_DIM : (head + 1) * HEAD_DIM]
        parts = [0.0, 0.0]
        for key, query in ((0, 0), (0, 1), (1, 1)):
            qb, ob, cut = qh[cuts[query]], oh[cuts[query]], cuts[query]
            s = mm_nt(k2[cuts[key]], qb) - lse[head][:, cut]
            if key == query:
                s = s + masks[key]
            p = jnp.exp(s)
            dp = mm_nt(v2[cuts[key]], ob)
            ds = (p * (dp - delta[head : head + 1, cut])).astype(BF)
            dv[key] = dv[key] + mm(p.astype(BF), ob)
            dk[key] = dk[key] + mm(ds, qb)
            parts[query] = parts[query] + mm(kh[:, cuts[key]], ds)
        dq.append(jnp.concatenate(parts, axis=1))
    dq = jnp.concatenate(dq, axis=0).T * HEAD_DIM**-0.5
    return dq, jnp.concatenate(dk, axis=0), jnp.concatenate(dv, axis=0)


def backward_plan(projs, fcs, groups, steps, slabs):
    out = projs + fcs
    plan = Reduce.plan(lambda t: 1.3 if t <= out else 1.0)
    pump = plan.pump
    pump("start", 0.0, start=[(0, 0), (0, 1)])
    pump("loaded", 4.0)
    late = list(range(2, projs))
    for f in range(fcs):
        for name, passed in (("da", 3.2), ("dh", 2.9)):
            j = late.pop(0) if late else None
            force = [] if j is None else [(0, j - 2)]
            if name == "dh" and f >= 2:
                force.append((0, projs + f - 2))
            pump((name, f), passed, force=force, start=[] if j is None else [(0, j)])
        pump(("gfc", f), 2.9, start=[(0, projs + f)])
    for i in range(slabs):
        pump(("ln2", i), 2.0)
    pump("dctx", 3.0, force=[(0, out - 2)])
    pump("gout", 3.0, start=[(0, out)])
    for g in range(groups):
        for i in range(steps):
            pump(("back", g, i), 0.0 if i == 0 else 2.0)
        pump(("grads", g), 2.0, force=[(0, out - 1 + g)])
        pump(("gqkv", g), 2.2, start=[(0, out + 1 + g)])
    for i in range(slabs):
        pump(("dx", i), 3.4)
    pump("end", 4.0, force=[(3, t) for t in range(out + 1 + groups)])
    return plan.table


def backward_kernel(dims, groups, sizes, comm, *refs):
    (lens, tokens, dy, vecs, stats, h1_i, qkv_i, lse_i, ctx_i, r1_i, h2_i, gp_i, terms, w_qkv, w_out, w_fc, w_proj) = refs[:17]
    (dx_o, g_qkv, g_out, g_fc, g_proj, g_small) = refs[17:23]
    slots, wp, f_dh, f_r1, gvec, gfc, lse, diag, stage, owns, sstage = refs[23:34]
    lsem, wsem, osem, qsem = refs[34:38]
    refs = refs[38:]
    d1, d2, d3 = dims
    n = d1 * d2 * d3 * 2
    rows, width = f_dh.shape
    hidden = gfc.shape[1]
    seq = rows // MB
    half = seq // 2
    per, per_fc = width // n, hidden // n
    fcs = hidden // width
    gw = width // groups
    pw = owns.shape[-1]
    projs = width // pw
    tile = rows // d1
    gpairs = gw // 128
    steps = MB * gpairs
    place = Place(dims)
    c = place.c
    plan = backward_plan(projs, fcs, groups, steps, d1)
    sets = []
    for size in sizes:
        sets.append(refs[:size])
        refs = refs[size:]
    parts = []
    for j in range(projs):
        cut = pl.ds(j * pw, pw)
        own = owns.at[j % 2]
        move = pltpu.make_async_copy(terms.at[:, :, :, c, :, cut], own, osem.at[j % 2])
        result = [(slice(None), g_proj.at[:, cut])]
        parts.append(Reduce(place, sets[j], terms.at[:, :, :, :, :, cut], own, result, load=move))
    for f in range(fcs):
        result = [(slice(None), g_fc.at[:, pl.ds(f * width, width)])]
        parts.append(Reduce(place, sets[projs + f], stage.at[f % 2], stage.at[f % 2, :, :, :, c], result))
    b = fcs % 2
    parts.append(Reduce(place, sets[projs + fcs], stage.at[b], stage.at[b, :, :, :, c], [(slice(None), g_out)]))
    gcut = pl.ds(0, 3 * gw)
    for g in range(groups):
        b = (fcs + 1 + g) % 2
        result = [
            (slice(k * gw, (k + 1) * gw), g_qkv.at[:, pl.ds(k * width + g * gw, gw)]) for k in range(3)
        ]
        source, own = stage.at[b, :, :, :, :, :, gcut], stage.at[b, :, :, :, c, :, gcut]
        parts.append(Reduce(place, sets[projs + fcs + 1 + g], source, own, result))

    def at_point(*key):
        if not comm:
            return
        for what, (step, t) in plan[key[0] if len(key) == 1 else key]:
            if what == "take":
                parts[t].take(step)
            else:
                parts[t].go(step)
                if step == 0 and parts[t].load is not None:
                    parts[t].load.start()

    def load(source, slot, k):
        return pltpu.make_async_copy(source, slots.at[slot], lsem.at[k])

    def cols(source, k):
        return source.at[:, :, :, :, :, pl.ds(pl.multiple_of(k * width, width), width)]

    def whole(slot):
        return slots[slot].reshape(rows, width)

    def piece(slot, i):
        return slots[slot, i].reshape(tile, width)

    def put(slot, i, value):
        slots[slot, i] = value.astype(BF).reshape(d2, d3, 2, per, width)

    def fetch_proj(f):
        return pltpu.make_async_copy(w_proj.at[f], wp.at[f % 2], wsem.at[f % 2])

    def fetch_ff(f):
        return [fetch_proj(f), load(cols(gp_i, f), 3 + f % 2, 3 + f % 2), load(cols(w_fc, f), 1 + f % 2, 1 + f % 2)]

    def w_third(k, target):
        return [
            pltpu.make_async_copy(
                w_qkv.at[:, :, :, :, :, pl.ds((3 * g + k) * gw, gw)],
                target.at[:, :, :, :, :, pl.ds(g * gw, gw)],
                qsem.at[k, g],
            )
            for g in range(groups)
        ]

    load(dy, 0, 0).start()
    for move in fetch_ff(0):
        move.start()
    load(h2_i, 6, 6).start()
    load(ctx_i, 7, 7).start()
    lload = pltpu.make_async_copy(lse_i, lse, lsem.at[5])
    lload.start()
    place.barrier(everyone=True)
    at_point("start")
    for slot in range(MB):
        causal = iota((half, half), 0) <= iota((half, half), 1)
        late = (iota((half, half), 0) + half).astype(F32) < lens[slot : slot + 1, 0:1]
        diag[0] = jnp.where(causal, 0.0, NEG)
        diag[1 + slot] = jnp.where(causal & late, 0.0, NEG)
    gvec[...] = jnp.zeros_like(gvec)
    gfc[...] = jnp.zeros_like(gfc)
    f_dh[...] = jnp.zeros_like(f_dh)
    gvec[7:8, :] = vecs[8:9, :]
    load(dy, 0, 0).wait()
    at_point("loaded")
    load(h2_i, 6, 6).wait()

    def each(index, count, *name):
        for k in range(count):
            key = (*name, k)
            if plan[key]:

                @pl.when(index == k)
                def _():
                    at_point(*key)

    @pl.loop(0, fcs)
    def _(f):
        for move in fetch_ff(f):
            move.wait()

        @pl.when(f + 1 < fcs)
        def _():
            for move in fetch_ff(f + 1):
                move.start()

        cut = pl.ds(pl.multiple_of(f * width, width), width)

        @pl.loop(0, d1 // 2)
        def _(h):
            for i in (2 * h, 2 * h + 1):
                da = mm_nt(piece(0, i), wp[f % 2].reshape(rows, width))
                du = (da * piece(3 + f % 2, i).astype(F32)).astype(BF)
                put(5, i, du)
                gfc[:, cut] += jnp.sum(du.astype(F32), axis=0, keepdims=True)

        each(f, fcs, "da")

        @pl.loop(0, d1 // 2)
        def _(h):
            for i in (2 * h, 2 * h + 1):
                at = pl.ds(pl.multiple_of(i * tile, tile), tile)
                f_dh[at, :] += mm_nt(piece(5, i), whole(1 + f % 2))

        each(f, fcs, "dh")

        @pl.loop(0, 2)
        def _(i):
            col = pl.ds(pl.multiple_of(i * (width // 2), width // 2), width // 2)
            value = mm_tn(slots[6, :, :, :, :, :, col].reshape(rows, width // 2), whole(5)).astype(BF)
            stage[f % 2, pl.ds(i * (d1 // 2), d1 // 2)] = value.reshape(d1 // 2, d2, d3, 2, per, width)

        each(f, fcs, "gfc")

    def r1_tile(i):
        return pltpu.make_async_copy(r1_i.at[pl.ds(i * tile, tile)], f_r1.at[i % 2], wsem.at[i % 2])

    r1_tile(0).start()
    load(w_out, 1, 1).start()
    for k, slot in enumerate((3, 4, 6)):
        load(cols(qkv_i, k), slot, slot).start()

    @pl.loop(0, d1)
    def _(i):
        r1_tile(i).wait()

        @pl.when(i + 1 < d1)
        def _():
            r1_tile(i + 1).start()

        at = pl.ds(pl.multiple_of(i * tile, tile), tile)
        grad = f_dh[at, :]
        value, norms = norm_back(f_r1[i % 2], stats[at, 2:4], vecs[5:6, :], grad)
        value = value + piece(0, i).astype(F32)
        f_dh[at, :] = value
        low = value.astype(BF)
        put(5, i, low)
        gvec[5:6, :] += jnp.sum(norms, axis=0, keepdims=True)
        gvec[6:7, :] += jnp.sum(grad, axis=0, keepdims=True)
        gvec[4:5, :] += jnp.sum(low.astype(F32), axis=0, keepdims=True)
        for k in range(d1):
            if plan["ln2", k]:

                @pl.when(i == k)
                def _():
                    at_point("ln2", k)

    load(ctx_i, 7, 7).wait()
    load(w_out, 1, 1).wait()
    load(h1_i, 0, 0).start()

    @pl.loop(0, d1)
    def _(i):
        put(2, i, mm_nt(piece(5, i), whole(1)))

    for move in w_third(0, slots.at[1]):
        move.start()
    at_point("dctx")

    @pl.loop(0, 2)
    def _(i):
        col = pl.ds(pl.multiple_of(i * (width // 2), width // 2), width // 2)
        value = mm_tn(slots[7, :, :, :, :, :, col].reshape(rows, width // 2), whole(5)).astype(BF)
        stage[fcs % 2, pl.ds(i * (d1 // 2), d1 // 2)] = value.reshape(d1 // 2, d2, d3, 2, per, width)

    for move in w_third(1, slots.at[5]):
        move.start()
    loadx = pltpu.make_async_copy(tokens, wp.at[0], lsem.at[2])
    loadx.start()
    at_point("gout")
    for k, slot in enumerate((3, 4, 6)):
        load(cols(qkv_i, k), slot, slot).wait()
    lload.wait()
    load(h1_i, 0, 0).wait()
    hslab = d1 // MB

    @pl.loop(0, groups)
    def _(g):
        @pl.loop(0, steps)
        def _(i):
            for k in range(groups):
                for m in range(steps):
                    if plan["back", k, m]:

                        @pl.when((g == k) & (i == m))
                        def _():
                            at_point("back", k, m)

            slot, pair = i // gpairs, g * gpairs + i % gpairs
            slab = pl.ds(slot * hslab, hslab)
            lanes = pl.ds(pl.multiple_of(pair * 128, 128), 128)

            def get(s):
                return slots[s, slab, :, :, :, :, lanes].reshape(seq, 128)

            head = slot * (width // HEAD_DIM) + 2 * pair
            grads = attend_back(
                get(3), get(4), get(6), get(2), get(7), [lse[head], lse[head + 1]], [diag[0], diag[1 + slot]], seq
            )
            for s, value in zip((3, 4, 6), grads):
                slots[s, slab, :, :, :, :, lanes] = value.astype(BF).reshape(hslab, d2, d3, 2, per, 128)

        for k in range(groups):
            if plan["grads", k] or k == groups - 1:

                @pl.when(g == k)
                def _():
                    at_point("grads", k)
                    if k == groups - 1:
                        for move in w_third(2, stage.at[(fcs + groups - 1) % 2]):
                            move.start()

        mine = pl.ds(pl.multiple_of(g * gw, gw), gw)
        buffer = (fcs + 1 + g) % 2

        @pl.loop(0, 2)
        def _(i):
            col = pl.ds(pl.multiple_of(i * (width // 2), width // 2), width // 2)
            left = slots[0, :, :, :, :, :, col].reshape(rows, width // 2)
            for k, s in enumerate((3, 4, 6)):
                value = mm_tn(left, slots[s, :, :, :, :, :, mine].reshape(rows, gw)).astype(BF)
                stage[buffer, pl.ds(i * (d1 // 2), d1 // 2), :, :, :, :, k * gw : (k + 1) * gw] = value.reshape(
                    d1 // 2, d2, d3, 2, per, gw
                )

        for k in range(groups):

            @pl.when(g == k)
            def _():
                at_point("gqkv", k)

    thirds = (slots.at[1], slots.at[5], stage.at[(fcs + groups - 1) % 2])
    for k, target in enumerate(thirds):
        for move in w_third(k, target):
            move.wait()
    loadx.wait()
    blocks = d2 * d3 // d1

    @pl.loop(0, d1)
    def _(i):
        at = pl.ds(pl.multiple_of(i * tile, tile), tile)
        x_tile = wp[0, i // d3, i % d3] if blocks == 1 else wp[0, i]
        x_tile = x_tile.reshape(tile, width)
        grad = mm_nt(piece(3, i), whole(1)) + mm_nt(piece(4, i), whole(5)) + mm_nt(piece(6, i), thirds[2][...].reshape(rows, width))
        value, norms = norm_back(x_tile.astype(F32), stats[at, 0:2], vecs[0:1, :], grad)
        put(2, i, value + f_dh[at, :])
        gvec[0:1, :] += jnp.sum(norms, axis=0, keepdims=True)
        gvec[1:2, :] += jnp.sum(grad, axis=0, keepdims=True)
        gvec[2:3, :] += jnp.sum(piece(3, i).astype(F32), axis=0, keepdims=True)
        gvec[3:4, :] += jnp.sum(piece(6, i).astype(F32), axis=0, keepdims=True)
        for k in range(d1):
            if plan["dx", k]:

                @pl.when(i == k)
                def _():
                    at_point("dx", k)

    save = pltpu.make_async_copy(slots.at[2], dx_o, lsem.at[0])
    save.start()
    lines = [0.0] * (sstage.shape[-1] // 128)
    for v in range(8):
        lines[v * per // 128] += pack_vector(gvec[v : v + 1, :], v * per, per, n)
    some = n // fcs
    packed = [pack_vector(gfc[:, k * width : (k + 1) * width], 8 * per, per_fc, some) for k in range(fcs)]
    lines[8 * per // 128] += jnp.concatenate(packed, axis=0)
    for k, line in enumerate(lines):
        for d in range(n):
            at = (d // (d2 * d3 * 2), d // (d3 * 2) % d2, d // 2 % d3, d % 2)
            sstage[(*at, slice(None), slice(k * 128, (k + 1) * 128))] = line[d : d + 1, :]
    mine, theirs, found, s_sem, r_sem = refs
    if comm:
        swap = send(sstage.at[:, :, :, 1 - c], mine, s_sem.at[0], r_sem.at[0], place.to_p)
        swap.start()
        swap.wait()
        theirs[...] = mine[...] + sstage[:, :, :, c]
        sends = [
            send(theirs.at[z, y, x], found.at[k], s_sem.at[k + 1], r_sem.at[k + 1], device)
            for k, (z, y, x, device) in enumerate(place.others())
        ]
        for copy in sends:
            copy.start()
    at_point("end")
    if comm:
        for copy in sends:
            copy.wait()
        value = theirs[place.z, place.y, place.x]
        for k in range(len(sends)):
            value = value + found[k]
        g_small[...] = value
    save.wait()


def backward(dims, lens, tokens, saved, weights, groups, comm=True):
    vecs, h1, qkv, lse, ctx, r1, h2, gp, dy, terms, stats = saved
    rows, width = tokens.shape
    n = dims[0] * dims[1] * dims[2] * 2
    hidden = gp.shape[1]
    seq = rows // MB
    per, per_fc = width // n, hidden // n
    fcs = hidden // width
    projs = 4
    pw = width // projs
    lanes = (8 * per + per_fc + 127) // 128 * 128

    def six(a):
        return a.reshape(*dims, 2, a.shape[0] // n, a.shape[1])

    sds = jax.ShapeDtypeStruct
    scratch = [
        pltpu.VMEM((8, *dims, 2, per, width), BF),
        pltpu.VMEM((2, *dims[1:], 2, per_fc, width), BF),
        pltpu.VMEM((rows, width), F32),
        pltpu.VMEM((2, rows // dims[0], width), F32),
        pltpu.VMEM((8, width), F32),
        pltpu.VMEM((1, hidden), F32),
        pltpu.VMEM(lse.shape, F32),
        pltpu.VMEM((1 + MB, seq // 2, seq // 2), F32),
        pltpu.VMEM((2, *dims, 2, per, width), BF),
        pltpu.VMEM((2, *dims, per_fc, pw), BF),
        pltpu.VMEM((*dims, 2, 1, lanes), F32),
        DMA((8,)),
        DMA((2,)),
        DMA((2,)),
        DMA((3, groups)),
    ]
    sizes = []
    shapes = [(per_fc, pw)] * projs + [(per, width)] * (fcs + 1) + [(per, 3 * width // groups)] * groups
    for block_rows, block_cols in shapes:
        made = Reduce.scratch(dims, block_rows, block_cols, BF)
        sizes.append(len(made))
        scratch += made
    half_n = n // 2
    scratch += [pltpu.VMEM((*dims, 1, lanes), F32)] * 2 + [pltpu.VMEM((half_n - 1, 1, lanes), F32)]
    scratch += [DMA((half_n,)), DMA((half_n,))]
    outs = [
        sds((*dims, 2, per, width), BF),
        sds((per, 3 * width), F32),
        sds((per, width), F32),
        sds((per, hidden), F32),
        sds((per_fc, width), F32),
        sds((1, lanes), F32),
    ]
    return pl.pallas_call(
        lambda *refs: backward_kernel(dims, groups, sizes, comm, *refs),
        out_shape=outs,
        in_specs=[VMEM, ANY, ANY, VMEM, VMEM] + [ANY] * 12,
        out_specs=[ANY] + [VMEM] * 5,
        scratch_shapes=scratch,
        compiler_params=pltpu.CompilerParams(
            collective_id=1, has_side_effects=True, vmem_limit_bytes=67043328
        ),
        name="backward",
    )(lens, tokens.reshape(*dims[1:], 2, rows // (2 * dims[1] * dims[2]), width), six(dy), vecs, stats, six(h1), six(qkv), lse, six(ctx), r1, six(h2), six(gp), terms, *weights)


def finish_kernel(sizes, *refs):
    arrays, small = refs[:6], refs[6]
    results, vectors = refs[7:13], refs[13 : 13 + len(sizes)]
    rest = refs[13 + len(sizes) :]
    buffers, (sems_in, sems_out) = rest[:6], rest[6:]
    pieces = []
    for k, (array, result, buffer) in enumerate(zip(arrays, results, buffers)):
        parts = 4 if array.shape[0] >= 512 else 1
        rows = array.shape[0] // parts
        for part in range(parts):
            cut = pl.ds(part * rows, rows)
            at = len(pieces)
            pieces.append(
                (
                    pltpu.make_async_copy(array.at[cut], buffer.at[cut], sems_in.at[at]),
                    pltpu.make_async_copy(buffer.at[cut], result.at[cut], sems_out.at[at]),
                )
            )
    for load, _ in pieces:
        load.start()
    first = 0
    for size, vector in zip(sizes, vectors):
        vector[...] = small[:, first : first + size]
        first += size
    for load, store in pieces:
        load.wait()
        store.start()
    for _, store in pieces:
        store.wait()


def finish(arrays, small, sizes):
    sds = jax.ShapeDtypeStruct
    count = sum(4 if a.shape[0] >= 512 else 1 for a in arrays)
    made = pl.pallas_call(
        lambda *refs: finish_kernel(sizes, *refs),
        out_shape=[sds(a.shape, a.dtype) for a in arrays] + [sds((1, size), F32) for size in sizes],
        in_specs=[ANY] * 6 + [VMEM],
        out_specs=[ANY] * 6 + [VMEM] * len(sizes),
        scratch_shapes=[pltpu.VMEM(a.shape, a.dtype) for a in arrays] + [DMA((count,)), DMA((count,))],
        name="finish",
    )(*arrays, small)
    return made[:6], [vector.reshape(-1) for vector in made[6:]]


def body(dims, tokens, cotangent, seq_lengths, seq_place, ln1_gain, ln1_bias, w_qkv, q_bias, v_bias, w_out, out_bias, ln2_gain, ln2_bias, w_fc, fc_bias, w_proj, proj_bias):
    rows, width = tokens.shape
    n = dims[0] * dims[1] * dims[2] * 2
    hidden = fc_bias.shape[0] * n
    seq = rows // MB
    per, per_fc = width // n, hidden // n
    slots = lax.axis_index("dp") * MB + jnp.arange(MB, dtype=jnp.int32)
    lengths = jnp.sum(jnp.where(seq_place[None, :] == slots[:, None], seq_lengths[None, :], 0), axis=1)
    lens = jnp.broadcast_to(jnp.pad(lengths, (0, 8 - MB))[:, None], (8, 128)).astype(F32)

    vectors = (ln1_gain, ln1_bias, q_bias, v_bias, out_bias, ln2_gain, ln2_bias, proj_bias, fc_bias)
    small, first = 0.0, 0
    for vector in vectors:
        small = small + jnp.pad(vector.astype(F32), (first, 1024 - first - vector.shape[0]))
        first += vector.shape[0]
    small = small.reshape(8, 128)
    groups = 4
    chunks = [(0, i, 3 * width // groups) for i in range(0, 3 * width, 3 * width // groups)] + [(1, 0, width)]
    chunks += [(2, i, width) for i in range(0, hidden, width)]
    chunks += [(3, i, width // 4) for i in range(0, width, width // 4)]
    kinds = [0, 0, 0, 0, 0, 0, 1, 0, 1, 0, 1, 0, 1]
    made = forward(dims, lens, tokens, cotangent, (w_qkv, w_out, w_fc, w_proj), small, chunks, kinds)
    out = made[14]
    dx, g_qkv, g_out, g_fc, g_proj, small = backward(dims, lens, tokens, (*made[4:14], made[15]), made[:4], groups)
    sizes = [per] * 8 + [per_fc]
    arrays, own = finish((out, dx.reshape(rows, width), g_qkv, g_out, g_fc, g_proj), small, sizes)
    out, dx, g_qkv, g_out, g_fc, g_proj = arrays
    g_ln1_gain, g_ln1_bias, g_q_bias, g_v_bias, g_out_bias, g_ln2_gain, g_ln2_bias, g_proj_bias, g_fc_bias = own
    return (out, dx, g_ln1_gain, g_ln1_bias, g_qkv, g_q_bias, g_v_bias, g_out, g_out_bias, g_ln2_gain, g_ln2_bias, g_fc, g_fc_bias, g_proj, g_proj_bias)


def solution(mesh):
    dims = grid_dims(mesh.shape["dp"])
    row, vec = P("dp", None), P("dp")
    return jax.shard_map(
        lambda *args: body(dims, *args),
        mesh=mesh,
        in_specs=(row, row, P(), P(), vec, vec, row, vec, vec, row, vec, vec, vec, row, vec, row, vec),
        out_specs=(row, row, vec, vec, row, vec, vec, row, vec, vec, vec, row, vec, row, vec),
        check_vma=False,
    )
```

```python
import jax
import jax.numpy as jnp
from jax import lax
from jax.experimental import pallas as pl
from jax.experimental.pallas import tpu as pltpu
from jax.sharding import PartitionSpec as P

MESH = pl.DeviceIdType.MESH
ANY = pl.BlockSpec(memory_space=pl.ANY)
VMEM = pl.BlockSpec(memory_space=pltpu.VMEM)
DMA = pltpu.SemaphoreType.DMA


def grid_dims(n):
    half = n // 2
    first = 4 if half % 4 == 0 else half
    rest = half // first
    second = 1
    while second * second < rest:
        second *= 2
    return first, second, rest // second


class Place:
    def __init__(self, dims):
        self.dims = dims
        d1, d2, d3 = dims
        me = lax.axis_index("dp")
        self.z = me // (d2 * d3 * 2)
        self.y = (me // (d3 * 2)) % d2
        self.x = (me // 2) % d3
        self.c = me % 2
        self.zs = [(self.z + k) % d1 for k in range(1, d1)]
        self.ys = [(self.y + k) % d2 for k in range(1, d2)]
        self.xs = [(self.x + k) % d3 for k in range(1, d3)]
        self.to_z = [self.dev(z=v) for v in self.zs]
        self.to_y = [self.dev(y=v) for v in self.ys]
        self.to_x = [self.dev(x=v) for v in self.xs]
        self.to_p = self.dev(c=1 - self.c)

    def dev(self, **at):
        z, y, x, c = (at.get(name, getattr(self, name)) for name in "zyxc")
        _, d2, d3 = self.dims
        return (((z * d2 + y) * d3 + x) * 2 + c,)

    def others(self):
        d1, d2, d3 = self.dims
        found = []
        for i in range(1, d1 * d2 * d3):
            z, y, x = (self.z + i // (d2 * d3)) % d1, (self.y + i // d3 % d2) % d2, (self.x + i % d3) % d3
            found.append((z, y, x, self.dev(z=z, y=y, x=x)))
        return found

    def barrier(self, everyone=False):
        semaphore = pltpu.get_barrier_semaphore()
        peers = self.to_z + self.to_y + self.to_x
        if everyone:
            peers = [device for _, _, _, device in self.others()]
        peers = peers + [self.to_p]
        for peer in peers:
            pl.semaphore_signal(semaphore, inc=1, device_id=peer, device_id_type=MESH)
        pl.semaphore_wait(semaphore, len(peers))


def send(source, target, send_sem, recv_sem, device):
    return pltpu.make_async_remote_copy(
        src_ref=source,
        dst_ref=target,
        send_sem=send_sem,
        recv_sem=recv_sem,
        device_id=device,
        device_id_type=MESH,
    )


class Plan:
    def __init__(self, costs, follow):
        self.costs, self.follow = costs, follow
        self.now, self.free, self.flying, self.taken, self.table = 0.0, {}, [], set(), {}

    def issue(self, key, events):
        lane, cost = self.costs(key)
        begin = max(self.now, self.free.get(lane, 0.0))
        self.free[lane] = begin + cost
        self.flying.append((begin + cost + 1.0, key))
        self.flying.sort()
        events.append(("go", key))

    def pump(self, point, passed=0.0, start=(), force=()):
        self.now += passed
        events = self.table.setdefault(point, [])

        def take():
            when, key = self.flying.pop(0)
            self.now = max(self.now, when)
            self.taken.add(key)
            events.append(("take", key))
            for after in self.follow(key, self.taken):
                self.issue(after, events)

        while self.flying and self.flying[0][0] <= self.now:
            take()
        while any(key not in self.taken for key in force):
            take()
        for key in start:
            self.issue(key, events)


class Gather:
    AHEAD = 3

    def __init__(self, place, shards, wholes, chunks, kinds, sems):
        self.at, self.shards, self.wholes = place, shards, wholes
        self.chunks, self.kinds, self.sems = chunks, kinds, sems
        self.first = [first for first, _ in Gather.starts(place.dims, kinds)]

    @staticmethod
    def starts(dims, kinds):
        d1, d2, d3 = dims
        near, starts = d2 + d3 - 2, []
        for stage in range(4):
            at, first = 0, []
            for kind in kinds:
                first.append(at)
                at += ((d1 - 1, near, near, 1), (near, 2 * (d1 - 1), near, 1))[kind][stage]
            starts.append((first, at))
        return starts

    @staticmethod
    def semaphores(dims, kinds):
        return [DMA((size,)) for _, size in Gather.starts(dims, kinds) for _ in range(2)]

    @staticmethod
    def plan(chunks, kinds, unit):
        def costs(key):
            stage, t = key
            size = unit(t)
            if stage == 3:
                return "p", 1.4 * size
            over_z = stage == kinds[t]
            if over_z:
                return "z", (8 if kinds[t] else 4) * size
            return "xy", (0.5, 2, 4)[stage] * size

        def follow(key, taken):
            stage, t = key
            after = [] if stage == 3 else [(stage + 1, t)]
            if stage == 0:
                more = ((1, 2), (3, 4))[t] if t < 2 else (t + Gather.AHEAD,)
                after += [(0, m) for m in more if m < len(chunks)]
            return after

        return Plan(costs, follow)

    def copies(self, stage, t):
        p = self.at
        z, y, x, c = p.z, p.y, p.x, p.c
        i, first, width = self.chunks[t]
        whole, shard, half = self.wholes[i], self.shards[i], width // 2
        full = pl.ds(first, width)
        a, b = pl.ds(first, half), pl.ds(first + half, half)
        pieces = []
        if stage == 0 and self.kinds[t] == 0:
            pieces = [(shard.at[:, full], whole.at[z, y, x, c, :, full], d) for d in p.to_z]
        elif stage == 0:
            pieces = [(shard.at[:, a], whole.at[z, y, x, c, :, a], d) for d in p.to_x]
            pieces += [(shard.at[:, b], whole.at[z, y, x, c, :, b], d) for d in p.to_y]
        elif stage == 1 and self.kinds[t] == 0:
            part = whole.at[:, y, x, c, :, a]
            pieces = [(part, part, d) for d in p.to_x]
            part = whole.at[:, y, x, c, :, b]
            pieces += [(part, part, d) for d in p.to_y]
        elif stage == 1:
            left, right = whole.at[z, y, :, c, :, a], whole.at[z, :, x, c, :, b]
            pieces = [(part, part, d) for d in p.to_z for part in (left, right)]
        elif stage == 2:
            part = whole.at[:, y, :, c, :, a]
            pieces = [(part, part, d) for d in p.to_y]
            part = whole.at[:, :, x, c, :, b]
            pieces += [(part, part, d) for d in p.to_x]
        else:
            part = whole.at[:, :, :, c, :, full]
            pieces = [(part, part, p.to_p)]
        out, back = self.sems[2 * stage], self.sems[2 * stage + 1]
        first = self.first[stage][t]
        return [send(s, d, out.at[first + k], back.at[first + k], to) for k, (s, d, to) in enumerate(pieces)]

    def run(self, events):
        for what, (stage, t) in events:
            for copy in self.copies(stage, t):
                if what == "go":
                    copy.start()
                else:
                    copy.wait_recv()

    def finish(self):
        for stage in range(4):
            for t in range(len(self.chunks)):
                for copy in self.copies(stage, t):
                    copy.wait_send()


def small_copies(place, source, target, sems, stage):
    z, y, x, c = place.z, place.y, place.x, place.c
    d1, d2, d3 = place.dims
    if stage == 0:
        pieces = [(source, target.at[z, y, x, c], d) for d in place.to_z]
    elif stage == 1:
        part = target.at[:, y, x, c]
        pieces = [(part, part, d) for d in place.to_x]
    elif stage == 2:
        part = target.at[:, y, :, c]
        pieces = [(part, part, d) for d in place.to_y]
    else:
        part = target.at[:, :, :, c]
        pieces = [(part, part, place.to_p)]
    base = (0, d1, d1 + d3, d1 + d2 + d3)[stage]
    return [send(s, d, sems[0].at[base + k], sems[1].at[base + k], to) for k, (s, d, to) in enumerate(pieces)]


class Reduce:
    @staticmethod
    def scratch(dims, rows, width, dtype, halves=True):
        d1, d2, d3 = dims
        half = width // 2 if halves else width
        shapes = [pltpu.VMEM((d1, d2, d3, rows, width), dtype)]
        shapes.append(pltpu.VMEM((d2 - 1, d1, d3, rows, half), dtype))
        shapes.append(pltpu.VMEM((d3 - 1, d1, rows, half), dtype))
        if halves:
            shapes.append(pltpu.VMEM((d3 - 1, d1, d2, rows, half), dtype))
            shapes.append(pltpu.VMEM((d2 - 1, d1, rows, half), dtype))
        shapes.append(pltpu.VMEM((d1 - 1, rows, width), dtype))
        near = d2 + d3 - 2
        sizes = (1, near, near, d1 - 1) if halves else (1, d2 - 1, d3 - 1, d1 - 1)
        for size in sizes:
            shapes += [DMA((size,)), DMA((size,))]
        return shapes

    @staticmethod
    def plan(unit):
        def costs(key):
            stage, t = key
            return ("p", "xy", "xy", "z")[stage], (1.4, 4, 2, 4)[stage] * unit(t)

        def follow(key, taken):
            stage, t = key
            after = []
            if stage == 0 and (t < 2 or (1, t - 2) in taken):
                after.append((1, t))
            if stage == 1:
                if (0, t + 2) in taken:
                    after.append((1, t + 2))
                after.append((2, t))
            if stage == 2:
                after.append((3, t))
            return after

        return Plan(costs, follow)

    def __init__(self, place, refs, source, own, result, halves=True, load=None):
        self.at, self.halves, self.load = place, halves, load
        self.source, self.own, self.result = source, own, result
        if halves:
            self.total, self.ya, self.xa, self.xb, self.yb, self.zz = refs[:6]
            self.sems = refs[6:]
        else:
            self.total, self.ya, self.xa, self.zz = refs[:4]
            self.sems = refs[4:]
        width = self.total.shape[-1]
        half = width // 2 if halves else width
        self.a, self.b = pl.ds(0, half), pl.ds(half, half)

    def pieces(self, stage):
        p, h = self.at, self.total
        y, x = p.y, p.x
        if stage == 0:
            return [(self.source.at[:, :, :, 1 - p.c], h, p.to_p)]
        if stage == 1:
            made = [
                (h.at[:, v, :, :, self.a], self.ya.at[k], d)
                for k, (v, d) in enumerate(zip(p.ys, p.to_y))
            ]
            if self.halves:
                made += [
                    (h.at[:, :, v, :, self.b], self.xb.at[k], d)
                    for k, (v, d) in enumerate(zip(p.xs, p.to_x))
                ]
            return made
        if stage == 2:
            made = [
                (h.at[:, y, v, :, self.a], self.xa.at[k], d)
                for k, (v, d) in enumerate(zip(p.xs, p.to_x))
            ]
            if self.halves:
                made += [
                    (h.at[:, v, x, :, self.b], self.yb.at[k], d)
                    for k, (v, d) in enumerate(zip(p.ys, p.to_y))
                ]
            return made
        return [(h.at[v, y, x], self.zz.at[k], d) for k, (v, d) in enumerate(zip(p.zs, p.to_z))]

    def go(self, stage):
        for copy in self.copies(stage):
            copy.start()

    def copies(self, stage):
        out, back = self.sems[2 * stage], self.sems[2 * stage + 1]
        return [
            send(s, d, out.at[k], back.at[k], to) for k, (s, d, to) in enumerate(self.pieces(stage))
        ]

    def arrived(self, stage):
        for copy in self.copies(stage):
            copy.wait()

    def add(self, stage):
        p, h = self.at, self.total
        d1, d2, d3 = p.dims
        f32 = jnp.float32

        def into(at, terms):
            value = h[at].astype(f32)
            for term in terms:
                value = value + term.astype(f32)
            h[at] = value.astype(h.dtype)

        if stage == 0:

            @pl.loop(0, d1)
            def _(i):
                for j in range(d2):
                    for k in range(d3):
                        into((i, j, k), [self.own[i, j, k]])

        elif stage == 1:

            @pl.loop(0, d1)
            def _(i):
                for k in range(d3):
                    into(
                        (i, p.y, k, slice(None), self.a),
                        [self.ya[m, i, k] for m in range(d2 - 1)],
                    )
                if self.halves:
                    for j in range(d2):
                        into(
                            (i, j, p.x, slice(None), self.b),
                            [self.xb[m, i, j] for m in range(d3 - 1)],
                        )

        elif stage == 2:

            @pl.loop(0, d1)
            def _(i):
                into((i, p.y, p.x, slice(None), self.a), [self.xa[m, i] for m in range(d3 - 1)])
                if self.halves:
                    into(
                        (i, p.y, p.x, slice(None), self.b),
                        [self.yb[m, i] for m in range(d2 - 1)],
                    )

        else:
            value = h[p.z, p.y, p.x].astype(f32)
            for m in range(d1 - 1):
                value = value + self.zz[m].astype(f32)
            for cut, target in self.result:
                target[...] = value[:, cut]

    def take(self, stage):
        if stage == 0 and self.load is not None:
            self.load.wait()
        self.arrived(stage)
        self.add(stage)


HEAD_DIM = 64
MB = 2
EPS = 1e-05
BF = jnp.bfloat16
F32 = jnp.float32
NEG = -1e30
GELU_A = 0.044715
GELU_C = 0.7978845608028654


def mm(left, right):
    return lax.dot_general(left, right, (((1,), (0,)), ((), ())), preferred_element_type=F32)


def mm_nt(left, right):
    return lax.dot_general(left, right, (((1,), (1,)), ((), ())), preferred_element_type=F32)


def mm_tn(left, right):
    return lax.dot_general(left, right, (((0,), (0,)), ((), ())), preferred_element_type=F32)


def iota(shape, axis):
    return lax.broadcasted_iota(jnp.int32, shape, axis)


def unpack_vector(block, start, per, width, first):
    row0, lane0 = start // 128, start % 128
    rows = block.shape[0]
    column = iota((128, width), 1) + first
    pick = (iota((128, width), 0) - lane0 == column % per).astype(BF)
    spread = mm(block, pick)
    column = iota((rows, width), 1) + first
    mine = iota((rows, width), 0) == column // per * 8 + row0
    return jnp.sum(jnp.where(mine, spread, 0.0), axis=0, keepdims=True)


def moments(value, keep, first):
    mean = jnp.mean(value, axis=-1, keepdims=True)
    center = value - mean
    scale = lax.rsqrt(jnp.mean(center * center, axis=-1, keepdims=True) + EPS)
    keep[:, first : first + 1] = mean
    keep[:, first + 1 : first + 2] = scale
    return center, scale


def attend_pair(q2, k2, v2, masks, seq):
    half = seq // 2
    lane = iota((1, 128), 1) // HEAD_DIM
    vt = v2.T
    q2 = q2 * jnp.asarray(HEAD_DIM**-0.5, BF)
    ka, kb = k2[:half], k2[half:]
    sums, rows = [], []
    for head in range(2):
        qh = jnp.where(lane == head, q2, 0)
        va, vb = (vt[head * HEAD_DIM : (head + 1) * HEAD_DIM, i * half : (i + 1) * half] for i in range(2))
        first, second = qh[:half], qh[half:]
        s = mm_nt(ka, first) + masks[0]
        sa, sb = mm_nt(ka, second), mm_nt(kb, second) + masks[1]
        top = jnp.max(s, axis=0, keepdims=True)
        e = jnp.exp(s - top)
        total = jnp.sum(e, axis=0, keepdims=True)
        low = mm(va, e.astype(BF)) * (1.0 / total)
        logs = top + jnp.log(total)
        top = jnp.maximum(jnp.max(sa, axis=0, keepdims=True), jnp.max(sb, axis=0, keepdims=True))
        ea, eb = jnp.exp(sa - top), jnp.exp(sb - top)
        total = jnp.sum(ea, axis=0, keepdims=True) + jnp.sum(eb, axis=0, keepdims=True)
        high = (mm(va, ea.astype(BF)) + mm(vb, eb.astype(BF))) * (1.0 / total)
        rows.append(jnp.concatenate([low, high], axis=1))
        sums.append(jnp.concatenate([logs, top + jnp.log(total)], axis=1))
    return jnp.concatenate(rows, axis=0).T, sums


def forward_plan(chunks, kinds, groups, fcs, projs, steps):
    widest = max(width for i, _, width in chunks if i != 3)
    plan = Gather.plan(chunks, kinds, lambda t: 1.2 * (1.0 if chunks[t][0] == 3 else chunks[t][2] / widest))
    fetched, used = set(), set()

    def pump(point, passed=0.0, done=None, **rest):
        if done is not None:
            used.add(done)
        plan.pump(point, passed, **rest)
        for t in range(len(chunks)):
            first = t < 2 or (chunks[t][0] == 3) != (chunks[t - 2][0] == 3)
            if (3, t) in plan.taken and t not in fetched and (first or t - 2 in used):
                fetched.add(t)
                plan.table[point].append(("fetch", (3, t)))

    pump("begin", 0.0, start=[(0, 0)])
    for k in range(4):
        pump(("small", k), 2.0, force=[(k - 1, 0)] if 0 < k < 3 else ())
    pump("spread", 2.5, force=[(2, 0)])
    pump("norm", 2.0)
    for g in range(groups):
        pump(("qkv", g), 0.0, force=[(3, g)])
        pump(("scores", g), 2.4, done=g)
        for i in range(steps):
            pump(("attend", g, i), 0.0 if i == 0 else 1.6)
        pump(("group", g), 1.6)
    t = groups
    pump("out", 0.0, force=[(3, t)])
    for i in range(2):
        pump(("norm2", i), 2.1)
    used.add(t)
    for k in range(fcs):
        pump(("fc", k), 0.0, force=[(3, t + 1 + k)])
        for i in range(2):
            pump(("gelu", k, i), 2.4)
        used.add(t + 1 + k)
        pump(("terms", k), 2.9, force=[(3, t + 2 + k)])
    for k in range(projs):
        pump(("proj", k), 0.0, force=[(3, t + 1 + fcs + k)])
        pump(("done", k), 2.8, done=t + 1 + fcs + k)
    pump("end", 0.0, force=[(3, k) for k in range(len(chunks))])
    return plan.table


def forward_kernel(dims, chunks, kinds, comm, *refs):
    (lens, tokens, cot, s_qkv, s_out, s_fc, s_proj, small) = refs[:8]
    (w_qkv, w_out, w_fc, w_proj, vecs_o, h1_o, qkv_o, lse_o, ctx_o, r1_o, h2_o, gp_o, dy_o, terms_o, out_o, stats_o) = refs[8:24]
    (x_, dy, live, vecs, fcb, h1, qkv, ctx, lse, r1, h2, act, gp, out, sm, wbuf, pbuf, tbuf, diag, shuffled, stats) = refs[24:45]
    local, wsem, psem, osem, outsem, gpsem, tsem, shsem, s_sem, r_sem = refs[45:55]
    sems = refs[55:]
    rows, width = x_.shape
    seq = rows // MB
    hidden = act.shape[1]
    n = dims[0] * dims[1] * dims[2] * 2
    per, per_fc = width // n, hidden // n
    tile = 256
    tiles = rows // tile
    fcs = hidden // width
    groups = sum(i == 0 for i, _, _ in chunks)
    gw = width // groups
    pw = chunks[-1][2]
    projs = width // pw
    gpairs = gw // 128
    steps = MB * gpairs
    plan = forward_plan(chunks, kinds, groups, fcs, projs, steps)
    place = Place(dims)
    z, y, x, c = place.z, place.y, place.x, place.c
    shards = (shuffled, s_out, s_fc, s_proj)
    wholes = (w_qkv, w_out, w_fc, w_proj)
    gather = Gather(place, shards, wholes, chunks, kinds, sems)

    def at_point(*key):
        for event in plan[key[0] if len(key) == 1 else key]:
            if event[0] == "fetch":
                fetch(event[1][1]).start()
            elif comm:
                gather.run([event])

    def fetch(t):
        i, first, w = chunks[t]
        source = wholes[i].at[:, :, :, :, :, pl.ds(first, w)]
        if i == 3:
            return pltpu.make_async_copy(source, pbuf.at[t % 2], psem.at[t % 2])
        return pltpu.make_async_copy(source, wbuf.at[t % 2, :, :, :, :, :, pl.ds(0, w)], wsem.at[t % 2])

    saves = []

    def keep(source, target):
        save = pltpu.make_async_copy(source, target, osem.at[len(saves)])
        save.start()
        saves.append(save)

    shuffle = [
        pltpu.make_async_copy(
            s_qkv.at[:, pl.ds(k * width + g * gw, gw)], shuffled.at[:, pl.ds((3 * g + k) * gw, gw)], shsem.at[3 * g + k]
        )
        for g in range(groups)
        for k in range(3)
    ]
    for move in shuffle:
        move.start()
    loads = [pltpu.make_async_copy(tokens, x_, gpsem.at[0]), pltpu.make_async_copy(cot, dy, gpsem.at[1])]
    for move in loads:
        move.start()
    moves = [
        pltpu.make_async_copy(s, w.at[z, y, x, c], local.at[i])
        for i, (s, w) in enumerate(zip((*shards, small), (*wholes, sm)))
    ]
    for move in moves[1:]:
        move.start()
    place.barrier()
    for move in shuffle:
        move.wait()
    moves[0].start()
    tiny = [small_copies(place, small, sm, (s_sem, r_sem), stage) for stage in range(4)]
    half = seq // 2
    for stage in range(4):
        if comm:
            for copy in tiny[stage]:
                copy.start()
        if stage == 0:
            at_point("begin")
            for slot in range(MB):
                length = lens[slot : slot + 1, 0:1]
                live[slot * seq : (slot + 1) * seq, :] = jnp.where(iota((seq, 1), 0).astype(F32) < length, 1.0, 0.0)
                causal = iota((half, half), 0) <= iota((half, half), 1)
                late = (iota((half, half), 0) + half).astype(F32) < length
                diag[0] = jnp.where(causal, 0.0, NEG)
                diag[1 + slot] = jnp.where(causal & late, 0.0, NEG)
            for move in moves:
                move.wait()
        if stage == 1:
            loads[1].wait()
            vecs[8:16, :] = jnp.zeros((8, width), F32)

            @pl.loop(0, tiles)
            def _(i):
                at = pl.ds(pl.multiple_of(i * tile, tile), tile)
                value = jnp.where(live[at, :] > 0.5, dy[at, :].astype(F32), 0.0)
                dy[at, :] = value.astype(BF)
                vecs[8:9, :] += jnp.sum(value, axis=0, keepdims=True)

            keep(dy, dy_o)
        if comm:
            for copy in tiny[stage]:
                copy.wait_recv()
        at_point("small", stage)
    block = sm[...].reshape(n * 8, 128).astype(BF)
    for v in range(8):
        vecs[v : v + 1, :] = unpack_vector(block, v * per, per, width, 0)
    for part in range(fcs):
        fcb[:, part * width : (part + 1) * width] = unpack_vector(block, 8 * per, per_fc, width, part * width)
    at_point("spread")
    loads[0].wait()

    @pl.loop(0, rows // 128)
    def _(i):
        at = pl.ds(pl.multiple_of(i * 128, 128), 128)
        center, scale = moments(x_[at, :].astype(F32), stats.at[at, :], 0)
        h1[at, :] = (center * scale * vecs[0:1, :] + vecs[1:2, :]).astype(BF)

    keep(h1, h1_o)
    keep(vecs, vecs_o)
    at_point("norm")

    @pl.loop(0, groups)
    def _(g):
        for k in range(groups):

            @pl.when(g == k)
            def _():
                at_point("qkv", k)
                fetch(k).wait()

        first = pl.multiple_of(g * gw, gw)

        @pl.loop(0, tiles)
        def _(i):
            at = pl.ds(pl.multiple_of(i * tile, tile), tile)
            value = mm(h1[at, :], wbuf[g % 2, :, :, :, :, :, 0 : 3 * gw].reshape(width, 3 * gw))
            for k, bias in ((0, 2), (1, None), (2, 3)):
                part = value[:, k * gw : (k + 1) * gw]
                if bias is not None:
                    part = part + vecs[bias : bias + 1, pl.ds(first, gw)]
                qkv[at, pl.ds(k * width + first, gw)] = part.astype(BF)

        for k in range(groups):
            if plan["scores", k]:

                @pl.when(g == k)
                def _():
                    at_point("scores", k)

        @pl.loop(0, steps)
        def _(i):
            for k in range(groups):
                for m in range(steps):
                    if plan["attend", k, m]:

                        @pl.when((g == k) & (i == m))
                        def _():
                            at_point("attend", k, m)

            slot, pair = i // gpairs, g * gpairs + i % gpairs
            at = pl.ds(pl.multiple_of(slot * seq, seq), seq)
            col = pl.multiple_of(pair * 128, 128)
            value, sums = attend_pair(
                qkv[at, pl.ds(col, 128)],
                qkv[at, pl.ds(width + col, 128)],
                qkv[at, pl.ds(2 * width + col, 128)],
                [diag[0], diag[1 + slot]],
                seq,
            )
            ctx[at, pl.ds(col, 128)] = value.astype(BF)
            for head in range(2):
                lse[slot * (width // HEAD_DIM) + pair * 2 + head] = sums[head]

        for k in range(groups):
            if plan["group", k]:

                @pl.when(g == k)
                def _():
                    at_point("group", k)

    keep(qkv, qkv_o)
    keep(ctx, ctx_o)
    keep(lse, lse_o)
    t = groups
    at_point("out")
    fetch(t).wait()

    @pl.loop(0, tiles)
    def _(i):
        at = pl.ds(pl.multiple_of(i * tile, tile), tile)
        value = mm(ctx[at, :], wbuf[t % 2].reshape(width, width)) + vecs[4:5, :]
        value = value + x_[at, :].astype(F32)
        r1[at, :] = value
        center, scale = moments(value, stats.at[at, :], 2)
        h2[at, :] = (center * scale * vecs[5:6, :] + vecs[6:7, :]).astype(BF)
        for k in range(2):

            @pl.when(i == (k + 1) * tiles // 2 - 1)
            def _():
                at_point("norm2", k)

    keep(r1, r1_o)
    keep(h2, h2_o)
    keep(stats, stats_o)

    def keep_gp(k):
        return pltpu.make_async_copy(gp.at[k % 2], gp_o.at[:, pl.ds(pl.multiple_of(k * width, width), width)], gpsem.at[k % 2])

    def each(index, count, *name):
        for k in range(count):
            key = (*name, k)
            if plan[key]:

                @pl.when(index == k)
                def _():
                    at_point(*key)

    def keep_terms(k):
        return pltpu.make_async_copy(tbuf.at[k % 2], terms_o.at[k], tsem.at[k % 2])

    @pl.loop(0, fcs)
    def _(k):
        each(k, fcs, "fc")
        buffer = (groups + 1 + k) % 2
        for m in range(fcs):

            @pl.when(k == m)
            def _():
                fetch(groups + 1 + m).wait()

        @pl.when(k >= 2)
        def _():
            keep_gp(k - 2).wait()
            keep_terms(k - 2).wait()

        cut = pl.ds(pl.multiple_of(k * width, width), width)

        @pl.loop(0, 2)
        def _(i):
            for part in range(tiles // 2):
                at = pl.ds(pl.multiple_of((i * (tiles // 2) + part) * tile, tile), tile)
                u = mm(h2[at, :], wbuf[buffer].reshape(width, width)) + fcb[:, cut]
                square = u * u
                inner = u * (GELU_C + (GELU_C * GELU_A) * square)
                gate = 0.5 + 0.5 * jnp.tanh(inner)
                value = u * gate
                act[at, cut] = value.astype(BF)
                slope = gate + value * (2.0 - 2.0 * gate) * (GELU_C + (3.0 * GELU_C * GELU_A) * square)
                gp[k % 2, at, :] = slope.astype(BF)
            for n_k in range(fcs):
                for m in range(2):
                    if plan["gelu", n_k, m]:

                        @pl.when((k == n_k) & (i == m))
                        def _():
                            at_point("gelu", n_k, m)

        keep_gp(k).start()

        @pl.loop(0, 2)
        def _(i):
            some = pl.ds(pl.multiple_of(k * width + i * (width // 2), width // 2), width // 2)
            value = mm_tn(act[:, some], dy[...]).astype(BF)
            blocks = (dims[1] // 2, dims[2], 2, per_fc, width)
            tbuf[k % 2, pl.ds(i * blocks[0], blocks[0])] = value.reshape(blocks)

        keep_terms(k).start()
        each(k, fcs, "terms")

    def keep_out(k):
        cut = pl.ds(pl.multiple_of(k * pw, pw), pw)
        return pltpu.make_async_copy(out.at[:, cut], out_o.at[:, cut], outsem.at[k])

    @pl.loop(0, projs)
    def _(k):
        cut = pl.ds(pl.multiple_of(k * pw, pw), pw)
        buffer = (groups + 1 + fcs + k) % 2

        for m in range(projs):

            @pl.when(k == m)
            def _():
                at_point("proj", m)
                fetch(groups + 1 + fcs + m).wait()

        @pl.loop(0, tiles)
        def _(i):
            at = pl.ds(pl.multiple_of(i * tile, tile), tile)
            value = mm(act[at, :], pbuf[buffer].reshape(hidden, pw)) + (r1[at, cut] + vecs[7:8, cut])
            out[at, cut] = jnp.where(live[at, :] > 0.5, value, 0.0).astype(BF)

        keep_out(k).start()
        each(k, projs, "done")

    at_point("end")
    for k in range(max(fcs - 2, 0), fcs):
        keep_gp(k).wait()
    for k in range(max(fcs - 2, 0), fcs):
        keep_terms(k).wait()
    for k in range(projs):
        keep_out(k).wait()
    for save in saves:
        save.wait()
    if comm:
        gather.finish()
        for copies in tiny:
            for copy in copies:
                copy.wait_send()


def forward(dims, lens, tokens, cot, shards, small, chunks, kinds, comm=True):
    rows, width = tokens.shape
    n = dims[0] * dims[1] * dims[2] * 2
    hidden = shards[2].shape[1]
    heads = width // HEAD_DIM
    seq = rows // MB
    pw = chunks[-1][2]
    groups = sum(i == 0 for i, _, _ in chunks)
    sds = jax.ShapeDtypeStruct
    shapes = [sds((*dims, 2, *s.shape), s.dtype) for s in shards]
    shapes += [
        sds((16, width), F32),
        sds((rows, width), BF),
        sds((rows, 3 * width), BF),
        sds((MB * heads, 1, seq), F32),
        sds((rows, width), BF),
        sds((rows, width), F32),
        sds((rows, width), BF),
        sds((rows, hidden), BF),
        sds((rows, width), BF),
        sds((*dims, 2, hidden // n, width), BF),
        sds((rows, width), BF),
        sds((rows, 128), F32),
    ]
    scratch = [
        pltpu.VMEM((rows, width), BF),
        pltpu.VMEM((rows, width), BF),
        pltpu.VMEM((rows, 1), F32),
        pltpu.VMEM((16, width), F32),
        pltpu.VMEM((1, hidden), F32),
        pltpu.VMEM((rows, width), BF),
        pltpu.VMEM((rows, 3 * width), BF),
        pltpu.VMEM((rows, width), BF),
        pltpu.VMEM((MB * heads, 1, seq), F32),
        pltpu.VMEM((rows, width), F32),
        pltpu.VMEM((rows, width), BF),
        pltpu.VMEM((rows, hidden), BF),
        pltpu.VMEM((2, rows, width), BF),
        pltpu.VMEM((rows, width), BF),
        pltpu.VMEM((*dims, 2, *small.shape), small.dtype),
        pltpu.VMEM((2, *dims, 2, width // n, width), BF),
        pltpu.VMEM((2, *dims, 2, hidden // n, pw), BF),
        pltpu.VMEM((2, *dims[1:], 2, hidden // n, width), BF),
        pltpu.VMEM((1 + MB, seq // 2, seq // 2), F32),
        pltpu.VMEM(shards[0].shape, BF),
        pltpu.VMEM((rows, 128), F32),
        DMA((5,)),
        DMA((2,)),
        DMA((2,)),
        DMA((9,)),
        DMA((width // pw,)),
        DMA((2,)),
        DMA((2,)),
        DMA((3 * groups,)),
        DMA((sum(dims) + 1,)),
        DMA((sum(dims) + 1,)),
        *Gather.semaphores(dims, kinds),
    ]
    return pl.pallas_call(
        lambda *refs: forward_kernel(dims, chunks, kinds, comm, *refs),
        out_shape=shapes,
        in_specs=[VMEM, ANY, ANY, ANY] + [VMEM] * 4,
        out_specs=[ANY] * 16,
        scratch_shapes=scratch,
        compiler_params=pltpu.CompilerParams(
            collective_id=0, has_side_effects=True, vmem_limit_bytes=60 * 1024 * 1024
        ),
        name="forward",
    )(lens, tokens, cot, *shards, small)


def pack_vector(row, start, per, n):
    width = row.shape[1]
    pick = (iota((128, width), 0) - start % 128 == iota((128, width), 1) % per).astype(BF)
    mine = iota((n, width), 0) == iota((n, width), 1) // per
    total = 0.0
    for _ in range(3):
        part = row.astype(BF)
        row = row - part.astype(F32)
        total = total + mm_nt(jnp.where(mine, part.astype(F32), 0.0).astype(BF), pick)
    return total


def norm_back(value, kept, gain, grad):
    scale = kept[:, 1:2]
    normed = (value - kept[:, 0:1]) * scale
    scaled = grad * gain
    mean = jnp.mean(scaled, axis=-1, keepdims=True)
    cross = jnp.mean(scaled * normed, axis=-1, keepdims=True)
    return (scaled - mean - normed * cross) * scale, grad * normed


def attend_back(q2, k2, v2, o2, c2, lse, masks, seq):
    half = seq // 2
    lane = iota((1, 128), 1) // HEAD_DIM
    prod = o2.astype(F32) * c2.astype(F32)
    heads = (iota((8, 128), 1) // HEAD_DIM == iota((8, 128), 0)).astype(BF)
    high = prod.astype(BF)
    delta = mm_nt(heads, high) + mm_nt(heads, (prod - high.astype(F32)).astype(BF))
    kt = k2.T
    q2 = q2 * jnp.asarray(HEAD_DIM**-0.5, BF)
    cuts = (slice(0, half), slice(half, seq))
    dk, dv, dq = [0.0, 0.0], [0.0, 0.0], []
    for head in range(2):
        qh = jnp.where(lane == head, q2, 0)
        oh = jnp.where(lane == head, o2, 0)
        kh = kt[head * HEAD_DIM : (head + 1) * HEAD_DIM]
        parts = [0.0, 0.0]
        for key, query in ((0, 0), (0, 1), (1, 1)):
            qb, ob, cut = qh[cuts[query]], oh[cuts[query]], cuts[query]
            s = mm_nt(k2[cuts[key]], qb) - lse[head][:, cut]
            if key == query:
                s = s + masks[key]
            p = jnp.exp(s)
            dp = mm_nt(v2[cuts[key]], ob)
            ds = (p * (dp - delta[head : head + 1, cut])).astype(BF)
            dv[key] = dv[key] + mm(p.astype(BF), ob)
            dk[key] = dk[key] + mm(ds, qb)
            parts[query] = parts[query] + mm(kh[:, cuts[key]], ds)
        dq.append(jnp.concatenate(parts, axis=1))
    dq = jnp.concatenate(dq, axis=0).T * HEAD_DIM**-0.5
    return dq, jnp.concatenate(dk, axis=0), jnp.concatenate(dv, axis=0)


def backward_plan(projs, fcs, groups, steps, slabs):
    out = projs + fcs
    plan = Reduce.plan(lambda t: 1.45 if t <= out else 1.08)
    pump = plan.pump
    pump("start", 0.0, start=[(0, 0), (0, 1)])
    pump("loaded", 1.0)
    late = list(range(2, projs))
    for f in range(fcs):
        for name, passed in (("da", 3.2), ("dh", 2.9)):
            j = late.pop(0) if late else None
            force = [] if j is None else [(0, j - 2)]
            if name == "dh" and f >= 2:
                force.append((0, projs + f - 2))
            pump((name, f), passed, force=force, start=[] if j is None else [(0, j)])
        pump(("gfc", f), 2.9, start=[(0, projs + f)])
    for i in range(slabs):
        pump(("ln2", i), 2.0)
    pump("dctx", 3.0, force=[(0, out - 2)])
    pump("gout", 3.0, start=[(0, out)])
    for g in range(groups):
        for i in range(steps):
            pump(("back", g, i), 0.0 if i == 0 else 2.0)
        pump(("grads", g), 2.0, force=[(0, out - 1 + g)])
        pump(("gqkv", g), 2.2, start=[(0, out + 1 + g)])
    for i in range(slabs):
        pump(("dx", i), 3.4)
    pump("end", 4.0, force=[(3, t) for t in range(out + 1 + groups)])
    return plan.table


def backward_kernel(dims, groups, sizes, comm, *refs):
    (lens, tokens, dy, vecs, stats, h1_i, qkv_i, lse_i, ctx_i, r1_i, h2_i, gp_i, terms, w_qkv, w_out, w_fc, w_proj) = refs[:17]
    (dx_o, g_qkv, g_out, g_fc, g_proj, g_small) = refs[17:23]
    slots, wp, f_dh, f_r1, gvec, gfc, lse, diag, stage, owns, sstage = refs[23:34]
    lsem, wsem, osem, qsem = refs[34:38]
    refs = refs[38:]
    d1, d2, d3 = dims
    n = d1 * d2 * d3 * 2
    rows, width = f_dh.shape
    hidden = gfc.shape[1]
    seq = rows // MB
    half = seq // 2
    per, per_fc = width // n, hidden // n
    fcs = hidden // width
    gw = width // groups
    pw = owns.shape[-1]
    projs = width // pw
    tile = rows // d1
    gpairs = gw // 128
    steps = MB * gpairs
    place = Place(dims)
    c = place.c
    plan = backward_plan(projs, fcs, groups, steps, d1)
    sets = []
    for size in sizes:
        sets.append(refs[:size])
        refs = refs[size:]
    parts = []
    for j in range(projs):
        cut = pl.ds(j * pw, pw)
        own = owns.at[j % 2]
        move = pltpu.make_async_copy(terms.at[:, :, :, c, :, cut], own, osem.at[j % 2])
        result = [(slice(None), g_proj.at[:, cut])]
        parts.append(Reduce(place, sets[j], terms.at[:, :, :, :, :, cut], own, result, load=move))
    for f in range(fcs):
        result = [(slice(None), g_fc.at[:, pl.ds(f * width, width)])]
        parts.append(Reduce(place, sets[projs + f], stage.at[f % 2], stage.at[f % 2, :, :, :, c], result))
    b = fcs % 2
    parts.append(Reduce(place, sets[projs + fcs], stage.at[b], stage.at[b, :, :, :, c], [(slice(None), g_out)]))
    gcut = pl.ds(0, 3 * gw)
    for g in range(groups):
        b = (fcs + 1 + g) % 2
        result = [
            (slice(k * gw, (k + 1) * gw), g_qkv.at[:, pl.ds(k * width + g * gw, gw)]) for k in range(3)
        ]
        source, own = stage.at[b, :, :, :, :, :, gcut], stage.at[b, :, :, :, c, :, gcut]
        parts.append(Reduce(place, sets[projs + fcs + 1 + g], source, own, result))

    def at_point(*key):
        if not comm:
            return
        for what, (step, t) in plan[key[0] if len(key) == 1 else key]:
            if what == "take":
                parts[t].take(step)
            else:
                parts[t].go(step)
                if step == 0 and parts[t].load is not None:
                    parts[t].load.start()

    def load(source, slot, k):
        return pltpu.make_async_copy(source, slots.at[slot], lsem.at[k])

    def cols(source, k):
        return source.at[:, :, :, :, :, pl.ds(pl.multiple_of(k * width, width), width)]

    def whole(slot):
        return slots[slot].reshape(rows, width)

    def piece(slot, i):
        return slots[slot, i].reshape(tile, width)

    def put(slot, i, value):
        slots[slot, i] = value.astype(BF).reshape(d2, d3, 2, per, width)

    def fetch_proj(f):
        return pltpu.make_async_copy(w_proj.at[f], wp.at[f % 2], wsem.at[f % 2])

    def fetch_ff(f):
        return [fetch_proj(f), load(cols(gp_i, f), 3 + f % 2, 3 + f % 2), load(cols(w_fc, f), 1 + f % 2, 1 + f % 2)]

    def w_third(k, target):
        return [
            pltpu.make_async_copy(
                w_qkv.at[:, :, :, :, :, pl.ds((3 * g + k) * gw, gw)],
                target.at[:, :, :, :, :, pl.ds(g * gw, gw)],
                qsem.at[k, g],
            )
            for g in range(groups)
        ]

    load(dy, 0, 0).start()
    for move in fetch_ff(0):
        move.start()
    load(h2_i, 6, 6).start()
    load(ctx_i, 7, 7).start()
    lload = pltpu.make_async_copy(lse_i, lse, lsem.at[5])
    lload.start()
    for slot in range(MB):
        causal = iota((half, half), 0) <= iota((half, half), 1)
        late = (iota((half, half), 0) + half).astype(F32) < lens[slot : slot + 1, 0:1]
        diag[0] = jnp.where(causal, 0.0, NEG)
        diag[1 + slot] = jnp.where(causal & late, 0.0, NEG)
    gvec[...] = jnp.zeros_like(gvec)
    gfc[...] = jnp.zeros_like(gfc)
    f_dh[...] = jnp.zeros_like(f_dh)
    gvec[7:8, :] = vecs[8:9, :]
    place.barrier(everyone=True)
    at_point("start")
    load(dy, 0, 0).wait()
    at_point("loaded")
    load(h2_i, 6, 6).wait()

    def each(index, count, *name):
        for k in range(count):
            key = (*name, k)
            if plan[key]:

                @pl.when(index == k)
                def _():
                    at_point(*key)

    @pl.loop(0, fcs)
    def _(f):
        for move in fetch_ff(f):
            move.wait()

        @pl.when(f + 1 < fcs)
        def _():
            for move in fetch_ff(f + 1):
                move.start()

        cut = pl.ds(pl.multiple_of(f * width, width), width)

        @pl.loop(0, d1 // 2)
        def _(h):
            for i in (2 * h, 2 * h + 1):
                da = mm_nt(piece(0, i), wp[f % 2].reshape(rows, width))
                du = (da * piece(3 + f % 2, i).astype(F32)).astype(BF)
                put(5, i, du)
                gfc[:, cut] += jnp.sum(du.astype(F32), axis=0, keepdims=True)

        each(f, fcs, "da")

        @pl.loop(0, d1 // 2)
        def _(h):
            for i in (2 * h, 2 * h + 1):
                at = pl.ds(pl.multiple_of(i * tile, tile), tile)
                f_dh[at, :] += mm_nt(piece(5, i), whole(1 + f % 2))

        each(f, fcs, "dh")

        @pl.loop(0, 2)
        def _(i):
            col = pl.ds(pl.multiple_of(i * (width // 2), width // 2), width // 2)
            value = mm_tn(slots[6, :, :, :, :, :, col].reshape(rows, width // 2), whole(5)).astype(BF)
            stage[f % 2, pl.ds(i * (d1 // 2), d1 // 2)] = value.reshape(d1 // 2, d2, d3, 2, per, width)

        each(f, fcs, "gfc")

    def r1_tile(i):
        return pltpu.make_async_copy(r1_i.at[pl.ds(i * tile, tile)], f_r1.at[i % 2], wsem.at[i % 2])

    r1_tile(0).start()
    load(w_out, 1, 1).start()
    for k, slot in enumerate((3, 4, 6)):
        load(cols(qkv_i, k), slot, slot).start()

    @pl.loop(0, d1)
    def _(i):
        r1_tile(i).wait()

        @pl.when(i + 1 < d1)
        def _():
            r1_tile(i + 1).start()

        at = pl.ds(pl.multiple_of(i * tile, tile), tile)
        grad = f_dh[at, :]
        value, norms = norm_back(f_r1[i % 2], stats[at, 2:4], vecs[5:6, :], grad)
        value = value + piece(0, i).astype(F32)
        f_dh[at, :] = value
        low = value.astype(BF)
        put(5, i, low)
        gvec[5:6, :] += jnp.sum(norms, axis=0, keepdims=True)
        gvec[6:7, :] += jnp.sum(grad, axis=0, keepdims=True)
        gvec[4:5, :] += jnp.sum(low.astype(F32), axis=0, keepdims=True)
        for k in range(d1):
            if plan["ln2", k]:

                @pl.when(i == k)
                def _():
                    at_point("ln2", k)

    load(ctx_i, 7, 7).wait()
    load(w_out, 1, 1).wait()
    load(h1_i, 0, 0).start()

    @pl.loop(0, d1)
    def _(i):
        put(2, i, mm_nt(piece(5, i), whole(1)))

    for move in w_third(0, slots.at[1]):
        move.start()
    at_point("dctx")

    @pl.loop(0, 2)
    def _(i):
        col = pl.ds(pl.multiple_of(i * (width // 2), width // 2), width // 2)
        value = mm_tn(slots[7, :, :, :, :, :, col].reshape(rows, width // 2), whole(5)).astype(BF)
        stage[fcs % 2, pl.ds(i * (d1 // 2), d1 // 2)] = value.reshape(d1 // 2, d2, d3, 2, per, width)

    for move in w_third(1, slots.at[5]):
        move.start()
    loadx = pltpu.make_async_copy(tokens, wp.at[0], lsem.at[2])
    loadx.start()
    at_point("gout")
    for k, slot in enumerate((3, 4, 6)):
        load(cols(qkv_i, k), slot, slot).wait()
    lload.wait()
    load(h1_i, 0, 0).wait()
    hslab = d1 // MB

    @pl.loop(0, groups)
    def _(g):
        @pl.loop(0, steps)
        def _(i):
            for k in range(groups):
                for m in range(steps):
                    if plan["back", k, m]:

                        @pl.when((g == k) & (i == m))
                        def _():
                            at_point("back", k, m)

            slot, pair = i // gpairs, g * gpairs + i % gpairs
            slab = pl.ds(slot * hslab, hslab)
            lanes = pl.ds(pl.multiple_of(pair * 128, 128), 128)

            def get(s):
                return slots[s, slab, :, :, :, :, lanes].reshape(seq, 128)

            head = slot * (width // HEAD_DIM) + 2 * pair
            grads = attend_back(
                get(3), get(4), get(6), get(2), get(7), [lse[head], lse[head + 1]], [diag[0], diag[1 + slot]], seq
            )
            for s, value in zip((3, 4, 6), grads):
                slots[s, slab, :, :, :, :, lanes] = value.astype(BF).reshape(hslab, d2, d3, 2, per, 128)

        for k in range(groups):
            if plan["grads", k] or k == groups - 1:

                @pl.when(g == k)
                def _():
                    at_point("grads", k)
                    if k == groups - 1:
                        for move in w_third(2, stage.at[(fcs + groups - 1) % 2]):
                            move.start()

        mine = pl.ds(pl.multiple_of(g * gw, gw), gw)
        buffer = (fcs + 1 + g) % 2

        @pl.loop(0, 2)
        def _(i):
            col = pl.ds(pl.multiple_of(i * (width // 2), width // 2), width // 2)
            left = slots[0, :, :, :, :, :, col].reshape(rows, width // 2)
            for k, s in enumerate((3, 4, 6)):
                value = mm_tn(left, slots[s, :, :, :, :, :, mine].reshape(rows, gw)).astype(BF)
                stage[buffer, pl.ds(i * (d1 // 2), d1 // 2), :, :, :, :, k * gw : (k + 1) * gw] = value.reshape(
                    d1 // 2, d2, d3, 2, per, gw
                )

        for k in range(groups):

            @pl.when(g == k)
            def _():
                at_point("gqkv", k)

    thirds = (slots.at[1], slots.at[5], stage.at[(fcs + groups - 1) % 2])
    for k, target in enumerate(thirds):
        for move in w_third(k, target):
            move.wait()
    loadx.wait()
    blocks = d2 * d3 // d1

    @pl.loop(0, d1)
    def _(i):
        at = pl.ds(pl.multiple_of(i * tile, tile), tile)
        x_tile = wp[0, i // d3, i % d3] if blocks == 1 else wp[0, i]
        x_tile = x_tile.reshape(tile, width)
        grad = mm_nt(piece(3, i), whole(1)) + mm_nt(piece(4, i), whole(5)) + mm_nt(piece(6, i), thirds[2][...].reshape(rows, width))
        value, norms = norm_back(x_tile.astype(F32), stats[at, 0:2], vecs[0:1, :], grad)
        put(2, i, value + f_dh[at, :])
        gvec[0:1, :] += jnp.sum(norms, axis=0, keepdims=True)
        gvec[1:2, :] += jnp.sum(grad, axis=0, keepdims=True)
        gvec[2:3, :] += jnp.sum(piece(3, i).astype(F32), axis=0, keepdims=True)
        gvec[3:4, :] += jnp.sum(piece(6, i).astype(F32), axis=0, keepdims=True)
        for k in range(d1):
            if plan["dx", k]:

                @pl.when(i == k)
                def _():
                    at_point("dx", k)

    save = pltpu.make_async_copy(slots.at[2], dx_o, lsem.at[0])
    save.start()
    lines = [0.0] * (sstage.shape[-1] // 128)
    for v in range(8):
        lines[v * per // 128] += pack_vector(gvec[v : v + 1, :], v * per, per, n)
    some = n // fcs
    packed = [pack_vector(gfc[:, k * width : (k + 1) * width], 8 * per, per_fc, some) for k in range(fcs)]
    lines[8 * per // 128] += jnp.concatenate(packed, axis=0)
    for k, line in enumerate(lines):
        for d in range(n):
            at = (d // (d2 * d3 * 2), d // (d3 * 2) % d2, d // 2 % d3, d % 2)
            sstage[(*at, slice(None), slice(k * 128, (k + 1) * 128))] = line[d : d + 1, :]
    mine, theirs, found, s_sem, r_sem = refs
    if comm:
        swap = send(sstage.at[:, :, :, 1 - c], mine, s_sem.at[0], r_sem.at[0], place.to_p)
        swap.start()
        swap.wait()
        theirs[...] = mine[...] + sstage[:, :, :, c]
        sends = [
            send(theirs.at[z, y, x], found.at[k], s_sem.at[k + 1], r_sem.at[k + 1], device)
            for k, (z, y, x, device) in enumerate(place.others())
        ]
        for copy in sends:
            copy.start()
    at_point("end")
    if comm:
        for copy in sends:
            copy.wait()
        value = theirs[place.z, place.y, place.x]
        for k in range(len(sends)):
            value = value + found[k]
        g_small[...] = value
    save.wait()


def backward(dims, lens, tokens, saved, weights, groups, comm=True):
    vecs, h1, qkv, lse, ctx, r1, h2, gp, dy, terms, stats = saved
    rows, width = tokens.shape
    n = dims[0] * dims[1] * dims[2] * 2
    hidden = gp.shape[1]
    seq = rows // MB
    per, per_fc = width // n, hidden // n
    fcs = hidden // width
    projs = 4
    pw = width // projs
    lanes = (8 * per + per_fc + 127) // 128 * 128

    def six(a):
        return a.reshape(*dims, 2, a.shape[0] // n, a.shape[1])

    sds = jax.ShapeDtypeStruct
    scratch = [
        pltpu.VMEM((8, *dims, 2, per, width), BF),
        pltpu.VMEM((2, *dims[1:], 2, per_fc, width), BF),
        pltpu.VMEM((rows, width), F32),
        pltpu.VMEM((2, rows // dims[0], width), F32),
        pltpu.VMEM((8, width), F32),
        pltpu.VMEM((1, hidden), F32),
        pltpu.VMEM(lse.shape, F32),
        pltpu.VMEM((1 + MB, seq // 2, seq // 2), F32),
        pltpu.VMEM((2, *dims, 2, per, width), BF),
        pltpu.VMEM((2, *dims, per_fc, pw), BF),
        pltpu.VMEM((*dims, 2, 1, lanes), F32),
        DMA((8,)),
        DMA((2,)),
        DMA((2,)),
        DMA((3, groups)),
    ]
    sizes = []
    shapes = [(per_fc, pw)] * projs + [(per, width)] * (fcs + 1) + [(per, 3 * width // groups)] * groups
    for block_rows, block_cols in shapes:
        made = Reduce.scratch(dims, block_rows, block_cols, BF)
        sizes.append(len(made))
        scratch += made
    half_n = n // 2
    scratch += [pltpu.VMEM((*dims, 1, lanes), F32)] * 2 + [pltpu.VMEM((half_n - 1, 1, lanes), F32)]
    scratch += [DMA((half_n,)), DMA((half_n,))]
    outs = [
        sds((*dims, 2, per, width), BF),
        sds((per, 3 * width), F32),
        sds((per, width), F32),
        sds((per, hidden), F32),
        sds((per_fc, width), F32),
        sds((1, lanes), F32),
    ]
    return pl.pallas_call(
        lambda *refs: backward_kernel(dims, groups, sizes, comm, *refs),
        out_shape=outs,
        in_specs=[VMEM, ANY, ANY, VMEM, VMEM] + [ANY] * 12,
        out_specs=[ANY] + [VMEM] * 5,
        scratch_shapes=scratch,
        compiler_params=pltpu.CompilerParams(
            collective_id=1, has_side_effects=True, vmem_limit_bytes=67043328
        ),
        name="backward",
    )(lens, tokens.reshape(*dims[1:], 2, rows // (2 * dims[1] * dims[2]), width), six(dy), vecs, stats, six(h1), six(qkv), lse, six(ctx), r1, six(h2), six(gp), terms, *weights)


def finish_kernel(sizes, *refs):
    arrays, small = refs[:6], refs[6]
    results, vectors = refs[7:13], refs[13 : 13 + len(sizes)]
    rest = refs[13 + len(sizes) :]
    buffers, (sems_in, sems_out) = rest[:6], rest[6:]
    pieces = []
    for k, (array, result, buffer) in enumerate(zip(arrays, results, buffers)):
        parts = 4 if array.shape[0] >= 512 else 1
        rows = array.shape[0] // parts
        for part in range(parts):
            cut = pl.ds(part * rows, rows)
            at = len(pieces)
            pieces.append(
                (
                    pltpu.make_async_copy(array.at[cut], buffer.at[cut], sems_in.at[at]),
                    pltpu.make_async_copy(buffer.at[cut], result.at[cut], sems_out.at[at]),
                )
            )
    for load, _ in pieces:
        load.start()
    first = 0
    for size, vector in zip(sizes, vectors):
        vector[...] = small[:, first : first + size]
        first += size
    for load, store in pieces:
        load.wait()
        store.start()
    for _, store in pieces:
        store.wait()


def finish(arrays, small, sizes):
    sds = jax.ShapeDtypeStruct
    count = sum(4 if a.shape[0] >= 512 else 1 for a in arrays)
    made = pl.pallas_call(
        lambda *refs: finish_kernel(sizes, *refs),
        out_shape=[sds(a.shape, a.dtype) for a in arrays] + [sds((1, size), F32) for size in sizes],
        in_specs=[ANY] * 6 + [VMEM],
        out_specs=[ANY] * 6 + [VMEM] * len(sizes),
        scratch_shapes=[pltpu.VMEM(a.shape, a.dtype) for a in arrays] + [DMA((count,)), DMA((count,))],
        name="finish",
    )(*arrays, small)
    return made[:6], [vector.reshape(-1) for vector in made[6:]]


def body(dims, tokens, cotangent, seq_lengths, seq_place, ln1_gain, ln1_bias, w_qkv, q_bias, v_bias, w_out, out_bias, ln2_gain, ln2_bias, w_fc, fc_bias, w_proj, proj_bias):
    rows, width = tokens.shape
    n = dims[0] * dims[1] * dims[2] * 2
    hidden = fc_bias.shape[0] * n
    seq = rows // MB
    per, per_fc = width // n, hidden // n
    slots = lax.axis_index("dp") * MB + iota((seq_place.shape[0], 8, 128), 1)
    lens = jnp.where(seq_place[:, None, None] == slots, seq_lengths[:, None, None], 0)
    lens = jnp.sum(lens, axis=0).astype(F32)

    vectors = (ln1_gain, ln1_bias, q_bias, v_bias, out_bias, ln2_gain, ln2_bias, proj_bias, fc_bias)
    small, first = 0.0, 0
    for vector in vectors:
        small = small + jnp.pad(vector.astype(F32), (first, 1024 - first - vector.shape[0]))
        first += vector.shape[0]
    small = small.reshape(8, 128)
    groups = 4
    chunks = [(0, i, 3 * width // groups) for i in range(0, 3 * width, 3 * width // groups)] + [(1, 0, width)]
    chunks += [(2, i, width) for i in range(0, hidden, width)]
    chunks += [(3, i, width // 4) for i in range(0, width, width // 4)]
    kinds = [0, 0, 0, 0, 0, 0, 1, 0, 1, 0, 1, 0, 1]
    made = forward(dims, lens, tokens, cotangent, (w_qkv, w_out, w_fc, w_proj), small, chunks, kinds)
    out = made[14]
    dx, g_qkv, g_out, g_fc, g_proj, small = backward(dims, lens, tokens, (*made[4:14], made[15]), made[:4], groups)
    sizes = [per] * 8 + [per_fc]
    arrays, own = finish((out, dx.reshape(rows, width), g_qkv, g_out, g_fc, g_proj), small, sizes)
    out, dx, g_qkv, g_out, g_fc, g_proj = arrays
    g_ln1_gain, g_ln1_bias, g_q_bias, g_v_bias, g_out_bias, g_ln2_gain, g_ln2_bias, g_proj_bias, g_fc_bias = own
    return (out, dx, g_ln1_gain, g_ln1_bias, g_qkv, g_q_bias, g_v_bias, g_out, g_out_bias, g_ln2_gain, g_ln2_bias, g_fc, g_fc_bias, g_proj, g_proj_bias)


def solution(mesh):
    dims = grid_dims(mesh.shape["dp"])
    row, vec = P("dp", None), P("dp")
    return jax.shard_map(
        lambda *args: body(dims, *args),
        mesh=mesh,
        in_specs=(row, row, P(), P(), vec, vec, row, vec, vec, row, vec, vec, vec, row, vec, row, vec),
        out_specs=(row, row, vec, vec, row, vec, vec, row, vec, vec, vec, row, vec, row, vec),
        check_vma=False,
    )
```

```python
import jax
import jax.numpy as jnp
from jax import lax
from jax.experimental import pallas as pl
from jax.experimental.pallas import tpu as pltpu
from jax.sharding import PartitionSpec as P

MESH = pl.DeviceIdType.MESH
ANY = pl.BlockSpec(memory_space=pl.ANY)
VMEM = pl.BlockSpec(memory_space=pltpu.VMEM)
DMA = pltpu.SemaphoreType.DMA


def grid_dims(n):
    half = n // 2
    first = 4 if half % 4 == 0 else half
    rest = half // first
    second = 1
    while second * second < rest:
        second *= 2
    return first, second, rest // second


class Place:
    def __init__(self, dims):
        self.dims = dims
        d1, d2, d3 = dims
        me = lax.axis_index("dp")
        self.z = me // (d2 * d3 * 2)
        self.y = (me // (d3 * 2)) % d2
        self.x = (me // 2) % d3
        self.c = me % 2
        self.zs = [(self.z + k) % d1 for k in range(1, d1)]
        self.ys = [(self.y + k) % d2 for k in range(1, d2)]
        self.xs = [(self.x + k) % d3 for k in range(1, d3)]
        self.to_z = [self.dev(z=v) for v in self.zs]
        self.to_y = [self.dev(y=v) for v in self.ys]
        self.to_x = [self.dev(x=v) for v in self.xs]
        self.to_p = self.dev(c=1 - self.c)

    def dev(self, **at):
        z, y, x, c = (at.get(name, getattr(self, name)) for name in "zyxc")
        _, d2, d3 = self.dims
        return (((z * d2 + y) * d3 + x) * 2 + c,)

    def others(self):
        d1, d2, d3 = self.dims
        found = []
        for i in range(1, d1 * d2 * d3):
            z, y, x = (self.z + i // (d2 * d3)) % d1, (self.y + i // d3 % d2) % d2, (self.x + i % d3) % d3
            found.append((z, y, x, self.dev(z=z, y=y, x=x)))
        return found

    def barrier(self, everyone=False):
        semaphore = pltpu.get_barrier_semaphore()
        peers = self.to_z + self.to_y + self.to_x
        if everyone:
            peers = [device for _, _, _, device in self.others()]
        peers = peers + [self.to_p]
        for peer in peers:
            pl.semaphore_signal(semaphore, inc=1, device_id=peer, device_id_type=MESH)
        pl.semaphore_wait(semaphore, len(peers))


def send(source, target, send_sem, recv_sem, device):
    return pltpu.make_async_remote_copy(
        src_ref=source,
        dst_ref=target,
        send_sem=send_sem,
        recv_sem=recv_sem,
        device_id=device,
        device_id_type=MESH,
    )


class Plan:
    def __init__(self, costs, follow):
        self.costs, self.follow = costs, follow
        self.now, self.free, self.flying, self.taken, self.table = 0.0, {}, [], set(), {}

    def issue(self, key, events):
        lane, cost = self.costs(key)
        begin = max(self.now, self.free.get(lane, 0.0))
        self.free[lane] = begin + cost
        self.flying.append((begin + cost + 1.0, key))
        self.flying.sort()
        events.append(("go", key))

    def pump(self, point, passed=0.0, start=(), force=()):
        self.now += passed
        events = self.table.setdefault(point, [])

        def take():
            when, key = self.flying.pop(0)
            self.now = max(self.now, when)
            self.taken.add(key)
            events.append(("take", key))
            for after in self.follow(key, self.taken):
                self.issue(after, events)

        while self.flying and self.flying[0][0] <= self.now:
            take()
        while any(key not in self.taken for key in force):
            take()
        for key in start:
            self.issue(key, events)


class Gather:
    AHEAD = 3

    def __init__(self, place, shards, wholes, chunks, kinds, sems):
        self.at, self.shards, self.wholes = place, shards, wholes
        self.chunks, self.kinds, self.sems = chunks, kinds, sems
        self.first = [first for first, _ in Gather.starts(place.dims, kinds)]

    @staticmethod
    def starts(dims, kinds):
        d1, d2, d3 = dims
        near, starts = d2 + d3 - 2, []
        for stage in range(4):
            at, first = 0, []
            for kind in kinds:
                first.append(at)
                at += ((d1 - 1, near, near, 1), (near, 2 * (d1 - 1), near, 1))[kind][stage]
            starts.append((first, at))
        return starts

    @staticmethod
    def semaphores(dims, kinds):
        return [DMA((size,)) for _, size in Gather.starts(dims, kinds) for _ in range(2)]

    @staticmethod
    def plan(chunks, kinds, unit):
        def costs(key):
            stage, t = key
            size = unit(t)
            if stage == 3:
                return "p", 1.4 * size
            over_z = stage == kinds[t]
            if over_z:
                return "z", (8 if kinds[t] else 4) * size
            return "xy", (0.5, 2, 4)[stage] * size

        def follow(key, taken):
            stage, t = key
            after = [] if stage == 3 else [(stage + 1, t)]
            if stage == 0:
                more = ((1, 2), (3, 4))[t] if t < 2 else (t + Gather.AHEAD,)
                after += [(0, m) for m in more if m < len(chunks)]
            return after

        return Plan(costs, follow)

    def copies(self, stage, t):
        p = self.at
        z, y, x, c = p.z, p.y, p.x, p.c
        i, first, width = self.chunks[t]
        whole, shard, half = self.wholes[i], self.shards[i], width // 2
        full = pl.ds(first, width)
        a, b = pl.ds(first, half), pl.ds(first + half, half)
        pieces = []
        if stage == 0 and self.kinds[t] == 0:
            pieces = [(shard.at[:, full], whole.at[z, y, x, c, :, full], d) for d in p.to_z]
        elif stage == 0:
            pieces = [(shard.at[:, a], whole.at[z, y, x, c, :, a], d) for d in p.to_x]
            pieces += [(shard.at[:, b], whole.at[z, y, x, c, :, b], d) for d in p.to_y]
        elif stage == 1 and self.kinds[t] == 0:
            part = whole.at[:, y, x, c, :, a]
            pieces = [(part, part, d) for d in p.to_x]
            part = whole.at[:, y, x, c, :, b]
            pieces += [(part, part, d) for d in p.to_y]
        elif stage == 1:
            left, right = whole.at[z, y, :, c, :, a], whole.at[z, :, x, c, :, b]
            pieces = [(part, part, d) for d in p.to_z for part in (left, right)]
        elif stage == 2:
            part = whole.at[:, y, :, c, :, a]
            pieces = [(part, part, d) for d in p.to_y]
            part = whole.at[:, :, x, c, :, b]
            pieces += [(part, part, d) for d in p.to_x]
        else:
            part = whole.at[:, :, :, c, :, full]
            pieces = [(part, part, p.to_p)]
        out, back = self.sems[2 * stage], self.sems[2 * stage + 1]
        first = self.first[stage][t]
        return [send(s, d, out.at[first + k], back.at[first + k], to) for k, (s, d, to) in enumerate(pieces)]

    def run(self, events):
        for what, (stage, t) in events:
            for copy in self.copies(stage, t):
                if what == "go":
                    copy.start()
                else:
                    copy.wait_recv()

    def finish(self):
        for stage in range(4):
            for t in range(len(self.chunks)):
                for copy in self.copies(stage, t):
                    copy.wait_send()


def small_copies(place, source, target, sems, stage):
    z, y, x, c = place.z, place.y, place.x, place.c
    d1, d2, d3 = place.dims
    if stage == 0:
        pieces = [(source, target.at[z, y, x, c], d) for d in place.to_z]
    elif stage == 1:
        part = target.at[:, y, x, c]
        pieces = [(part, part, d) for d in place.to_x]
    elif stage == 2:
        part = target.at[:, y, :, c]
        pieces = [(part, part, d) for d in place.to_y]
    else:
        part = target.at[:, :, :, c]
        pieces = [(part, part, place.to_p)]
    base = (0, d1, d1 + d3, d1 + d2 + d3)[stage]
    return [send(s, d, sems[0].at[base + k], sems[1].at[base + k], to) for k, (s, d, to) in enumerate(pieces)]


class Reduce:
    @staticmethod
    def scratch(dims, rows, width, dtype, halves=True):
        d1, d2, d3 = dims
        half = width // 2 if halves else width
        shapes = [pltpu.VMEM((d1, d2, d3, rows, width), dtype)]
        shapes.append(pltpu.VMEM((d2 - 1, d1, d3, rows, half), dtype))
        shapes.append(pltpu.VMEM((d3 - 1, d1, rows, half), dtype))
        if halves:
            shapes.append(pltpu.VMEM((d3 - 1, d1, d2, rows, half), dtype))
            shapes.append(pltpu.VMEM((d2 - 1, d1, rows, half), dtype))
        shapes.append(pltpu.VMEM((d1 - 1, rows, width), dtype))
        near = d2 + d3 - 2
        sizes = (1, near, near, d1 - 1) if halves else (1, d2 - 1, d3 - 1, d1 - 1)
        for size in sizes:
            shapes += [DMA((size,)), DMA((size,))]
        return shapes

    @staticmethod
    def plan(unit):
        def costs(key):
            stage, t = key
            return ("p", "xy", "xy", "z")[stage], (1.4, 4, 2, 4)[stage] * unit(t)

        def follow(key, taken):
            stage, t = key
            after = []
            if stage == 0 and (t < 2 or (1, t - 2) in taken):
                after.append((1, t))
            if stage == 1:
                if (0, t + 2) in taken:
                    after.append((1, t + 2))
                after.append((2, t))
            if stage == 2:
                after.append((3, t))
            return after

        return Plan(costs, follow)

    def __init__(self, place, refs, source, own, result, halves=True, load=None):
        self.at, self.halves, self.load = place, halves, load
        self.source, self.own, self.result = source, own, result
        if halves:
            self.total, self.ya, self.xa, self.xb, self.yb, self.zz = refs[:6]
            self.sems = refs[6:]
        else:
            self.total, self.ya, self.xa, self.zz = refs[:4]
            self.sems = refs[4:]
        width = self.total.shape[-1]
        half = width // 2 if halves else width
        self.a, self.b = pl.ds(0, half), pl.ds(half, half)

    def pieces(self, stage):
        p, h = self.at, self.total
        y, x = p.y, p.x
        if stage == 0:
            return [(self.source.at[:, :, :, 1 - p.c], h, p.to_p)]
        if stage == 1:
            made = [
                (h.at[:, v, :, :, self.a], self.ya.at[k], d)
                for k, (v, d) in enumerate(zip(p.ys, p.to_y))
            ]
            if self.halves:
                made += [
                    (h.at[:, :, v, :, self.b], self.xb.at[k], d)
                    for k, (v, d) in enumerate(zip(p.xs, p.to_x))
                ]
            return made
        if stage == 2:
            made = [
                (h.at[:, y, v, :, self.a], self.xa.at[k], d)
                for k, (v, d) in enumerate(zip(p.xs, p.to_x))
            ]
            if self.halves:
                made += [
                    (h.at[:, v, x, :, self.b], self.yb.at[k], d)
                    for k, (v, d) in enumerate(zip(p.ys, p.to_y))
                ]
            return made
        return [(h.at[v, y, x], self.zz.at[k], d) for k, (v, d) in enumerate(zip(p.zs, p.to_z))]

    def go(self, stage):
        for copy in self.copies(stage):
            copy.start()

    def copies(self, stage):
        out, back = self.sems[2 * stage], self.sems[2 * stage + 1]
        return [
            send(s, d, out.at[k], back.at[k], to) for k, (s, d, to) in enumerate(self.pieces(stage))
        ]

    def arrived(self, stage):
        for copy in self.copies(stage):
            copy.wait()

    def add(self, stage):
        p, h = self.at, self.total
        d1, d2, d3 = p.dims
        f32 = jnp.float32

        def into(at, terms):
            value = h[at].astype(f32)
            for term in terms:
                value = value + term.astype(f32)
            h[at] = value.astype(h.dtype)

        if stage == 0:

            @pl.loop(0, d1)
            def _(i):
                for j in range(d2):
                    for k in range(d3):
                        into((i, j, k), [self.own[i, j, k]])

        elif stage == 1:

            @pl.loop(0, d1)
            def _(i):
                for k in range(d3):
                    into(
                        (i, p.y, k, slice(None), self.a),
                        [self.ya[m, i, k] for m in range(d2 - 1)],
                    )
                if self.halves:
                    for j in range(d2):
                        into(
                            (i, j, p.x, slice(None), self.b),
                            [self.xb[m, i, j] for m in range(d3 - 1)],
                        )

        elif stage == 2:

            @pl.loop(0, d1)
            def _(i):
                into((i, p.y, p.x, slice(None), self.a), [self.xa[m, i] for m in range(d3 - 1)])
                if self.halves:
                    into(
                        (i, p.y, p.x, slice(None), self.b),
                        [self.yb[m, i] for m in range(d2 - 1)],
                    )

        else:
            value = h[p.z, p.y, p.x].astype(f32)
            for m in range(d1 - 1):
                value = value + self.zz[m].astype(f32)
            for cut, target in self.result:
                target[...] = value[:, cut]

    def take(self, stage):
        if stage == 0 and self.load is not None:
            self.load.wait()
        self.arrived(stage)
        self.add(stage)


HEAD_DIM = 64
MB = 2
EPS = 1e-05
BF = jnp.bfloat16
F32 = jnp.float32
NEG = -1e30
GELU_A = 0.044715
GELU_C = 0.7978845608028654


def mm(left, right):
    return lax.dot_general(left, right, (((1,), (0,)), ((), ())), preferred_element_type=F32)


def mm_nt(left, right):
    return lax.dot_general(left, right, (((1,), (1,)), ((), ())), preferred_element_type=F32)


def mm_tn(left, right):
    return lax.dot_general(left, right, (((0,), (0,)), ((), ())), preferred_element_type=F32)


def iota(shape, axis):
    return lax.broadcasted_iota(jnp.int32, shape, axis)


def unpack_vector(block, start, per, width, first):
    row0, lane0 = start // 128, start % 128
    rows = block.shape[0]
    column = iota((128, width), 1) + first
    pick = (iota((128, width), 0) - lane0 == column % per).astype(BF)
    spread = mm(block, pick)
    column = iota((rows, width), 1) + first
    mine = iota((rows, width), 0) == column // per * 8 + row0
    return jnp.sum(jnp.where(mine, spread, 0.0), axis=0, keepdims=True)


def moments(value, keep, first):
    mean = jnp.mean(value, axis=-1, keepdims=True)
    center = value - mean
    scale = lax.rsqrt(jnp.mean(center * center, axis=-1, keepdims=True) + EPS)
    keep[:, first : first + 1] = mean
    keep[:, first + 1 : first + 2] = scale
    return center, scale


def attend_pair(q2, k2, v2, masks, seq):
    half = seq // 2
    lane = iota((1, 128), 1) // HEAD_DIM
    vt = v2.T
    q2 = q2 * jnp.asarray(HEAD_DIM**-0.5, BF)
    ka, kb = k2[:half], k2[half:]
    sums, rows = [], []
    for head in range(2):
        qh = jnp.where(lane == head, q2, 0)
        va, vb = (vt[head * HEAD_DIM : (head + 1) * HEAD_DIM, i * half : (i + 1) * half] for i in range(2))
        first, second = qh[:half], qh[half:]
        s = mm_nt(ka, first) + masks[0]
        sa, sb = mm_nt(ka, second), mm_nt(kb, second) + masks[1]
        top = jnp.max(s, axis=0, keepdims=True)
        e = jnp.exp(s - top)
        total = jnp.sum(e, axis=0, keepdims=True)
        low = mm(va, e.astype(BF)) * (1.0 / total)
        logs = top + jnp.log(total)
        top = jnp.maximum(jnp.max(sa, axis=0, keepdims=True), jnp.max(sb, axis=0, keepdims=True))
        ea, eb = jnp.exp(sa - top), jnp.exp(sb - top)
        total = jnp.sum(ea, axis=0, keepdims=True) + jnp.sum(eb, axis=0, keepdims=True)
        high = (mm(va, ea.astype(BF)) + mm(vb, eb.astype(BF))) * (1.0 / total)
        rows.append(jnp.concatenate([low, high], axis=1))
        sums.append(jnp.concatenate([logs, top + jnp.log(total)], axis=1))
    return jnp.concatenate(rows, axis=0).T, sums


def forward_plan(chunks, kinds, groups, fcs, projs, steps):
    widest = max(width for i, _, width in chunks if i != 3)
    plan = Gather.plan(chunks, kinds, lambda t: 1.2 * (1.0 if chunks[t][0] == 3 else chunks[t][2] / widest))
    fetched, used = set(), set()

    def pump(point, passed=0.0, done=None, **rest):
        if done is not None:
            used.add(done)
        plan.pump(point, passed, **rest)
        for t in range(len(chunks)):
            first = t < 2 or (chunks[t][0] == 3) != (chunks[t - 2][0] == 3)
            if (3, t) in plan.taken and t not in fetched and (first or t - 2 in used):
                fetched.add(t)
                plan.table[point].append(("fetch", (3, t)))

    pump("begin", 0.0, start=[(0, 0)])
    for k in range(4):
        pump(("small", k), 2.0, force=[(k - 1, 0)] if 0 < k < 3 else ())
    pump("spread", 2.5, force=[(2, 0)])
    pump("norm", 2.0)
    for g in range(groups):
        pump(("qkv", g), 0.0, force=[(3, g)])
        pump(("scores", g), 2.4, done=g)
        for i in range(steps):
            pump(("attend", g, i), 0.0 if i == 0 else 1.6)
        pump(("group", g), 1.6)
    t = groups
    pump("out", 0.0, force=[(3, t)])
    for i in range(2):
        pump(("norm2", i), 2.1)
    used.add(t)
    for k in range(fcs):
        pump(("fc", k), 0.0, force=[(3, t + 1 + k)])
        for i in range(2):
            pump(("gelu", k, i), 2.4)
        used.add(t + 1 + k)
        pump(("terms", k), 2.9, force=[(3, t + 2 + k)])
    for k in range(projs):
        pump(("proj", k), 0.0, force=[(3, t + 1 + fcs + k)])
        pump(("done", k), 2.8, done=t + 1 + fcs + k)
    pump("end", 0.0, force=[(3, k) for k in range(len(chunks))])
    return plan.table


def forward_kernel(dims, chunks, kinds, comm, *refs):
    (lens, tokens, cot, s_qkv, s_out, s_fc, s_proj, small) = refs[:8]
    (w_qkv, w_out, w_fc, w_proj, vecs_o, h1_o, qkv_o, lse_o, ctx_o, r1_o, h2_o, gp_o, dy_o, terms_o, out_o, stats_o) = refs[8:24]
    (x_, dy, live, vecs, fcb, h1, qkv, ctx, lse, r1, h2, act, gp, out, sm, wbuf, pbuf, tbuf, diag, shuffled, stats) = refs[24:45]
    local, wsem, psem, osem, outsem, gpsem, tsem, shsem, s_sem, r_sem = refs[45:55]
    sems = refs[55:]
    rows, width = x_.shape
    seq = rows // MB
    hidden = act.shape[1]
    n = dims[0] * dims[1] * dims[2] * 2
    per, per_fc = width // n, hidden // n
    tile = 256
    tiles = rows // tile
    fcs = hidden // width
    groups = sum(i == 0 for i, _, _ in chunks)
    gw = width // groups
    pw = chunks[-1][2]
    projs = width // pw
    gpairs = gw // 128
    steps = MB * gpairs
    plan = forward_plan(chunks, kinds, groups, fcs, projs, steps)
    place = Place(dims)
    z, y, x, c = place.z, place.y, place.x, place.c
    shards = (shuffled, s_out, s_fc, s_proj)
    wholes = (w_qkv, w_out, w_fc, w_proj)
    gather = Gather(place, shards, wholes, chunks, kinds, sems)

    def at_point(*key):
        for event in plan[key[0] if len(key) == 1 else key]:
            if event[0] == "fetch":
                fetch(event[1][1]).start()
            elif comm:
                gather.run([event])

    def fetch(t):
        i, first, w = chunks[t]
        source = wholes[i].at[:, :, :, :, :, pl.ds(first, w)]
        if i == 3:
            return pltpu.make_async_copy(source, pbuf.at[t % 2], psem.at[t % 2])
        return pltpu.make_async_copy(source, wbuf.at[t % 2, :, :, :, :, :, pl.ds(0, w)], wsem.at[t % 2])

    saves = []

    def keep(source, target):
        save = pltpu.make_async_copy(source, target, osem.at[len(saves)])
        save.start()
        saves.append(save)

    shuffle = [
        pltpu.make_async_copy(
            s_qkv.at[:, pl.ds(k * width + g * gw, gw)], shuffled.at[:, pl.ds((3 * g + k) * gw, gw)], shsem.at[3 * g + k]
        )
        for g in range(groups)
        for k in range(3)
    ]
    for move in shuffle:
        move.start()
    loads = [pltpu.make_async_copy(tokens, x_, gpsem.at[0]), pltpu.make_async_copy(cot, dy, gpsem.at[1])]
    for move in loads:
        move.start()
    moves = [
        pltpu.make_async_copy(s, w.at[z, y, x, c], local.at[i])
        for i, (s, w) in enumerate(zip((*shards, small), (*wholes, sm)))
    ]
    for move in moves[1:]:
        move.start()
    place.barrier()
    for move in shuffle:
        move.wait()
    moves[0].start()
    tiny = [small_copies(place, small, sm, (s_sem, r_sem), stage) for stage in range(4)]
    half = seq // 2
    for stage in range(4):
        if comm:
            for copy in tiny[stage]:
                copy.start()
        if stage == 0:
            at_point("begin")
            for slot in range(MB):
                length = lens[slot : slot + 1, 0:1]
                live[slot * seq : (slot + 1) * seq, :] = jnp.where(iota((seq, 1), 0).astype(F32) < length, 1.0, 0.0)
                causal = iota((half, half), 0) <= iota((half, half), 1)
                late = (iota((half, half), 0) + half).astype(F32) < length
                diag[0] = jnp.where(causal, 0.0, NEG)
                diag[1 + slot] = jnp.where(causal & late, 0.0, NEG)
            for move in moves:
                move.wait()
        if stage == 1:
            loads[1].wait()
            vecs[8:16, :] = jnp.zeros((8, width), F32)

            @pl.loop(0, tiles)
            def _(i):
                at = pl.ds(pl.multiple_of(i * tile, tile), tile)
                value = jnp.where(live[at, :] > 0.5, dy[at, :].astype(F32), 0.0)
                dy[at, :] = value.astype(BF)
                vecs[8:9, :] += jnp.sum(value, axis=0, keepdims=True)

            keep(dy, dy_o)
        if comm:
            for copy in tiny[stage]:
                copy.wait_recv()
        at_point("small", stage)
    block = sm[...].reshape(n * 8, 128).astype(BF)
    for v in range(8):
        vecs[v : v + 1, :] = unpack_vector(block, v * per, per, width, 0)
    for part in range(fcs):
        fcb[:, part * width : (part + 1) * width] = unpack_vector(block, 8 * per, per_fc, width, part * width)
    at_point("spread")
    loads[0].wait()

    @pl.loop(0, rows // 128)
    def _(i):
        at = pl.ds(pl.multiple_of(i * 128, 128), 128)
        center, scale = moments(x_[at, :].astype(F32), stats.at[at, :], 0)
        h1[at, :] = (center * scale * vecs[0:1, :] + vecs[1:2, :]).astype(BF)

    keep(h1, h1_o)
    keep(vecs, vecs_o)
    at_point("norm")

    @pl.loop(0, groups)
    def _(g):
        for k in range(groups):

            @pl.when(g == k)
            def _():
                at_point("qkv", k)
                fetch(k).wait()

        first = pl.multiple_of(g * gw, gw)

        @pl.loop(0, tiles)
        def _(i):
            at = pl.ds(pl.multiple_of(i * tile, tile), tile)
            value = mm(h1[at, :], wbuf[g % 2, :, :, :, :, :, 0 : 3 * gw].reshape(width, 3 * gw))
            for k, bias in ((0, 2), (1, None), (2, 3)):
                part = value[:, k * gw : (k + 1) * gw]
                if bias is not None:
                    part = part + vecs[bias : bias + 1, pl.ds(first, gw)]
                qkv[at, pl.ds(k * width + first, gw)] = part.astype(BF)

        for k in range(groups):
            if plan["scores", k]:

                @pl.when(g == k)
                def _():
                    at_point("scores", k)

        @pl.loop(0, steps)
        def _(i):
            for k in range(groups):
                for m in range(steps):
                    if plan["attend", k, m]:

                        @pl.when((g == k) & (i == m))
                        def _():
                            at_point("attend", k, m)

            slot, pair = i // gpairs, g * gpairs + i % gpairs
            at = pl.ds(pl.multiple_of(slot * seq, seq), seq)
            col = pl.multiple_of(pair * 128, 128)
            value, sums = attend_pair(
                qkv[at, pl.ds(col, 128)],
                qkv[at, pl.ds(width + col, 128)],
                qkv[at, pl.ds(2 * width + col, 128)],
                [diag[0], diag[1 + slot]],
                seq,
            )
            ctx[at, pl.ds(col, 128)] = value.astype(BF)
            for head in range(2):
                lse[slot * (width // HEAD_DIM) + pair * 2 + head] = sums[head]

        for k in range(groups):
            if plan["group", k]:

                @pl.when(g == k)
                def _():
                    at_point("group", k)

    keep(qkv, qkv_o)
    keep(ctx, ctx_o)
    keep(lse, lse_o)
    t = groups
    at_point("out")
    fetch(t).wait()

    @pl.loop(0, tiles)
    def _(i):
        at = pl.ds(pl.multiple_of(i * tile, tile), tile)
        value = mm(ctx[at, :], wbuf[t % 2].reshape(width, width)) + vecs[4:5, :]
        value = value + x_[at, :].astype(F32)
        r1[at, :] = value
        center, scale = moments(value, stats.at[at, :], 2)
        h2[at, :] = (center * scale * vecs[5:6, :] + vecs[6:7, :]).astype(BF)
        for k in range(2):

            @pl.when(i == (k + 1) * tiles // 2 - 1)
            def _():
                at_point("norm2", k)

    keep(r1, r1_o)
    keep(h2, h2_o)
    keep(stats, stats_o)

    def keep_gp(k):
        return pltpu.make_async_copy(gp.at[k % 2], gp_o.at[:, pl.ds(pl.multiple_of(k * width, width), width)], gpsem.at[k % 2])

    def each(index, count, *name):
        for k in range(count):
            key = (*name, k)
            if plan[key]:

                @pl.when(index == k)
                def _():
                    at_point(*key)

    def keep_terms(k):
        return pltpu.make_async_copy(tbuf.at[k % 2], terms_o.at[k], tsem.at[k % 2])

    @pl.loop(0, fcs)
    def _(k):
        each(k, fcs, "fc")
        buffer = (groups + 1 + k) % 2
        for m in range(fcs):

            @pl.when(k == m)
            def _():
                fetch(groups + 1 + m).wait()

        @pl.when(k >= 2)
        def _():
            keep_gp(k - 2).wait()
            keep_terms(k - 2).wait()

        cut = pl.ds(pl.multiple_of(k * width, width), width)

        @pl.loop(0, 2)
        def _(i):
            for part in range(tiles // 2):
                at = pl.ds(pl.multiple_of((i * (tiles // 2) + part) * tile, tile), tile)
                u = mm(h2[at, :], wbuf[buffer].reshape(width, width)) + fcb[:, cut]
                square = u * u
                inner = u * (GELU_C + (GELU_C * GELU_A) * square)
                gate = 0.5 + 0.5 * jnp.tanh(inner)
                value = u * gate
                act[at, cut] = value.astype(BF)
                slope = gate + value * (2.0 - 2.0 * gate) * (GELU_C + (3.0 * GELU_C * GELU_A) * square)
                gp[k % 2, at, :] = slope.astype(BF)
            for n_k in range(fcs):
                for m in range(2):
                    if plan["gelu", n_k, m]:

                        @pl.when((k == n_k) & (i == m))
                        def _():
                            at_point("gelu", n_k, m)

        keep_gp(k).start()

        @pl.loop(0, 2)
        def _(i):
            some = pl.ds(pl.multiple_of(k * width + i * (width // 2), width // 2), width // 2)
            value = mm_tn(act[:, some], dy[...]).astype(BF)
            blocks = (dims[1] // 2, dims[2], 2, per_fc, width)
            tbuf[k % 2, pl.ds(i * blocks[0], blocks[0])] = value.reshape(blocks)

        keep_terms(k).start()
        each(k, fcs, "terms")

    def keep_out(k):
        cut = pl.ds(pl.multiple_of(k * pw, pw), pw)
        return pltpu.make_async_copy(out.at[:, cut], out_o.at[:, cut], outsem.at[k])

    @pl.loop(0, projs)
    def _(k):
        cut = pl.ds(pl.multiple_of(k * pw, pw), pw)
        buffer = (groups + 1 + fcs + k) % 2

        for m in range(projs):

            @pl.when(k == m)
            def _():
                at_point("proj", m)
                fetch(groups + 1 + fcs + m).wait()

        @pl.loop(0, tiles)
        def _(i):
            at = pl.ds(pl.multiple_of(i * tile, tile), tile)
            value = mm(act[at, :], pbuf[buffer].reshape(hidden, pw)) + (r1[at, cut] + vecs[7:8, cut])
            out[at, cut] = jnp.where(live[at, :] > 0.5, value, 0.0).astype(BF)

        keep_out(k).start()
        each(k, projs, "done")

    at_point("end")
    for k in range(max(fcs - 2, 0), fcs):
        keep_gp(k).wait()
    for k in range(max(fcs - 2, 0), fcs):
        keep_terms(k).wait()
    for k in range(projs):
        keep_out(k).wait()
    for save in saves:
        save.wait()
    if comm:
        gather.finish()
        for copies in tiny:
            for copy in copies:
                copy.wait_send()


def forward(dims, lens, tokens, cot, shards, small, chunks, kinds, comm=True):
    rows, width = tokens.shape
    n = dims[0] * dims[1] * dims[2] * 2
    hidden = shards[2].shape[1]
    heads = width // HEAD_DIM
    seq = rows // MB
    pw = chunks[-1][2]
    groups = sum(i == 0 for i, _, _ in chunks)
    sds = jax.ShapeDtypeStruct
    shapes = [sds((*dims, 2, *s.shape), s.dtype) for s in shards]
    shapes += [
        sds((16, width), F32),
        sds((rows, width), BF),
        sds((rows, 3 * width), BF),
        sds((MB * heads, 1, seq), F32),
        sds((rows, width), BF),
        sds((rows, width), F32),
        sds((rows, width), BF),
        sds((rows, hidden), BF),
        sds((rows, width), BF),
        sds((*dims, 2, hidden // n, width), BF),
        sds((rows, width), BF),
        sds((rows, 128), F32),
    ]
    scratch = [
        pltpu.VMEM((rows, width), BF),
        pltpu.VMEM((rows, width), BF),
        pltpu.VMEM((rows, 1), F32),
        pltpu.VMEM((16, width), F32),
        pltpu.VMEM((1, hidden), F32),
        pltpu.VMEM((rows, width), BF),
        pltpu.VMEM((rows, 3 * width), BF),
        pltpu.VMEM((rows, width), BF),
        pltpu.VMEM((MB * heads, 1, seq), F32),
        pltpu.VMEM((rows, width), F32),
        pltpu.VMEM((rows, width), BF),
        pltpu.VMEM((rows, hidden), BF),
        pltpu.VMEM((2, rows, width), BF),
        pltpu.VMEM((rows, width), BF),
        pltpu.VMEM((*dims, 2, *small.shape), small.dtype),
        pltpu.VMEM((2, *dims, 2, width // n, width), BF),
        pltpu.VMEM((2, *dims, 2, hidden // n, pw), BF),
        pltpu.VMEM((2, *dims[1:], 2, hidden // n, width), BF),
        pltpu.VMEM((1 + MB, seq // 2, seq // 2), F32),
        pltpu.VMEM(shards[0].shape, BF),
        pltpu.VMEM((rows, 128), F32),
        DMA((5,)),
        DMA((2,)),
        DMA((2,)),
        DMA((9,)),
        DMA((width // pw,)),
        DMA((2,)),
        DMA((2,)),
        DMA((3 * groups,)),
        DMA((sum(dims) + 1,)),
        DMA((sum(dims) + 1,)),
        *Gather.semaphores(dims, kinds),
    ]
    return pl.pallas_call(
        lambda *refs: forward_kernel(dims, chunks, kinds, comm, *refs),
        out_shape=shapes,
        in_specs=[VMEM, ANY, ANY, ANY] + [VMEM] * 4,
        out_specs=[ANY] * 16,
        scratch_shapes=scratch,
        compiler_params=pltpu.CompilerParams(
            collective_id=0, has_side_effects=True, vmem_limit_bytes=60 * 1024 * 1024
        ),
        name="forward",
    )(lens, tokens, cot, *shards, small)


def pack_vector(row, start, per, n):
    width = row.shape[1]
    pick = (iota((128, width), 0) - start % 128 == iota((128, width), 1) % per).astype(BF)
    mine = iota((n, width), 0) == iota((n, width), 1) // per
    total = 0.0
    for _ in range(3):
        part = row.astype(BF)
        row = row - part.astype(F32)
        total = total + mm_nt(jnp.where(mine, part.astype(F32), 0.0).astype(BF), pick)
    return total


def norm_back(value, kept, gain, grad):
    scale = kept[:, 1:2]
    normed = (value - kept[:, 0:1]) * scale
    scaled = grad * gain
    mean = jnp.mean(scaled, axis=-1, keepdims=True)
    cross = jnp.mean(scaled * normed, axis=-1, keepdims=True)
    return (scaled - mean - normed * cross) * scale, grad * normed


def attend_back(q2, k2, v2, o2, c2, lse, masks, seq):
    half = seq // 2
    lane = iota((1, 128), 1) // HEAD_DIM
    prod = o2.astype(F32) * c2.astype(F32)
    heads = (iota((8, 128), 1) // HEAD_DIM == iota((8, 128), 0)).astype(BF)
    high = prod.astype(BF)
    delta = mm_nt(heads, high) + mm_nt(heads, (prod - high.astype(F32)).astype(BF))
    kt = k2.T
    q2 = q2 * jnp.asarray(HEAD_DIM**-0.5, BF)
    cuts = (slice(0, half), slice(half, seq))
    dk, dv, dq = [0.0, 0.0], [0.0, 0.0], []
    for head in range(2):
        qh = jnp.where(lane == head, q2, 0)
        oh = jnp.where(lane == head, o2, 0)
        kh = kt[head * HEAD_DIM : (head + 1) * HEAD_DIM]
        parts = [0.0, 0.0]
        for key, query in ((0, 0), (0, 1), (1, 1)):
            qb, ob, cut = qh[cuts[query]], oh[cuts[query]], cuts[query]
            s = mm_nt(k2[cuts[key]], qb) - lse[head][:, cut]
            if key == query:
                s = s + masks[key]
            p = jnp.exp(s)
            dp = mm_nt(v2[cuts[key]], ob)
            ds = (p * (dp - delta[head : head + 1, cut])).astype(BF)
            dv[key] = dv[key] + mm(p.astype(BF), ob)
            dk[key] = dk[key] + mm(ds, qb)
            parts[query] = parts[query] + mm(kh[:, cuts[key]], ds)
        dq.append(jnp.concatenate(parts, axis=1))
    dq = jnp.concatenate(dq, axis=0).T * HEAD_DIM**-0.5
    return dq, jnp.concatenate(dk, axis=0), jnp.concatenate(dv, axis=0)


def backward_plan(projs, fcs, groups, steps, slabs):
    out = projs + fcs
    plan = Reduce.plan(lambda t: 1.45 if t <= out else 1.08)
    pump = plan.pump
    pump("start", 0.0, start=[(0, 0), (0, 1)])
    pump("loaded", 1.0)
    late = list(range(2, projs))
    for f in range(fcs):
        for name, passed in (("da", 3.2), ("dh", 2.9)):
            j = late.pop(0) if late else None
            force = [] if j is None else [(0, j - 2)]
            if name == "dh" and f >= 2:
                force.append((0, projs + f - 2))
            pump((name, f), passed, force=force, start=[] if j is None else [(0, j)])
        pump(("gfc", f), 2.9, start=[(0, projs + f)])
    for i in range(slabs):
        pump(("ln2", i), 2.0)
    pump("dctx", 3.0, force=[(0, out - 2)])
    pump("gout", 3.0, start=[(0, out)])
    for g in range(groups):
        for i in range(steps):
            pump(("back", g, i), 0.0 if i == 0 else 2.0)
        pump(("grads", g), 2.0, force=[(0, out - 1 + g)])
        pump(("gqkv", g), 2.2, start=[(0, out + 1 + g)])
    for i in range(slabs):
        pump(("dx", i), 3.4)
    pump("end", 4.0, force=[(3, t) for t in range(out + 1 + groups)])
    return plan.table


def backward_kernel(dims, groups, sizes, comm, *refs):
    (lens, tokens, dy, vecs, stats, h1_i, qkv_i, lse_i, ctx_i, r1_i, h2_i, gp_i, terms, w_qkv, w_out, w_fc, w_proj) = refs[:17]
    (dx_o, g_qkv, g_out, g_fc, g_proj, g_small) = refs[17:23]
    slots, wp, f_dh, f_r1, gvec, gfc, lse, diag, stage, owns, sstage = refs[23:34]
    lsem, wsem, osem, qsem = refs[34:38]
    refs = refs[38:]
    d1, d2, d3 = dims
    n = d1 * d2 * d3 * 2
    rows, width = f_dh.shape
    hidden = gfc.shape[1]
    seq = rows // MB
    half = seq // 2
    per, per_fc = width // n, hidden // n
    fcs = hidden // width
    gw = width // groups
    pw = owns.shape[-1]
    projs = width // pw
    tile = rows // d1
    gpairs = gw // 128
    steps = MB * gpairs
    place = Place(dims)
    c = place.c
    plan = backward_plan(projs, fcs, groups, steps, d1)
    sets = []
    for size in sizes:
        sets.append(refs[:size])
        refs = refs[size:]
    parts = []
    for j in range(projs):
        cut = pl.ds(j * pw, pw)
        own = owns.at[j % 2]
        move = pltpu.make_async_copy(terms.at[:, :, :, c, :, cut], own, osem.at[j % 2])
        result = [(slice(None), g_proj.at[:, cut])]
        parts.append(Reduce(place, sets[j], terms.at[:, :, :, :, :, cut], own, result, load=move))
    for f in range(fcs):
        result = [(slice(None), g_fc.at[:, pl.ds(f * width, width)])]
        parts.append(Reduce(place, sets[projs + f], stage.at[f % 2], stage.at[f % 2, :, :, :, c], result))
    b = fcs % 2
    parts.append(Reduce(place, sets[projs + fcs], stage.at[b], stage.at[b, :, :, :, c], [(slice(None), g_out)]))
    gcut = pl.ds(0, 3 * gw)
    for g in range(groups):
        b = (fcs + 1 + g) % 2
        result = [
            (slice(k * gw, (k + 1) * gw), g_qkv.at[:, pl.ds(k * width + g * gw, gw)]) for k in range(3)
        ]
        source, own = stage.at[b, :, :, :, :, :, gcut], stage.at[b, :, :, :, c, :, gcut]
        parts.append(Reduce(place, sets[projs + fcs + 1 + g], source, own, result))

    def at_point(*key):
        if not comm:
            return
        for what, (step, t) in plan[key[0] if len(key) == 1 else key]:
            if what == "take":
                parts[t].take(step)
            else:
                parts[t].go(step)
                if step == 0 and parts[t].load is not None:
                    parts[t].load.start()

    def load(source, slot, k):
        return pltpu.make_async_copy(source, slots.at[slot], lsem.at[k])

    def cols(source, k):
        return source.at[:, :, :, :, :, pl.ds(pl.multiple_of(k * width, width), width)]

    def whole(slot):
        return slots[slot].reshape(rows, width)

    def piece(slot, i):
        return slots[slot, i].reshape(tile, width)

    def put(slot, i, value):
        slots[slot, i] = value.astype(BF).reshape(d2, d3, 2, per, width)

    def fetch_proj(f):
        return pltpu.make_async_copy(w_proj.at[f], wp.at[f % 2], wsem.at[f % 2])

    def fetch_ff(f):
        return [fetch_proj(f), load(cols(gp_i, f), 3 + f % 2, 3 + f % 2), load(cols(w_fc, f), 1 + f % 2, 1 + f % 2)]

    def w_third(k, target):
        return [
            pltpu.make_async_copy(
                w_qkv.at[:, :, :, :, :, pl.ds((3 * g + k) * gw, gw)],
                target.at[:, :, :, :, :, pl.ds(g * gw, gw)],
                qsem.at[k, g],
            )
            for g in range(groups)
        ]

    load(dy, 0, 0).start()
    for move in fetch_ff(0):
        move.start()
    load(h2_i, 6, 6).start()
    load(ctx_i, 7, 7).start()
    lload = pltpu.make_async_copy(lse_i, lse, lsem.at[5])
    lload.start()
    for slot in range(MB):
        causal = iota((half, half), 0) <= iota((half, half), 1)
        late = (iota((half, half), 0) + half).astype(F32) < lens[slot : slot + 1, 0:1]
        diag[0] = jnp.where(causal, 0.0, NEG)
        diag[1 + slot] = jnp.where(causal & late, 0.0, NEG)
    gvec[...] = jnp.zeros_like(gvec)
    gfc[...] = jnp.zeros_like(gfc)
    f_dh[...] = jnp.zeros_like(f_dh)
    gvec[7:8, :] = vecs[8:9, :]
    place.barrier(everyone=True)
    at_point("start")
    load(dy, 0, 0).wait()
    at_point("loaded")
    load(h2_i, 6, 6).wait()

    def each(index, count, *name):
        for k in range(count):
            key = (*name, k)
            if plan[key]:

                @pl.when(index == k)
                def _():
                    at_point(*key)

    @pl.loop(0, fcs)
    def _(f):
        for move in fetch_ff(f):
            move.wait()

        @pl.when(f + 1 < fcs)
        def _():
            for move in fetch_ff(f + 1):
                move.start()

        cut = pl.ds(pl.multiple_of(f * width, width), width)

        @pl.loop(0, d1 // 2)
        def _(h):
            for i in (2 * h, 2 * h + 1):
                da = mm_nt(piece(0, i), wp[f % 2].reshape(rows, width))
                du = (da * piece(3 + f % 2, i).astype(F32)).astype(BF)
                put(5, i, du)
                gfc[:, cut] += jnp.sum(du.astype(F32), axis=0, keepdims=True)

        each(f, fcs, "da")

        @pl.loop(0, d1 // 2)
        def _(h):
            for i in (2 * h, 2 * h + 1):
                at = pl.ds(pl.multiple_of(i * tile, tile), tile)
                f_dh[at, :] += mm_nt(piece(5, i), whole(1 + f % 2))

        each(f, fcs, "dh")

        @pl.loop(0, 2)
        def _(i):
            col = pl.ds(pl.multiple_of(i * (width // 2), width // 2), width // 2)
            value = mm_tn(slots[6, :, :, :, :, :, col].reshape(rows, width // 2), whole(5)).astype(BF)
            stage[f % 2, pl.ds(i * (d1 // 2), d1 // 2)] = value.reshape(d1 // 2, d2, d3, 2, per, width)

        each(f, fcs, "gfc")

    def r1_tile(i):
        return pltpu.make_async_copy(r1_i.at[pl.ds(i * tile, tile)], f_r1.at[i % 2], wsem.at[i % 2])

    r1_tile(0).start()
    load(w_out, 1, 1).start()
    for k, slot in enumerate((3, 4, 6)):
        load(cols(qkv_i, k), slot, slot).start()

    @pl.loop(0, d1)
    def _(i):
        r1_tile(i).wait()

        @pl.when(i + 1 < d1)
        def _():
            r1_tile(i + 1).start()

        at = pl.ds(pl.multiple_of(i * tile, tile), tile)
        grad = f_dh[at, :]
        value, norms = norm_back(f_r1[i % 2], stats[at, 2:4], vecs[5:6, :], grad)
        value = value + piece(0, i).astype(F32)
        f_dh[at, :] = value
        low = value.astype(BF)
        put(5, i, low)
        gvec[5:6, :] += jnp.sum(norms, axis=0, keepdims=True)
        gvec[6:7, :] += jnp.sum(grad, axis=0, keepdims=True)
        gvec[4:5, :] += jnp.sum(low.astype(F32), axis=0, keepdims=True)
        for k in range(d1):
            if plan["ln2", k]:

                @pl.when(i == k)
                def _():
                    at_point("ln2", k)

    load(ctx_i, 7, 7).wait()
    load(w_out, 1, 1).wait()
    load(h1_i, 0, 0).start()

    @pl.loop(0, d1)
    def _(i):
        put(2, i, mm_nt(piece(5, i), whole(1)))

    for move in w_third(0, slots.at[1]):
        move.start()
    at_point("dctx")

    @pl.loop(0, 2)
    def _(i):
        col = pl.ds(pl.multiple_of(i * (width // 2), width // 2), width // 2)
        value = mm_tn(slots[7, :, :, :, :, :, col].reshape(rows, width // 2), whole(5)).astype(BF)
        stage[fcs % 2, pl.ds(i * (d1 // 2), d1 // 2)] = value.reshape(d1 // 2, d2, d3, 2, per, width)

    for move in w_third(1, slots.at[5]):
        move.start()
    loadx = pltpu.make_async_copy(tokens, wp.at[0], lsem.at[2])
    loadx.start()
    at_point("gout")
    for k, slot in enumerate((3, 4, 6)):
        load(cols(qkv_i, k), slot, slot).wait()
    lload.wait()
    load(h1_i, 0, 0).wait()
    hslab = d1 // MB

    @pl.loop(0, groups)
    def _(g):
        @pl.loop(0, steps)
        def _(i):
            for k in range(groups):
                for m in range(steps):
                    if plan["back", k, m]:

                        @pl.when((g == k) & (i == m))
                        def _():
                            at_point("back", k, m)

            slot, pair = i // gpairs, g * gpairs + i % gpairs
            slab = pl.ds(slot * hslab, hslab)
            lanes = pl.ds(pl.multiple_of(pair * 128, 128), 128)

            def get(s):
                return slots[s, slab, :, :, :, :, lanes].reshape(seq, 128)

            head = slot * (width // HEAD_DIM) + 2 * pair
            grads = attend_back(
                get(3), get(4), get(6), get(2), get(7), [lse[head], lse[head + 1]], [diag[0], diag[1 + slot]], seq
            )
            for s, value in zip((3, 4, 6), grads):
                slots[s, slab, :, :, :, :, lanes] = value.astype(BF).reshape(hslab, d2, d3, 2, per, 128)

        for k in range(groups):
            if plan["grads", k] or k == groups - 1:

                @pl.when(g == k)
                def _():
                    at_point("grads", k)
                    if k == groups - 1:
                        for move in w_third(2, stage.at[(fcs + groups - 1) % 2]):
                            move.start()

        mine = pl.ds(pl.multiple_of(g * gw, gw), gw)
        buffer = (fcs + 1 + g) % 2

        @pl.loop(0, 2)
        def _(i):
            col = pl.ds(pl.multiple_of(i * (width // 2), width // 2), width // 2)
            left = slots[0, :, :, :, :, :, col].reshape(rows, width // 2)
            for k, s in enumerate((3, 4, 6)):
                value = mm_tn(left, slots[s, :, :, :, :, :, mine].reshape(rows, gw)).astype(BF)
                stage[buffer, pl.ds(i * (d1 // 2), d1 // 2), :, :, :, :, k * gw : (k + 1) * gw] = value.reshape(
                    d1 // 2, d2, d3, 2, per, gw
                )

        for k in range(groups):

            @pl.when(g == k)
            def _():
                at_point("gqkv", k)

    thirds = (slots.at[1], slots.at[5], stage.at[(fcs + groups - 1) % 2])
    for k, target in enumerate(thirds):
        for move in w_third(k, target):
            move.wait()
    loadx.wait()
    blocks = d2 * d3 // d1

    @pl.loop(0, d1)
    def _(i):
        at = pl.ds(pl.multiple_of(i * tile, tile), tile)
        x_tile = wp[0, i // d3, i % d3] if blocks == 1 else wp[0, i]
        x_tile = x_tile.reshape(tile, width)
        grad = mm_nt(piece(3, i), whole(1)) + mm_nt(piece(4, i), whole(5)) + mm_nt(piece(6, i), thirds[2][...].reshape(rows, width))
        value, norms = norm_back(x_tile.astype(F32), stats[at, 0:2], vecs[0:1, :], grad)
        put(2, i, value + f_dh[at, :])
        gvec[0:1, :] += jnp.sum(norms, axis=0, keepdims=True)
        gvec[1:2, :] += jnp.sum(grad, axis=0, keepdims=True)
        gvec[2:3, :] += jnp.sum(piece(3, i).astype(F32), axis=0, keepdims=True)
        gvec[3:4, :] += jnp.sum(piece(6, i).astype(F32), axis=0, keepdims=True)
        for k in range(d1):
            if plan["dx", k]:

                @pl.when(i == k)
                def _():
                    at_point("dx", k)

    save = pltpu.make_async_copy(slots.at[2], dx_o, lsem.at[0])
    save.start()
    lines = [0.0] * (sstage.shape[-1] // 128)
    for v in range(8):
        lines[v * per // 128] += pack_vector(gvec[v : v + 1, :], v * per, per, n)
    some = n // fcs
    packed = [pack_vector(gfc[:, k * width : (k + 1) * width], 8 * per, per_fc, some) for k in range(fcs)]
    lines[8 * per // 128] += jnp.concatenate(packed, axis=0)
    for k, line in enumerate(lines):
        for d in range(n):
            at = (d // (d2 * d3 * 2), d // (d3 * 2) % d2, d // 2 % d3, d % 2)
            sstage[(*at, slice(None), slice(k * 128, (k + 1) * 128))] = line[d : d + 1, :]
    mine, theirs, found, s_sem, r_sem = refs
    if comm:
        swap = send(sstage.at[:, :, :, 1 - c], mine, s_sem.at[0], r_sem.at[0], place.to_p)
        swap.start()
        swap.wait()
        theirs[...] = mine[...] + sstage[:, :, :, c]
        sends = [
            send(theirs.at[z, y, x], found.at[k], s_sem.at[k + 1], r_sem.at[k + 1], device)
            for k, (z, y, x, device) in enumerate(place.others())
        ]
        for copy in sends:
            copy.start()
    at_point("end")
    if comm:
        for copy in sends:
            copy.wait()
        value = theirs[place.z, place.y, place.x]
        for k in range(len(sends)):
            value = value + found[k]
        g_small[...] = value
    save.wait()


def backward(dims, lens, tokens, saved, weights, groups, comm=True):
    vecs, h1, qkv, lse, ctx, r1, h2, gp, dy, terms, stats = saved
    rows, width = tokens.shape
    n = dims[0] * dims[1] * dims[2] * 2
    hidden = gp.shape[1]
    seq = rows // MB
    per, per_fc = width // n, hidden // n
    fcs = hidden // width
    projs = 4
    pw = width // projs
    lanes = (8 * per + per_fc + 127) // 128 * 128

    def six(a):
        return a.reshape(*dims, 2, a.shape[0] // n, a.shape[1])

    sds = jax.ShapeDtypeStruct
    scratch = [
        pltpu.VMEM((8, *dims, 2, per, width), BF),
        pltpu.VMEM((2, *dims[1:], 2, per_fc, width), BF),
        pltpu.VMEM((rows, width), F32),
        pltpu.VMEM((2, rows // dims[0], width), F32),
        pltpu.VMEM((8, width), F32),
        pltpu.VMEM((1, hidden), F32),
        pltpu.VMEM(lse.shape, F32),
        pltpu.VMEM((1 + MB, seq // 2, seq // 2), F32),
        pltpu.VMEM((2, *dims, 2, per, width), BF),
        pltpu.VMEM((2, *dims, per_fc, pw), BF),
        pltpu.VMEM((*dims, 2, 1, lanes), F32),
        DMA((8,)),
        DMA((2,)),
        DMA((2,)),
        DMA((3, groups)),
    ]
    sizes = []
    shapes = [(per_fc, pw)] * projs + [(per, width)] * (fcs + 1) + [(per, 3 * width // groups)] * groups
    for block_rows, block_cols in shapes:
        made = Reduce.scratch(dims, block_rows, block_cols, BF)
        sizes.append(len(made))
        scratch += made
    half_n = n // 2
    scratch += [pltpu.VMEM((*dims, 1, lanes), F32)] * 2 + [pltpu.VMEM((half_n - 1, 1, lanes), F32)]
    scratch += [DMA((half_n,)), DMA((half_n,))]
    outs = [
        sds((*dims, 2, per, width), BF),
        sds((per, 3 * width), F32),
        sds((per, width), F32),
        sds((per, hidden), F32),
        sds((per_fc, width), F32),
        sds((1, lanes), F32),
    ]
    return pl.pallas_call(
        lambda *refs: backward_kernel(dims, groups, sizes, comm, *refs),
        out_shape=outs,
        in_specs=[VMEM, ANY, ANY, VMEM, VMEM] + [ANY] * 12,
        out_specs=[ANY] + [VMEM] * 5,
        scratch_shapes=scratch,
        compiler_params=pltpu.CompilerParams(
            collective_id=1, has_side_effects=True, vmem_limit_bytes=67043328
        ),
        name="backward",
    )(lens, tokens.reshape(*dims[1:], 2, rows // (2 * dims[1] * dims[2]), width), six(dy), vecs, stats, six(h1), six(qkv), lse, six(ctx), r1, six(h2), six(gp), terms, *weights)


def finish_kernel(sizes, *refs):
    arrays, small = refs[:6], refs[6]
    results, vectors = refs[7:13], refs[13 : 13 + len(sizes)]
    rest = refs[13 + len(sizes) :]
    buffers, (sems_in, sems_out) = rest[:6], rest[6:]
    pieces = []
    for k, (array, result, buffer) in enumerate(zip(arrays, results, buffers)):
        pieces.append(
            (
                pltpu.make_async_copy(array, buffer, sems_in.at[k]),
                pltpu.make_async_copy(buffer, result, sems_out.at[k]),
            )
        )
    for load, _ in pieces:
        load.start()
    first = 0
    for size, vector in zip(sizes, vectors):
        vector[...] = small[:, first : first + size]
        first += size
    for load, store in pieces:
        load.wait()
        store.start()
    for _, store in pieces:
        store.wait()


def finish(arrays, small, sizes):
    sds = jax.ShapeDtypeStruct
    count = len(arrays)
    made = pl.pallas_call(
        lambda *refs: finish_kernel(sizes, *refs),
        out_shape=[sds(a.shape, a.dtype) for a in arrays] + [sds((1, size), F32) for size in sizes],
        in_specs=[ANY] * 6 + [VMEM],
        out_specs=[ANY] * 6 + [VMEM] * len(sizes),
        scratch_shapes=[pltpu.VMEM(a.shape, a.dtype) for a in arrays] + [DMA((count,)), DMA((count,))],
        name="finish",
    )(*arrays, small)
    return made[:6], [vector.reshape(-1) for vector in made[6:]]


def body(dims, tokens, cotangent, seq_lengths, seq_place, ln1_gain, ln1_bias, w_qkv, q_bias, v_bias, w_out, out_bias, ln2_gain, ln2_bias, w_fc, fc_bias, w_proj, proj_bias):
    rows, width = tokens.shape
    n = dims[0] * dims[1] * dims[2] * 2
    hidden = fc_bias.shape[0] * n
    seq = rows // MB
    per, per_fc = width // n, hidden // n
    slots = lax.axis_index("dp") * MB + iota((seq_place.shape[0], 8, 128), 1)
    lens = jnp.where(seq_place[:, None, None] == slots, seq_lengths[:, None, None], 0)
    lens = jnp.sum(lens, axis=0).astype(F32)

    vectors = (ln1_gain, ln1_bias, q_bias, v_bias, out_bias, ln2_gain, ln2_bias, proj_bias, fc_bias)
    small, first = 0.0, 0
    for vector in vectors:
        small = small + jnp.pad(vector.astype(F32), (first, 1024 - first - vector.shape[0]))
        first += vector.shape[0]
    small = small.reshape(8, 128)
    groups = 4
    chunks = [(0, i, 3 * width // groups) for i in range(0, 3 * width, 3 * width // groups)] + [(1, 0, width)]
    chunks += [(2, i, width) for i in range(0, hidden, width)]
    chunks += [(3, i, width // 4) for i in range(0, width, width // 4)]
    kinds = [0, 0, 0, 0, 0, 0, 1, 0, 1, 0, 1, 0, 1]
    made = forward(dims, lens, tokens, cotangent, (w_qkv, w_out, w_fc, w_proj), small, chunks, kinds)
    out = made[14]
    dx, g_qkv, g_out, g_fc, g_proj, small = backward(dims, lens, tokens, (*made[4:14], made[15]), made[:4], groups)
    sizes = [per] * 8 + [per_fc]
    arrays, own = finish((out, dx.reshape(rows, width), g_qkv, g_out, g_fc, g_proj), small, sizes)
    out, dx, g_qkv, g_out, g_fc, g_proj = arrays
    g_ln1_gain, g_ln1_bias, g_q_bias, g_v_bias, g_out_bias, g_ln2_gain, g_ln2_bias, g_proj_bias, g_fc_bias = own
    return (out, dx, g_ln1_gain, g_ln1_bias, g_qkv, g_q_bias, g_v_bias, g_out, g_out_bias, g_ln2_gain, g_ln2_bias, g_fc, g_fc_bias, g_proj, g_proj_bias)


def solution(mesh):
    dims = grid_dims(mesh.shape["dp"])
    row, vec = P("dp", None), P("dp")
    return jax.shard_map(
        lambda *args: body(dims, *args),
        mesh=mesh,
        in_specs=(row, row, P(), P(), vec, vec, row, vec, vec, row, vec, vec, vec, row, vec, row, vec),
        out_specs=(row, row, vec, vec, row, vec, vec, row, vec, vec, vec, row, vec, row, vec),
        check_vma=False,
    )
```

```python
import jax
import jax.numpy as jnp
from jax import lax
from jax.experimental import pallas as pl
from jax.experimental.pallas import tpu as pltpu
from jax.sharding import PartitionSpec as P

MESH = pl.DeviceIdType.MESH
ANY = pl.BlockSpec(memory_space=pl.ANY)
VMEM = pl.BlockSpec(memory_space=pltpu.VMEM)
DMA = pltpu.SemaphoreType.DMA


def grid_dims(n):
    half = n // 2
    first = 4 if half % 4 == 0 else half
    rest = half // first
    second = 1
    while second * second < rest:
        second *= 2
    return first, second, rest // second


class Place:
    def __init__(self, dims):
        self.dims = dims
        d1, d2, d3 = dims
        me = lax.axis_index("dp")
        self.z = me // (d2 * d3 * 2)
        self.y = (me // (d3 * 2)) % d2
        self.x = (me // 2) % d3
        self.c = me % 2
        self.zs = [(self.z + k) % d1 for k in range(1, d1)]
        self.ys = [(self.y + k) % d2 for k in range(1, d2)]
        self.xs = [(self.x + k) % d3 for k in range(1, d3)]
        self.to_z = [self.dev(z=v) for v in self.zs]
        self.to_y = [self.dev(y=v) for v in self.ys]
        self.to_x = [self.dev(x=v) for v in self.xs]
        self.to_p = self.dev(c=1 - self.c)

    def dev(self, **at):
        z, y, x, c = (at.get(name, getattr(self, name)) for name in "zyxc")
        _, d2, d3 = self.dims
        return (((z * d2 + y) * d3 + x) * 2 + c,)

    def others(self):
        d1, d2, d3 = self.dims
        found = []
        for i in range(1, d1 * d2 * d3):
            z, y, x = (self.z + i // (d2 * d3)) % d1, (self.y + i // d3 % d2) % d2, (self.x + i % d3) % d3
            found.append((z, y, x, self.dev(z=z, y=y, x=x)))
        return found

    def barrier(self, everyone=False):
        semaphore = pltpu.get_barrier_semaphore()
        peers = self.to_z + self.to_y + self.to_x
        if everyone:
            peers = [device for _, _, _, device in self.others()]
        peers = peers + [self.to_p]
        for peer in peers:
            pl.semaphore_signal(semaphore, inc=1, device_id=peer, device_id_type=MESH)
        pl.semaphore_wait(semaphore, len(peers))


def send(source, target, send_sem, recv_sem, device):
    return pltpu.make_async_remote_copy(
        src_ref=source,
        dst_ref=target,
        send_sem=send_sem,
        recv_sem=recv_sem,
        device_id=device,
        device_id_type=MESH,
    )


class Plan:
    def __init__(self, costs, follow):
        self.costs, self.follow = costs, follow
        self.now, self.free, self.flying, self.taken, self.table = 0.0, {}, [], set(), {}

    def issue(self, key, events):
        lane, cost = self.costs(key)
        begin = max(self.now, self.free.get(lane, 0.0))
        self.free[lane] = begin + cost
        self.flying.append((begin + cost + 1.0, key))
        self.flying.sort()
        events.append(("go", key))

    def pump(self, point, passed=0.0, start=(), force=()):
        self.now += passed
        events = self.table.setdefault(point, [])

        def take():
            when, key = self.flying.pop(0)
            self.now = max(self.now, when)
            self.taken.add(key)
            events.append(("take", key))
            for after in self.follow(key, self.taken):
                self.issue(after, events)

        while self.flying and self.flying[0][0] <= self.now:
            take()
        while any(key not in self.taken for key in force):
            take()
        for key in start:
            self.issue(key, events)


class Gather:
    AHEAD = 3

    def __init__(self, place, shards, wholes, chunks, kinds, sems):
        self.at, self.shards, self.wholes = place, shards, wholes
        self.chunks, self.kinds, self.sems = chunks, kinds, sems
        self.first = [first for first, _ in Gather.starts(place.dims, kinds)]

    @staticmethod
    def starts(dims, kinds):
        d1, d2, d3 = dims
        near, starts = d2 + d3 - 2, []
        for stage in range(4):
            at, first = 0, []
            for kind in kinds:
                first.append(at)
                at += ((d1 - 1, near, near, 1), (near, 2 * (d1 - 1), near, 1))[kind][stage]
            starts.append((first, at))
        return starts

    @staticmethod
    def semaphores(dims, kinds):
        return [DMA((size,)) for _, size in Gather.starts(dims, kinds) for _ in range(2)]

    @staticmethod
    def plan(chunks, kinds, unit):
        def costs(key):
            stage, t = key
            size = unit(t)
            if stage == 3:
                return "p", 1.4 * size
            over_z = stage == kinds[t]
            if over_z:
                return "z", (8 if kinds[t] else 4) * size
            return "xy", (0.5, 2, 4)[stage] * size

        def follow(key, taken):
            stage, t = key
            after = [] if stage == 3 else [(stage + 1, t)]
            if stage == 0:
                more = ((1, 2), (3, 4))[t] if t < 2 else (t + Gather.AHEAD,)
                after += [(0, m) for m in more if m < len(chunks)]
            return after

        return Plan(costs, follow)

    def copies(self, stage, t):
        p = self.at
        z, y, x, c = p.z, p.y, p.x, p.c
        i, first, width = self.chunks[t]
        whole, shard, half = self.wholes[i], self.shards[i], width // 2
        full = pl.ds(first, width)
        a, b = pl.ds(first, half), pl.ds(first + half, half)
        pieces = []
        if stage == 0 and self.kinds[t] == 0:
            pieces = [(shard.at[:, full], whole.at[z, y, x, c, :, full], d) for d in p.to_z]
        elif stage == 0:
            pieces = [(shard.at[:, a], whole.at[z, y, x, c, :, a], d) for d in p.to_x]
            pieces += [(shard.at[:, b], whole.at[z, y, x, c, :, b], d) for d in p.to_y]
        elif stage == 1 and self.kinds[t] == 0:
            part = whole.at[:, y, x, c, :, a]
            pieces = [(part, part, d) for d in p.to_x]
            part = whole.at[:, y, x, c, :, b]
            pieces += [(part, part, d) for d in p.to_y]
        elif stage == 1:
            left, right = whole.at[z, y, :, c, :, a], whole.at[z, :, x, c, :, b]
            pieces = [(part, part, d) for d in p.to_z for part in (left, right)]
        elif stage == 2:
            part = whole.at[:, y, :, c, :, a]
            pieces = [(part, part, d) for d in p.to_y]
            part = whole.at[:, :, x, c, :, b]
            pieces += [(part, part, d) for d in p.to_x]
        else:
            part = whole.at[:, :, :, c, :, full]
            pieces = [(part, part, p.to_p)]
        out, back = self.sems[2 * stage], self.sems[2 * stage + 1]
        first = self.first[stage][t]
        return [send(s, d, out.at[first + k], back.at[first + k], to) for k, (s, d, to) in enumerate(pieces)]

    def run(self, events):
        for what, (stage, t) in events:
            for copy in self.copies(stage, t):
                if what == "go":
                    copy.start()
                else:
                    copy.wait_recv()

    def finish(self):
        for stage in range(4):
            for t in range(len(self.chunks)):
                for copy in self.copies(stage, t):
                    copy.wait_send()


def small_copies(place, source, target, sems, stage):
    z, y, x, c = place.z, place.y, place.x, place.c
    d1, d2, d3 = place.dims
    if stage == 0:
        pieces = [(source, target.at[z, y, x, c], d) for d in place.to_z]
    elif stage == 1:
        part = target.at[:, y, x, c]
        pieces = [(part, part, d) for d in place.to_x]
    elif stage == 2:
        part = target.at[:, y, :, c]
        pieces = [(part, part, d) for d in place.to_y]
    else:
        part = target.at[:, :, :, c]
        pieces = [(part, part, place.to_p)]
    base = (0, d1, d1 + d3, d1 + d2 + d3)[stage]
    return [send(s, d, sems[0].at[base + k], sems[1].at[base + k], to) for k, (s, d, to) in enumerate(pieces)]


class Reduce:
    @staticmethod
    def scratch(dims, rows, width, dtype, halves=True):
        d1, d2, d3 = dims
        half = width // 2 if halves else width
        shapes = [pltpu.VMEM((d1, d2, d3, rows, width), dtype)]
        shapes.append(pltpu.VMEM((d2 - 1, d1, d3, rows, half), dtype))
        shapes.append(pltpu.VMEM((d3 - 1, d1, rows, half), dtype))
        if halves:
            shapes.append(pltpu.VMEM((d3 - 1, d1, d2, rows, half), dtype))
            shapes.append(pltpu.VMEM((d2 - 1, d1, rows, half), dtype))
        shapes.append(pltpu.VMEM((d1 - 1, rows, width), dtype))
        near = d2 + d3 - 2
        sizes = (1, near, near, d1 - 1) if halves else (1, d2 - 1, d3 - 1, d1 - 1)
        for size in sizes:
            shapes += [DMA((size,)), DMA((size,))]
        return shapes

    @staticmethod
    def plan(unit):
        def costs(key):
            stage, t = key
            return ("p", "xy", "xy", "z")[stage], (1.4, 4, 2, 4)[stage] * unit(t)

        def follow(key, taken):
            stage, t = key
            after = []
            if stage == 0 and (t < 2 or (1, t - 2) in taken):
                after.append((1, t))
            if stage == 1:
                if (0, t + 2) in taken:
                    after.append((1, t + 2))
                after.append((2, t))
            if stage == 2:
                after.append((3, t))
            return after

        return Plan(costs, follow)

    def __init__(self, place, refs, source, own, result, halves=True, load=None):
        self.at, self.halves, self.load = place, halves, load
        self.source, self.own, self.result = source, own, result
        if halves:
            self.total, self.ya, self.xa, self.xb, self.yb, self.zz = refs[:6]
            self.sems = refs[6:]
        else:
            self.total, self.ya, self.xa, self.zz = refs[:4]
            self.sems = refs[4:]
        width = self.total.shape[-1]
        half = width // 2 if halves else width
        self.a, self.b = pl.ds(0, half), pl.ds(half, half)

    def pieces(self, stage):
        p, h = self.at, self.total
        y, x = p.y, p.x
        if stage == 0:
            return [(self.source.at[:, :, :, 1 - p.c], h, p.to_p)]
        if stage == 1:
            made = [
                (h.at[:, v, :, :, self.a], self.ya.at[k], d)
                for k, (v, d) in enumerate(zip(p.ys, p.to_y))
            ]
            if self.halves:
                made += [
                    (h.at[:, :, v, :, self.b], self.xb.at[k], d)
                    for k, (v, d) in enumerate(zip(p.xs, p.to_x))
                ]
            return made
        if stage == 2:
            made = [
                (h.at[:, y, v, :, self.a], self.xa.at[k], d)
                for k, (v, d) in enumerate(zip(p.xs, p.to_x))
            ]
            if self.halves:
                made += [
                    (h.at[:, v, x, :, self.b], self.yb.at[k], d)
                    for k, (v, d) in enumerate(zip(p.ys, p.to_y))
                ]
            return made
        return [(h.at[v, y, x], self.zz.at[k], d) for k, (v, d) in enumerate(zip(p.zs, p.to_z))]

    def go(self, stage):
        for copy in self.copies(stage):
            copy.start()

    def copies(self, stage):
        out, back = self.sems[2 * stage], self.sems[2 * stage + 1]
        return [
            send(s, d, out.at[k], back.at[k], to) for k, (s, d, to) in enumerate(self.pieces(stage))
        ]

    def arrived(self, stage):
        for copy in self.copies(stage):
            copy.wait()

    def add(self, stage):
        p, h = self.at, self.total
        d1, d2, d3 = p.dims
        f32 = jnp.float32

        def into(at, terms):
            value = h[at].astype(f32)
            for term in terms:
                value = value + term.astype(f32)
            h[at] = value.astype(h.dtype)

        if stage == 0:

            @pl.loop(0, d1)
            def _(i):
                for j in range(d2):
                    for k in range(d3):
                        into((i, j, k), [self.own[i, j, k]])

        elif stage == 1:

            @pl.loop(0, d1)
            def _(i):
                for k in range(d3):
                    into(
                        (i, p.y, k, slice(None), self.a),
                        [self.ya[m, i, k] for m in range(d2 - 1)],
                    )
                if self.halves:
                    for j in range(d2):
                        into(
                            (i, j, p.x, slice(None), self.b),
                            [self.xb[m, i, j] for m in range(d3 - 1)],
                        )

        elif stage == 2:

            @pl.loop(0, d1)
            def _(i):
                into((i, p.y, p.x, slice(None), self.a), [self.xa[m, i] for m in range(d3 - 1)])
                if self.halves:
                    into(
                        (i, p.y, p.x, slice(None), self.b),
                        [self.yb[m, i] for m in range(d2 - 1)],
                    )

        else:
            value = h[p.z, p.y, p.x].astype(f32)
            for m in range(d1 - 1):
                value = value + self.zz[m].astype(f32)
            for cut, target in self.result:
                target[...] = value[:, cut]

    def take(self, stage):
        if stage == 0 and self.load is not None:
            self.load.wait()
        self.arrived(stage)
        self.add(stage)


HEAD_DIM = 64
MB = 2
EPS = 1e-05
BF = jnp.bfloat16
F32 = jnp.float32
NEG = -1e30
GELU_A = 0.044715
GELU_C = 0.7978845608028654


def mm(left, right):
    return lax.dot_general(left, right, (((1,), (0,)), ((), ())), preferred_element_type=F32)


def mm_nt(left, right):
    return lax.dot_general(left, right, (((1,), (1,)), ((), ())), preferred_element_type=F32)


def mm_tn(left, right):
    return lax.dot_general(left, right, (((0,), (0,)), ((), ())), preferred_element_type=F32)


def iota(shape, axis):
    return lax.broadcasted_iota(jnp.int32, shape, axis)


def unpack_vector(block, start, per, width, first):
    row0, lane0 = start // 128, start % 128
    rows = block.shape[0]
    column = iota((128, width), 1) + first
    pick = (iota((128, width), 0) - lane0 == column % per).astype(BF)
    spread = mm(block, pick)
    column = iota((rows, width), 1) + first
    mine = iota((rows, width), 0) == column // per * 8 + row0
    return jnp.sum(jnp.where(mine, spread, 0.0), axis=0, keepdims=True)


def moments(value, keep, first):
    mean = jnp.mean(value, axis=-1, keepdims=True)
    center = value - mean
    scale = lax.rsqrt(jnp.mean(center * center, axis=-1, keepdims=True) + EPS)
    keep[:, first : first + 1] = mean
    keep[:, first + 1 : first + 2] = scale
    return center, scale


def attend_pair(q2, k2, v2, masks, seq):
    half = seq // 2
    lane = iota((1, 128), 1) // HEAD_DIM
    vt = v2.T
    q2 = q2 * jnp.asarray(HEAD_DIM**-0.5, BF)
    ka, kb = k2[:half], k2[half:]
    sums, rows = [], []
    for head in range(2):
        qh = jnp.where(lane == head, q2, 0)
        va, vb = (vt[head * HEAD_DIM : (head + 1) * HEAD_DIM, i * half : (i + 1) * half] for i in range(2))
        first, second = qh[:half], qh[half:]
        s = mm_nt(ka, first) + masks[0]
        sa, sb = mm_nt(ka, second), mm_nt(kb, second) + masks[1]
        top = jnp.max(s, axis=0, keepdims=True)
        e = jnp.exp(s - top)
        total = jnp.sum(e, axis=0, keepdims=True)
        low = mm(va, e.astype(BF)) * (1.0 / total)
        logs = top + jnp.log(total)
        top = jnp.maximum(jnp.max(sa, axis=0, keepdims=True), jnp.max(sb, axis=0, keepdims=True))
        ea, eb = jnp.exp(sa - top), jnp.exp(sb - top)
        total = jnp.sum(ea, axis=0, keepdims=True) + jnp.sum(eb, axis=0, keepdims=True)
        high = (mm(va, ea.astype(BF)) + mm(vb, eb.astype(BF))) * (1.0 / total)
        rows.append(jnp.concatenate([low, high], axis=1))
        sums.append(jnp.concatenate([logs, top + jnp.log(total)], axis=1))
    return jnp.concatenate(rows, axis=0).T, sums


def forward_plan(chunks, kinds, groups, fcs, projs, steps):
    widest = max(width for i, _, width in chunks if i != 3)
    plan = Gather.plan(chunks, kinds, lambda t: 1.2 * (1.0 if chunks[t][0] == 3 else chunks[t][2] / widest))
    fetched, used = set(), set()

    def pump(point, passed=0.0, done=None, **rest):
        if done is not None:
            used.add(done)
        plan.pump(point, passed, **rest)
        for t in range(len(chunks)):
            first = t < 2 or (chunks[t][0] == 3) != (chunks[t - 2][0] == 3)
            if (3, t) in plan.taken and t not in fetched and (first or t - 2 in used):
                fetched.add(t)
                plan.table[point].append(("fetch", (3, t)))

    pump("begin", 0.0, start=[(0, 0)])
    for k in range(4):
        pump(("small", k), 2.0, force=[(k - 1, 0)] if 0 < k < 3 else ())
    pump("spread", 2.5, force=[(2, 0)])
    pump("norm", 2.0)
    for g in range(groups):
        pump(("qkv", g), 0.0, force=[(3, g)])
        pump(("scores", g), 2.4, done=g)
        for i in range(steps):
            pump(("attend", g, i), 0.0 if i == 0 else 1.6)
        pump(("group", g), 1.6)
    t = groups
    pump("out", 0.0, force=[(3, t)])
    for i in range(2):
        pump(("norm2", i), 2.1)
    used.add(t)
    for k in range(fcs):
        pump(("fc", k), 0.0, force=[(3, t + 1 + k)])
        for i in range(2):
            pump(("gelu", k, i), 2.4)
        used.add(t + 1 + k)
        pump(("terms", k), 2.9, force=[(3, t + 2 + k)])
    for k in range(projs):
        pump(("proj", k), 0.0, force=[(3, t + 1 + fcs + k)])
        pump(("done", k), 2.8, done=t + 1 + fcs + k)
    pump("end", 0.0, force=[(3, k) for k in range(len(chunks))])
    return plan.table


def forward_kernel(dims, chunks, kinds, comm, *refs):
    (lens, tokens, cot, s_qkv, s_out, s_fc, s_proj, small) = refs[:8]
    (w_qkv, w_out, w_fc, w_proj, vecs_o, h1_o, qkv_o, lse_o, ctx_o, r1_o, h2_o, gp_o, dy_o, terms_o, out_o, stats_o) = refs[8:24]
    (x_, dy, live, vecs, fcb, h1, qkv, ctx, lse, r1, h2, act, gp, out, sm, wbuf, pbuf, tbuf, diag, shuffled, stats) = refs[24:45]
    local, wsem, psem, osem, outsem, gpsem, tsem, shsem, s_sem, r_sem = refs[45:55]
    sems = refs[55:]
    rows, width = x_.shape
    seq = rows // MB
    hidden = act.shape[1]
    n = dims[0] * dims[1] * dims[2] * 2
    per, per_fc = width // n, hidden // n
    tile = 256
    tiles = rows // tile
    fcs = hidden // width
    groups = sum(i == 0 for i, _, _ in chunks)
    gw = width // groups
    pw = chunks[-1][2]
    projs = width // pw
    gpairs = gw // 128
    steps = MB * gpairs
    plan = forward_plan(chunks, kinds, groups, fcs, projs, steps)
    place = Place(dims)
    z, y, x, c = place.z, place.y, place.x, place.c
    shards = (shuffled, s_out, s_fc, s_proj)
    wholes = (w_qkv, w_out, w_fc, w_proj)
    gather = Gather(place, shards, wholes, chunks, kinds, sems)

    def at_point(*key):
        for event in plan[key[0] if len(key) == 1 else key]:
            if event[0] == "fetch":
                fetch(event[1][1]).start()
            elif comm:
                gather.run([event])

    def fetch(t):
        i, first, w = chunks[t]
        source = wholes[i].at[:, :, :, :, :, pl.ds(first, w)]
        if i == 3:
            return pltpu.make_async_copy(source, pbuf.at[t % 2], psem.at[t % 2])
        return pltpu.make_async_copy(source, wbuf.at[t % 2, :, :, :, :, :, pl.ds(0, w)], wsem.at[t % 2])

    saves = []

    def keep(source, target):
        save = pltpu.make_async_copy(source, target, osem.at[len(saves)])
        save.start()
        saves.append(save)

    shuffle = [
        pltpu.make_async_copy(
            s_qkv.at[:, pl.ds(k * width + g * gw, gw)], shuffled.at[:, pl.ds((3 * g + k) * gw, gw)], shsem.at[3 * g + k]
        )
        for g in range(groups)
        for k in range(3)
    ]
    for move in shuffle:
        move.start()
    loads = [pltpu.make_async_copy(tokens, x_, gpsem.at[0]), pltpu.make_async_copy(cot, dy, gpsem.at[1])]
    for move in loads:
        move.start()
    moves = [
        pltpu.make_async_copy(s, w.at[z, y, x, c], local.at[i])
        for i, (s, w) in enumerate(zip((*shards, small), (*wholes, sm)))
    ]
    for move in moves[1:]:
        move.start()
    place.barrier()
    for move in shuffle:
        move.wait()
    moves[0].start()
    tiny = [small_copies(place, small, sm, (s_sem, r_sem), stage) for stage in range(4)]
    half = seq // 2
    for stage in range(4):
        if comm:
            for copy in tiny[stage]:
                copy.start()
        if stage == 0:
            at_point("begin")
            for slot in range(MB):
                length = lens[slot : slot + 1, 0:1]
                live[slot * seq : (slot + 1) * seq, :] = jnp.where(iota((seq, 1), 0).astype(F32) < length, 1.0, 0.0)
                causal = iota((half, half), 0) <= iota((half, half), 1)
                late = (iota((half, half), 0) + half).astype(F32) < length
                diag[0] = jnp.where(causal, 0.0, NEG)
                diag[1 + slot] = jnp.where(causal & late, 0.0, NEG)
            for move in moves:
                move.wait()
        if stage == 1:
            loads[1].wait()
            vecs[8:16, :] = jnp.zeros((8, width), F32)

            @pl.loop(0, tiles)
            def _(i):
                at = pl.ds(pl.multiple_of(i * tile, tile), tile)
                value = jnp.where(live[at, :] > 0.5, dy[at, :].astype(F32), 0.0)
                dy[at, :] = value.astype(BF)
                vecs[8:9, :] += jnp.sum(value, axis=0, keepdims=True)

            keep(dy, dy_o)
        if comm:
            for copy in tiny[stage]:
                copy.wait_recv()
        at_point("small", stage)
    block = sm[...].reshape(n * 8, 128).astype(BF)
    for v in range(8):
        vecs[v : v + 1, :] = unpack_vector(block, v * per, per, width, 0)
    for part in range(fcs):
        fcb[:, part * width : (part + 1) * width] = unpack_vector(block, 8 * per, per_fc, width, part * width)
    at_point("spread")
    loads[0].wait()

    @pl.loop(0, rows // 128)
    def _(i):
        at = pl.ds(pl.multiple_of(i * 128, 128), 128)
        center, scale = moments(x_[at, :].astype(F32), stats.at[at, :], 0)
        h1[at, :] = (center * scale * vecs[0:1, :] + vecs[1:2, :]).astype(BF)

    keep(h1, h1_o)
    keep(vecs, vecs_o)
    at_point("norm")

    @pl.loop(0, groups)
    def _(g):
        for k in range(groups):

            @pl.when(g == k)
            def _():
                at_point("qkv", k)
                fetch(k).wait()

        first = pl.multiple_of(g * gw, gw)

        @pl.loop(0, tiles)
        def _(i):
            at = pl.ds(pl.multiple_of(i * tile, tile), tile)
            value = mm(h1[at, :], wbuf[g % 2, :, :, :, :, :, 0 : 3 * gw].reshape(width, 3 * gw))
            for k, bias in ((0, 2), (1, None), (2, 3)):
                part = value[:, k * gw : (k + 1) * gw]
                if bias is not None:
                    part = part + vecs[bias : bias + 1, pl.ds(first, gw)]
                qkv[at, pl.ds(k * width + first, gw)] = part.astype(BF)

        for k in range(groups):
            if plan["scores", k]:

                @pl.when(g == k)
                def _():
                    at_point("scores", k)

        @pl.loop(0, steps)
        def _(i):
            for k in range(groups):
                for m in range(steps):
                    if plan["attend", k, m]:

                        @pl.when((g == k) & (i == m))
                        def _():
                            at_point("attend", k, m)

            slot, pair = i // gpairs, g * gpairs + i % gpairs
            at = pl.ds(pl.multiple_of(slot * seq, seq), seq)
            col = pl.multiple_of(pair * 128, 128)
            value, sums = attend_pair(
                qkv[at, pl.ds(col, 128)],
                qkv[at, pl.ds(width + col, 128)],
                qkv[at, pl.ds(2 * width + col, 128)],
                [diag[0], diag[1 + slot]],
                seq,
            )
            ctx[at, pl.ds(col, 128)] = value.astype(BF)
            for head in range(2):
                lse[slot * (width // HEAD_DIM) + pair * 2 + head] = sums[head]

        for k in range(groups):
            if plan["group", k]:

                @pl.when(g == k)
                def _():
                    at_point("group", k)

    keep(qkv, qkv_o)
    keep(ctx, ctx_o)
    keep(lse, lse_o)
    t = groups
    at_point("out")
    fetch(t).wait()

    @pl.loop(0, tiles)
    def _(i):
        at = pl.ds(pl.multiple_of(i * tile, tile), tile)
        value = mm(ctx[at, :], wbuf[t % 2].reshape(width, width)) + vecs[4:5, :]
        value = value + x_[at, :].astype(F32)
        r1[at, :] = value
        center, scale = moments(value, stats.at[at, :], 2)
        h2[at, :] = (center * scale * vecs[5:6, :] + vecs[6:7, :]).astype(BF)
        for k in range(2):

            @pl.when(i == (k + 1) * tiles // 2 - 1)
            def _():
                at_point("norm2", k)

    keep(r1, r1_o)
    keep(h2, h2_o)
    keep(stats, stats_o)

    def keep_gp(k):
        return pltpu.make_async_copy(gp.at[k % 2], gp_o.at[:, pl.ds(pl.multiple_of(k * width, width), width)], gpsem.at[k % 2])

    def each(index, count, *name):
        for k in range(count):
            key = (*name, k)
            if plan[key]:

                @pl.when(index == k)
                def _():
                    at_point(*key)

    def keep_terms(k):
        return pltpu.make_async_copy(tbuf.at[k % 2], terms_o.at[k], tsem.at[k % 2])

    @pl.loop(0, fcs)
    def _(k):
        each(k, fcs, "fc")
        buffer = (groups + 1 + k) % 2
        for m in range(fcs):

            @pl.when(k == m)
            def _():
                fetch(groups + 1 + m).wait()

        @pl.when(k >= 2)
        def _():
            keep_gp(k - 2).wait()
            keep_terms(k - 2).wait()

        cut = pl.ds(pl.multiple_of(k * width, width), width)

        @pl.loop(0, 2)
        def _(i):
            for part in range(tiles // 2):
                at = pl.ds(pl.multiple_of((i * (tiles // 2) + part) * tile, tile), tile)
                u = mm(h2[at, :], wbuf[buffer].reshape(width, width)) + fcb[:, cut]
                square = u * u
                inner = u * (GELU_C + (GELU_C * GELU_A) * square)
                gate = 0.5 + 0.5 * jnp.tanh(inner)
                value = u * gate
                act[at, cut] = value.astype(BF)
                slope = gate + value * (2.0 - 2.0 * gate) * (GELU_C + (3.0 * GELU_C * GELU_A) * square)
                gp[k % 2, at, :] = slope.astype(BF)
            for n_k in range(fcs):
                for m in range(2):
                    if plan["gelu", n_k, m]:

                        @pl.when((k == n_k) & (i == m))
                        def _():
                            at_point("gelu", n_k, m)

        keep_gp(k).start()

        @pl.loop(0, 2)
        def _(i):
            some = pl.ds(pl.multiple_of(k * width + i * (width // 2), width // 2), width // 2)
            value = mm_tn(act[:, some], dy[...]).astype(BF)
            blocks = (dims[1] // 2, dims[2], 2, per_fc, width)
            tbuf[k % 2, pl.ds(i * blocks[0], blocks[0])] = value.reshape(blocks)

        keep_terms(k).start()
        each(k, fcs, "terms")

    def keep_out(k):
        cut = pl.ds(pl.multiple_of(k * pw, pw), pw)
        return pltpu.make_async_copy(out.at[:, cut], out_o.at[:, cut], outsem.at[k])

    @pl.loop(0, projs)
    def _(k):
        cut = pl.ds(pl.multiple_of(k * pw, pw), pw)
        buffer = (groups + 1 + fcs + k) % 2

        for m in range(projs):

            @pl.when(k == m)
            def _():
                at_point("proj", m)
                fetch(groups + 1 + fcs + m).wait()

        @pl.loop(0, tiles)
        def _(i):
            at = pl.ds(pl.multiple_of(i * tile, tile), tile)
            value = mm(act[at, :], pbuf[buffer].reshape(hidden, pw)) + (r1[at, cut] + vecs[7:8, cut])
            out[at, cut] = jnp.where(live[at, :] > 0.5, value, 0.0).astype(BF)

        keep_out(k).start()
        each(k, projs, "done")

    at_point("end")
    for k in range(max(fcs - 2, 0), fcs):
        keep_gp(k).wait()
    for k in range(max(fcs - 2, 0), fcs):
        keep_terms(k).wait()
    for k in range(projs):
        keep_out(k).wait()
    for save in saves:
        save.wait()
    if comm:
        gather.finish()
        for copies in tiny:
            for copy in copies:
                copy.wait_send()


def forward(dims, lens, tokens, cot, shards, small, chunks, kinds, comm=True):
    rows, width = tokens.shape
    n = dims[0] * dims[1] * dims[2] * 2
    hidden = shards[2].shape[1]
    heads = width // HEAD_DIM
    seq = rows // MB
    pw = chunks[-1][2]
    groups = sum(i == 0 for i, _, _ in chunks)
    sds = jax.ShapeDtypeStruct
    shapes = [sds((*dims, 2, *s.shape), s.dtype) for s in shards]
    shapes += [
        sds((16, width), F32),
        sds((rows, width), BF),
        sds((rows, 3 * width), BF),
        sds((MB * heads, 1, seq), F32),
        sds((rows, width), BF),
        sds((rows, width), F32),
        sds((rows, width), BF),
        sds((rows, hidden), BF),
        sds((rows, width), BF),
        sds((*dims, 2, hidden // n, width), BF),
        sds((rows, width), BF),
        sds((rows, 128), F32),
    ]
    scratch = [
        pltpu.VMEM((rows, width), BF),
        pltpu.VMEM((rows, width), BF),
        pltpu.VMEM((rows, 1), F32),
        pltpu.VMEM((16, width), F32),
        pltpu.VMEM((1, hidden), F32),
        pltpu.VMEM((rows, width), BF),
        pltpu.VMEM((rows, 3 * width), BF),
        pltpu.VMEM((rows, width), BF),
        pltpu.VMEM((MB * heads, 1, seq), F32),
        pltpu.VMEM((rows, width), F32),
        pltpu.VMEM((rows, width), BF),
        pltpu.VMEM((rows, hidden), BF),
        pltpu.VMEM((2, rows, width), BF),
        pltpu.VMEM((rows, width), BF),
        pltpu.VMEM((*dims, 2, *small.shape), small.dtype),
        pltpu.VMEM((2, *dims, 2, width // n, width), BF),
        pltpu.VMEM((2, *dims, 2, hidden // n, pw), BF),
        pltpu.VMEM((2, *dims[1:], 2, hidden // n, width), BF),
        pltpu.VMEM((1 + MB, seq // 2, seq // 2), F32),
        pltpu.VMEM(shards[0].shape, BF),
        pltpu.VMEM((rows, 128), F32),
        DMA((5,)),
        DMA((2,)),
        DMA((2,)),
        DMA((9,)),
        DMA((width // pw,)),
        DMA((2,)),
        DMA((2,)),
        DMA((3 * groups,)),
        DMA((sum(dims) + 1,)),
        DMA((sum(dims) + 1,)),
        *Gather.semaphores(dims, kinds),
    ]
    return pl.pallas_call(
        lambda *refs: forward_kernel(dims, chunks, kinds, comm, *refs),
        out_shape=shapes,
        in_specs=[VMEM, ANY, ANY, ANY] + [VMEM] * 4,
        out_specs=[ANY] * 16,
        scratch_shapes=scratch,
        compiler_params=pltpu.CompilerParams(
            collective_id=0, has_side_effects=True, vmem_limit_bytes=60 * 1024 * 1024
        ),
        name="forward",
    )(lens, tokens, cot, *shards, small)


def pack_vector(row, start, per, n):
    width = row.shape[1]
    pick = (iota((128, width), 0) - start % 128 == iota((128, width), 1) % per).astype(BF)
    mine = iota((n, width), 0) == iota((n, width), 1) // per
    total = 0.0
    for _ in range(3):
        part = row.astype(BF)
        row = row - part.astype(F32)
        total = total + mm_nt(jnp.where(mine, part.astype(F32), 0.0).astype(BF), pick)
    return total


def norm_back(value, kept, gain, grad):
    scale = kept[:, 1:2]
    normed = (value - kept[:, 0:1]) * scale
    scaled = grad * gain
    mean = jnp.mean(scaled, axis=-1, keepdims=True)
    cross = jnp.mean(scaled * normed, axis=-1, keepdims=True)
    return (scaled - mean - normed * cross) * scale, grad * normed


def attend_back(q2, k2, v2, o2, c2, lse, masks, seq):
    half = seq // 2
    lane = iota((1, 128), 1) // HEAD_DIM
    prod = o2.astype(F32) * c2.astype(F32)
    heads = (iota((8, 128), 1) // HEAD_DIM == iota((8, 128), 0)).astype(BF)
    high = prod.astype(BF)
    delta = mm_nt(heads, high) + mm_nt(heads, (prod - high.astype(F32)).astype(BF))
    kt = k2.T
    q2 = q2 * jnp.asarray(HEAD_DIM**-0.5, BF)
    cuts = (slice(0, half), slice(half, seq))
    dk, dv, dq = [0.0, 0.0], [0.0, 0.0], []
    for head in range(2):
        qh = jnp.where(lane == head, q2, 0)
        oh = jnp.where(lane == head, o2, 0)
        kh = kt[head * HEAD_DIM : (head + 1) * HEAD_DIM]
        parts = [0.0, 0.0]
        for key, query in ((0, 0), (0, 1), (1, 1)):
            qb, ob, cut = qh[cuts[query]], oh[cuts[query]], cuts[query]
            s = mm_nt(k2[cuts[key]], qb) - lse[head][:, cut]
            if key == query:
                s = s + masks[key]
            p = jnp.exp(s)
            dp = mm_nt(v2[cuts[key]], ob)
            ds = (p * (dp - delta[head : head + 1, cut])).astype(BF)
            dv[key] = dv[key] + mm(p.astype(BF), ob)
            dk[key] = dk[key] + mm(ds, qb)
            parts[query] = parts[query] + mm(kh[:, cuts[key]], ds)
        dq.append(jnp.concatenate(parts, axis=1))
    dq = jnp.concatenate(dq, axis=0).T * HEAD_DIM**-0.5
    return dq, jnp.concatenate(dk, axis=0), jnp.concatenate(dv, axis=0)


def backward_plan(projs, fcs, groups, steps, slabs):
    out = projs + fcs
    plan = Reduce.plan(lambda t: 1.45 if t <= out else 1.08)
    pump = plan.pump
    pump("start", 0.0, start=[(0, 0), (0, 1)])
    pump("loaded", 1.0)
    late = list(range(2, projs))
    for f in range(fcs):
        for name, passed in (("da", 3.2), ("dh", 2.9)):
            j = late.pop(0) if late else None
            force = [] if j is None else [(0, j - 2)]
            if name == "dh" and f >= 2:
                force.append((0, projs + f - 2))
            pump((name, f), passed, force=force, start=[] if j is None else [(0, j)])
        pump(("gfc", f), 2.9, start=[(0, projs + f)])
    for i in range(slabs):
        pump(("ln2", i), 2.0)
    pump("dctx", 3.0, force=[(0, out - 2)])
    pump("gout", 3.0, start=[(0, out)])
    for g in range(groups):
        for i in range(steps):
            pump(("back", g, i), 0.0 if i == 0 else 2.0)
        pump(("grads", g), 2.0, force=[(0, out - 1 + g)])
        pump(("gqkv", g), 2.2, start=[(0, out + 1 + g)])
    for i in range(slabs):
        pump(("dx", i), 3.4)
    pump("end", 4.0, force=[(3, t) for t in range(out + 1 + groups)])
    return plan.table


def backward_kernel(dims, groups, sizes, comm, *refs):
    (lens, tokens, dy, vecs, stats, h1_i, qkv_i, lse_i, ctx_i, r1_i, h2_i, gp_i, terms, w_qkv, w_out, w_fc, w_proj) = refs[:17]
    dx_o, finals, g_small = refs[17], refs[18:22], refs[22]
    slots, wp, f_dh, f_r1, gvec, gfc, lse, diag, stage, owns, sstage = refs[23:34]
    lsem, wsem, osem, qsem, fsem = refs[34:39]
    g_qkv, g_out, g_fc, g_proj = refs[39:43]
    refs = refs[43:]
    d1, d2, d3 = dims
    n = d1 * d2 * d3 * 2
    rows, width = f_dh.shape
    hidden = gfc.shape[1]
    seq = rows // MB
    half = seq // 2
    per, per_fc = width // n, hidden // n
    fcs = hidden // width
    gw = width // groups
    pw = owns.shape[-1]
    projs = width // pw
    tile = rows // d1
    gpairs = gw // 128
    steps = MB * gpairs
    place = Place(dims)
    c = place.c
    plan = backward_plan(projs, fcs, groups, steps, d1)
    sets = []
    for size in sizes:
        sets.append(refs[:size])
        refs = refs[size:]
    parts = []
    for j in range(projs):
        cut = pl.ds(j * pw, pw)
        own = owns.at[j % 2]
        move = pltpu.make_async_copy(terms.at[:, :, :, c, :, cut], own, osem.at[j % 2])
        result = [(slice(None), g_proj.at[:, cut])]
        parts.append(Reduce(place, sets[j], terms.at[:, :, :, :, :, cut], own, result, load=move))
    for f in range(fcs):
        result = [(slice(None), g_fc.at[:, pl.ds(f * width, width)])]
        parts.append(Reduce(place, sets[projs + f], stage.at[f % 2], stage.at[f % 2, :, :, :, c], result))
    b = fcs % 2
    parts.append(Reduce(place, sets[projs + fcs], stage.at[b], stage.at[b, :, :, :, c], [(slice(None), g_out)]))
    gcut = pl.ds(0, 3 * gw)
    for g in range(groups):
        b = (fcs + 1 + g) % 2
        result = [
            (slice(k * gw, (k + 1) * gw), g_qkv.at[:, pl.ds(k * width + g * gw, gw)]) for k in range(3)
        ]
        source, own = stage.at[b, :, :, :, :, :, gcut], stage.at[b, :, :, :, c, :, gcut]
        parts.append(Reduce(place, sets[projs + fcs + 1 + g], source, own, result))

    spans = [[(3, j * pw, pw)] for j in range(projs)] + [[(2, f * width, width)] for f in range(fcs)]
    spans += [[(1, 0, width)]] + [[(0, k * width + g * gw, gw) for k in range(3)] for g in range(groups)]
    held, copies, at = (g_qkv, g_out, g_fc, g_proj), [], 0
    for span in spans:
        copies.append([])
        for i, first, size in span:
            cut = pl.ds(first, size)
            copies[-1].append(pltpu.make_async_copy(held[i].at[:, cut], finals[i].at[:, cut], fsem.at[at]))
            at += 1

    def at_point(*key):
        if not comm:
            return
        for what, (step, t) in plan[key[0] if len(key) == 1 else key]:
            if what == "take":
                parts[t].take(step)
                if step == 3:
                    for copy in copies[t]:
                        copy.start()
            else:
                parts[t].go(step)
                if step == 0 and parts[t].load is not None:
                    parts[t].load.start()

    def load(source, slot, k):
        return pltpu.make_async_copy(source, slots.at[slot], lsem.at[k])

    def cols(source, k):
        return source.at[:, :, :, :, :, pl.ds(pl.multiple_of(k * width, width), width)]

    def whole(slot):
        return slots[slot].reshape(rows, width)

    def piece(slot, i):
        return slots[slot, i].reshape(tile, width)

    def put(slot, i, value):
        slots[slot, i] = value.astype(BF).reshape(d2, d3, 2, per, width)

    def fetch_proj(f):
        return pltpu.make_async_copy(w_proj.at[f], wp.at[f % 2], wsem.at[f % 2])

    def fetch_ff(f):
        return [fetch_proj(f), load(cols(gp_i, f), 3 + f % 2, 3 + f % 2), load(cols(w_fc, f), 1 + f % 2, 1 + f % 2)]

    def w_third(k, target):
        return [
            pltpu.make_async_copy(
                w_qkv.at[:, :, :, :, :, pl.ds((3 * g + k) * gw, gw)],
                target.at[:, :, :, :, :, pl.ds(g * gw, gw)],
                qsem.at[k, g],
            )
            for g in range(groups)
        ]

    load(dy, 0, 0).start()
    for move in fetch_ff(0):
        move.start()
    load(h2_i, 6, 6).start()
    load(ctx_i, 7, 7).start()
    lload = pltpu.make_async_copy(lse_i, lse, lsem.at[5])
    lload.start()
    for slot in range(MB):
        causal = iota((half, half), 0) <= iota((half, half), 1)
        late = (iota((half, half), 0) + half).astype(F32) < lens[slot : slot + 1, 0:1]
        diag[0] = jnp.where(causal, 0.0, NEG)
        diag[1 + slot] = jnp.where(causal & late, 0.0, NEG)
    gvec[...] = jnp.zeros_like(gvec)
    gfc[...] = jnp.zeros_like(gfc)
    f_dh[...] = jnp.zeros_like(f_dh)
    gvec[7:8, :] = vecs[8:9, :]
    place.barrier(everyone=True)
    at_point("start")
    load(dy, 0, 0).wait()
    at_point("loaded")
    load(h2_i, 6, 6).wait()

    def each(index, count, *name):
        for k in range(count):
            key = (*name, k)
            if plan[key]:

                @pl.when(index == k)
                def _():
                    at_point(*key)

    @pl.loop(0, fcs)
    def _(f):
        for move in fetch_ff(f):
            move.wait()

        @pl.when(f + 1 < fcs)
        def _():
            for move in fetch_ff(f + 1):
                move.start()

        cut = pl.ds(pl.multiple_of(f * width, width), width)

        @pl.loop(0, d1 // 2)
        def _(h):
            for i in (2 * h, 2 * h + 1):
                da = mm_nt(piece(0, i), wp[f % 2].reshape(rows, width))
                du = (da * piece(3 + f % 2, i).astype(F32)).astype(BF)
                put(5, i, du)
                gfc[:, cut] += jnp.sum(du.astype(F32), axis=0, keepdims=True)

        each(f, fcs, "da")

        @pl.loop(0, d1 // 2)
        def _(h):
            for i in (2 * h, 2 * h + 1):
                at = pl.ds(pl.multiple_of(i * tile, tile), tile)
                f_dh[at, :] += mm_nt(piece(5, i), whole(1 + f % 2))

        each(f, fcs, "dh")

        @pl.loop(0, 2)
        def _(i):
            col = pl.ds(pl.multiple_of(i * (width // 2), width // 2), width // 2)
            value = mm_tn(slots[6, :, :, :, :, :, col].reshape(rows, width // 2), whole(5)).astype(BF)
            stage[f % 2, pl.ds(i * (d1 // 2), d1 // 2)] = value.reshape(d1 // 2, d2, d3, 2, per, width)

        each(f, fcs, "gfc")

    def r1_tile(i):
        return pltpu.make_async_copy(r1_i.at[pl.ds(i * tile, tile)], f_r1.at[i % 2], wsem.at[i % 2])

    r1_tile(0).start()
    load(w_out, 1, 1).start()
    for k, slot in enumerate((3, 4, 6)):
        load(cols(qkv_i, k), slot, slot).start()

    @pl.loop(0, d1)
    def _(i):
        r1_tile(i).wait()

        @pl.when(i + 1 < d1)
        def _():
            r1_tile(i + 1).start()

        at = pl.ds(pl.multiple_of(i * tile, tile), tile)
        grad = f_dh[at, :]
        value, norms = norm_back(f_r1[i % 2], stats[at, 2:4], vecs[5:6, :], grad)
        value = value + piece(0, i).astype(F32)
        f_dh[at, :] = value
        low = value.astype(BF)
        put(5, i, low)
        gvec[5:6, :] += jnp.sum(norms, axis=0, keepdims=True)
        gvec[6:7, :] += jnp.sum(grad, axis=0, keepdims=True)
        gvec[4:5, :] += jnp.sum(low.astype(F32), axis=0, keepdims=True)
        for k in range(d1):
            if plan["ln2", k]:

                @pl.when(i == k)
                def _():
                    at_point("ln2", k)

    load(ctx_i, 7, 7).wait()
    load(w_out, 1, 1).wait()
    load(h1_i, 0, 0).start()

    @pl.loop(0, d1)
    def _(i):
        put(2, i, mm_nt(piece(5, i), whole(1)))

    for move in w_third(0, slots.at[1]):
        move.start()
    at_point("dctx")

    @pl.loop(0, 2)
    def _(i):
        col = pl.ds(pl.multiple_of(i * (width // 2), width // 2), width // 2)
        value = mm_tn(slots[7, :, :, :, :, :, col].reshape(rows, width // 2), whole(5)).astype(BF)
        stage[fcs % 2, pl.ds(i * (d1 // 2), d1 // 2)] = value.reshape(d1 // 2, d2, d3, 2, per, width)

    for move in w_third(1, slots.at[5]):
        move.start()
    loadx = pltpu.make_async_copy(tokens, wp.at[0], lsem.at[2])
    loadx.start()
    at_point("gout")
    for k, slot in enumerate((3, 4, 6)):
        load(cols(qkv_i, k), slot, slot).wait()
    lload.wait()
    load(h1_i, 0, 0).wait()
    hslab = d1 // MB

    @pl.loop(0, groups)
    def _(g):
        @pl.loop(0, steps)
        def _(i):
            for k in range(groups):
                for m in range(steps):
                    if plan["back", k, m]:

                        @pl.when((g == k) & (i == m))
                        def _():
                            at_point("back", k, m)

            slot, pair = i // gpairs, g * gpairs + i % gpairs
            slab = pl.ds(slot * hslab, hslab)
            lanes = pl.ds(pl.multiple_of(pair * 128, 128), 128)

            def get(s):
                return slots[s, slab, :, :, :, :, lanes].reshape(seq, 128)

            head = slot * (width // HEAD_DIM) + 2 * pair
            grads = attend_back(
                get(3), get(4), get(6), get(2), get(7), [lse[head], lse[head + 1]], [diag[0], diag[1 + slot]], seq
            )
            for s, value in zip((3, 4, 6), grads):
                slots[s, slab, :, :, :, :, lanes] = value.astype(BF).reshape(hslab, d2, d3, 2, per, 128)

        for k in range(groups):
            if plan["grads", k] or k == groups - 1:

                @pl.when(g == k)
                def _():
                    at_point("grads", k)
                    if k == groups - 1:
                        for move in w_third(2, stage.at[(fcs + groups - 1) % 2]):
                            move.start()

        mine = pl.ds(pl.multiple_of(g * gw, gw), gw)
        buffer = (fcs + 1 + g) % 2

        @pl.loop(0, 2)
        def _(i):
            col = pl.ds(pl.multiple_of(i * (width // 2), width // 2), width // 2)
            left = slots[0, :, :, :, :, :, col].reshape(rows, width // 2)
            for k, s in enumerate((3, 4, 6)):
                value = mm_tn(left, slots[s, :, :, :, :, :, mine].reshape(rows, gw)).astype(BF)
                stage[buffer, pl.ds(i * (d1 // 2), d1 // 2), :, :, :, :, k * gw : (k + 1) * gw] = value.reshape(
                    d1 // 2, d2, d3, 2, per, gw
                )

        for k in range(groups):

            @pl.when(g == k)
            def _():
                at_point("gqkv", k)

    thirds = (slots.at[1], slots.at[5], stage.at[(fcs + groups - 1) % 2])
    for k, target in enumerate(thirds):
        for move in w_third(k, target):
            move.wait()
    loadx.wait()
    blocks = d2 * d3 // d1

    @pl.loop(0, d1)
    def _(i):
        at = pl.ds(pl.multiple_of(i * tile, tile), tile)
        x_tile = wp[0, i // d3, i % d3] if blocks == 1 else wp[0, i]
        x_tile = x_tile.reshape(tile, width)
        grad = mm_nt(piece(3, i), whole(1)) + mm_nt(piece(4, i), whole(5)) + mm_nt(piece(6, i), thirds[2][...].reshape(rows, width))
        value, norms = norm_back(x_tile.astype(F32), stats[at, 0:2], vecs[0:1, :], grad)
        put(2, i, value + f_dh[at, :])
        gvec[0:1, :] += jnp.sum(norms, axis=0, keepdims=True)
        gvec[1:2, :] += jnp.sum(grad, axis=0, keepdims=True)
        gvec[2:3, :] += jnp.sum(piece(3, i).astype(F32), axis=0, keepdims=True)
        gvec[3:4, :] += jnp.sum(piece(6, i).astype(F32), axis=0, keepdims=True)
        for k in range(d1):
            if plan["dx", k]:

                @pl.when(i == k)
                def _():
                    at_point("dx", k)

    save = pltpu.make_async_copy(slots.at[2], dx_o, lsem.at[0])
    save.start()
    lines = [0.0] * (sstage.shape[-1] // 128)
    for v in range(8):
        lines[v * per // 128] += pack_vector(gvec[v : v + 1, :], v * per, per, n)
    some = n // fcs
    packed = [pack_vector(gfc[:, k * width : (k + 1) * width], 8 * per, per_fc, some) for k in range(fcs)]
    lines[8 * per // 128] += jnp.concatenate(packed, axis=0)
    for k, line in enumerate(lines):
        for d in range(n):
            at = (d // (d2 * d3 * 2), d // (d3 * 2) % d2, d // 2 % d3, d % 2)
            sstage[(*at, slice(None), slice(k * 128, (k + 1) * 128))] = line[d : d + 1, :]
    mine, theirs, found, s_sem, r_sem = refs
    if comm:
        swap = send(sstage.at[:, :, :, 1 - c], mine, s_sem.at[0], r_sem.at[0], place.to_p)
        swap.start()
        swap.wait()
        theirs[...] = mine[...] + sstage[:, :, :, c]
        sends = [
            send(theirs.at[z, y, x], found.at[k], s_sem.at[k + 1], r_sem.at[k + 1], device)
            for k, (z, y, x, device) in enumerate(place.others())
        ]
        for copy in sends:
            copy.start()
    at_point("end")
    if comm:
        for copy in sends:
            copy.wait()
        value = theirs[place.z, place.y, place.x]
        for k in range(len(sends)):
            value = value + found[k]
        g_small[...] = value
        for some in copies:
            for copy in some:
                copy.wait()
    save.wait()


def backward(dims, lens, tokens, saved, weights, groups, comm=True):
    vecs, h1, qkv, lse, ctx, r1, h2, gp, dy, terms, stats = saved
    rows, width = tokens.shape
    n = dims[0] * dims[1] * dims[2] * 2
    hidden = gp.shape[1]
    seq = rows // MB
    per, per_fc = width // n, hidden // n
    fcs = hidden // width
    projs = 4
    pw = width // projs
    lanes = (8 * per + per_fc + 127) // 128 * 128

    def six(a):
        return a.reshape(*dims, 2, a.shape[0] // n, a.shape[1])

    sds = jax.ShapeDtypeStruct
    scratch = [
        pltpu.VMEM((8, *dims, 2, per, width), BF),
        pltpu.VMEM((2, *dims[1:], 2, per_fc, width), BF),
        pltpu.VMEM((rows, width), F32),
        pltpu.VMEM((2, rows // dims[0], width), F32),
        pltpu.VMEM((8, width), F32),
        pltpu.VMEM((1, hidden), F32),
        pltpu.VMEM(lse.shape, F32),
        pltpu.VMEM((1 + MB, seq // 2, seq // 2), F32),
        pltpu.VMEM((2, *dims, 2, per, width), BF),
        pltpu.VMEM((2, *dims, per_fc, pw), BF),
        pltpu.VMEM((*dims, 2, 1, lanes), F32),
        DMA((8,)),
        DMA((2,)),
        DMA((2,)),
        DMA((3, groups)),
        DMA((projs + fcs + 1 + 3 * groups,)),
        pltpu.VMEM((per, 3 * width), F32),
        pltpu.VMEM((per, width), F32),
        pltpu.VMEM((per, hidden), F32),
        pltpu.VMEM((per_fc, width), F32),
    ]
    sizes = []
    shapes = [(per_fc, pw)] * projs + [(per, width)] * (fcs + 1) + [(per, 3 * width // groups)] * groups
    for block_rows, block_cols in shapes:
        made = Reduce.scratch(dims, block_rows, block_cols, BF)
        sizes.append(len(made))
        scratch += made
    half_n = n // 2
    scratch += [pltpu.VMEM((*dims, 1, lanes), F32)] * 2 + [pltpu.VMEM((half_n - 1, 1, lanes), F32)]
    scratch += [DMA((half_n,)), DMA((half_n,))]
    outs = [
        sds((*dims, 2, per, width), BF),
        sds((per, 3 * width), F32),
        sds((per, width), F32),
        sds((per, hidden), F32),
        sds((per_fc, width), F32),
        sds((1, lanes), F32),
    ]
    return pl.pallas_call(
        lambda *refs: backward_kernel(dims, groups, sizes, comm, *refs),
        out_shape=outs,
        in_specs=[VMEM, ANY, ANY, VMEM, VMEM] + [ANY] * 12,
        out_specs=[ANY] * 5 + [VMEM],
        scratch_shapes=scratch,
        compiler_params=pltpu.CompilerParams(
            collective_id=1, has_side_effects=True, vmem_limit_bytes=67043328
        ),
        name="backward",
    )(lens, tokens.reshape(*dims[1:], 2, rows // (2 * dims[1] * dims[2]), width), six(dy), vecs, stats, six(h1), six(qkv), lse, six(ctx), r1, six(h2), six(gp), terms, *weights)


def finish_kernel(sizes, *refs):
    arrays, small = refs[:6], refs[6]
    results, vectors = refs[7:13], refs[13 : 13 + len(sizes)]
    rest = refs[13 + len(sizes) :]
    buffers, (sems_in, sems_out) = rest[:6], rest[6:]
    pieces = []
    for k, (array, result, buffer) in enumerate(zip(arrays, results, buffers)):
        pieces.append(
            (
                pltpu.make_async_copy(array, buffer, sems_in.at[k]),
                pltpu.make_async_copy(buffer, result, sems_out.at[k]),
            )
        )
    for load, _ in pieces:
        load.start()
    first = 0
    for size, vector in zip(sizes, vectors):
        vector[...] = small[:, first : first + size]
        first += size
    for load, store in pieces:
        load.wait()
        store.start()
    for _, store in pieces:
        store.wait()


def finish(arrays, small, sizes):
    sds = jax.ShapeDtypeStruct
    count = len(arrays)
    made = pl.pallas_call(
        lambda *refs: finish_kernel(sizes, *refs),
        out_shape=[sds(a.shape, a.dtype) for a in arrays] + [sds((1, size), F32) for size in sizes],
        in_specs=[ANY] * 6 + [VMEM],
        out_specs=[ANY] * 6 + [VMEM] * len(sizes),
        scratch_shapes=[pltpu.VMEM(a.shape, a.dtype) for a in arrays] + [DMA((count,)), DMA((count,))],
        name="finish",
    )(*arrays, small)
    return made[:6], [vector.reshape(-1) for vector in made[6:]]


def body(dims, tokens, cotangent, seq_lengths, seq_place, ln1_gain, ln1_bias, w_qkv, q_bias, v_bias, w_out, out_bias, ln2_gain, ln2_bias, w_fc, fc_bias, w_proj, proj_bias):
    rows, width = tokens.shape
    n = dims[0] * dims[1] * dims[2] * 2
    hidden = fc_bias.shape[0] * n
    seq = rows // MB
    per, per_fc = width // n, hidden // n
    slots = lax.axis_index("dp") * MB + iota((seq_place.shape[0], 8, 128), 1)
    lens = jnp.where(seq_place[:, None, None] == slots, seq_lengths[:, None, None], 0)
    lens = jnp.sum(lens, axis=0).astype(F32)

    vectors = (ln1_gain, ln1_bias, q_bias, v_bias, out_bias, ln2_gain, ln2_bias, proj_bias, fc_bias)
    small, first = 0.0, 0
    for vector in vectors:
        small = small + jnp.pad(vector.astype(F32), (first, 1024 - first - vector.shape[0]))
        first += vector.shape[0]
    small = small.reshape(8, 128)
    groups = 4
    chunks = [(0, i, 3 * width // groups) for i in range(0, 3 * width, 3 * width // groups)] + [(1, 0, width)]
    chunks += [(2, i, width) for i in range(0, hidden, width)]
    chunks += [(3, i, width // 4) for i in range(0, width, width // 4)]
    kinds = [0, 0, 0, 0, 0, 0, 1, 0, 1, 0, 1, 0, 1]
    made = forward(dims, lens, tokens, cotangent, (w_qkv, w_out, w_fc, w_proj), small, chunks, kinds)
    out = made[14]
    dx, g_qkv, g_out, g_fc, g_proj, small = backward(dims, lens, tokens, (*made[4:14], made[15]), made[:4], groups)
    sizes = [per] * 8 + [per_fc]
    arrays, own = finish((out, dx.reshape(rows, width), g_qkv, g_out, g_fc, g_proj), small, sizes)
    out, dx, g_qkv, g_out, g_fc, g_proj = arrays
    g_ln1_gain, g_ln1_bias, g_q_bias, g_v_bias, g_out_bias, g_ln2_gain, g_ln2_bias, g_proj_bias, g_fc_bias = own
    return (out, dx, g_ln1_gain, g_ln1_bias, g_qkv, g_q_bias, g_v_bias, g_out, g_out_bias, g_ln2_gain, g_ln2_bias, g_fc, g_fc_bias, g_proj, g_proj_bias)


def solution(mesh):
    dims = grid_dims(mesh.shape["dp"])
    row, vec = P("dp", None), P("dp")
    return jax.shard_map(
        lambda *args: body(dims, *args),
        mesh=mesh,
        in_specs=(row, row, P(), P(), vec, vec, row, vec, vec, row, vec, vec, vec, row, vec, row, vec),
        out_specs=(row, row, vec, vec, row, vec, vec, row, vec, vec, vec, row, vec, row, vec),
        check_vma=False,
    )
```
